32 devices in a mesh: row: 8 (over z, x), col: 4 (over y, core).
Axes of the slice: x: 2, y: 2, z: 4, core: 2. Of those that a mesh axis runs over, the one named last changes fastest.
Arguments:
- layer_in: bfloat16 [8192, 768], P('row', 'col'), may hold values from -6 to 6
- cotangent: bfloat16 [8192, 768], P('row', 'col'), may hold values from -6 to 6
- token_ids: int32 [8192], P('row'), may hold values from 0 to 50303, as said below
- hash_table: int32 [50304], replicated, may hold values from 0 to 15, as said below
- prefix_len: int32 [1], replicated, may hold values from 819 to 4096
- w_query: bfloat16 [768, 768], P('row', 'col'), may hold values from -0.21875 to 0.21875
- w_key: bfloat16 [768, 768], P('row', 'col'), may hold values from -0.21875 to 0.21875
- w_value: bfloat16 [768, 768], P('row', 'col'), may hold values from -0.21875 to 0.21875
- w_output: bfloat16 [768, 768], P('row', 'col'), may hold values from -6 to 6
- bias_query: bfloat16 [64, 12], P('row', 'col'), may hold values from -0.59765625 to 0.59765625
- bias_value: bfloat16 [64, 12], P('row', 'col'), may hold values from -0.119628906 to 0.119628906
- gain_attn: bfloat16 [768], P('row'), may hold values from 0.5 to 1.5
- shift_attn: bfloat16 [768], P('row'), may hold values from -0.59765625 to 0.59765625
- gain_moe: bfloat16 [768], P('row'), may hold values from 0.5 to 1.5
- shift_moe: bfloat16 [768], P('row'), may hold values from -0.59765625 to 0.59765625
- bias_output: bfloat16 [768], P('row'), may hold values from -1.1953125 to 1.1953125
- w_up: bfloat16 [16, 768, 3072], P('row', None, 'col'), may hold values from -0.21875 to 0.21875
- bias_up: bfloat16 [16, 3072], P('row', 'col'), may hold values from -0.59765625 to 0.59765625
- w_down: bfloat16 [16, 3072, 768], P('row', 'col'), may hold values from -0.109375 to 0.109375
- bias_down: bfloat16 [16, 768], P('row'), may hold values from -0.59765625 to 0.59765625
Outputs:
- layer_out: bfloat16 [8192, 768], P('row', 'col')
- grad_in: float32 [8192, 768], P('row', 'col')
- grad_w_query: float32 [768, 768], P('row', 'col')
- grad_w_key: float32 [768, 768], P('row', 'col')
- grad_w_value: float32 [768, 768], P('row', 'col')
- grad_w_output: float32 [768, 768], P('row', 'col')
- grad_bias_query: float32 [64, 12], P('row', 'col')
- grad_bias_value: float32 [64, 12], P('row', 'col')
- grad_gain_attn: float32 [768], P('row')
- grad_shift_attn: float32 [768], P('row')
- grad_gain_moe: float32 [768], P('row')
- grad_shift_moe: float32 [768], P('row')
- grad_bias_output: float32 [768], P('row')
- grad_w_up: float32 [16, 768, 3072], P('row', None, 'col')
- grad_bias_up: float32 [16, 3072], P('row', 'col')
- grad_w_down: float32 [16, 3072, 768], P('row', 'col')
- grad_bias_down: float32 [16, 768], P('row')
The draws below stay inside these ranges and needn't reach their ends.
Inputs may be any that keep to these rules, and one draw needn't show every extreme that they name: `hash_table`: each expert is named by the same number of vocabulary ids. `token_ids`: in each aligned block of 1024 tokens (the tokens of one index of row) no expert receives more than 128 tokens, and one expert, the same in every block, receives exactly 128.
All inputs are finite; a program needn't handle non-finite values.
Results may differ from the reference program's by a relative error of at most 0.024.
Values may be sent and summed in bfloat16 or wider, within the bound.
A program may use at most 256 MiB of HBM per device.

```python
import jax
import jax.numpy as jnp
from jax import lax

D = 768
HEADS = 12
HD = 64
FF = 3072
VOCAB = 50304
TOK_DEV = 1024
TOKENS = 8192
SEQ_LEN = 8192
SEQS = 1
EXPERTS = 16
CAP = 128
N_ROW = 8


def routing_pair(key):
    order = jax.random.permutation(jax.random.fold_in(key, 11), VOCAB)
    table = jnp.zeros((VOCAB,), jnp.int32).at[order].set(jnp.arange(VOCAB, dtype=jnp.int32) % EXPERTS)
    star = jax.random.randint(jax.random.fold_in(key, 12), (), 0, EXPERTS)
    block_keys = jax.random.split(jax.random.fold_in(key, 13), TOKENS // TOK_DEV)

    def one_block(block_key):
        slot_key, row_key, pick_key = jax.random.split(block_key, 3)
        slots = jax.random.permutation(slot_key, (EXPERTS - 1) * CAP)[:TOK_DEV - CAP]
        others = slots // CAP
        others = (others + (others >= star).astype(jnp.int32)).astype(jnp.int32)
        chosen = jnp.concatenate([jnp.full((CAP,), star, jnp.int32), others])
        chosen = jax.random.permutation(row_key, chosen)
        column = jax.random.randint(pick_key, (TOK_DEV,), 0, VOCAB // EXPERTS)
        return order[chosen + EXPERTS * column]
    ids = jax.vmap(one_block)(block_keys).reshape(TOKENS)
    return (ids.astype(jnp.int32), table)


def draw_token_ids(key, part):
    return routing_pair(key)[0]


def draw_hash_table(key, part):
    return routing_pair(key)[1]


def steps_of(key, extent, pieces, least, high):
    level = 1.0
    for dim, blocks in pieces:
        draws = jax.random.uniform(jax.random.fold_in(jax.random.fold_in(key, 6), dim), (blocks,), jnp.float32, least / len(pieces), high / len(pieces))
        level = level * jnp.repeat(jnp.exp(draws), extent[dim] // blocks).reshape((-1,) + (1,) * (len(extent) - 1 - dim))
    return level


def normal_values(rng, shape, scale, bound, pieces=(), kind=jnp.bfloat16):
    loudness = steps_of(rng, shape, pieces, -0.22, 0.18) if pieces else 1.0
    drawn = jax.random.normal(rng, shape, jnp.float32) * scale * loudness
    return jnp.minimum(jnp.maximum(drawn, -bound), bound).astype(kind)


def setup_inputs(seed: int = 0) -> dict:
    key_list = jax.random.split(jax.random.key(seed), 21)
    layer_in = normal_values(key_list[0], (TOKENS, D), 1.0, 6.0, ((0, 8), (1, 4)))
    cotangent = normal_values(key_list[1], (TOKENS, D), 1.0, 6.0, ((0, 8), (1, 4)))
    token_ids = draw_token_ids(jax.random.fold_in(key_list[20], 71), 0)
    hash_table = draw_hash_table(jax.random.fold_in(key_list[20], 71), 0)
    prefix_len = jax.random.randint(key_list[4], (SEQS,), SEQ_LEN // 10, SEQ_LEN // 2 + 1).astype(jnp.int32)
    w_query = normal_values(key_list[5], (D, D), D ** -0.5, 0.21875, ((0, 8), (1, 4)))
    w_key = normal_values(key_list[6], (D, D), D ** -0.5, 0.21875, ((0, 8), (1, 4)))
    w_value = normal_values(key_list[7], (D, D), D ** -0.5, 0.21875, ((0, 8), (1, 4)))
    w_output = normal_values(key_list[8], (D, D), 1 ** -0.5, 6.0, ((0, 8), (1, 4)))
    bias_query = normal_values(key_list[9], (HD, HEADS), 0.1, 0.59765625, ((0, 8), (1, 4)))
    bias_value = normal_values(key_list[10], (HD, HEADS), 0.02, 0.119628906, ((0, 8), (1, 4)))
    gain_attn = jnp.clip(1.0 + 0.1 * jax.random.normal(key_list[11], (D,), jnp.float32), 0.5, 1.5).astype(jnp.bfloat16)
    shift_attn = normal_values(key_list[12], (D,), 0.1, 0.59765625, ((0, 8),))
    gain_moe = jnp.clip(1.0 + 0.1 * jax.random.normal(key_list[13], (D,), jnp.float32), 0.5, 1.5).astype(jnp.bfloat16)
    shift_moe = normal_values(key_list[14], (D,), 0.1, 0.59765625, ((0, 8),))
    bias_output = normal_values(key_list[15], (D,), 0.2, 1.1953125, ((0, 8),))
    w_up = normal_values(key_list[16], (EXPERTS, D, FF), D ** -0.5, 0.21875, ((0, 8), (2, 4)))
    bias_up = normal_values(key_list[17], (EXPERTS, FF), 0.1, 0.59765625, ((0, 8), (1, 4)))
    w_down = normal_values(key_list[18], (EXPERTS, FF, D), FF ** -0.5, 0.109375, ((0, 8), (1, 4)))
    bias_down = normal_values(key_list[19], (EXPERTS, D), 0.1, 0.59765625, ((0, 8),))
    return dict(layer_in=layer_in, cotangent=cotangent, token_ids=token_ids, hash_table=hash_table, prefix_len=prefix_len, w_query=w_query, w_key=w_key, w_value=w_value, w_output=w_output, bias_query=bias_query, bias_value=bias_value, gain_attn=gain_attn, shift_attn=shift_attn, gain_moe=gain_moe, shift_moe=shift_moe, bias_output=bias_output, w_up=w_up, bias_up=bias_up, w_down=w_down, bias_down=bias_down)


@jax.custom_vjp
def low(v):
    return lax.optimization_barrier(v.astype(jnp.bfloat16)).astype(jnp.float32)

@jax.custom_vjp
def low_back(v):
    return v

def low_keep(v):
    return (low(v), None)

def low_pass(kept, grad):
    return (grad,)

def back_keep(v):
    return (v, None)

def back_low(kept, grad):
    return (low(grad),)
low.defvjp(low_keep, low_pass)
low_back.defvjp(back_keep, back_low)
epsilon = 1e-05
neg_big = -1e+30
highest = lax.Precision.HIGHEST

def norm_rows(rows, gain, shift):
    centred = rows - lax.optimization_barrier(jnp.mean(rows, axis=-1, keepdims=True))
    spread = lax.optimization_barrier(jnp.mean(centred * centred, axis=-1, keepdims=True))
    return centred * lax.rsqrt(spread + epsilon) * gain + shift

def attend_sequence(seq_q, seq_k, seq_v, prefix):
    length = seq_q.shape[0]
    qblock = min(512, length)
    key_pos = jnp.arange(length, dtype=jnp.int32)
    scale = HD ** (-0.5)

    def one_block(start):
        block_q = lax.dynamic_slice_in_dim(seq_q, start, qblock, 0)
        query_pos = start + jnp.arange(qblock, dtype=jnp.int32)
        raw = jnp.einsum('qhd,khd->hqk', block_q, seq_k, precision=highest) * scale
        raw = low_back(raw)
        allowed = (key_pos[None, :] < prefix) | (key_pos[None, :] <= query_pos[:, None])
        scores = jnp.where(allowed[None], raw, neg_big)
        peak = lax.optimization_barrier(jnp.max(scores, axis=-1, keepdims=True))
        weights = jnp.exp(scores - peak)
        probs = weights / lax.optimization_barrier(jnp.sum(weights, axis=-1, keepdims=True))
        return jnp.einsum('hqk,khd->qhd', low(probs), seq_v, precision=highest)
    starts = (jnp.arange(length // qblock) * qblock).astype(jnp.int32)
    blocks = lax.map(jax.checkpoint(one_block), starts)
    return blocks.reshape(length, HEADS, HD)

def layer(layer_in, w_query, w_key, w_value, w_output, bias_query, bias_value, gain_attn, shift_attn, gain_moe, shift_moe, bias_output, w_up, bias_up, w_down, bias_down, expert_of, slot_of, prefix_len):
    h_attn = low(norm_rows(layer_in, gain_attn, shift_attn))
    queries = low(low_back(jnp.dot(h_attn, w_query, precision=highest) + bias_query.T.reshape(D)))
    keys = low(low_back(jnp.dot(h_attn, w_key, precision=highest)))
    values = low(low_back(jnp.dot(h_attn, w_value, precision=highest) + bias_value.T.reshape(D)))

    def per_sequence(carry, item):
        seq_q, seq_k, seq_v, prefix = item
        return (carry, attend_sequence(seq_q, seq_k, seq_v, prefix))
    shaped = (queries.reshape(SEQS, SEQ_LEN, HEADS, HD), keys.reshape(SEQS, SEQ_LEN, HEADS, HD), values.reshape(SEQS, SEQ_LEN, HEADS, HD), prefix_len)
    _, attended = lax.scan(per_sequence, None, shaped)
    attended = low(low_back(attended.reshape(TOKENS, D)))
    branch = low_back(jnp.dot(attended, w_output.T, precision=highest))
    mid = layer_in + branch + bias_output
    h_moe = low(low_back(norm_rows(mid, gain_moe, shift_moe)))
    buffer = jnp.zeros((EXPERTS, N_ROW * CAP, D), jnp.float32).at[expert_of, slot_of].set(h_moe)
    pre_act = jnp.einsum('ecd,edf->ecf', buffer, w_up, precision=highest) + bias_up[:, None, :]
    hidden = low(jax.nn.gelu(low_back(pre_act), approximate=False))
    expert_out = jnp.einsum('ecf,efd->ecd', hidden, w_down, precision=highest) + bias_down[:, None, :]
    expert_out = low(low_back(expert_out))
    return mid + expert_out[expert_of, slot_of]

def reference(layer_in, cotangent, token_ids, hash_table, prefix_len, w_query, w_key, w_value, w_output, bias_query, bias_value, gain_attn, shift_attn, gain_moe, shift_moe, bias_output, w_up, bias_up, w_down, bias_down):
    expert_of = hash_table[token_ids].astype(jnp.int32)
    hits = (expert_of[:, None] == jnp.arange(EXPERTS, dtype=jnp.int32)[None, :]).astype(jnp.int32)
    slot_of = lax.optimization_barrier(jnp.sum(hits * (jnp.cumsum(hits, axis=0).astype(jnp.int32) - 1), axis=1)).astype(jnp.int32)
    floats = [a.astype(jnp.float32) for a in (layer_in, w_query, w_key, w_value, w_output, bias_query, bias_value, gain_attn, shift_attn, gain_moe, shift_moe, bias_output, w_up, bias_up, w_down, bias_down)]

    def forward(*values_in):
        return layer(*values_in, expert_of, slot_of, prefix_len)
    result, pull = jax.vjp(forward, *floats)
    grads = pull(cotangent.astype(jnp.float32))
    return (result.astype(jnp.bfloat16), grads[0], grads[1], grads[2], grads[3], grads[4], grads[5], grads[6], grads[7], grads[8], grads[9], grads[10], grads[11], grads[12], grads[13], grads[14], grads[15])
```

```python
import functools

import jax
import jax.numpy as jnp
from jax import lax
from jax.experimental import pallas as pl
from jax.experimental.pallas import tpu as pltpu
from jax.sharding import PartitionSpec as P

D = 768
HD = 64
EXP_DEV = 2
LENGTH = 8192
PREFIX_MAX = 4096
COLS = 4

F32 = jnp.float32
BF16 = jnp.bfloat16
MESH = pl.DeviceIdType.MESH
LOG2E = 1.4426950408889634

epsilon = 1e-05
neg_big = -1e30

VSPEC = pl.BlockSpec(memory_space=pltpu.VMEM)
SSPEC = pl.BlockSpec(memory_space=pltpu.SMEM)
VMEM_BYTES = 64 * 1000 * 1000
DMA = pltpu.SemaphoreType.DMA


def params(collective=None):
    if collective is None:
        return pltpu.CompilerParams(vmem_limit_bytes=VMEM_BYTES)
    return pltpu.CompilerParams(
        vmem_limit_bytes=VMEM_BYTES, collective_id=collective, has_side_effects=True
    )


def push(src, dst, send_sem, recv_sem, peer):
    return pltpu.make_async_remote_copy(
        src_ref=src,
        dst_ref=dst,
        send_sem=send_sem,
        recv_sem=recv_sem,
        device_id=peer,
        device_id_type=MESH,
    )


def greet(peers):
    barrier = pltpu.get_barrier_semaphore()
    for peer in peers:
        pl.semaphore_signal(barrier, inc=1, device_id=peer, device_id_type=MESH)
    pl.semaphore_wait(barrier, len(peers))


def col_places():
    me = lax.axis_index("col")
    sib = me + 1 - 2 * (me % 2)
    across = (me + 2) % COLS
    diag = (sib + 2) % COLS
    return me, sib, across, diag


def start_kernel(
    rows, pieces, x_ref, w_ref, s_ref, xo_ref, wo_ref, so_ref, c_send, c_recv, r_send, r_recv
):
    me, sib, across, _ = col_places()
    row = lax.axis_index("row")
    peers = [{"row": (row + k) % rows} for k in range(1, rows)]
    greet(peers + [{"col": sib}, {"col": across}])
    step = x_ref.shape[0] // pieces
    sent = []
    for i in range(pieces):
        part = pl.ds(i * step, step)
        for way, peer in ((0, across), (1, sib)):
            copy = push(
                x_ref.at[part],
                xo_ref.at[me, part],
                c_send.at[way, i],
                c_recv.at[way, i],
                {"col": peer},
            )
            copy.start()
            sent.append(copy)
    row_copies = []
    for k, peer in enumerate(peers):
        for j, (src, dst) in enumerate(((w_ref, wo_ref), (s_ref, so_ref))):
            copy = push(src, dst.at[row], r_send.at[j, k], r_recv.at[j, k], peer)
            copy.start()
            row_copies.append(copy)
    xo_ref[me] = x_ref[...]
    wo_ref[row] = w_ref[...]
    so_ref[row] = s_ref[...]
    for i in range(pieces):
        part = pl.ds(i * step, step)
        sent[2 * i].wait_recv()
        copy = push(
            xo_ref.at[across, part],
            xo_ref.at[across, part],
            c_send.at[2, i],
            c_recv.at[2, i],
            {"col": sib},
        )
        copy.start()
        row_copies.append(copy)
    for i in range(pieces):
        sent[2 * i].wait_send()
        sent[2 * i + 1].wait()
    for copy in row_copies:
        copy.wait()


def start_gather(x, w, s, rows):
    pieces = 4
    return pl.pallas_call(
        functools.partial(start_kernel, rows, pieces),
        out_shape=(
            jax.ShapeDtypeStruct((COLS,) + x.shape, x.dtype),
            jax.ShapeDtypeStruct((rows,) + w.shape, w.dtype),
            jax.ShapeDtypeStruct((rows,) + s.shape, s.dtype),
        ),
        in_specs=[VSPEC] * 3,
        out_specs=(VSPEC,) * 3,
        scratch_shapes=[
            DMA((3, pieces)),
            DMA((3, pieces)),
            DMA((2, rows - 1)),
            DMA((2, rows - 1)),
        ],
        compiler_params=params(0),
    )(x, w, s)


def col_gather_kernel(pieces, x_ref, xo_ref, c_send, c_recv):
    me, sib, across, _ = col_places()
    greet([{"col": sib}, {"col": across}])
    step = x_ref.shape[0] // pieces
    sent, late = [], []
    for i in range(pieces):
        part = pl.ds(i * step, step)
        for way, peer in ((0, across), (1, sib)):
            copy = push(
                x_ref.at[part],
                xo_ref.at[me, part],
                c_send.at[way, i],
                c_recv.at[way, i],
                {"col": peer},
            )
            copy.start()
            sent.append(copy)
    xo_ref[me] = x_ref[...]
    for i in range(pieces):
        part = pl.ds(i * step, step)
        sent[2 * i].wait_recv()
        copy = push(
            xo_ref.at[across, part],
            xo_ref.at[across, part],
            c_send.at[2, i],
            c_recv.at[2, i],
            {"col": sib},
        )
        copy.start()
        late.append(copy)
    for i in range(pieces):
        sent[2 * i].wait_send()
        sent[2 * i + 1].wait()
        late[i].wait()


def col_gather(x, collective):
    pieces = 4
    return pl.pallas_call(
        functools.partial(col_gather_kernel, pieces),
        out_shape=jax.ShapeDtypeStruct((COLS,) + x.shape, x.dtype),
        in_specs=[VSPEC],
        out_specs=VSPEC,
        scratch_shapes=[DMA((3, pieces)), DMA((3, pieces))],
        compiler_params=params(collective),
    )(x)


def small_kernel(x_ref, xo_ref, c_send, c_recv):
    me = lax.axis_index("col")
    peers = [{"col": (me + k) % COLS} for k in range(1, COLS)]
    greet(peers)
    copies = []
    for k, peer in enumerate(peers):
        copy = push(x_ref, xo_ref.at[me], c_send.at[k], c_recv.at[k], peer)
        copy.start()
        copies.append(copy)
    xo_ref[me] = x_ref[...]
    for copy in copies:
        copy.wait()


def small_gather(x, collective):
    return pl.pallas_call(
        small_kernel,
        out_shape=jax.ShapeDtypeStruct((COLS,) + x.shape, x.dtype),
        in_specs=[VSPEC],
        out_specs=VSPEC,
        scratch_shapes=[DMA((COLS - 1,)), DMA((COLS - 1,))],
        compiler_params=params(collective),
    )(x)


def line_places(group):
    row = lax.axis_index("row")
    place = row % group
    level, side = place // 2, place % 2
    return row, place, level, side, row + 1 - 2 * side


def line_greet(levels, row, level, partner):
    barrier = pltpu.get_barrier_semaphore()
    pl.semaphore_signal(barrier, inc=1, device_id={"row": partner}, device_id_type=MESH)

    @pl.when(level > 0)
    def _():
        pl.semaphore_signal(barrier, inc=1, device_id={"row": row - 2}, device_id_type=MESH)

    @pl.when(level < levels - 1)
    def _():
        pl.semaphore_signal(barrier, inc=1, device_id={"row": row + 2}, device_id_type=MESH)

    count = 1 + (level > 0).astype(jnp.int32) + (level < levels - 1).astype(jnp.int32)
    pl.semaphore_wait(barrier, count)


def kv_kernel(
    group, low, pieces, kv_ref, out_ref, u_send, u_recv, d_send, d_recv, x_send, x_recv
):
    levels = group // 2
    row, place, level, side, partner = line_places(group)
    step = kv_ref.shape[0] // pieces
    line_greet(levels, row, level, partner)

    def make(at, i, way, src=None):
        part = pl.ds(i * step, step)
        dst = out_ref.at[2 * at + side, part]
        sems = ((u_send, u_recv), (d_send, d_recv), (x_send, x_recv))[way]
        peer = (row + 2, row - 2, partner)[way]
        return push(
            dst if src is None else src.at[part],
            dst,
            sems[0].at[at, i],
            sems[1].at[at, i],
            {"row": peer},
        )

    def other(at, i):
        part = pl.ds(i * step, step)
        dst = out_ref.at[2 * at + 1 - side, part]
        return push(dst, dst, x_send.at[at, i], x_recv.at[at, i], {"row": partner})

    def when(cond, run):
        @pl.when(cond)
        def _():
            for i in range(pieces):
                run(i)

    to_up = level < levels - 1
    own_down = (level > 0) & (level < low)
    own_side = (level < low) | (side == 0)
    for i in range(pieces):

        @pl.when(to_up)
        def _(i=i):
            make(level, i, 0, kv_ref).start()

        @pl.when(own_side)
        def _(i=i):
            make(level, i, 2, kv_ref).start()

        @pl.when(own_down)
        def _(i=i):
            make(level, i, 1, kv_ref).start()

    out_ref[place] = kv_ref[...]

    for k in range(1, levels):
        at = level - k
        for i in range(pieces):

            @pl.when(at >= 0)
            def _(at=at, i=i):
                make(at, i, 0).wait_recv()

                @pl.when(to_up)
                def _():
                    make(at, i, 0).start()

                make(at, i, 2).start()

    for k in range(1, low):
        at = level + k
        for i in range(pieces):

            @pl.when(at < low)
            def _(at=at, i=i):
                make(at, i, 1).wait_recv()

                @pl.when(level > 0)
                def _():
                    make(at, i, 1).start()

                make(at, i, 2).start()

    for at in range(levels):
        comes = (at < level) | ((at == level) & (side == 1)) if at >= low else None
        if comes is None:
            for i in range(pieces):
                other(at, i).wait_recv()
        else:
            when(comes, lambda i, at=at: other(at, i).wait_recv())

    when(to_up, lambda i: make(level, i, 0, kv_ref).wait_send())
    when(own_side, lambda i: make(level, i, 2, kv_ref).wait_send())
    when(own_down, lambda i: make(level, i, 1, kv_ref).wait_send())
    for k in range(1, levels):
        at = level - k
        when((at >= 0) & to_up, lambda i, at=at: make(at, i, 0).wait_send())
        when(at >= 0, lambda i, at=at: make(at, i, 2).wait_send())
    for k in range(1, low):
        at = level + k
        when((at < low) & (level > 0), lambda i, at=at: make(at, i, 1).wait_send())
        when(at < low, lambda i, at=at: make(at, i, 2).wait_send())


def kv_gather(kv, group, low, collective):
    pieces = 4
    levels = group // 2
    return pl.pallas_call(
        functools.partial(kv_kernel, group, low, pieces),
        out_shape=jax.ShapeDtypeStruct((group,) + kv.shape, kv.dtype),
        in_specs=[VSPEC],
        out_specs=VSPEC,
        scratch_shapes=[DMA((levels, pieces))] * 6,
        compiler_params=params(collective),
    )(kv)


def dkv_kernel(
    group,
    low,
    pieces,
    part_ref,
    out_ref,
    rx_ref,
    above_ref,
    below_ref,
    snd_ref,
    acc_ref,
    u_send,
    u_recv,
    d_send,
    d_recv,
    x_send,
    x_recv,
):
    levels = group // 2
    row, place, level, side, partner = line_places(group)
    step = out_ref.shape[0] // pieces
    line_greet(levels, row, level, partner)

    def cross(at, i):
        part = pl.ds(i * step, step)
        return push(
            part_ref.at[2 * at + 1 - side, part],
            rx_ref.at[at, part],
            x_send.at[at, i],
            x_recv.at[at, i],
            {"row": partner},
        )

    def line(at, i, up):
        part = pl.ds(i * step, step)
        sems = (u_send, u_recv) if up else (d_send, d_recv)
        return push(
            snd_ref.at[at, part],
            (below_ref if up else above_ref).at[at, part],
            sems[0].at[at, i],
            sems[1].at[at, i],
            {"row": row + 2 if up else row - 2},
        )

    def gone(at):
        return (at < low) | (at < level) | ((at == level) & (side == 1))

    def comes(at):
        return (at < low) | (at < level) | ((at == level) & (side == 0))

    for at in range(levels):
        for i in range(pieces):

            @pl.when(gone(at))
            def _(at=at, i=i):
                cross(at, i).start()

    def total(at, i, from_above, from_below):
        part = pl.ds(i * step, step)
        acc_ref[...] = part_ref[2 * at + side, part].astype(F32)

        @pl.when(comes(at))
        def _():
            cross(at, i).wait_recv()
            acc_ref[...] += rx_ref[at, part].astype(F32)

        @pl.when(from_above)
        def _():
            line(at, i, False).wait_recv()
            acc_ref[...] += above_ref[at, part].astype(F32)

        @pl.when(from_below)
        def _():
            line(at, i, True).wait_recv()
            acc_ref[...] += below_ref[at, part].astype(F32)

    not_top = level < levels - 1
    for at in range(levels - 1):
        for i in range(pieces):

            @pl.when(at < level)
            def _(at=at, i=i):
                total(at, i, not_top, jnp.bool_(False) if at >= low else jnp.bool_(False))
                snd_ref[at, pl.ds(i * step, step)] = acc_ref[...].astype(BF16)
                line(at, i, False).start()

    for at in range(low - 1, 0, -1):
        for i in range(pieces):

            @pl.when(at > level)
            def _(at=at, i=i):
                total(at, i, jnp.bool_(False), level > 0)
                snd_ref[at, pl.ds(i * step, step)] = acc_ref[...].astype(BF16)
                line(at, i, True).start()

    for i in range(pieces):
        total(level, i, not_top, (level > 0) & (level < low))
        out_ref[pl.ds(i * step, step)] = acc_ref[...].astype(BF16)

    for at in range(levels):
        for i in range(pieces):

            @pl.when(gone(at))
            def _(at=at, i=i):
                cross(at, i).wait_send()

            @pl.when(at < level)
            def _(at=at, i=i):
                line(at, i, False).wait_send()

            if at < low:

                @pl.when(at > level)
                def _(at=at, i=i):
                    line(at, i, True).wait_send()


def dkv_scatter(parts, group, low, collective):
    pieces = 4
    levels = group // 2
    _, tokens, width = parts.shape
    block = pltpu.VMEM((levels, tokens, width), BF16)
    return pl.pallas_call(
        functools.partial(dkv_kernel, group, low, pieces),
        out_shape=jax.ShapeDtypeStruct((tokens, width), BF16),
        in_specs=[VSPEC],
        out_specs=VSPEC,
        scratch_shapes=[
            block,
            block,
            pltpu.VMEM((low, tokens, width), BF16),
            block,
            pltpu.VMEM((tokens // pieces, width), F32),
        ]
        + [DMA((levels, pieces))] * 6,
        compiler_params=params(collective),
    )(parts)


def product_kernel(pieces, a_ref, b_ref, out_ref, snd_ref, rx_ref, far_ref, tot_ref, send, recv):
    me, sib, across, diag = col_places()
    greet([{"col": sib}, {"col": across}])
    step = a_ref.shape[0] // pieces

    def term(i, who):
        return lax.dot_general(
            a_ref[pl.ds(i * step, step)],
            b_ref[who],
            (((1,), (1,)), ((), ())),
            preferred_element_type=F32,
        )

    def near(i, j):
        part = pl.ds(i * step, step)
        return push(
            snd_ref.at[j, part], rx_ref.at[j, part], send.at[j, i], recv.at[j, i], {"col": sib}
        )

    def over(i):
        part = pl.ds(i * step, step)
        return push(tot_ref.at[part], far_ref.at[part], send.at[2, i], recv.at[2, i], {"col": across})

    for i in range(pieces):
        snd_ref[0, pl.ds(i * step, step)] = term(i, diag).astype(BF16)
        near(i, 0).start()
    for i in range(pieces):
        part = pl.ds(i * step, step)
        mine = term(i, across)
        near(i, 0).wait_recv()
        tot_ref[part] = (mine + rx_ref[0, part].astype(F32)).astype(BF16)
        over(i).start()
    for i in range(pieces):
        snd_ref[1, pl.ds(i * step, step)] = term(i, sib).astype(BF16)
        near(i, 1).start()
    for i in range(pieces):
        part = pl.ds(i * step, step)
        mine = term(i, me)
        near(i, 1).wait_recv()
        mine = mine + rx_ref[1, part].astype(F32)
        over(i).wait_recv()
        out_ref[part] = mine + far_ref[part].astype(F32)
    for i in range(pieces):
        near(i, 0).wait_send()
        near(i, 1).wait_send()
        over(i).wait_send()


def product_scatter(a, b, collective):
    pieces = 4
    tokens, width = a.shape[0], b.shape[1]
    block = pltpu.VMEM((tokens, width), BF16)
    pair = pltpu.VMEM((2, tokens, width), BF16)
    return pl.pallas_call(
        functools.partial(product_kernel, pieces),
        out_shape=jax.ShapeDtypeStruct((tokens, width), F32),
        in_specs=[VSPEC] * 2,
        out_specs=VSPEC,
        scratch_shapes=[pair, pair, block, block, DMA((3, pieces)), DMA((3, pieces))],
        compiler_params=params(collective),
    )(a, b)


def dispatch_kernel(rows, in_ref, out_ref, r_send, r_recv, c_send, c_recv):
    me, sib, across, _ = col_places()
    row = lax.axis_index("row")
    peers = [(row + k) % rows for k in range(1, rows)]
    greet([{"row": p} for p in peers] + [{"col": sib}, {"col": across}])
    copies = []
    for k, peer in enumerate(peers):
        copy = push(
            in_ref.at[peer], out_ref.at[me, row], r_send.at[k], r_recv.at[k], {"row": peer}
        )
        copy.start()
        copies.append(copy)

    def col(src, dst, k, way):
        return push(
            src, dst, c_send.at[way, k], c_recv.at[way, k], {"col": across if way == 0 else sib}
        )

    done, first = [], []
    for way in range(2):
        copy = col(in_ref.at[row], out_ref.at[me, row], 0, way)
        copy.start()
        (first if way == 0 else done).append(copy)
    out_ref[me, row] = in_ref[row]
    sources = [row] + [(row + rows - k) % rows for k in range(1, rows)]

    def forward(k):
        first[k].wait_recv()
        src = sources[k]
        copy = col(out_ref.at[across, src], out_ref.at[across, src], k, 2)
        copy.start()
        done.append(copy)

    for k in range(1, rows):
        copies[k - 1].wait_recv()
        block = out_ref.at[me, sources[k]]
        for way in range(2):
            copy = col(block, block, k, way)
            copy.start()
            (first if way == 0 else done).append(copy)
        forward(k - 1)
    forward(rows - 1)
    for copy in copies:
        copy.wait_send()
    for copy in first:
        copy.wait_send()
    for copy in done:
        copy.wait()


def dispatch(x, rows, collective):
    return pl.pallas_call(
        functools.partial(dispatch_kernel, rows),
        out_shape=jax.ShapeDtypeStruct((COLS,) + x.shape, x.dtype),
        in_specs=[VSPEC],
        out_specs=VSPEC,
        scratch_shapes=[DMA((rows - 1,)), DMA((rows - 1,)), DMA((3, rows)), DMA((3, rows))],
        compiler_params=params(collective),
    )(x)


def giveback_kernel(
    rows, in_ref, bias_ref, out_ref, rx_ref, far_ref, tot_ref, fin_ref, send, recv, r_send, r_recv
):
    me, sib, across, diag = col_places()
    row = lax.axis_index("row")
    order = [(row + k) % rows for k in range(1, rows)] + [row]
    greet([{"row": p} for p in order[:-1]] + [{"col": sib}, {"col": across}])

    def near(k, j):
        who = diag if j == 0 else sib
        return push(
            in_ref.at[who, order[k]], rx_ref.at[j, k], send.at[j, k], recv.at[j, k], {"col": sib}
        )

    def over(k):
        return push(tot_ref.at[k], far_ref.at[k], send.at[2, k], recv.at[2, k], {"col": across})

    def home(k):
        return push(
            fin_ref.at[k], out_ref.at[row], r_send.at[k], r_recv.at[k], {"row": order[k]}
        )

    for k in range(rows):
        near(k, 0).start()
        near(k, 1).start()

    def finish(k):
        near(k, 1).wait_recv()
        over(k).wait_recv()
        total = in_ref[me, order[k]].astype(F32) + rx_ref[1, k].astype(F32)
        total = total + far_ref[k].astype(F32) + bias_ref[...]
        if k == rows - 1:
            out_ref[row] = total.astype(BF16)
        else:
            fin_ref[k] = total.astype(BF16)
            home(k).start()

    for k in range(rows):
        near(k, 0).wait_recv()
        tot_ref[k] = (in_ref[across, order[k]].astype(F32) + rx_ref[0, k].astype(F32)).astype(BF16)
        over(k).start()
        if k >= 1:
            finish(k - 1)
    finish(rows - 1)
    for k in range(rows):
        near(k, 0).wait_send()
        near(k, 1).wait_send()
        over(k).wait_send()
        if k < rows - 1:
            home(k).wait()


def giveback(parts, bias, rows, collective):
    block = parts.shape[2:]
    one = pltpu.VMEM((rows,) + block, BF16)
    return pl.pallas_call(
        functools.partial(giveback_kernel, rows),
        out_shape=jax.ShapeDtypeStruct((rows,) + block, BF16),
        in_specs=[VSPEC] * 2,
        out_specs=VSPEC,
        scratch_shapes=[
            pltpu.VMEM((2, rows) + block, BF16),
            one,
            one,
            one,
            DMA((3, rows)),
            DMA((3, rows)),
            DMA((rows - 1,)),
            DMA((rows - 1,)),
        ],
        compiler_params=params(collective),
    )(parts, bias)


def end_kernel(rows, w_ref, s_ref, wo_ref, so_ref, wr_ref, sr_ref, send, recv):
    row = lax.axis_index("row")
    peers = [(row + k) % rows for k in range(1, rows)]
    greet([{"row": p} for p in peers])
    copies = []
    for k, peer in enumerate(peers):
        for j, (src, dst) in enumerate(((w_ref, wr_ref), (s_ref, sr_ref))):
            copy = push(src.at[peer], dst.at[k], send.at[j, k], recv.at[j, k], {"row": peer})
            copy.start()
            copies.append(copy)
    wo_ref[...] = w_ref[row].astype(F32)
    so_ref[...] = s_ref[row]
    for k in range(rows - 1):
        copies[2 * k].wait_recv()
        copies[2 * k + 1].wait_recv()
        wo_ref[...] += wr_ref[k].astype(F32)
        so_ref[...] += sr_ref[k]
    for copy in copies:
        copy.wait_send()


def end_scatter(w, s, rows, collective):
    return pl.pallas_call(
        functools.partial(end_kernel, rows),
        out_shape=(
            jax.ShapeDtypeStruct(w.shape[1:], F32),
            jax.ShapeDtypeStruct(s.shape[1:], F32),
        ),
        in_specs=[VSPEC] * 2,
        out_specs=(VSPEC,) * 2,
        scratch_shapes=[
            pltpu.VMEM((rows - 1,) + w.shape[1:], w.dtype),
            pltpu.VMEM((rows - 1,) + s.shape[1:], s.dtype),
            DMA((2, rows - 1)),
            DMA((2, rows - 1)),
        ],
        compiler_params=params(collective),
    )(w, s)


def nt(left, right):
    return lax.dot_general(left, right, (((1,), (1,)), ((), ())), preferred_element_type=F32)


def nn(left, right):
    return lax.dot_general(left, right, (((1,), (0,)), ((), ())), preferred_element_type=F32)


def tn(left, right):
    return lax.dot_general(left, right, (((0,), (0,)), ((), ())), preferred_element_type=F32)


def seen(key_start, query_start, shape, prefix):
    key = key_start + lax.broadcasted_iota(jnp.int32, shape, 0)
    query = query_start + lax.broadcasted_iota(jnp.int32, shape, 1)
    return (key < prefix) | (key <= query)


def forward_kernel(
    low_blocks, kb, qb, info_ref, q_ref, kv_ref, o_ref, ob_ref, lse_ref, m_ref, acc_ref
):
    place, prefix = info_ref[0], info_ref[1]
    tokens, width = q_ref.shape
    heads = width // HD
    per = tokens // kb
    ext = HD + 16
    m_ref[...] = jnp.full(m_ref.shape, neg_big, F32)
    acc_ref[...] = jnp.zeros(acc_ref.shape, F32)

    def block(j, masked):
        blk = j // per
        start = pl.multiple_of((j % per) * kb, kb)
        rows = kv_ref[blk, pl.ds(start, kb), :]
        for h in range(heads):
            k = rows[:, h * HD : (h + 1) * HD]
            v = rows[:, width + h * HD : width + (h + 1) * HD]
            v_ext = jnp.concatenate([v.T, jnp.ones((16, kb), BF16)], axis=0)
            for i in range(tokens // qb):
                cols = slice(i * qb, (i + 1) * qb)
                raw = nt(k, q_ref[cols, h * HD : (h + 1) * HD]) * LOG2E
                if masked:
                    allowed = seen(j * kb, place * tokens + i * qb, raw.shape, prefix)
                    raw = jnp.where(allowed, raw, neg_big)
                old = m_ref[h : h + 1, cols]
                new = jnp.maximum(old, jnp.max(raw, axis=0, keepdims=True))
                m_ref[h : h + 1, cols] = new
                weights = jnp.exp2(raw - new).astype(BF16)
                acc_ref[h, :, cols] = acc_ref[h, :, cols] * jnp.exp2(old - new) + nn(
                    v_ext, weights
                )

    def run(masked):
        def body(j, carry):
            block(j, masked)
            return carry

        return body

    lax.fori_loop(0, place * per, run(False), 0)
    lax.fori_loop(place * per, jnp.maximum(place + 1, low_blocks) * per, run(True), 0)
    for h in range(heads):
        total = acc_ref[h, HD : HD + 1, :]
        out = (acc_ref[h, :HD, :] / total).T
        o_ref[:, h * HD : (h + 1) * HD] = out
        ob_ref[:, h * HD : (h + 1) * HD] = out.astype(BF16)
        lse_ref[h : h + 1, :] = m_ref[h : h + 1, :] + jnp.log2(total)


def attention_forward(info, q, kv_all, low_blocks):
    tokens, width = q.shape
    heads = width // HD
    return pl.pallas_call(
        functools.partial(forward_kernel, low_blocks, 512, 512),
        out_shape=(
            jax.ShapeDtypeStruct((tokens, width), F32),
            jax.ShapeDtypeStruct((tokens, width), BF16),
            jax.ShapeDtypeStruct((8, tokens), F32),
        ),
        in_specs=[SSPEC, VSPEC, VSPEC],
        out_specs=(VSPEC,) * 3,
        scratch_shapes=[
            pltpu.VMEM((8, tokens), F32),
            pltpu.VMEM((heads, HD + 16, tokens), F32),
        ],
        compiler_params=params(),
    )(info, q, kv_all)


def backward_kernel(
    low_blocks, kb, info_ref, q_ref, kv_ref, do_ref, lse_ref, delta_ref, dq_ref, dkv_ref, dqt_ref
):
    place, prefix = info_ref[0], info_ref[1]
    tokens, width = q_ref.shape
    heads = width // HD
    per = tokens // kb
    dqt_ref[...] = jnp.zeros(dqt_ref.shape, F32)

    def block(j, masked):
        blk = j // per
        start = pl.multiple_of((j % per) * kb, kb)
        rows = kv_ref[blk, pl.ds(start, kb), :]
        for h in range(heads):
            feats = slice(h * HD, (h + 1) * HD)
            k = rows[:, feats]
            v = rows[:, width + h * HD : width + (h + 1) * HD]
            q, do = q_ref[:, feats], do_ref[:, feats]
            probs = jnp.exp2(nt(k, q) * LOG2E - lse_ref[h : h + 1, :])
            if masked:
                allowed = seen(j * kb, place * tokens, probs.shape, prefix)
                probs = jnp.where(allowed, probs, 0.0)
            grad = (probs * (nt(v, do) - delta_ref[h : h + 1, :])).astype(BF16)
            dkv_ref[blk, pl.ds(start, kb), feats] = nn(grad, q).astype(BF16)
            dkv_ref[blk, pl.ds(start, kb), width + h * HD : width + (h + 1) * HD] = nn(
                probs.astype(BF16), do
            ).astype(BF16)
            dqt_ref[feats, :] += nn(k.T, grad)

    def run(masked):
        def body(j, carry):
            block(j, masked)
            return carry

        return body

    lax.fori_loop(0, place * per, run(False), 0)
    lax.fori_loop(place * per, jnp.maximum(place + 1, low_blocks) * per, run(True), 0)
    dq_ref[...] = (dqt_ref[...] * HD**-0.5).T.astype(BF16)


def attention_backward(info, q, kv_all, do, lse, delta, low_blocks):
    tokens, width = q.shape
    return pl.pallas_call(
        functools.partial(backward_kernel, low_blocks, 256),
        out_shape=(
            jax.ShapeDtypeStruct((tokens, width), BF16),
            jax.ShapeDtypeStruct(kv_all.shape, BF16),
        ),
        in_specs=[SSPEC] + [VSPEC] * 5,
        out_specs=(VSPEC,) * 2,
        scratch_shapes=[pltpu.VMEM((width, tokens), F32)],
        compiler_params=params(),
    )(info, q, kv_all, do, lse, delta)


def expert_kernel(
    x_ref, up_ref, bias_ref, down_ref, part_ref, gup_ref, gbu_ref, gdown_ref, gbd_ref
):
    cols, rows, _, cap, both = x_ref.shape
    width = both // 2
    slots = rows * cap
    blocks = [x_ref[b, :, 0].reshape(slots, both) for b in range(cols)]
    x = jnp.concatenate([b[:, :width] for b in blocks], axis=1)
    g = jnp.concatenate([b[:, width:] for b in blocks], axis=1)
    gbd_ref[...] = jnp.sum(g.astype(F32), axis=0).reshape(gbd_ref.shape)
    hidden_units = up_ref.shape[2]
    chunk = 256
    part = jnp.zeros((slots, cols * width), F32)
    gx = jnp.zeros((slots, cols * width), F32)
    for f in range(hidden_units // chunk):
        cut = slice(f * chunk, (f + 1) * chunk)
        up, down = up_ref[0, :, cut], down_ref[0, cut, :]
        pre = nn(x, up) + bias_ref[0, :, cut].astype(F32)
        cdf = 0.5 * (1.0 + lax.erf(pre * (0.5**0.5)))
        slope = cdf + pre * (jnp.exp(-0.5 * pre * pre) * 0.3989422804014327)
        hidden = (pre * cdf).astype(BF16)
        grad = nt(g, down) * slope
        grad = grad.astype(BF16)
        part = part + nn(hidden, down)
        gx = gx + nt(grad, up)
        gdown_ref[0, cut, :] = tn(hidden, g)
        gup_ref[0, :, cut] = tn(x, grad)
        gbu_ref[0, :, cut] = jnp.sum(grad.astype(F32), axis=0, keepdims=True)
    for b in range(cols):
        cut = slice(b * width, (b + 1) * width)
        both_parts = jnp.concatenate([part[:, cut].astype(BF16), gx[:, cut].astype(BF16)], axis=1)
        part_ref[b, :, 0] = both_parts.reshape(rows, cap, both)


def experts(x, w_up, bias_up, w_down):
    cols, rows, count, cap, both = x.shape
    _, features, hidden = w_up.shape
    return pl.pallas_call(
        expert_kernel,
        grid=(count,),
        out_shape=(
            jax.ShapeDtypeStruct(x.shape, BF16),
            jax.ShapeDtypeStruct(w_up.shape, F32),
            jax.ShapeDtypeStruct((count, 1, hidden), F32),
            jax.ShapeDtypeStruct(w_down.shape, F32),
            jax.ShapeDtypeStruct((count, 1, features), F32),
        ),
        in_specs=[
            pl.BlockSpec((cols, rows, 1, cap, both), lambda e: (0, 0, e, 0, 0)),
            pl.BlockSpec((1, features, hidden), lambda e: (e, 0, 0)),
            pl.BlockSpec((1, 1, hidden), lambda e: (e, 0, 0)),
            pl.BlockSpec((1, hidden, features), lambda e: (e, 0, 0)),
        ],
        out_specs=(
            pl.BlockSpec((cols, rows, 1, cap, both), lambda e: (0, 0, e, 0, 0)),
            pl.BlockSpec((1, features, hidden), lambda e: (e, 0, 0)),
            pl.BlockSpec((1, 1, hidden), lambda e: (e, 0, 0)),
            pl.BlockSpec((1, hidden, features), lambda e: (e, 0, 0)),
            pl.BlockSpec((1, 1, features), lambda e: (e, 0, 0)),
        ),
        compiler_params=params(),
    )(x, w_up, bias_up.reshape(count, 1, hidden), w_down)


def per_device(
    layer_in,
    cotangent,
    token_ids,
    hash_table,
    prefix_len,
    w_query,
    w_key,
    w_value,
    w_output,
    bias_query,
    bias_value,
    gain_attn,
    shift_attn,
    gain_moe,
    shift_moe,
    bias_output,
    w_up,
    bias_up,
    w_down,
    bias_down,
):
    rows = lax.axis_size("row")
    row = lax.axis_index("row")
    col = lax.axis_index("col")
    tokens, width = layer_in.shape
    heads = width // HD
    seq_len = min(LENGTH, tokens * rows)
    group = seq_len // tokens
    low = -(-PREFIX_MAX // (2 * tokens))
    share = w_query.shape[0]
    bias_share = bias_query.shape[0]

    def line(v):
        return jnp.pad(v.astype(F32), (0, 128 - v.shape[0]))

    small = jnp.stack(
        [
            line(gain_attn),
            line(shift_attn),
            line(gain_moe),
            line(shift_moe),
            line(bias_output),
            line(bias_query.T.reshape(-1)),
            line(bias_value.T.reshape(-1)),
            jnp.zeros((128,), F32),
        ]
    )
    weights = jnp.concatenate([w_query, w_key, w_value, w_output], axis=1)
    x_all, w_all, s_all = start_gather(layer_in, weights, small, rows)
    w_all = w_all.reshape(D, 4 * width)
    w_qkv = w_all[:, : 3 * width]
    w_out = w_all[:, 3 * width :].reshape(COLS, width, width)
    gain_one, shift_one, gain_two, shift_two, out_bias = (
        s_all[:, i, :share].reshape(D) for i in range(5)
    )

    def own(v):
        return lax.dynamic_slice_in_dim(v, col * width, width, 0)

    query_bias, value_bias = (
        s_all[:, i, : heads * bias_share]
        .reshape(rows, heads, bias_share)
        .transpose(1, 0, 2)
        .reshape(width)
        for i in (5, 6)
    )

    expert_total = EXP_DEV * rows
    capacity = max(2, 2 * tokens // expert_total)
    expert_of = hash_table[token_ids]
    hits = expert_of[:, None] == jnp.arange(expert_total, dtype=jnp.int32)[None, :]
    earlier = (
        jnp.arange(tokens, dtype=jnp.int32)[None, :] < jnp.arange(tokens, dtype=jnp.int32)[:, None]
    )
    before = jnp.dot(earlier.astype(BF16), hits.astype(BF16), preferred_element_type=F32)
    slot_of = jnp.sum(jnp.where(hits, before, 0.0), axis=1).astype(jnp.int32)
    target = expert_of * capacity + slot_of
    chosen = (
        jnp.arange(expert_total * capacity, dtype=jnp.int32)[:, None] == target[None, :]
    ).astype(BF16)

    resid = x_all.transpose(1, 0, 2).reshape(tokens, D).astype(F32)
    mean_one = jnp.mean(resid, axis=-1, keepdims=True)
    centred = resid - mean_one
    rstd_one = lax.rsqrt(jnp.mean(centred * centred, axis=-1, keepdims=True) + epsilon)
    h_one = (centred * rstd_one * gain_one + shift_one).astype(BF16)
    qkv_bias = jnp.concatenate([query_bias, jnp.zeros_like(query_bias), value_bias])
    qkv = (jnp.dot(h_one, w_qkv, preferred_element_type=F32) + qkv_bias).astype(BF16)
    queries = qkv[:, :width] * jnp.asarray(HD**-0.5, BF16)
    kv_all = kv_gather(qkv[:, width:], group, low, 1)
    place = row % group
    seq_hit = row // group == jnp.arange(prefix_len.shape[0], dtype=jnp.int32)
    prefix = jnp.sum(jnp.where(seq_hit, prefix_len, 0))
    info = jnp.stack([place.astype(jnp.int32), prefix.astype(jnp.int32)])
    attended, attended_low, lse = attention_forward(info, queries, kv_all, 2 * low)
    branch = product_scatter(attended_low, w_out, 2)
    x_own = layer_in.astype(F32)
    mid = x_own + branch + own(out_bias)

    part_mean = jnp.mean(mid, axis=-1)
    part_spread = jnp.sum((mid - part_mean[:, None]) ** 2, axis=-1)
    stats = jnp.stack([part_mean, part_spread]).reshape(-1, 128)
    stats = small_gather(stats, 3).reshape(COLS, 2, tokens)
    mean_two = jnp.mean(stats[:, 0], axis=0)
    spread = jnp.sum(stats[:, 1] + width * (stats[:, 0] - mean_two) ** 2, axis=0) / D
    rstd_two = lax.rsqrt(spread + epsilon)[:, None]
    normed_two = (mid - mean_two[:, None]) * rstd_two
    gain_two_own = own(gain_two)
    h_two = (normed_two * gain_two_own + own(shift_two)).astype(BF16)

    outgoing = jnp.dot(
        chosen, jnp.concatenate([h_two, cotangent], axis=1), preferred_element_type=F32
    ).astype(BF16)
    block = (rows, EXP_DEV, capacity, 2 * width)
    received = dispatch(outgoing.reshape(block), rows, 4)
    parts, grad_w_up, grad_bias_up, grad_w_down, grad_bias_down = experts(
        received, w_up, bias_up, w_down
    )
    down_own = lax.dynamic_slice_in_dim(bias_down, col * width, width, 1).astype(F32)
    down_own = jnp.concatenate([down_own, jnp.zeros_like(down_own)], axis=1)[:, None, :]
    returned = giveback(parts, down_own, rows, 5).reshape(-1, 2 * width)
    combined = lax.dot_general(
        chosen, returned, (((0,), (0,)), ((), ())), preferred_element_type=F32
    )
    layer_out = (mid + combined[:, :width]).astype(BF16)
    grad_h_two = combined[:, width:]

    scaled = grad_h_two * gain_two_own
    sums = jnp.stack([jnp.sum(scaled, axis=-1), jnp.sum(scaled * normed_two, axis=-1)])
    sums = small_gather(sums.reshape(-1, 128), 6).reshape(COLS, 2, tokens)
    sums = jnp.sum(sums, axis=0) / D
    grad_mid = cotangent.astype(F32) + rstd_two * (
        scaled - sums[0][:, None] - normed_two * sums[1][:, None]
    )
    grad_all = col_gather(grad_mid.astype(BF16), 7)
    grad_wide = grad_all.transpose(1, 0, 2).reshape(tokens, D)
    grad_w_out = lax.dot_general(
        grad_wide, attended_low, (((0,), (0,)), ((), ())), preferred_element_type=F32
    )
    grad_attended = jnp.dot(
        grad_wide, w_out.reshape(D, width), preferred_element_type=F32
    ).astype(BF16)
    delta = jnp.sum(
        (grad_attended.astype(F32) * attended).reshape(tokens, heads, HD), axis=-1
    ).T
    delta = jnp.pad(delta, ((0, 8 - heads), (0, 0)))
    grad_q, kv_terms = attention_backward(
        info, queries, kv_all, grad_attended, lse, delta, 2 * low
    )
    grad_kv = dkv_scatter(kv_terms, group, low, 8)
    grad_qkv = jnp.concatenate([grad_q, grad_kv], axis=1)
    grad_w_qkv = lax.dot_general(
        h_one, grad_qkv, (((0,), (0,)), ((), ())), preferred_element_type=F32
    )
    grad_bias = jnp.sum(grad_qkv, axis=0, dtype=F32)
    grad_h_one = product_scatter(grad_qkv, w_qkv.reshape(COLS, width, 3 * width), 9)
    normed_one = (x_own - mean_one) * rstd_one
    scaled = grad_h_one * own(gain_one)
    sums = jnp.stack([jnp.sum(scaled, axis=-1), jnp.sum(scaled * normed_one, axis=-1)])
    vectors = jnp.stack(
        [
            jnp.sum(grad_h_one * normed_one, axis=0),
            jnp.sum(grad_h_one, axis=0),
            jnp.sum(grad_h_two * normed_two, axis=0),
            jnp.sum(grad_h_two, axis=0),
            jnp.sum(grad_mid, axis=0),
        ]
    )
    vectors = jnp.pad(vectors, ((0, 3), (0, 256 - width))).reshape(-1, 128)
    shared = small_gather(jnp.concatenate([sums.reshape(-1, 128), vectors]), 10)
    used = 2 * tokens // 128
    sums = jnp.sum(shared[:, :used].reshape(COLS, 2, tokens), axis=0) / D
    grad_in = grad_mid + rstd_one * (scaled - sums[0][:, None] - normed_one * sums[1][:, None])
    vectors = shared[:, used:].reshape(COLS, 8, 256)[:, :5, :width]
    vectors = vectors.transpose(1, 0, 2).reshape(5, rows, share).transpose(1, 0, 2)

    def by_row(v):
        v = v.reshape(heads, rows, bias_share).transpose(1, 0, 2).reshape(rows, 1, -1)
        return jnp.pad(v, ((0, 0), (0, 0), (0, 128 - v.shape[2])))

    small_terms = jnp.concatenate(
        [
            jnp.pad(vectors, ((0, 0), (0, 0), (0, 128 - share))),
            by_row(grad_bias[:width]),
            by_row(grad_bias[2 * width :]),
            jnp.zeros((rows, 1, 128), F32),
        ],
        axis=1,
    )
    weight_terms = jnp.concatenate([grad_w_qkv, grad_w_out], axis=1).astype(BF16)
    weight_sums, small_sums = end_scatter(
        weight_terms.reshape(rows, share, 4 * width), small_terms, rows, 11
    )

    def bias_back(v):
        return v[: heads * bias_share].reshape(heads, bias_share).T

    return (
        layer_out,
        grad_in,
        weight_sums[:, :width],
        weight_sums[:, width : 2 * width],
        weight_sums[:, 2 * width : 3 * width],
        weight_sums[:, 3 * width :],
        bias_back(small_sums[5]),
        bias_back(small_sums[6]),
        small_sums[0, :share],
        small_sums[1, :share],
        small_sums[2, :share],
        small_sums[3, :share],
        small_sums[4, :share],
        grad_w_up,
        grad_bias_up[:, 0],
        grad_w_down,
        grad_bias_down[:, 0],
    )


def solution(mesh):
    placed = (
        P("row", "col"),
        P("row", "col"),
        P("row"),
        P(),
        P(),
        P("row", "col"),
        P("row", "col"),
        P("row", "col"),
        P("row", "col"),
        P("row", "col"),
        P("row", "col"),
        P("row"),
        P("row"),
        P("row"),
        P("row"),
        P("row"),
        P("row", None, "col"),
        P("row", "col"),
        P("row", "col", None),
        P("row", None),
    )
    return jax.shard_map(
        per_device,
        mesh=mesh,
        in_specs=placed,
        out_specs=(
            P("row", "col"),
            P("row", "col"),
            P("row", "col"),
            P("row", "col"),
            P("row", "col"),
            P("row", "col"),
            P("row", "col"),
            P("row", "col"),
            P("row"),
            P("row"),
            P("row"),
            P("row"),
            P("row"),
            P("row", None, "col"),
            P("row", "col"),
            P("row", "col", None),
            P("row", None),
        ),
        check_vma=False,
    )
```

```python
import functools

import jax
import jax.numpy as jnp
from jax import lax
from jax.experimental import pallas as pl
from jax.experimental.pallas import tpu as pltpu
from jax.sharding import PartitionSpec as P

D = 768
HD = 64
EXP_DEV = 2
LENGTH = 8192
PREFIX_MAX = 4096
COLS = 4

F32 = jnp.float32
BF16 = jnp.bfloat16
MESH = pl.DeviceIdType.MESH
LOG2E = 1.4426950408889634

epsilon = 1e-05
neg_big = -1e30

VSPEC = pl.BlockSpec(memory_space=pltpu.VMEM)
SSPEC = pl.BlockSpec(memory_space=pltpu.SMEM)
VMEM_BYTES = 64 * 1000 * 1000
DMA = pltpu.SemaphoreType.DMA


def params(collective=None):
    if collective is None:
        return pltpu.CompilerParams(vmem_limit_bytes=VMEM_BYTES)
    return pltpu.CompilerParams(
        vmem_limit_bytes=VMEM_BYTES, collective_id=collective, has_side_effects=True
    )


def push(src, dst, send_sem, recv_sem, peer):
    return pltpu.make_async_remote_copy(
        src_ref=src,
        dst_ref=dst,
        send_sem=send_sem,
        recv_sem=recv_sem,
        device_id=peer,
        device_id_type=MESH,
    )


def greet(peers):
    barrier = pltpu.get_barrier_semaphore()
    for peer in peers:
        pl.semaphore_signal(barrier, inc=1, device_id=peer, device_id_type=MESH)
    pl.semaphore_wait(barrier, len(peers))


def col_places():
    me = lax.axis_index("col")
    sib = me + 1 - 2 * (me % 2)
    across = (me + 2) % COLS
    diag = (sib + 2) % COLS
    return me, sib, across, diag


def start_kernel(
    rows, pieces, x_ref, w_ref, s_ref, xo_ref, wo_ref, so_ref, c_send, c_recv, r_send, r_recv
):
    me, sib, across, _ = col_places()
    row = lax.axis_index("row")
    peers = [{"row": (row + k) % rows} for k in range(1, rows)]
    greet(peers + [{"col": sib}, {"col": across}])
    step = x_ref.shape[0] // pieces
    sent = []
    for i in range(pieces):
        part = pl.ds(i * step, step)
        for way, peer in ((0, across), (1, sib)):
            copy = push(
                x_ref.at[part],
                xo_ref.at[me, part],
                c_send.at[way, i],
                c_recv.at[way, i],
                {"col": peer},
            )
            copy.start()
            sent.append(copy)
    row_copies = []
    for k, peer in enumerate(peers):
        for j, (src, dst) in enumerate(((w_ref, wo_ref), (s_ref, so_ref))):
            copy = push(src, dst.at[row], r_send.at[j, k], r_recv.at[j, k], peer)
            copy.start()
            row_copies.append(copy)
    xo_ref[me] = x_ref[...]
    wo_ref[row] = w_ref[...]
    so_ref[row] = s_ref[...]
    for i in range(pieces):
        part = pl.ds(i * step, step)
        sent[2 * i].wait_recv()
        copy = push(
            xo_ref.at[across, part],
            xo_ref.at[across, part],
            c_send.at[2, i],
            c_recv.at[2, i],
            {"col": sib},
        )
        copy.start()
        row_copies.append(copy)
    for i in range(pieces):
        sent[2 * i].wait_send()
        sent[2 * i + 1].wait()
    for copy in row_copies:
        copy.wait()


def start_gather(x, w, s, rows):
    pieces = 4
    return pl.pallas_call(
        functools.partial(start_kernel, rows, pieces),
        out_shape=(
            jax.ShapeDtypeStruct((COLS,) + x.shape, x.dtype),
            jax.ShapeDtypeStruct((rows,) + w.shape, w.dtype),
            jax.ShapeDtypeStruct((rows,) + s.shape, s.dtype),
        ),
        in_specs=[VSPEC] * 3,
        out_specs=(VSPEC,) * 3,
        scratch_shapes=[
            DMA((3, pieces)),
            DMA((3, pieces)),
            DMA((2, rows - 1)),
            DMA((2, rows - 1)),
        ],
        compiler_params=params(0),
    )(x, w, s)


def col_gather_kernel(pieces, x_ref, xo_ref, c_send, c_recv):
    me, sib, across, _ = col_places()
    greet([{"col": sib}, {"col": across}])
    step = x_ref.shape[0] // pieces
    sent, late = [], []
    for i in range(pieces):
        part = pl.ds(i * step, step)
        for way, peer in ((0, across), (1, sib)):
            copy = push(
                x_ref.at[part],
                xo_ref.at[me, part],
                c_send.at[way, i],
                c_recv.at[way, i],
                {"col": peer},
            )
            copy.start()
            sent.append(copy)
    xo_ref[me] = x_ref[...]
    for i in range(pieces):
        part = pl.ds(i * step, step)
        sent[2 * i].wait_recv()
        copy = push(
            xo_ref.at[across, part],
            xo_ref.at[across, part],
            c_send.at[2, i],
            c_recv.at[2, i],
            {"col": sib},
        )
        copy.start()
        late.append(copy)
    for i in range(pieces):
        sent[2 * i].wait_send()
        sent[2 * i + 1].wait()
        late[i].wait()


def col_gather(x, collective):
    pieces = 4
    return pl.pallas_call(
        functools.partial(col_gather_kernel, pieces),
        out_shape=jax.ShapeDtypeStruct((COLS,) + x.shape, x.dtype),
        in_specs=[VSPEC],
        out_specs=VSPEC,
        scratch_shapes=[DMA((3, pieces)), DMA((3, pieces))],
        compiler_params=params(collective),
    )(x)


def small_kernel(x_ref, xo_ref, c_send, c_recv):
    me = lax.axis_index("col")
    peers = [{"col": (me + k) % COLS} for k in range(1, COLS)]
    greet(peers)
    copies = []
    for k, peer in enumerate(peers):
        copy = push(x_ref, xo_ref.at[me], c_send.at[k], c_recv.at[k], peer)
        copy.start()
        copies.append(copy)
    xo_ref[me] = x_ref[...]
    for copy in copies:
        copy.wait()


def small_gather(x, collective):
    return pl.pallas_call(
        small_kernel,
        out_shape=jax.ShapeDtypeStruct((COLS,) + x.shape, x.dtype),
        in_specs=[VSPEC],
        out_specs=VSPEC,
        scratch_shapes=[DMA((COLS - 1,)), DMA((COLS - 1,))],
        compiler_params=params(collective),
    )(x)


def line_places(group):
    row = lax.axis_index("row")
    place = row % group
    level, side = place // 2, place % 2
    return row, place, level, side, row + 1 - 2 * side


def line_greet(levels, row, level, partner):
    barrier = pltpu.get_barrier_semaphore()
    pl.semaphore_signal(barrier, inc=1, device_id={"row": partner}, device_id_type=MESH)

    @pl.when(level > 0)
    def _():
        pl.semaphore_signal(barrier, inc=1, device_id={"row": row - 2}, device_id_type=MESH)

    @pl.when(level < levels - 1)
    def _():
        pl.semaphore_signal(barrier, inc=1, device_id={"row": row + 2}, device_id_type=MESH)

    count = 1 + (level > 0).astype(jnp.int32) + (level < levels - 1).astype(jnp.int32)
    pl.semaphore_wait(barrier, count)


def nt(left, right):
    return lax.dot_general(left, right, (((1,), (1,)), ((), ())), preferred_element_type=F32)


def nn(left, right):
    return lax.dot_general(left, right, (((1,), (0,)), ((), ())), preferred_element_type=F32)


def tn(left, right):
    return lax.dot_general(left, right, (((0,), (0,)), ((), ())), preferred_element_type=F32)


def seen(key_start, query_start, shape, prefix):
    key = key_start + lax.broadcasted_iota(jnp.int32, shape, 0)
    query = query_start + lax.broadcasted_iota(jnp.int32, shape, 1)
    return (key < prefix) | (key <= query)


def forward_kernel(
    group,
    low,
    pieces,
    qb,
    info_ref,
    q_ref,
    kv_ref,
    out_ref,
    o_ref,
    ob_ref,
    lse_ref,
    m_ref,
    acc_ref,
    u_send,
    u_recv,
    d_send,
    d_recv,
    x_send,
    x_recv,
):
    levels = group // 2
    row, place, level, side, partner = line_places(group)
    prefix = info_ref[0]
    tokens, width = q_ref.shape
    heads = width // HD
    step = tokens // pieces
    line_greet(levels, row, level, partner)

    def make(at, i, way, src=None):
        part = pl.ds(i * step, step)
        dst = out_ref.at[2 * at + side, part]
        sems = ((u_send, u_recv), (d_send, d_recv), (x_send, x_recv))[way]
        peer = (row + 2, row - 2, partner)[way]
        return push(
            dst if src is None else src.at[part],
            dst,
            sems[0].at[at, i],
            sems[1].at[at, i],
            {"row": peer},
        )

    def other(at, i):
        part = pl.ds(i * step, step)
        dst = out_ref.at[2 * at + 1 - side, part]
        return push(dst, dst, x_send.at[at, i], x_recv.at[at, i], {"row": partner})

    def when(cond, run):
        @pl.when(cond)
        def _():
            for i in range(pieces):
                run(i)

    to_up = level < levels - 1
    own_down = (level > 0) & (level < low)
    own_side = (level < low) | (side == 0)
    for i in range(pieces):

        @pl.when(to_up)
        def _(i=i):
            make(level, i, 0, kv_ref).start()

        @pl.when(own_side)
        def _(i=i):
            make(level, i, 2, kv_ref).start()

        @pl.when(own_down)
        def _(i=i):
            make(level, i, 1, kv_ref).start()

    out_ref[place] = kv_ref[...]
    m_ref[...] = jnp.full(m_ref.shape, neg_big, F32)
    acc_ref[...] = jnp.zeros(acc_ref.shape, F32)
    units = [(h, i) for h in range(heads) for i in range(tokens // qb)]

    def block(blk, masked):
        def raw_of(h, i):
            feats = slice(h * HD, (h + 1) * HD)
            raw = nt(out_ref[blk, :, feats], q_ref[i * qb : (i + 1) * qb, feats])
            if masked:
                allowed = seen(blk * tokens, place * tokens + i * qb, raw.shape, prefix)
                raw = jnp.where(allowed, raw, neg_big)
            return raw

        def soften(h, i, raw):
            cols = slice(i * qb, (i + 1) * qb)
            old = m_ref[h : h + 1, cols]
            new = jnp.maximum(old, jnp.max(raw, axis=0, keepdims=True))
            m_ref[h : h + 1, cols] = new
            weights = jnp.exp2((raw - new) * LOG2E).astype(BF16)
            return weights, jnp.exp2((old - new) * LOG2E)

        def gather(h, i, weights, scale):
            cols = slice(i * qb, (i + 1) * qb)
            v = out_ref[blk, :, width + h * HD : width + (h + 1) * HD]
            v_ext = jnp.concatenate([v.T, jnp.ones((16, tokens), BF16)], axis=0)
            acc_ref[h, :, cols] = acc_ref[h, :, cols] * scale + nn(v_ext, weights)

        coming, waiting = raw_of(*units[0]), None
        for n, unit in enumerate(units):
            raw = coming
            if n + 1 < len(units):
                coming = raw_of(*units[n + 1])
            soft = soften(*unit, raw)
            if waiting is not None:
                gather(*waiting)
            waiting = unit + soft
        gather(*waiting)

    def event(e, carry):
        t, cross = e // 2, e % 2
        at = jnp.where(t <= level, level - t, t)
        live = (t <= level) | (t < low)
        line_in = live & (cross == 0)

        @pl.when(line_in & (at < level))
        def _():
            for i in range(pieces):
                make(at, i, 0).wait_recv()

                @pl.when(to_up)
                def _(i=i):
                    make(at, i, 0).start()

                make(at, i, 2).start()

        @pl.when(line_in & (at > level))
        def _():
            for i in range(pieces):
                make(at, i, 1).wait_recv()

                @pl.when(level > 0)
                def _(i=i):
                    make(at, i, 1).start()

                make(at, i, 2).start()

        comes = live & (cross == 1) & ((at < low) | (at < level) | (side == 1))
        when(comes, lambda i: other(at, i).wait_recv())
        blk = 2 * at + jnp.where(cross == 0, side, 1 - side)
        needed = line_in | comes

        @pl.when(needed & (blk < place))
        def _():
            block(blk, False)

        @pl.when(needed & (blk >= place))
        def _():
            block(blk, True)

        return carry

    lax.fori_loop(0, 2 * levels, event, 0)

    for h in range(heads):
        total = acc_ref[h, HD : HD + 1, :]
        out = (acc_ref[h, :HD, :] / total).T
        o_ref[:, h * HD : (h + 1) * HD] = out
        ob_ref[:, h * HD : (h + 1) * HD] = out.astype(BF16)
        lse_ref[h : h + 1, :] = m_ref[h : h + 1, :] * LOG2E + jnp.log2(total)

    when(to_up, lambda i: make(level, i, 0, kv_ref).wait_send())
    when(own_side, lambda i: make(level, i, 2, kv_ref).wait_send())
    when(own_down, lambda i: make(level, i, 1, kv_ref).wait_send())
    for k in range(1, levels):
        at = level - k
        when((at >= 0) & to_up, lambda i, at=at: make(at, i, 0).wait_send())
        when(at >= 0, lambda i, at=at: make(at, i, 2).wait_send())
    for k in range(1, low):
        at = level + k
        when((at < low) & (level > 0), lambda i, at=at: make(at, i, 1).wait_send())
        when(at < low, lambda i, at=at: make(at, i, 2).wait_send())


def attention_forward(info, q, kv, group, low, collective):
    pieces = 4
    levels = group // 2
    tokens, width = q.shape
    heads = width // HD
    return pl.pallas_call(
        functools.partial(forward_kernel, group, low, pieces, tokens // 2),
        out_shape=(
            jax.ShapeDtypeStruct((group,) + kv.shape, kv.dtype),
            jax.ShapeDtypeStruct((tokens, width), F32),
            jax.ShapeDtypeStruct((tokens, width), BF16),
            jax.ShapeDtypeStruct((8, tokens), F32),
        ),
        in_specs=[SSPEC, VSPEC, VSPEC],
        out_specs=(VSPEC,) * 4,
        scratch_shapes=[
            pltpu.VMEM((8, tokens), F32),
            pltpu.VMEM((heads, HD + 16, tokens), F32),
        ]
        + [DMA((levels, pieces))] * 6,
        compiler_params=params(collective),
    )(info, q, kv)


def backward_kernel(
    group,
    low,
    pieces,
    kb,
    info_ref,
    q_ref,
    kv_ref,
    do_ref,
    lse_ref,
    delta_ref,
    dq_ref,
    out_ref,
    part_ref,
    rx_ref,
    above_ref,
    below_ref,
    snd_ref,
    acc_ref,
    dqt_ref,
    u_send,
    u_recv,
    d_send,
    d_recv,
    x_send,
    x_recv,
):
    levels = group // 2
    row, place, level, side, partner = line_places(group)
    prefix = info_ref[0]
    tokens, width = q_ref.shape
    heads = width // HD
    step = tokens // pieces
    line_greet(levels, row, level, partner)
    dqt_ref[...] = jnp.zeros(dqt_ref.shape, F32)

    def block(blk, masked):
        def body(j, carry):
            start = pl.multiple_of(j * kb, kb)
            keys = pl.ds(start, kb)
            for h in range(heads):
                feats = slice(h * HD, (h + 1) * HD)
                vals = slice(width + h * HD, width + (h + 1) * HD)
                k, v = kv_ref[blk, keys, feats], kv_ref[blk, keys, vals]
                q, do = q_ref[:, feats], do_ref[:, feats]
                probs = jnp.exp2(nt(k, q) * LOG2E - lse_ref[h : h + 1, :])
                if masked:
                    allowed = seen(blk * tokens + start, place * tokens, probs.shape, prefix)
                    probs = jnp.where(allowed, probs, 0.0)
                grad = (probs * (nt(v, do) - delta_ref[h : h + 1, :])).astype(BF16)
                part_ref[blk, keys, feats] = nn(grad, q).astype(BF16)
                part_ref[blk, keys, vals] = nn(probs.astype(BF16), do).astype(BF16)
                dqt_ref[feats, :] += nn(k.T, grad)
            return carry

        lax.fori_loop(0, tokens // kb, body, 0)

    def cross(at, i):
        part = pl.ds(i * step, step)
        return push(
            part_ref.at[2 * at + 1 - side, part],
            rx_ref.at[at, part],
            x_send.at[at, i],
            x_recv.at[at, i],
            {"row": partner},
        )

    def line(at, i, up):
        part = pl.ds(i * step, step)
        sems = (u_send, u_recv) if up else (d_send, d_recv)
        return push(
            snd_ref.at[at, part],
            (below_ref if up else above_ref).at[at, part],
            sems[0].at[at, i],
            sems[1].at[at, i],
            {"row": row + 2 if up else row - 2},
        )

    def gone(at):
        return (at < low) | (at < level) | ((at == level) & (side == 1))

    def comes(at):
        return (at < low) | (at < level) | ((at == level) & (side == 0))

    def total(at, i, from_above, from_below):
        part = pl.ds(i * step, step)
        acc_ref[...] = part_ref[2 * at + side, part].astype(F32)

        @pl.when(comes(at))
        def _():
            cross(at, i).wait_recv()
            acc_ref[...] += rx_ref[at, part].astype(F32)

        if from_above is not None:

            @pl.when(from_above)
            def _():
                line(at, i, False).wait_recv()
                acc_ref[...] += above_ref[at, part].astype(F32)

        if from_below is not None:

            @pl.when(from_below)
            def _():
                line(at, i, True).wait_recv()
                acc_ref[...] += below_ref[at, part].astype(F32)

    not_top = level < levels - 1
    above = jnp.maximum(low - 1 - level, 0)

    def level_of(t):
        return jnp.where(t < above, low - 1 - t, t - above)

    def event(e, carry):
        t, own = e // 2, e % 2
        at = level_of(t)
        live = (t < above) | (at <= level)

        down = t - (levels - level)

        @pl.when((own == 1) & (down >= 0) & (down < level))
        def _():
            for i in range(pieces):
                total(down, i, not_top, None)
                snd_ref[down, pl.ds(i * step, step)] = acc_ref[...].astype(BF16)
                line(down, i, False).start()

        @pl.when((own == 1) & (t >= 1) & (t - 1 < above))
        def _():
            up = level_of(t - 1)
            for i in range(pieces):
                total(up, i, None, level > 0)
                snd_ref[up, pl.ds(i * step, step)] = acc_ref[...].astype(BF16)
                line(up, i, True).start()

        goes = live & (own == 0) & gone(at)
        blk = 2 * at + jnp.where(own == 1, side, 1 - side)
        needed = goes | (live & (own == 1))

        @pl.when(needed & (blk < place))
        def _():
            block(blk, False)

        @pl.when(needed & (blk >= place))
        def _():
            block(blk, True)

        @pl.when(goes)
        def _():
            for i in range(pieces):
                cross(at, i).start()

        return carry

    lax.fori_loop(0, 2 * levels, event, 0)
    dq_ref[...] = (dqt_ref[...] * HD**-0.5).T.astype(BF16)

    for i in range(pieces):
        total(level, i, not_top, (level > 0) & (level < low))
        out_ref[pl.ds(i * step, step)] = acc_ref[...].astype(BF16)

    for at in range(levels):
        for i in range(pieces):

            @pl.when(gone(at))
            def _(at=at, i=i):
                cross(at, i).wait_send()

            @pl.when(at < level)
            def _(at=at, i=i):
                line(at, i, False).wait_send()

            if at < low:

                @pl.when(at > level)
                def _(at=at, i=i):
                    line(at, i, True).wait_send()


def attention_backward(info, q, kv_all, do, lse, delta, group, low, collective):
    pieces = 4
    levels = group // 2
    tokens, width = q.shape
    both = 2 * width
    block = pltpu.VMEM((levels, tokens, both), BF16)
    return pl.pallas_call(
        functools.partial(backward_kernel, group, low, pieces, tokens // 2),
        out_shape=(
            jax.ShapeDtypeStruct((tokens, width), BF16),
            jax.ShapeDtypeStruct((tokens, both), BF16),
        ),
        in_specs=[SSPEC] + [VSPEC] * 5,
        out_specs=(VSPEC,) * 2,
        scratch_shapes=[
            pltpu.VMEM(kv_all.shape, BF16),
            block,
            block,
            pltpu.VMEM((low, tokens, both), BF16),
            block,
            pltpu.VMEM((tokens // pieces, both), F32),
            pltpu.VMEM((width, tokens), F32),
        ]
        + [DMA((levels, pieces))] * 6,
        compiler_params=params(collective),
    )(info, q, kv_all, do, lse, delta)


def product_kernel(pieces, a_ref, b_ref, out_ref, snd_ref, rx_ref, far_ref, tot_ref, send, recv):
    me, sib, across, diag = col_places()
    greet([{"col": sib}, {"col": across}])
    step = a_ref.shape[0] // pieces

    def term(i, who):
        return lax.dot_general(
            a_ref[pl.ds(i * step, step)],
            b_ref[who],
            (((1,), (1,)), ((), ())),
            preferred_element_type=F32,
        )

    def near(i, j):
        part = pl.ds(i * step, step)
        return push(
            snd_ref.at[j, part], rx_ref.at[j, part], send.at[j, i], recv.at[j, i], {"col": sib}
        )

    def over(i):
        part = pl.ds(i * step, step)
        return push(tot_ref.at[part], far_ref.at[part], send.at[2, i], recv.at[2, i], {"col": across})

    for i in range(pieces):
        snd_ref[0, pl.ds(i * step, step)] = term(i, diag).astype(BF16)
        near(i, 0).start()
    for i in range(pieces):
        part = pl.ds(i * step, step)
        mine = term(i, across)
        near(i, 0).wait_recv()
        tot_ref[part] = (mine + rx_ref[0, part].astype(F32)).astype(BF16)
        over(i).start()
    for i in range(pieces):
        snd_ref[1, pl.ds(i * step, step)] = term(i, sib).astype(BF16)
        near(i, 1).start()
    for i in range(pieces):
        part = pl.ds(i * step, step)
        mine = term(i, me)
        near(i, 1).wait_recv()
        mine = mine + rx_ref[1, part].astype(F32)
        over(i).wait_recv()
        out_ref[part] = mine + far_ref[part].astype(F32)
    for i in range(pieces):
        near(i, 0).wait_send()
        near(i, 1).wait_send()
        over(i).wait_send()


def product_scatter(a, b, collective):
    pieces = 4
    tokens, width = a.shape[0], b.shape[1]
    block = pltpu.VMEM((tokens, width), BF16)
    pair = pltpu.VMEM((2, tokens, width), BF16)
    return pl.pallas_call(
        functools.partial(product_kernel, pieces),
        out_shape=jax.ShapeDtypeStruct((tokens, width), F32),
        in_specs=[VSPEC] * 2,
        out_specs=VSPEC,
        scratch_shapes=[pair, pair, block, block, DMA((3, pieces)), DMA((3, pieces))],
        compiler_params=params(collective),
    )(a, b)


def dispatch_kernel(rows, in_ref, out_ref, r_send, r_recv, c_send, c_recv):
    me, sib, across, _ = col_places()
    row = lax.axis_index("row")
    peers = [(row + k) % rows for k in range(1, rows)]
    greet([{"row": p} for p in peers] + [{"col": sib}, {"col": across}])
    copies = []
    for k, peer in enumerate(peers):
        copy = push(
            in_ref.at[peer], out_ref.at[me, row], r_send.at[k], r_recv.at[k], {"row": peer}
        )
        copy.start()
        copies.append(copy)

    def col(src, dst, k, way):
        return push(
            src, dst, c_send.at[way, k], c_recv.at[way, k], {"col": across if way == 0 else sib}
        )

    done, first = [], []
    for way in range(2):
        copy = col(in_ref.at[row], out_ref.at[me, row], 0, way)
        copy.start()
        (first if way == 0 else done).append(copy)
    out_ref[me, row] = in_ref[row]
    sources = [row] + [(row + rows - k) % rows for k in range(1, rows)]

    def forward(k):
        first[k].wait_recv()
        src = sources[k]
        copy = col(out_ref.at[across, src], out_ref.at[across, src], k, 2)
        copy.start()
        done.append(copy)

    for k in range(1, rows):
        copies[k - 1].wait_recv()
        block = out_ref.at[me, sources[k]]
        for way in range(2):
            copy = col(block, block, k, way)
            copy.start()
            (first if way == 0 else done).append(copy)
        forward(k - 1)
    forward(rows - 1)
    for copy in copies:
        copy.wait_send()
    for copy in first:
        copy.wait_send()
    for copy in done:
        copy.wait()


def dispatch(x, rows, collective):
    return pl.pallas_call(
        functools.partial(dispatch_kernel, rows),
        out_shape=jax.ShapeDtypeStruct((COLS,) + x.shape, x.dtype),
        in_specs=[VSPEC],
        out_specs=VSPEC,
        scratch_shapes=[DMA((rows - 1,)), DMA((rows - 1,)), DMA((3, rows)), DMA((3, rows))],
        compiler_params=params(collective),
    )(x)


def giveback_kernel(
    rows, in_ref, bias_ref, out_ref, rx_ref, far_ref, tot_ref, fin_ref, send, recv, r_send, r_recv
):
    me, sib, across, diag = col_places()
    row = lax.axis_index("row")
    order = [(row + k) % rows for k in range(1, rows)] + [row]
    greet([{"row": p} for p in order[:-1]] + [{"col": sib}, {"col": across}])

    def near(k, j):
        who = diag if j == 0 else sib
        return push(
            in_ref.at[who, order[k]], rx_ref.at[j, k], send.at[j, k], recv.at[j, k], {"col": sib}
        )

    def over(k):
        return push(tot_ref.at[k], far_ref.at[k], send.at[2, k], recv.at[2, k], {"col": across})

    def home(k):
        return push(
            fin_ref.at[k], out_ref.at[row], r_send.at[k], r_recv.at[k], {"row": order[k]}
        )

    for k in range(rows):
        near(k, 0).start()
        near(k, 1).start()

    def finish(k):
        near(k, 1).wait_recv()
        over(k).wait_recv()
        total = in_ref[me, order[k]].astype(F32) + rx_ref[1, k].astype(F32)
        total = total + far_ref[k].astype(F32) + bias_ref[...]
        if k == rows - 1:
            out_ref[row] = total.astype(BF16)
        else:
            fin_ref[k] = total.astype(BF16)
            home(k).start()

    for k in range(rows):
        near(k, 0).wait_recv()
        tot_ref[k] = (in_ref[across, order[k]].astype(F32) + rx_ref[0, k].astype(F32)).astype(BF16)
        over(k).start()
        if k >= 1:
            finish(k - 1)
    finish(rows - 1)
    for k in range(rows):
        near(k, 0).wait_send()
        near(k, 1).wait_send()
        over(k).wait_send()
        if k < rows - 1:
            home(k).wait()


def giveback(parts, bias, rows, collective):
    block = parts.shape[2:]
    one = pltpu.VMEM((rows,) + block, BF16)
    return pl.pallas_call(
        functools.partial(giveback_kernel, rows),
        out_shape=jax.ShapeDtypeStruct((rows,) + block, BF16),
        in_specs=[VSPEC] * 2,
        out_specs=VSPEC,
        scratch_shapes=[
            pltpu.VMEM((2, rows) + block, BF16),
            one,
            one,
            one,
            DMA((3, rows)),
            DMA((3, rows)),
            DMA((rows - 1,)),
            DMA((rows - 1,)),
        ],
        compiler_params=params(collective),
    )(parts, bias)


def end_kernel(rows, w_ref, s_ref, wo_ref, so_ref, wr_ref, sr_ref, send, recv):
    row = lax.axis_index("row")
    peers = [(row + k) % rows for k in range(1, rows)]
    greet([{"row": p} for p in peers])
    copies = []
    for k, peer in enumerate(peers):
        for j, (src, dst) in enumerate(((w_ref, wr_ref), (s_ref, sr_ref))):
            copy = push(src.at[peer], dst.at[k], send.at[j, k], recv.at[j, k], {"row": peer})
            copy.start()
            copies.append(copy)
    wo_ref[...] = w_ref[row].astype(F32)
    so_ref[...] = s_ref[row]
    for k in range(rows - 1):
        copies[2 * k].wait_recv()
        copies[2 * k + 1].wait_recv()
        wo_ref[...] += wr_ref[k].astype(F32)
        so_ref[...] += sr_ref[k]
    for copy in copies:
        copy.wait_send()


def end_scatter(w, s, rows, collective):
    return pl.pallas_call(
        functools.partial(end_kernel, rows),
        out_shape=(
            jax.ShapeDtypeStruct(w.shape[1:], F32),
            jax.ShapeDtypeStruct(s.shape[1:], F32),
        ),
        in_specs=[VSPEC] * 2,
        out_specs=(VSPEC,) * 2,
        scratch_shapes=[
            pltpu.VMEM((rows - 1,) + w.shape[1:], w.dtype),
            pltpu.VMEM((rows - 1,) + s.shape[1:], s.dtype),
            DMA((2, rows - 1)),
            DMA((2, rows - 1)),
        ],
        compiler_params=params(collective),
    )(w, s)


def expert_kernel(
    x_ref, up_ref, bias_ref, down_ref, part_ref, gup_ref, gbu_ref, gdown_ref, gbd_ref
):
    cols, rows, _, cap, both = x_ref.shape
    width = both // 2
    slots = rows * cap
    blocks = [x_ref[b, :, 0].reshape(slots, both) for b in range(cols)]
    x = jnp.concatenate([b[:, :width] for b in blocks], axis=1)
    g = jnp.concatenate([b[:, width:] for b in blocks], axis=1)
    gbd_ref[...] = jnp.sum(g.astype(F32), axis=0).reshape(gbd_ref.shape)
    hidden_units = up_ref.shape[2]
    chunk = 256
    part = jnp.zeros((slots, cols * width), F32)
    gx = jnp.zeros((slots, cols * width), F32)
    for f in range(hidden_units // chunk):
        cut = slice(f * chunk, (f + 1) * chunk)
        up, down = up_ref[0, :, cut], down_ref[0, cut, :]
        pre = nn(x, up) + bias_ref[0, :, cut].astype(F32)
        cdf = 0.5 * (1.0 + lax.erf(pre * (0.5**0.5)))
        slope = cdf + pre * (jnp.exp(-0.5 * pre * pre) * 0.3989422804014327)
        hidden = (pre * cdf).astype(BF16)
        grad = nt(g, down) * slope
        grad = grad.astype(BF16)
        part = part + nn(hidden, down)
        gx = gx + nt(grad, up)
        gdown_ref[0, cut, :] = tn(hidden, g)
        gup_ref[0, :, cut] = tn(x, grad)
        gbu_ref[0, :, cut] = jnp.sum(grad.astype(F32), axis=0, keepdims=True)
    for b in range(cols):
        cut = slice(b * width, (b + 1) * width)
        both_parts = jnp.concatenate([part[:, cut].astype(BF16), gx[:, cut].astype(BF16)], axis=1)
        part_ref[b, :, 0] = both_parts.reshape(rows, cap, both)


def experts(x, w_up, bias_up, w_down):
    cols, rows, count, cap, both = x.shape
    _, features, hidden = w_up.shape
    return pl.pallas_call(
        expert_kernel,
        grid=(count,),
        out_shape=(
            jax.ShapeDtypeStruct(x.shape, BF16),
            jax.ShapeDtypeStruct(w_up.shape, F32),
            jax.ShapeDtypeStruct((count, 1, hidden), F32),
            jax.ShapeDtypeStruct(w_down.shape, F32),
            jax.ShapeDtypeStruct((count, 1, features), F32),
        ),
        in_specs=[
            pl.BlockSpec((cols, rows, 1, cap, both), lambda e: (0, 0, e, 0, 0)),
            pl.BlockSpec((1, features, hidden), lambda e: (e, 0, 0)),
            pl.BlockSpec((1, 1, hidden), lambda e: (e, 0, 0)),
            pl.BlockSpec((1, hidden, features), lambda e: (e, 0, 0)),
        ],
        out_specs=(
            pl.BlockSpec((cols, rows, 1, cap, both), lambda e: (0, 0, e, 0, 0)),
            pl.BlockSpec((1, features, hidden), lambda e: (e, 0, 0)),
            pl.BlockSpec((1, 1, hidden), lambda e: (e, 0, 0)),
            pl.BlockSpec((1, hidden, features), lambda e: (e, 0, 0)),
            pl.BlockSpec((1, 1, features), lambda e: (e, 0, 0)),
        ),
        compiler_params=params(),
    )(x, w_up, bias_up.reshape(count, 1, hidden), w_down)


def per_device(
    layer_in,
    cotangent,
    token_ids,
    hash_table,
    prefix_len,
    w_query,
    w_key,
    w_value,
    w_output,
    bias_query,
    bias_value,
    gain_attn,
    shift_attn,
    gain_moe,
    shift_moe,
    bias_output,
    w_up,
    bias_up,
    w_down,
    bias_down,
):
    rows = lax.axis_size("row")
    row = lax.axis_index("row")
    col = lax.axis_index("col")
    tokens, width = layer_in.shape
    heads = width // HD
    seq_len = min(LENGTH, tokens * rows)
    group = seq_len // tokens
    low = -(-PREFIX_MAX // (2 * tokens))
    share = w_query.shape[0]
    bias_share = bias_query.shape[0]

    def line(v):
        return jnp.pad(v.astype(F32), (0, 128 - v.shape[0]))

    small = jnp.stack(
        [
            line(gain_attn),
            line(shift_attn),
            line(gain_moe),
            line(shift_moe),
            line(bias_output),
            line(bias_query.T.reshape(-1)),
            line(bias_value.T.reshape(-1)),
            jnp.zeros((128,), F32),
        ]
    )
    weights = jnp.concatenate([w_query, w_key, w_value, w_output], axis=1)
    x_all, w_all, s_all = start_gather(layer_in, weights, small, rows)
    w_all = w_all.reshape(D, 4 * width)
    w_qkv = w_all[:, : 3 * width]
    w_out = w_all[:, 3 * width :].reshape(COLS, width, width)
    gain_one, shift_one, gain_two, shift_two, out_bias = (
        s_all[:, i, :share].reshape(D) for i in range(5)
    )

    def own(v):
        return lax.dynamic_slice_in_dim(v, col * width, width, 0)

    query_bias, value_bias = (
        s_all[:, i, : heads * bias_share]
        .reshape(rows, heads, bias_share)
        .transpose(1, 0, 2)
        .reshape(width)
        for i in (5, 6)
    )

    expert_total = EXP_DEV * rows
    capacity = max(2, 2 * tokens // expert_total)
    expert_of = hash_table[token_ids]
    hits = expert_of[:, None] == jnp.arange(expert_total, dtype=jnp.int32)[None, :]
    earlier = (
        jnp.arange(tokens, dtype=jnp.int32)[None, :] < jnp.arange(tokens, dtype=jnp.int32)[:, None]
    )
    before = jnp.dot(earlier.astype(BF16), hits.astype(BF16), preferred_element_type=F32)
    slot_of = jnp.sum(jnp.where(hits, before, 0.0), axis=1).astype(jnp.int32)
    target = expert_of * capacity + slot_of
    chosen = (
        jnp.arange(expert_total * capacity, dtype=jnp.int32)[:, None] == target[None, :]
    ).astype(BF16)

    resid = x_all.transpose(1, 0, 2).reshape(tokens, D).astype(F32)
    mean_one = jnp.mean(resid, axis=-1, keepdims=True)
    centred = resid - mean_one
    rstd_one = lax.rsqrt(jnp.mean(centred * centred, axis=-1, keepdims=True) + epsilon)
    h_one = (centred * rstd_one * gain_one + shift_one).astype(BF16)
    qkv_bias = jnp.concatenate([query_bias, jnp.zeros_like(query_bias), value_bias])
    qkv = (jnp.dot(h_one, w_qkv, preferred_element_type=F32) + qkv_bias).astype(BF16)
    queries = qkv[:, :width] * jnp.asarray(HD**-0.5, BF16)
    seq_hit = row // group == jnp.arange(prefix_len.shape[0], dtype=jnp.int32)
    prefix = jnp.sum(jnp.where(seq_hit, prefix_len, 0))
    info = prefix.astype(jnp.int32).reshape(1)
    kv_all, attended, attended_low, lse = attention_forward(
        info, queries, qkv[:, width:], group, low, 1
    )
    branch = product_scatter(attended_low, w_out, 2)
    x_own = layer_in.astype(F32)
    mid = x_own + branch + own(out_bias)

    part_mean = jnp.mean(mid, axis=-1)
    part_spread = jnp.sum((mid - part_mean[:, None]) ** 2, axis=-1)
    stats = jnp.stack([part_mean, part_spread]).reshape(-1, 128)
    stats = small_gather(stats, 3).reshape(COLS, 2, tokens)
    mean_two = jnp.mean(stats[:, 0], axis=0)
    spread = jnp.sum(stats[:, 1] + width * (stats[:, 0] - mean_two) ** 2, axis=0) / D
    rstd_two = lax.rsqrt(spread + epsilon)[:, None]
    normed_two = (mid - mean_two[:, None]) * rstd_two
    gain_two_own = own(gain_two)
    h_two = (normed_two * gain_two_own + own(shift_two)).astype(BF16)

    outgoing = jnp.dot(
        chosen, jnp.concatenate([h_two, cotangent], axis=1), preferred_element_type=F32
    ).astype(BF16)
    block = (rows, EXP_DEV, capacity, 2 * width)
    received = dispatch(outgoing.reshape(block), rows, 4)
    parts, grad_w_up, grad_bias_up, grad_w_down, grad_bias_down = experts(
        received, w_up, bias_up, w_down
    )
    down_own = lax.dynamic_slice_in_dim(bias_down, col * width, width, 1).astype(F32)
    down_own = jnp.concatenate([down_own, jnp.zeros_like(down_own)], axis=1)[:, None, :]
    returned = giveback(parts, down_own, rows, 5).reshape(-1, 2 * width)
    combined = lax.dot_general(
        chosen, returned, (((0,), (0,)), ((), ())), preferred_element_type=F32
    )
    layer_out = (mid + combined[:, :width]).astype(BF16)
    grad_h_two = combined[:, width:]

    scaled = grad_h_two * gain_two_own
    sums = jnp.stack([jnp.sum(scaled, axis=-1), jnp.sum(scaled * normed_two, axis=-1)])
    sums = small_gather(sums.reshape(-1, 128), 6).reshape(COLS, 2, tokens)
    sums = jnp.sum(sums, axis=0) / D
    grad_mid = cotangent.astype(F32) + rstd_two * (
        scaled - sums[0][:, None] - normed_two * sums[1][:, None]
    )
    grad_all = col_gather(grad_mid.astype(BF16), 7)
    grad_wide = grad_all.transpose(1, 0, 2).reshape(tokens, D)
    grad_w_out = lax.dot_general(
        grad_wide, attended_low, (((0,), (0,)), ((), ())), preferred_element_type=F32
    )
    grad_attended = jnp.dot(
        grad_wide, w_out.reshape(D, width), preferred_element_type=F32
    ).astype(BF16)
    delta = jnp.sum(
        (grad_attended.astype(F32) * attended).reshape(tokens, heads, HD), axis=-1
    ).T
    delta = jnp.pad(delta, ((0, 8 - heads), (0, 0)))
    grad_q, grad_kv = attention_backward(
        info, queries, kv_all, grad_attended, lse, delta, group, low, 8
    )
    grad_qkv = jnp.concatenate([grad_q, grad_kv], axis=1)
    grad_w_qkv = lax.dot_general(
        h_one, grad_qkv, (((0,), (0,)), ((), ())), preferred_element_type=F32
    )
    grad_bias = jnp.sum(grad_qkv, axis=0, dtype=F32)
    grad_h_one = product_scatter(grad_qkv, w_qkv.reshape(COLS, width, 3 * width), 9)
    normed_one = (x_own - mean_one) * rstd_one
    scaled = grad_h_one * own(gain_one)
    sums = jnp.stack([jnp.sum(scaled, axis=-1), jnp.sum(scaled * normed_one, axis=-1)])
    vectors = jnp.stack(
        [
            jnp.sum(grad_h_one * normed_one, axis=0),
            jnp.sum(grad_h_one, axis=0),
            jnp.sum(grad_h_two * normed_two, axis=0),
            jnp.sum(grad_h_two, axis=0),
            jnp.sum(grad_mid, axis=0),
        ]
    )
    vectors = jnp.pad(vectors, ((0, 3), (0, 256 - width))).reshape(-1, 128)
    shared = small_gather(jnp.concatenate([sums.reshape(-1, 128), vectors]), 10)
    used = 2 * tokens // 128
    sums = jnp.sum(shared[:, :used].reshape(COLS, 2, tokens), axis=0) / D
    grad_in = grad_mid + rstd_one * (scaled - sums[0][:, None] - normed_one * sums[1][:, None])
    vectors = shared[:, used:].reshape(COLS, 8, 256)[:, :5, :width]
    vectors = vectors.transpose(1, 0, 2).reshape(5, rows, share).transpose(1, 0, 2)

    def by_row(v):
        v = v.reshape(heads, rows, bias_share).transpose(1, 0, 2).reshape(rows, 1, -1)
        return jnp.pad(v, ((0, 0), (0, 0), (0, 128 - v.shape[2])))

    small_terms = jnp.concatenate(
        [
            jnp.pad(vectors, ((0, 0), (0, 0), (0, 128 - share))),
            by_row(grad_bias[:width]),
            by_row(grad_bias[2 * width :]),
            jnp.zeros((rows, 1, 128), F32),
        ],
        axis=1,
    )
    weight_terms = jnp.concatenate([grad_w_qkv, grad_w_out], axis=1).astype(BF16)
    weight_sums, small_sums = end_scatter(
        weight_terms.reshape(rows, share, 4 * width), small_terms, rows, 11
    )

    def bias_back(v):
        return v[: heads * bias_share].reshape(heads, bias_share).T

    return (
        layer_out,
        grad_in,
        weight_sums[:, :width],
        weight_sums[:, width : 2 * width],
        weight_sums[:, 2 * width : 3 * width],
        weight_sums[:, 3 * width :],
        bias_back(small_sums[5]),
        bias_back(small_sums[6]),
        small_sums[0, :share],
        small_sums[1, :share],
        small_sums[2, :share],
        small_sums[3, :share],
        small_sums[4, :share],
        grad_w_up,
        grad_bias_up[:, 0],
        grad_w_down,
        grad_bias_down[:, 0],
    )


def solution(mesh):
    placed = (
        P("row", "col"),
        P("row", "col"),
        P("row"),
        P(),
        P(),
        P("row", "col"),
        P("row", "col"),
        P("row", "col"),
        P("row", "col"),
        P("row", "col"),
        P("row", "col"),
        P("row"),
        P("row"),
        P("row"),
        P("row"),
        P("row"),
        P("row", None, "col"),
        P("row", "col"),
        P("row", "col", None),
        P("row", None),
    )
    return jax.shard_map(
        per_device,
        mesh=mesh,
        in_specs=placed,
        out_specs=(
            P("row", "col"),
            P("row", "col"),
            P("row", "col"),
            P("row", "col"),
            P("row", "col"),
            P("row", "col"),
            P("row", "col"),
            P("row", "col"),
            P("row"),
            P("row"),
            P("row"),
            P("row"),
            P("row"),
            P("row", None, "col"),
            P("row", "col"),
            P("row", "col", None),
            P("row", None),
        ),
        check_vma=False,
    )
```

```python
import functools

import jax
import jax.numpy as jnp
from jax import lax
from jax.experimental import pallas as pl
from jax.experimental.pallas import tpu as pltpu
from jax.sharding import PartitionSpec as P

D = 768
HD = 64
EXP_DEV = 2
LENGTH = 8192
PREFIX_MAX = 4096
COLS = 4

F32 = jnp.float32
BF16 = jnp.bfloat16
MESH = pl.DeviceIdType.MESH
LOG2E = 1.4426950408889634

epsilon = 1e-05
neg_big = -1e30

VSPEC = pl.BlockSpec(memory_space=pltpu.VMEM)
SSPEC = pl.BlockSpec(memory_space=pltpu.SMEM)
VMEM_BYTES = 64 * 1000 * 1000
DMA = pltpu.SemaphoreType.DMA


def params(collective=None):
    if collective is None:
        return pltpu.CompilerParams(vmem_limit_bytes=VMEM_BYTES)
    return pltpu.CompilerParams(
        vmem_limit_bytes=VMEM_BYTES, collective_id=collective, has_side_effects=True
    )


def push(src, dst, send_sem, recv_sem, peer):
    return pltpu.make_async_remote_copy(
        src_ref=src,
        dst_ref=dst,
        send_sem=send_sem,
        recv_sem=recv_sem,
        device_id=peer,
        device_id_type=MESH,
    )


def greet(peers):
    barrier = pltpu.get_barrier_semaphore()
    for peer in peers:
        pl.semaphore_signal(barrier, inc=1, device_id=peer, device_id_type=MESH)
    pl.semaphore_wait(barrier, len(peers))


def col_places():
    me = lax.axis_index("col")
    sib = me + 1 - 2 * (me % 2)
    across = (me + 2) % COLS
    diag = (sib + 2) % COLS
    return me, sib, across, diag


def line_places(group):
    row = lax.axis_index("row")
    place = row % group
    level, side = place // 2, place % 2
    return row, place, level, side, row + 1 - 2 * side


def far_first(rows):
    return sorted(range(1, rows), key=lambda k: -min(k, rows - k))


def start_kernel(
    rows,
    pieces,
    x_ref,
    g_ref,
    w_ref,
    s_ref,
    xo_ref,
    go_ref,
    wo_ref,
    so_ref,
    c_send,
    c_recv,
    r_send,
    r_recv,
    l_send,
    l_recv,
):
    me, sib, across, _ = col_places()
    row, _, level, side, partner = line_places(rows)
    levels = rows // 2
    order = far_first(rows)
    peers = [{"row": (row + k) % rows} for k in order]
    greet(peers + [{"col": sib}, {"col": across}])
    step = x_ref.shape[0] // pieces
    to_up, to_down = level < levels - 1, level > 0

    def weight(at, way, src=None):
        dst = wo_ref.at[2 * at + side]
        peer = (row + 2, row - 2, partner)[way]
        return push(
            dst if src is None else src,
            dst,
            l_send.at[way, at],
            l_recv.at[way, at],
            {"row": peer},
        )

    def weight_other(at):
        dst = wo_ref.at[2 * at + 1 - side]
        return push(dst, dst, l_send.at[2, at], l_recv.at[2, at], {"row": partner})

    @pl.when(to_up)
    def _():
        weight(level, 0, w_ref).start()

    @pl.when(to_down)
    def _():
        weight(level, 1, w_ref).start()

    weight(level, 2, w_ref).start()
    sent = []
    for i in range(pieces):
        part = pl.ds(i * step, step)
        for way, peer in ((0, across), (1, sib)):
            copy = push(
                x_ref.at[part],
                xo_ref.at[me, part],
                c_send.at[way, i],
                c_recv.at[way, i],
                {"col": peer},
            )
            copy.start()
            sent.append(copy)
    row_copies = []
    for k, peer in enumerate(peers):
        target = (row + order[k]) % rows
        for j, (src, dst) in enumerate(((s_ref, so_ref), (g_ref.at[target], go_ref))):
            copy = push(src, dst.at[row], r_send.at[j, k], r_recv.at[j, k], peer)
            copy.start()
            row_copies.append(copy)
    xo_ref[me] = x_ref[...]
    wo_ref[row] = w_ref[...]
    so_ref[row] = s_ref[...]
    go_ref[row] = g_ref[row]

    def pass_on(k):
        at = level - k

        @pl.when(at >= 0)
        def _():
            weight(at, 0).wait_recv()

            @pl.when(to_up)
            def _():
                weight(at, 0).start()

            weight(at, 2).start()

        up = level + k

        @pl.when(up < levels)
        def _():
            weight(up, 1).wait_recv()

            @pl.when(to_down)
            def _():
                weight(up, 1).start()

            weight(up, 2).start()

    late = []
    for k in range(1, max(levels, pieces + 1)):
        if k < levels:
            pass_on(k)
        if k <= pieces:
            part = pl.ds((k - 1) * step, step)
            sent[2 * k - 2].wait_recv()
            copy = push(
                xo_ref.at[across, part],
                xo_ref.at[across, part],
                c_send.at[2, k - 1],
                c_recv.at[2, k - 1],
                {"col": sib},
            )
            copy.start()
            late.append(copy)
    for i in range(pieces):
        sent[2 * i].wait_send()
        sent[2 * i + 1].wait()
        late[i].wait()
    for at in range(levels):
        weight_other(at).wait_recv()
        weight(at, 2).wait_send()

        @pl.when((at <= level) & to_up)
        def _(at=at):
            weight(at, 0).wait_send()

        @pl.when((at >= level) & to_down)
        def _(at=at):
            weight(at, 1).wait_send()

    for copy in row_copies:
        copy.wait()


def start_gather(x, g, w, s, rows):
    pieces = 4
    return pl.pallas_call(
        functools.partial(start_kernel, rows, pieces),
        out_shape=(
            jax.ShapeDtypeStruct((COLS,) + x.shape, x.dtype),
            jax.ShapeDtypeStruct(g.shape, g.dtype),
            jax.ShapeDtypeStruct((rows,) + w.shape, w.dtype),
            jax.ShapeDtypeStruct((rows,) + s.shape, s.dtype),
        ),
        in_specs=[VSPEC] * 4,
        out_specs=(VSPEC,) * 4,
        scratch_shapes=[
            DMA((3, pieces)),
            DMA((3, pieces)),
            DMA((2, rows - 1)),
            DMA((2, rows - 1)),
            DMA((3, rows // 2)),
            DMA((3, rows // 2)),
        ],
        compiler_params=params(0),
    )(x, g, w, s)


def col_gather_kernel(pieces, x_ref, xo_ref, c_send, c_recv):
    me, sib, across, _ = col_places()
    greet([{"col": sib}, {"col": across}])
    step = x_ref.shape[0] // pieces
    sent, late = [], []
    for i in range(pieces):
        part = pl.ds(i * step, step)
        for way, peer in ((0, across), (1, sib)):
            copy = push(
                x_ref.at[part],
                xo_ref.at[me, part],
                c_send.at[way, i],
                c_recv.at[way, i],
                {"col": peer},
            )
            copy.start()
            sent.append(copy)
    xo_ref[me] = x_ref[...]
    for i in range(pieces):
        part = pl.ds(i * step, step)
        sent[2 * i].wait_recv()
        copy = push(
            xo_ref.at[across, part],
            xo_ref.at[across, part],
            c_send.at[2, i],
            c_recv.at[2, i],
            {"col": sib},
        )
        copy.start()
        late.append(copy)
    for i in range(pieces):
        sent[2 * i].wait_send()
        sent[2 * i + 1].wait()
        late[i].wait()


def col_gather(x, collective):
    pieces = 4
    return pl.pallas_call(
        functools.partial(col_gather_kernel, pieces),
        out_shape=jax.ShapeDtypeStruct((COLS,) + x.shape, x.dtype),
        in_specs=[VSPEC],
        out_specs=VSPEC,
        scratch_shapes=[DMA((3, pieces)), DMA((3, pieces))],
        compiler_params=params(collective),
    )(x)


def small_kernel(x_ref, xo_ref, c_send, c_recv):
    me = lax.axis_index("col")
    peers = [{"col": (me + k) % COLS} for k in range(1, COLS)]
    greet(peers)
    copies = []
    for k, peer in enumerate(peers):
        copy = push(x_ref, xo_ref.at[me], c_send.at[k], c_recv.at[k], peer)
        copy.start()
        copies.append(copy)
    xo_ref[me] = x_ref[...]
    for copy in copies:
        copy.wait()


def small_gather(x, collective):
    return pl.pallas_call(
        small_kernel,
        out_shape=jax.ShapeDtypeStruct((COLS,) + x.shape, x.dtype),
        in_specs=[VSPEC],
        out_specs=VSPEC,
        scratch_shapes=[DMA((COLS - 1,)), DMA((COLS - 1,))],
        compiler_params=params(collective),
    )(x)


def line_greet(levels, row, level, partner):
    barrier = pltpu.get_barrier_semaphore()
    me = lax.axis_index("col")
    for k in range(1, COLS):
        peer = {"col": (me + k) % COLS}
        pl.semaphore_signal(barrier, inc=1, device_id=peer, device_id_type=MESH)
    pl.semaphore_signal(barrier, inc=1, device_id={"row": partner}, device_id_type=MESH)

    @pl.when(level > 0)
    def _():
        pl.semaphore_signal(barrier, inc=1, device_id={"row": row - 2}, device_id_type=MESH)

    @pl.when(level < levels - 1)
    def _():
        pl.semaphore_signal(barrier, inc=1, device_id={"row": row + 2}, device_id_type=MESH)

    count = COLS + (level > 0).astype(jnp.int32) + (level < levels - 1).astype(jnp.int32)
    pl.semaphore_wait(barrier, count)


def nt(left, right):
    return lax.dot_general(left, right, (((1,), (1,)), ((), ())), preferred_element_type=F32)


def nn(left, right):
    return lax.dot_general(left, right, (((1,), (0,)), ((), ())), preferred_element_type=F32)


def tn(left, right):
    return lax.dot_general(left, right, (((0,), (0,)), ((), ())), preferred_element_type=F32)


def seen(key_start, query_start, shape, prefix):
    key = key_start + lax.broadcasted_iota(jnp.int32, shape, 0)
    query = query_start + lax.broadcasted_iota(jnp.int32, shape, 1)
    return (key < prefix) | (key <= query)


def forward_kernel(
    group,
    low,
    pieces,
    qb,
    info_ref,
    q_ref,
    kv_ref,
    g_ref,
    out_ref,
    o_ref,
    ob_ref,
    lse_ref,
    ga_ref,
    m_ref,
    acc_ref,
    u_send,
    u_recv,
    d_send,
    d_recv,
    x_send,
    x_recv,
    g_send,
    g_recv,
):
    levels = group // 2
    row, place, level, side, partner = line_places(group)
    prefix = info_ref[0]
    tokens, width = q_ref.shape
    heads = width // HD
    step = tokens // pieces
    line_greet(levels, row, level, partner)

    def make(at, i, way, src=None):
        part = pl.ds(i * step, step)
        dst = out_ref.at[2 * at + side, part]
        sems = ((u_send, u_recv), (d_send, d_recv), (x_send, x_recv))[way]
        peer = (row + 2, row - 2, partner)[way]
        return push(
            dst if src is None else src.at[part],
            dst,
            sems[0].at[at, i],
            sems[1].at[at, i],
            {"row": peer},
        )

    def other(at, i):
        part = pl.ds(i * step, step)
        dst = out_ref.at[2 * at + 1 - side, part]
        return push(dst, dst, x_send.at[at, i], x_recv.at[at, i], {"row": partner})

    def when(cond, run):
        @pl.when(cond)
        def _():
            for i in range(pieces):
                run(i)

    to_up = level < levels - 1
    own_down = (level > 0) & (level < low)
    own_side = (level < low) | (side == 0)
    for i in range(pieces):

        @pl.when(to_up)
        def _(i=i):
            make(level, i, 0, kv_ref).start()

        @pl.when(own_side)
        def _(i=i):
            make(level, i, 2, kv_ref).start()

        @pl.when(own_down)
        def _(i=i):
            make(level, i, 1, kv_ref).start()

    me = lax.axis_index("col")
    wide = []
    for k in range(1, COLS):
        peer = {"col": (me + k) % COLS}
        copy = push(g_ref, ga_ref.at[me], g_send.at[k - 1], g_recv.at[k - 1], peer)
        copy.start()
        wide.append(copy)
    ga_ref[me] = g_ref[...]
    out_ref[place] = kv_ref[...]
    m_ref[...] = jnp.full(m_ref.shape, neg_big, F32)
    acc_ref[...] = jnp.zeros(acc_ref.shape, F32)
    units = [(h, i) for h in range(heads) for i in range(tokens // qb)]

    def block(blk, masked):
        def raw_of(h, i):
            feats = slice(h * HD, (h + 1) * HD)
            raw = nt(out_ref[blk, :, feats], q_ref[i * qb : (i + 1) * qb, feats])
            if masked:
                allowed = seen(blk * tokens, place * tokens + i * qb, raw.shape, prefix)
                raw = jnp.where(allowed, raw, neg_big)
            return raw

        def soften(h, i, raw):
            cols = slice(i * qb, (i + 1) * qb)
            old = m_ref[h : h + 1, cols]
            new = jnp.maximum(old, jnp.max(raw, axis=0, keepdims=True))
            m_ref[h : h + 1, cols] = new
            weights = jnp.exp2((raw - new) * LOG2E).astype(BF16)
            return weights, jnp.exp2((old - new) * LOG2E)

        def gather(h, i, weights, scale):
            cols = slice(i * qb, (i + 1) * qb)
            v = out_ref[blk, :, width + h * HD : width + (h + 1) * HD]
            v_ext = jnp.concatenate([v.T, jnp.ones((16, tokens), BF16)], axis=0)
            acc_ref[h, :, cols] = acc_ref[h, :, cols] * scale + nn(v_ext, weights)

        coming, waiting = raw_of(*units[0]), None
        for n, unit in enumerate(units):
            raw = coming
            if n + 1 < len(units):
                coming = raw_of(*units[n + 1])
            soft = soften(*unit, raw)
            if waiting is not None:
                gather(*waiting)
            waiting = unit + soft
        gather(*waiting)

    def event(e, carry):
        t, cross = e // 2, e % 2
        at = jnp.where(t <= level, level - t, t)
        live = (t <= level) | (t < low)
        line_in = live & (cross == 0)

        @pl.when(line_in & (at < level))
        def _():
            for i in range(pieces):
                make(at, i, 0).wait_recv()

                @pl.when(to_up)
                def _(i=i):
                    make(at, i, 0).start()

                make(at, i, 2).start()

        @pl.when(line_in & (at > level))
        def _():
            for i in range(pieces):
                make(at, i, 1).wait_recv()

                @pl.when(level > 0)
                def _(i=i):
                    make(at, i, 1).start()

                make(at, i, 2).start()

        comes = live & (cross == 1) & ((at < low) | (at < level) | (side == 1))
        when(comes, lambda i: other(at, i).wait_recv())
        blk = 2 * at + jnp.where(cross == 0, side, 1 - side)
        needed = line_in | comes

        @pl.when(needed & (blk < place))
        def _():
            block(blk, False)

        @pl.when(needed & (blk >= place))
        def _():
            block(blk, True)

        return carry

    lax.fori_loop(0, 2 * levels, event, 0)

    for h in range(heads):
        total = acc_ref[h, HD : HD + 1, :]
        out = (acc_ref[h, :HD, :] / total).T
        o_ref[:, h * HD : (h + 1) * HD] = out
        ob_ref[:, h * HD : (h + 1) * HD] = out.astype(BF16)
        lse_ref[h : h + 1, :] = m_ref[h : h + 1, :] * LOG2E + jnp.log2(total)

    when(to_up, lambda i: make(level, i, 0, kv_ref).wait_send())
    when(own_side, lambda i: make(level, i, 2, kv_ref).wait_send())
    when(own_down, lambda i: make(level, i, 1, kv_ref).wait_send())
    for k in range(1, levels):
        at = level - k
        when((at >= 0) & to_up, lambda i, at=at: make(at, i, 0).wait_send())
        when(at >= 0, lambda i, at=at: make(at, i, 2).wait_send())
    for k in range(1, low):
        at = level + k
        when((at < low) & (level > 0), lambda i, at=at: make(at, i, 1).wait_send())
        when(at < low, lambda i, at=at: make(at, i, 2).wait_send())
    for copy in wide:
        copy.wait()


def attention_forward(info, q, kv, g, group, low, collective):
    pieces = 4
    levels = group // 2
    tokens, width = q.shape
    heads = width // HD
    return pl.pallas_call(
        functools.partial(forward_kernel, group, low, pieces, tokens // 2),
        out_shape=(
            jax.ShapeDtypeStruct((group,) + kv.shape, kv.dtype),
            jax.ShapeDtypeStruct((tokens, width), F32),
            jax.ShapeDtypeStruct((tokens, width), BF16),
            jax.ShapeDtypeStruct((8, tokens), F32),
            jax.ShapeDtypeStruct((COLS,) + g.shape, g.dtype),
        ),
        in_specs=[SSPEC, VSPEC, VSPEC, VSPEC],
        out_specs=(VSPEC,) * 5,
        scratch_shapes=[
            pltpu.VMEM((8, tokens), F32),
            pltpu.VMEM((heads, HD + 16, tokens), F32),
        ]
        + [DMA((levels, pieces))] * 6
        + [DMA((COLS - 1,))] * 2,
        compiler_params=params(collective),
    )(info, q, kv, g)


def backward_kernel(
    group,
    low,
    pieces,
    kb,
    info_ref,
    q_ref,
    kv_ref,
    do_ref,
    lse_ref,
    delta_ref,
    e_ref,
    bias_ref,
    dq_ref,
    out_ref,
    eo_ref,
    part_ref,
    rx_ref,
    above_ref,
    below_ref,
    snd_ref,
    acc_ref,
    dqt_ref,
    er_ref,
    u_send,
    u_recv,
    d_send,
    d_recv,
    x_send,
    x_recv,
    e_send,
    e_recv,
):
    levels = group // 2
    row, place, level, side, partner = line_places(group)
    prefix = info_ref[0]
    tokens, width = q_ref.shape
    heads = width // HD
    step = tokens // pieces
    line_greet(levels, row, level, partner)
    me = lax.axis_index("col")
    terms = []
    for k in range(1, COLS):
        peer = (me + k) % COLS
        copy = push(
            e_ref.at[peer], er_ref.at[k - 1], e_send.at[k - 1], e_recv.at[k - 1], {"col": peer}
        )
        copy.start()
        terms.append(copy)
    dqt_ref[...] = jnp.zeros(dqt_ref.shape, F32)

    def block(blk, masked):
        def body(j, carry):
            start = pl.multiple_of(j * kb, kb)
            keys = pl.ds(start, kb)
            for h in range(heads):
                feats = slice(h * HD, (h + 1) * HD)
                vals = slice(width + h * HD, width + (h + 1) * HD)
                k, v = kv_ref[blk, keys, feats], kv_ref[blk, keys, vals]
                q, do = q_ref[:, feats], do_ref[:, feats]
                probs = jnp.exp2(nt(k, q) * LOG2E - lse_ref[h : h + 1, :])
                if masked:
                    allowed = seen(blk * tokens + start, place * tokens, probs.shape, prefix)
                    probs = jnp.where(allowed, probs, 0.0)
                grad = (probs * (nt(v, do) - delta_ref[h : h + 1, :])).astype(BF16)
                part_ref[blk, keys, feats] = nn(grad, q).astype(BF16)
                part_ref[blk, keys, vals] = nn(probs.astype(BF16), do).astype(BF16)
                dqt_ref[feats, :] += nn(k.T, grad)
            return carry

        lax.fori_loop(0, tokens // kb, body, 0)

    def cross(at, i):
        part = pl.ds(i * step, step)
        return push(
            part_ref.at[2 * at + 1 - side, part],
            rx_ref.at[at, part],
            x_send.at[at, i],
            x_recv.at[at, i],
            {"row": partner},
        )

    def line(at, i, up):
        part = pl.ds(i * step, step)
        sems = (u_send, u_recv) if up else (d_send, d_recv)
        return push(
            snd_ref.at[at, part],
            (below_ref if up else above_ref).at[at, part],
            sems[0].at[at, i],
            sems[1].at[at, i],
            {"row": row + 2 if up else row - 2},
        )

    def gone(at):
        return (at < low) | (at < level) | ((at == level) & (side == 1))

    def comes(at):
        return (at < low) | (at < level) | ((at == level) & (side == 0))

    def total(at, i, from_above, from_below):
        part = pl.ds(i * step, step)
        acc_ref[...] = part_ref[2 * at + side, part].astype(F32)

        @pl.when(comes(at))
        def _():
            cross(at, i).wait_recv()
            acc_ref[...] += rx_ref[at, part].astype(F32)

        if from_above is not None:

            @pl.when(from_above)
            def _():
                line(at, i, False).wait_recv()
                acc_ref[...] += above_ref[at, part].astype(F32)

        if from_below is not None:

            @pl.when(from_below)
            def _():
                line(at, i, True).wait_recv()
                acc_ref[...] += below_ref[at, part].astype(F32)

    not_top = level < levels - 1
    above = jnp.maximum(low - 1 - level, 0)

    def level_of(t):
        return jnp.where(t < above, low - 1 - t, t - above)

    def event(e, carry):
        t, own = e // 2, e % 2
        at = level_of(t)
        live = (t < above) | (at <= level)

        down = t - (levels - level)

        @pl.when((own == 1) & (down >= 0) & (down < level))
        def _():
            for i in range(pieces):
                total(down, i, not_top, None)
                snd_ref[down, pl.ds(i * step, step)] = acc_ref[...].astype(BF16)
                line(down, i, False).start()

        @pl.when((own == 1) & (t >= 1) & (t - 1 < above))
        def _():
            up = level_of(t - 1)
            for i in range(pieces):
                total(up, i, None, level > 0)
                snd_ref[up, pl.ds(i * step, step)] = acc_ref[...].astype(BF16)
                line(up, i, True).start()

        goes = live & (own == 0) & gone(at)
        blk = 2 * at + jnp.where(own == 1, side, 1 - side)
        needed = goes | (live & (own == 1))

        @pl.when(needed & (blk < place))
        def _():
            block(blk, False)

        @pl.when(needed & (blk >= place))
        def _():
            block(blk, True)

        @pl.when(goes)
        def _():
            for i in range(pieces):
                cross(at, i).start()

        return carry

    lax.fori_loop(0, 2 * levels, event, 0)
    for copy in terms:
        copy.wait()

    def finish(r, carry):
        total = e_ref[me, r].astype(F32) + bias_ref[...]
        for k in range(COLS - 1):
            total = total + er_ref[k, r].astype(F32)
        eo_ref[r] = total.astype(BF16)
        return carry

    lax.fori_loop(0, e_ref.shape[1], finish, 0)
    dq_ref[...] = (dqt_ref[...] * HD**-0.5).T.astype(BF16)

    for i in range(pieces):
        total(level, i, not_top, (level > 0) & (level < low))
        out_ref[pl.ds(i * step, step)] = acc_ref[...].astype(BF16)

    for at in range(levels):
        for i in range(pieces):

            @pl.when(gone(at))
            def _(at=at, i=i):
                cross(at, i).wait_send()

            @pl.when(at < level)
            def _(at=at, i=i):
                line(at, i, False).wait_send()

            if at < low:

                @pl.when(at > level)
                def _(at=at, i=i):
                    line(at, i, True).wait_send()


def attention_backward(info, q, kv_all, do, lse, delta, e, bias, group, low, collective):
    pieces = 4
    levels = group // 2
    tokens, width = q.shape
    both = 2 * width
    block = pltpu.VMEM((levels, tokens, both), BF16)
    return pl.pallas_call(
        functools.partial(backward_kernel, group, low, pieces, tokens // 2),
        out_shape=(
            jax.ShapeDtypeStruct((tokens, width), BF16),
            jax.ShapeDtypeStruct((tokens, both), BF16),
            jax.ShapeDtypeStruct(e.shape[1:], BF16),
        ),
        in_specs=[SSPEC] + [VSPEC] * 7,
        out_specs=(VSPEC,) * 3,
        scratch_shapes=[
            pltpu.VMEM(kv_all.shape, BF16),
            block,
            block,
            pltpu.VMEM((low, tokens, both), BF16),
            block,
            pltpu.VMEM((tokens // pieces, both), F32),
            pltpu.VMEM((width, tokens), F32),
            pltpu.VMEM((COLS - 1,) + e.shape[1:], BF16),
        ]
        + [DMA((levels, pieces))] * 6
        + [DMA((COLS - 1,))] * 2,
        compiler_params=params(collective),
    )(info, q, kv_all, do, lse, delta, e, bias)


def product_kernel(pieces, rows, *refs):
    if rows:
        a_ref, b_ref, e_ref, out_ref, eo_ref = refs[:5]
        snd_ref, rx_ref, far_ref, tot_ref, send, recv, e_send, e_recv = refs[5:]
    else:
        a_ref, b_ref, out_ref, snd_ref, rx_ref, far_ref, tot_ref, send, recv = refs
    me, sib, across, diag = col_places()
    row = lax.axis_index("row")
    order = far_first(rows)
    greet([{"row": (row + k) % rows} for k in order] + [{"col": sib}, {"col": across}])
    home = []
    for n, k in enumerate(order):
        peer = (row + k) % rows
        copy = push(e_ref.at[peer], eo_ref.at[row], e_send.at[n], e_recv.at[n], {"row": peer})
        copy.start()
        home.append(copy)
    if rows:
        eo_ref[row] = e_ref[row]
    step = a_ref.shape[0] // pieces

    def term(i, who):
        return lax.dot_general(
            a_ref[pl.ds(i * step, step)],
            b_ref[who],
            (((1,), (1,)), ((), ())),
            preferred_element_type=F32,
        )

    def near(i, j):
        part = pl.ds(i * step, step)
        return push(
            snd_ref.at[j, part], rx_ref.at[j, part], send.at[j, i], recv.at[j, i], {"col": sib}
        )

    def over(i):
        part = pl.ds(i * step, step)
        return push(tot_ref.at[part], far_ref.at[part], send.at[2, i], recv.at[2, i], {"col": across})

    for i in range(pieces):
        snd_ref[0, pl.ds(i * step, step)] = term(i, diag).astype(BF16)
        near(i, 0).start()
    for i in range(pieces):
        part = pl.ds(i * step, step)
        mine = term(i, across)
        near(i, 0).wait_recv()
        tot_ref[part] = (mine + rx_ref[0, part].astype(F32)).astype(BF16)
        over(i).start()
    for i in range(pieces):
        snd_ref[1, pl.ds(i * step, step)] = term(i, sib).astype(BF16)
        near(i, 1).start()
    for i in range(pieces):
        part = pl.ds(i * step, step)
        mine = term(i, me)
        near(i, 1).wait_recv()
        mine = mine + rx_ref[1, part].astype(F32)
        over(i).wait_recv()
        out_ref[part] = mine + far_ref[part].astype(F32)
    for i in range(pieces):
        near(i, 0).wait_send()
        near(i, 1).wait_send()
        over(i).wait_send()
    for copy in home:
        copy.wait()


def product_scatter(a, b, collective, back=None):
    pieces = 4
    tokens, width = a.shape[0], b.shape[1]
    block = pltpu.VMEM((tokens, width), BF16)
    pair = pltpu.VMEM((2, tokens, width), BF16)
    out = jax.ShapeDtypeStruct((tokens, width), F32)
    scratch = [pair, pair, block, block, DMA((3, pieces)), DMA((3, pieces))]
    rows = 0
    if back is not None:
        rows = back.shape[0]
        out = (out, jax.ShapeDtypeStruct(back.shape, back.dtype))
        scratch = scratch + [DMA((rows - 1,))] * 2
    return pl.pallas_call(
        functools.partial(product_kernel, pieces, rows),
        out_shape=out,
        in_specs=[VSPEC] * (3 if rows else 2),
        out_specs=(VSPEC, VSPEC) if rows else VSPEC,
        scratch_shapes=scratch,
        compiler_params=params(collective),
    )(*((a, b, back) if rows else (a, b)))


def dispatch_kernel(rows, in_ref, out_ref, r_send, r_recv, c_send, c_recv):
    me, sib, across, _ = col_places()
    row = lax.axis_index("row")
    order = far_first(rows)
    peers = [(row + k) % rows for k in order]
    greet([{"row": p} for p in peers] + [{"col": sib}, {"col": across}])
    copies = []
    for k, peer in enumerate(peers):
        copy = push(
            in_ref.at[peer], out_ref.at[me, row], r_send.at[k], r_recv.at[k], {"row": peer}
        )
        copy.start()
        copies.append(copy)

    def col(src, dst, k, way):
        return push(
            src, dst, c_send.at[way, k], c_recv.at[way, k], {"col": across if way == 0 else sib}
        )

    done, first = [], []
    for way in range(2):
        copy = col(in_ref.at[row], out_ref.at[me, row], 0, way)
        copy.start()
        (first if way == 0 else done).append(copy)
    out_ref[me, row] = in_ref[row]
    sources = [row] + [(row + rows - k) % rows for k in order]

    def forward(k):
        first[k].wait_recv()
        src = sources[k]
        copy = col(out_ref.at[across, src], out_ref.at[across, src], k, 2)
        copy.start()
        done.append(copy)

    for k in range(1, rows):
        copies[k - 1].wait_recv()
        block = out_ref.at[me, sources[k]]
        for way in range(2):
            copy = col(block, block, k, way)
            copy.start()
            (first if way == 0 else done).append(copy)
        forward(k - 1)
    forward(rows - 1)
    for copy in copies:
        copy.wait_send()
    for copy in first:
        copy.wait_send()
    for copy in done:
        copy.wait()


def dispatch(x, rows, collective):
    return pl.pallas_call(
        functools.partial(dispatch_kernel, rows),
        out_shape=jax.ShapeDtypeStruct((COLS,) + x.shape, x.dtype),
        in_specs=[VSPEC],
        out_specs=VSPEC,
        scratch_shapes=[DMA((rows - 1,)), DMA((rows - 1,)), DMA((3, rows)), DMA((3, rows))],
        compiler_params=params(collective),
    )(x)


def giveback_kernel(
    rows, in_ref, out_ref, rx_ref, far_ref, tot_ref, fin_ref, send, recv, r_send, r_recv
):
    me, sib, across, diag = col_places()
    row = lax.axis_index("row")
    order = [(row + k) % rows for k in far_first(rows)] + [row]
    greet([{"row": p} for p in order[:-1]] + [{"col": sib}, {"col": across}])

    def near(k, j):
        who = diag if j == 0 else sib
        return push(
            in_ref.at[who, order[k]], rx_ref.at[j, k], send.at[j, k], recv.at[j, k], {"col": sib}
        )

    def over(k):
        return push(tot_ref.at[k], far_ref.at[k], send.at[2, k], recv.at[2, k], {"col": across})

    def home(k):
        return push(
            fin_ref.at[k], out_ref.at[row], r_send.at[k], r_recv.at[k], {"row": order[k]}
        )

    for k in range(rows):
        near(k, 0).start()
        near(k, 1).start()

    def finish(k):
        near(k, 1).wait_recv()
        over(k).wait_recv()
        total = in_ref[me, order[k]].astype(F32) + rx_ref[1, k].astype(F32)
        total = total + far_ref[k].astype(F32)
        if k == rows - 1:
            out_ref[row] = total.astype(BF16)
        else:
            fin_ref[k] = total.astype(BF16)
            home(k).start()

    for k in range(rows):
        near(k, 0).wait_recv()
        tot_ref[k] = (in_ref[across, order[k]].astype(F32) + rx_ref[0, k].astype(F32)).astype(BF16)
        over(k).start()
        if k >= 1:
            finish(k - 1)
    finish(rows - 1)
    for k in range(rows):
        near(k, 0).wait_send()
        near(k, 1).wait_send()
        over(k).wait_send()
        if k < rows - 1:
            home(k).wait()


def giveback(parts, rows, collective):
    block = parts.shape[2:]
    one = pltpu.VMEM((rows,) + block, BF16)
    return pl.pallas_call(
        functools.partial(giveback_kernel, rows),
        out_shape=jax.ShapeDtypeStruct((rows,) + block, BF16),
        in_specs=[VSPEC],
        out_specs=VSPEC,
        scratch_shapes=[
            pltpu.VMEM((2, rows) + block, BF16),
            one,
            one,
            one,
            DMA((3, rows)),
            DMA((3, rows)),
            DMA((rows - 1,)),
            DMA((rows - 1,)),
        ],
        compiler_params=params(collective),
    )(parts)


def end_kernel(rows, w_ref, s_ref, wo_ref, so_ref, wr_ref, sr_ref, send, recv):
    row = lax.axis_index("row")
    peers = [(row + k) % rows for k in range(1, rows)]
    greet([{"row": p} for p in peers])
    copies = []
    for k, peer in enumerate(peers):
        for j, (src, dst) in enumerate(((w_ref, wr_ref), (s_ref, sr_ref))):
            copy = push(src.at[peer], dst.at[k], send.at[j, k], recv.at[j, k], {"row": peer})
            copy.start()
            copies.append(copy)
    wo_ref[...] = w_ref[row].astype(F32)
    so_ref[...] = s_ref[row]
    for k in range(rows - 1):
        copies[2 * k].wait_recv()
        copies[2 * k + 1].wait_recv()
        wo_ref[...] += wr_ref[k].astype(F32)
        so_ref[...] += sr_ref[k]
    for copy in copies:
        copy.wait_send()


def end_scatter(w, s, rows, collective):
    return pl.pallas_call(
        functools.partial(end_kernel, rows),
        out_shape=(
            jax.ShapeDtypeStruct(w.shape[1:], F32),
            jax.ShapeDtypeStruct(s.shape[1:], F32),
        ),
        in_specs=[VSPEC] * 2,
        out_specs=(VSPEC,) * 2,
        scratch_shapes=[
            pltpu.VMEM((rows - 1,) + w.shape[1:], w.dtype),
            pltpu.VMEM((rows - 1,) + s.shape[1:], s.dtype),
            DMA((2, rows - 1)),
            DMA((2, rows - 1)),
        ],
        compiler_params=params(collective),
    )(w, s)


def expert_kernel(
    x_ref,
    g_ref,
    up_ref,
    bias_ref,
    down_ref,
    part_ref,
    gx_ref,
    gup_ref,
    gbu_ref,
    gdown_ref,
    gbd_ref,
):
    cols, rows, _, cap, width = x_ref.shape
    slots = rows * cap
    x = jnp.concatenate([x_ref[b, :, 0].reshape(slots, width) for b in range(cols)], axis=1)
    g = jnp.concatenate([g_ref[b, :, 0].reshape(slots, width) for b in range(cols)], axis=1)
    gbd_ref[...] = jnp.sum(g.astype(F32), axis=0).reshape(gbd_ref.shape)
    hidden_units = up_ref.shape[2]
    chunk = 256
    part = jnp.zeros((slots, cols * width), F32)
    gx = jnp.zeros((slots, cols * width), F32)
    for f in range(hidden_units // chunk):
        cut = slice(f * chunk, (f + 1) * chunk)
        up, down = up_ref[0, :, cut], down_ref[0, cut, :]
        pre = nn(x, up) + bias_ref[0, :, cut].astype(F32)
        cdf = 0.5 * (1.0 + lax.erf(pre * (0.5**0.5)))
        slope = cdf + pre * (jnp.exp(-0.5 * pre * pre) * 0.3989422804014327)
        hidden = (pre * cdf).astype(BF16)
        grad = nt(g, down) * slope
        grad = grad.astype(BF16)
        part = part + nn(hidden, down)
        gx = gx + nt(grad, up)
        gdown_ref[0, cut, :] = tn(hidden, g)
        gup_ref[0, :, cut] = tn(x, grad)
        gbu_ref[0, :, cut] = jnp.sum(grad.astype(F32), axis=0, keepdims=True)
    for b in range(cols):
        cut = slice(b * width, (b + 1) * width)
        part_ref[b, :, 0] = part[:, cut].astype(BF16).reshape(rows, cap, width)
        gx_ref[b, :, 0] = gx[:, cut].astype(BF16).reshape(rows, cap, width)


def experts(x, g, w_up, bias_up, w_down):
    cols, rows, count, cap, width = x.shape
    slots = pl.BlockSpec((cols, rows, 1, cap, width), lambda e: (0, 0, e, 0, 0))
    _, features, hidden = w_up.shape
    return pl.pallas_call(
        expert_kernel,
        grid=(count,),
        out_shape=(
            jax.ShapeDtypeStruct(x.shape, BF16),
            jax.ShapeDtypeStruct(x.shape, BF16),
            jax.ShapeDtypeStruct(w_up.shape, F32),
            jax.ShapeDtypeStruct((count, 1, hidden), F32),
            jax.ShapeDtypeStruct(w_down.shape, F32),
            jax.ShapeDtypeStruct((count, 1, features), F32),
        ),
        in_specs=[
            slots,
            slots,
            pl.BlockSpec((1, features, hidden), lambda e: (e, 0, 0)),
            pl.BlockSpec((1, 1, hidden), lambda e: (e, 0, 0)),
            pl.BlockSpec((1, hidden, features), lambda e: (e, 0, 0)),
        ],
        out_specs=(
            slots,
            slots,
            pl.BlockSpec((1, features, hidden), lambda e: (e, 0, 0)),
            pl.BlockSpec((1, 1, hidden), lambda e: (e, 0, 0)),
            pl.BlockSpec((1, hidden, features), lambda e: (e, 0, 0)),
            pl.BlockSpec((1, 1, features), lambda e: (e, 0, 0)),
        ),
        compiler_params=params(),
    )(x, g, w_up, bias_up.reshape(count, 1, hidden), w_down)


def per_device(
    layer_in,
    cotangent,
    token_ids,
    hash_table,
    prefix_len,
    w_query,
    w_key,
    w_value,
    w_output,
    bias_query,
    bias_value,
    gain_attn,
    shift_attn,
    gain_moe,
    shift_moe,
    bias_output,
    w_up,
    bias_up,
    w_down,
    bias_down,
):
    rows = lax.axis_size("row")
    row = lax.axis_index("row")
    col = lax.axis_index("col")
    tokens, width = layer_in.shape
    heads = width // HD
    seq_len = min(LENGTH, tokens * rows)
    group = seq_len // tokens
    low = -(-PREFIX_MAX // (2 * tokens))
    share = w_query.shape[0]
    bias_share = bias_query.shape[0]

    def line(v):
        return jnp.pad(v.astype(F32), (0, 128 - v.shape[0]))

    small = jnp.stack(
        [
            line(gain_attn),
            line(shift_attn),
            line(gain_moe),
            line(shift_moe),
            line(bias_output),
            line(bias_query.T.reshape(-1)),
            line(bias_value.T.reshape(-1)),
            jnp.zeros((128,), F32),
        ]
    )
    expert_total = EXP_DEV * rows
    capacity = max(2, 2 * tokens // expert_total)
    expert_of = hash_table[token_ids]
    hits = expert_of[:, None] == jnp.arange(expert_total, dtype=jnp.int32)[None, :]
    earlier = (
        jnp.arange(tokens, dtype=jnp.int32)[None, :] < jnp.arange(tokens, dtype=jnp.int32)[:, None]
    )
    before = jnp.dot(earlier.astype(BF16), hits.astype(BF16), preferred_element_type=F32)
    slot_of = jnp.sum(jnp.where(hits, before, 0.0), axis=1).astype(jnp.int32)
    target = expert_of * capacity + slot_of
    chosen = (
        jnp.arange(expert_total * capacity, dtype=jnp.int32)[:, None] == target[None, :]
    ).astype(BF16)

    def place_rows(v):
        v = jnp.dot(chosen, v, preferred_element_type=F32).astype(BF16)
        return v.reshape(rows, EXP_DEV, capacity, width)

    weights = jnp.concatenate([w_query, w_key, w_value, w_output], axis=1)
    x_all, g_own, w_all, s_all = start_gather(
        layer_in, place_rows(cotangent), weights, small, rows
    )
    w_all = w_all.reshape(D, 4 * width)
    w_qkv = w_all[:, : 3 * width]
    w_out = w_all[:, 3 * width :].reshape(COLS, width, width)
    gain_one, shift_one, gain_two, shift_two, out_bias = (
        s_all[:, i, :share].reshape(D) for i in range(5)
    )

    def own(v):
        return lax.dynamic_slice_in_dim(v, col * width, width, 0)

    query_bias, value_bias = (
        s_all[:, i, : heads * bias_share]
        .reshape(rows, heads, bias_share)
        .transpose(1, 0, 2)
        .reshape(width)
        for i in (5, 6)
    )

    resid = x_all.transpose(1, 0, 2).reshape(tokens, D).astype(F32)
    mean_one = jnp.mean(resid, axis=-1, keepdims=True)
    centred = resid - mean_one
    rstd_one = lax.rsqrt(jnp.mean(centred * centred, axis=-1, keepdims=True) + epsilon)
    h_one = (centred * rstd_one * gain_one + shift_one).astype(BF16)
    qkv_bias = jnp.concatenate([query_bias, jnp.zeros_like(query_bias), value_bias])
    qkv = (jnp.dot(h_one, w_qkv, preferred_element_type=F32) + qkv_bias).astype(BF16)
    queries = qkv[:, :width] * jnp.asarray(HD**-0.5, BF16)
    seq_hit = row // group == jnp.arange(prefix_len.shape[0], dtype=jnp.int32)
    prefix = jnp.sum(jnp.where(seq_hit, prefix_len, 0))
    info = prefix.astype(jnp.int32).reshape(1)
    kv_all, attended, attended_low, lse, g_all = attention_forward(
        info, queries, qkv[:, width:], g_own, group, low, 1
    )
    branch = product_scatter(attended_low, w_out, 2)
    x_own = layer_in.astype(F32)
    mid = x_own + branch + own(out_bias)

    part_mean = jnp.mean(mid, axis=-1)
    part_spread = jnp.sum((mid - part_mean[:, None]) ** 2, axis=-1)
    stats = jnp.stack([part_mean, part_spread]).reshape(-1, 128)
    stats = small_gather(stats, 3).reshape(COLS, 2, tokens)
    mean_two = jnp.mean(stats[:, 0], axis=0)
    spread = jnp.sum(stats[:, 1] + width * (stats[:, 0] - mean_two) ** 2, axis=0) / D
    rstd_two = lax.rsqrt(spread + epsilon)[:, None]
    normed_two = (mid - mean_two[:, None]) * rstd_two
    gain_two_own = own(gain_two)
    h_two = (normed_two * gain_two_own + own(shift_two)).astype(BF16)

    received = dispatch(place_rows(h_two), rows, 4)
    parts, grad_parts, grad_w_up, grad_bias_up, grad_w_down, grad_bias_down = experts(
        received, g_all, w_up, bias_up, w_down
    )
    grad_h_two = tn(chosen, giveback(grad_parts, rows, 5).reshape(-1, width))

    scaled = grad_h_two * gain_two_own
    sums = jnp.stack([jnp.sum(scaled, axis=-1), jnp.sum(scaled * normed_two, axis=-1)])
    sums = small_gather(sums.reshape(-1, 128), 6).reshape(COLS, 2, tokens)
    sums = jnp.sum(sums, axis=0) / D
    grad_mid = cotangent.astype(F32) + rstd_two * (
        scaled - sums[0][:, None] - normed_two * sums[1][:, None]
    )
    grad_all = col_gather(grad_mid.astype(BF16), 7)
    grad_wide = grad_all.transpose(1, 0, 2).reshape(tokens, D)
    grad_w_out = lax.dot_general(
        grad_wide, attended_low, (((0,), (0,)), ((), ())), preferred_element_type=F32
    )
    grad_attended = jnp.dot(
        grad_wide, w_out.reshape(D, width), preferred_element_type=F32
    ).astype(BF16)
    delta = jnp.sum(
        (grad_attended.astype(F32) * attended).reshape(tokens, heads, HD), axis=-1
    ).T
    delta = jnp.pad(delta, ((0, 8 - heads), (0, 0)))
    down_own = lax.dynamic_slice_in_dim(bias_down, col * width, width, 1).astype(F32)
    grad_q, grad_kv, outs = attention_backward(
        info,
        queries,
        kv_all,
        grad_attended,
        lse,
        delta,
        parts,
        down_own[:, None, :],
        group,
        low,
        8,
    )
    grad_qkv = jnp.concatenate([grad_q, grad_kv], axis=1)
    grad_w_qkv = lax.dot_general(
        h_one, grad_qkv, (((0,), (0,)), ((), ())), preferred_element_type=F32
    )
    grad_bias = jnp.sum(grad_qkv, axis=0, dtype=F32)
    grad_h_one, outs = product_scatter(grad_qkv, w_qkv.reshape(COLS, width, 3 * width), 9, outs)
    layer_out = (mid + tn(chosen, outs.reshape(-1, width))).astype(BF16)
    normed_one = (x_own - mean_one) * rstd_one
    scaled = grad_h_one * own(gain_one)
    sums = jnp.stack([jnp.sum(scaled, axis=-1), jnp.sum(scaled * normed_one, axis=-1)])
    vectors = jnp.stack(
        [
            jnp.sum(grad_h_one * normed_one, axis=0),
            jnp.sum(grad_h_one, axis=0),
            jnp.sum(grad_h_two * normed_two, axis=0),
            jnp.sum(grad_h_two, axis=0),
            jnp.sum(grad_mid, axis=0),
        ]
    )
    vectors = jnp.pad(vectors, ((0, 3), (0, 256 - width))).reshape(-1, 128)
    shared = small_gather(jnp.concatenate([sums.reshape(-1, 128), vectors]), 10)
    used = 2 * tokens // 128
    sums = jnp.sum(shared[:, :used].reshape(COLS, 2, tokens), axis=0) / D
    grad_in = grad_mid + rstd_one * (scaled - sums[0][:, None] - normed_one * sums[1][:, None])
    vectors = shared[:, used:].reshape(COLS, 8, 256)[:, :5, :width]
    vectors = vectors.transpose(1, 0, 2).reshape(5, rows, share).transpose(1, 0, 2)

    def by_row(v):
        v = v.reshape(heads, rows, bias_share).transpose(1, 0, 2).reshape(rows, 1, -1)
        return jnp.pad(v, ((0, 0), (0, 0), (0, 128 - v.shape[2])))

    small_terms = jnp.concatenate(
        [
            jnp.pad(vectors, ((0, 0), (0, 0), (0, 128 - share))),
            by_row(grad_bias[:width]),
            by_row(grad_bias[2 * width :]),
            jnp.zeros((rows, 1, 128), F32),
        ],
        axis=1,
    )
    weight_terms = jnp.concatenate([grad_w_qkv, grad_w_out], axis=1).astype(BF16)
    weight_sums, small_sums = end_scatter(
        weight_terms.reshape(rows, share, 4 * width), small_terms, rows, 11
    )

    def bias_back(v):
        return v[: heads * bias_share].reshape(heads, bias_share).T

    return (
        layer_out,
        grad_in,
        weight_sums[:, :width],
        weight_sums[:, width : 2 * width],
        weight_sums[:, 2 * width : 3 * width],
        weight_sums[:, 3 * width :],
        bias_back(small_sums[5]),
        bias_back(small_sums[6]),
        small_sums[0, :share],
        small_sums[1, :share],
        small_sums[2, :share],
        small_sums[3, :share],
        small_sums[4, :share],
        grad_w_up,
        grad_bias_up[:, 0],
        grad_w_down,
        grad_bias_down[:, 0],
    )


def solution(mesh):
    placed = (
        P("row", "col"),
        P("row", "col"),
        P("row"),
        P(),
        P(),
        P("row", "col"),
        P("row", "col"),
        P("row", "col"),
        P("row", "col"),
        P("row", "col"),
        P("row", "col"),
        P("row"),
        P("row"),
        P("row"),
        P("row"),
        P("row"),
        P("row", None, "col"),
        P("row", "col"),
        P("row", "col", None),
        P("row", None),
    )
    return jax.shard_map(
        per_device,
        mesh=mesh,
        in_specs=placed,
        out_specs=(
            P("row", "col"),
            P("row", "col"),
            P("row", "col"),
            P("row", "col"),
            P("row", "col"),
            P("row", "col"),
            P("row", "col"),
            P("row", "col"),
            P("row"),
            P("row"),
            P("row"),
            P("row"),
            P("row"),
            P("row", None, "col"),
            P("row", "col"),
            P("row", "col", None),
            P("row", None),
        ),
        check_vma=False,
    )
```

```python
import functools

import jax
import jax.numpy as jnp
from jax import lax
from jax.experimental import pallas as pl
from jax.experimental.pallas import tpu as pltpu
from jax.sharding import PartitionSpec as P

D = 768
HD = 64
EXP_DEV = 2
LENGTH = 8192
PREFIX_MAX = 4096
COLS = 4

F32 = jnp.float32
BF16 = jnp.bfloat16
MESH = pl.DeviceIdType.MESH
LOG2E = 1.4426950408889634

epsilon = 1e-05
neg_big = -1e30

VSPEC = pl.BlockSpec(memory_space=pltpu.VMEM)
SSPEC = pl.BlockSpec(memory_space=pltpu.SMEM)
VMEM_BYTES = 64 * 1000 * 1000
DMA = pltpu.SemaphoreType.DMA


def params(collective=None):
    if collective is None:
        return pltpu.CompilerParams(vmem_limit_bytes=VMEM_BYTES)
    return pltpu.CompilerParams(
        vmem_limit_bytes=VMEM_BYTES, collective_id=collective, has_side_effects=True
    )


def push(src, dst, send_sem, recv_sem, peer):
    return pltpu.make_async_remote_copy(
        src_ref=src,
        dst_ref=dst,
        send_sem=send_sem,
        recv_sem=recv_sem,
        device_id=peer,
        device_id_type=MESH,
    )


def greet(peers):
    barrier = pltpu.get_barrier_semaphore()
    for peer in peers:
        pl.semaphore_signal(barrier, inc=1, device_id=peer, device_id_type=MESH)
    pl.semaphore_wait(barrier, len(peers))


def col_places():
    me = lax.axis_index("col")
    sib = me + 1 - 2 * (me % 2)
    across = (me + 2) % COLS
    diag = (sib + 2) % COLS
    return me, sib, across, diag


def line_places(group):
    row = lax.axis_index("row")
    place = row % group
    level, side = place // 2, place % 2
    return row, place, level, side, row + 1 - 2 * side


def far_first(rows):
    return sorted(range(1, rows), key=lambda k: -min(k, rows - k))


def nt(left, right):
    return lax.dot_general(left, right, (((1,), (1,)), ((), ())), preferred_element_type=F32)


def nn(left, right):
    return lax.dot_general(left, right, (((1,), (0,)), ((), ())), preferred_element_type=F32)


def tn(left, right):
    return lax.dot_general(left, right, (((0,), (0,)), ((), ())), preferred_element_type=F32)


def side_by_side(v):
    half = v.shape[0] // 2
    return jnp.concatenate([v[:half], v[half:]], axis=1)


def slots_of(target_ref, row, count):
    base = row * count
    slot = base + lax.broadcasted_iota(jnp.int32, (count, target_ref.shape[1]), 0)
    return jnp.where(slot == target_ref[...], 1.0, 0.0).astype(BF16)


def placed(target_ref, v, row, cap):
    return side_by_side(nn(slots_of(target_ref, row, 2 * cap), v).astype(BF16))


def combined(target_ref, block, row, cap):
    width = block.shape[1] // 2
    stacked = jnp.concatenate([block[:, :width], block[:, width:]], axis=0)
    return tn(slots_of(target_ref, row, 2 * cap), stacked)


def start_kernel(
    rows,
    pieces,
    x_ref,
    g_ref,
    t_ref,
    w_ref,
    s_ref,
    xo_ref,
    go_ref,
    wo_ref,
    so_ref,
    xp_ref,
    gp_ref,
    c_send,
    c_recv,
    r_send,
    r_recv,
    l_send,
    l_recv,
):
    me, sib, across, _ = col_places()
    row, _, level, side, partner = line_places(rows)
    levels = rows // 2
    order = far_first(rows)
    peers = [{"row": (row + k) % rows} for k in order]
    greet(peers + [{"col": sib}, {"col": across}])
    xp_ref[...] = side_by_side(x_ref[...])
    step = xp_ref.shape[0] // pieces
    cap = gp_ref.shape[1]
    to_up, to_down = level < levels - 1, level > 0

    def weight(at, way, src=None):
        dst = wo_ref.at[2 * at + side]
        peer = (row + 2, row - 2, partner)[way]
        return push(
            dst if src is None else src,
            dst,
            l_send.at[way, at],
            l_recv.at[way, at],
            {"row": peer},
        )

    def weight_other(at):
        dst = wo_ref.at[2 * at + 1 - side]
        return push(dst, dst, l_send.at[2, at], l_recv.at[2, at], {"row": partner})

    @pl.when(to_up)
    def _():
        weight(level, 0, w_ref).start()

    @pl.when(to_down)
    def _():
        weight(level, 1, w_ref).start()

    weight(level, 2, w_ref).start()
    sent = []
    for i in range(pieces):
        part = pl.ds(i * step, step)
        for way, peer in ((0, across), (1, sib)):
            copy = push(
                xp_ref.at[part],
                xo_ref.at[me, part],
                c_send.at[way, i],
                c_recv.at[way, i],
                {"col": peer},
            )
            copy.start()
            sent.append(copy)
    row_copies = []
    for k, peer in enumerate(peers):
        copy = push(s_ref, so_ref.at[row], r_send.at[0, k], r_recv.at[0, k], peer)
        copy.start()
        row_copies.append(copy)

    def send_rows(k):
        target = (row + order[k]) % rows
        gp_ref[k] = placed(t_ref, g_ref[...], target, cap)
        copy = push(gp_ref.at[k], go_ref.at[row], r_send.at[1, k], r_recv.at[1, k], peers[k])
        copy.start()
        row_copies.append(copy)

    send_rows(0)
    xo_ref[me] = xp_ref[...]
    wo_ref[row] = w_ref[...]
    so_ref[row] = s_ref[...]
    todo = list(range(1, rows - 1))

    def pass_on(k):
        at = level - k

        @pl.when(at >= 0)
        def _():
            weight(at, 0).wait_recv()

            @pl.when(to_up)
            def _():
                weight(at, 0).start()

            weight(at, 2).start()

        up = level + k

        @pl.when(up < levels)
        def _():
            weight(up, 1).wait_recv()

            @pl.when(to_down)
            def _():
                weight(up, 1).start()

            weight(up, 2).start()

    late = []
    for k in range(1, max(levels, pieces + 1)):
        if k < levels:
            pass_on(k)
        if k <= pieces:
            part = pl.ds((k - 1) * step, step)
            sent[2 * k - 2].wait_recv()
            copy = push(
                xo_ref.at[across, part],
                xo_ref.at[across, part],
                c_send.at[2, k - 1],
                c_recv.at[2, k - 1],
                {"col": sib},
            )
            copy.start()
            late.append(copy)
        for _ in range(2):
            if todo:
                send_rows(todo.pop(0))
    while todo:
        send_rows(todo.pop(0))
    go_ref[row] = placed(t_ref, g_ref[...], row, cap)
    for i in range(pieces):
        sent[2 * i].wait_send()
        sent[2 * i + 1].wait()
        late[i].wait()
    for at in range(levels):
        weight_other(at).wait_recv()
        weight(at, 2).wait_send()

        @pl.when((at <= level) & to_up)
        def _(at=at):
            weight(at, 0).wait_send()

        @pl.when((at >= level) & to_down)
        def _(at=at):
            weight(at, 1).wait_send()

    for copy in row_copies:
        copy.wait()


def start_gather(x, g, target, w, s, rows, cap):
    pieces = 4
    tokens, width = x.shape
    packed = (tokens // 2, 2 * width)
    return pl.pallas_call(
        functools.partial(start_kernel, rows, pieces),
        out_shape=(
            jax.ShapeDtypeStruct((COLS,) + packed, x.dtype),
            jax.ShapeDtypeStruct((rows, cap, 2 * width), g.dtype),
            jax.ShapeDtypeStruct((rows,) + w.shape, w.dtype),
            jax.ShapeDtypeStruct((rows,) + s.shape, s.dtype),
        ),
        in_specs=[VSPEC] * 5,
        out_specs=(VSPEC,) * 4,
        scratch_shapes=[
            pltpu.VMEM(packed, x.dtype),
            pltpu.VMEM((rows - 1, cap, 2 * width), g.dtype),
            DMA((3, pieces)),
            DMA((3, pieces)),
            DMA((2, rows - 1)),
            DMA((2, rows - 1)),
            DMA((3, rows // 2)),
            DMA((3, rows // 2)),
        ],
        compiler_params=params(0),
    )(x, g, target, w, s)


def project_kernel(
    x_ref, w_ref, gain_ref, shift_ref, bias_ref, q_ref, kv_ref, h_ref, n_ref, r_ref
):
    me = lax.axis_index("col")
    half, width = x_ref.shape[1], x_ref.shape[2] // 2
    w = w_ref[...].reshape(D, 4 * width)[:, : 3 * width]
    step = min(half, 256)
    for i in range(2 * half // step):
        side, start = i * step // half, i * step % half
        rows, feats = slice(start, start + step), slice(side * width, (side + 1) * width)
        x = jnp.concatenate([x_ref[b, rows, feats] for b in range(COLS)], axis=1).astype(F32)
        mean = jnp.mean(x, axis=-1, keepdims=True)
        centred = x - mean
        rstd = lax.rsqrt(jnp.mean(centred * centred, axis=-1, keepdims=True) + epsilon)
        h = (centred * rstd * gain_ref[...] + shift_ref[...]).astype(BF16)
        out = slice(i * step, (i + 1) * step)
        h_ref[out] = h
        n_ref[out] = (x_ref[me, rows, feats].astype(F32) - mean) * rstd
        r_ref[out] = rstd
        qkv = (nn(h, w) + bias_ref[...]).astype(BF16)
        q_ref[out] = qkv[:, :width] * jnp.asarray(HD**-0.5, BF16)
        kv_ref[out] = qkv[:, width:]


def project(x, w, gain, shift, bias):
    tokens, width = 2 * x.shape[1], x.shape[2] // 2
    return pl.pallas_call(
        project_kernel,
        out_shape=(
            jax.ShapeDtypeStruct((tokens, width), BF16),
            jax.ShapeDtypeStruct((tokens, 2 * width), BF16),
            jax.ShapeDtypeStruct((tokens, D), BF16),
            jax.ShapeDtypeStruct((tokens, width), F32),
            jax.ShapeDtypeStruct((tokens, 1), F32),
        ),
        in_specs=[VSPEC] * 5,
        out_specs=(VSPEC,) * 5,
        compiler_params=params(),
    )(x, w, gain, shift, bias)


def mid_kernel(
    pieces,
    x_ref,
    w_ref,
    att_ref,
    low_ref,
    do_ref,
    delta_ref,
    gw_ref,
    xp_ref,
    xo_ref,
    wide_ref,
    c_send,
    c_recv,
):
    me, sib, across, _ = col_places()
    greet([{"col": sib}, {"col": across}])
    xp_ref[...] = side_by_side(x_ref[...].astype(BF16))
    step = xp_ref.shape[0] // pieces
    sent, late = [], []
    for i in range(pieces):
        part = pl.ds(i * step, step)
        for way, peer in ((0, across), (1, sib)):
            copy = push(
                xp_ref.at[part],
                xo_ref.at[me, part],
                c_send.at[way, i],
                c_recv.at[way, i],
                {"col": peer},
            )
            copy.start()
            sent.append(copy)
    xo_ref[me] = xp_ref[...]
    tokens, width = x_ref.shape
    w = w_ref[...].reshape(D, 4 * width)[:, 3 * width :]
    for i in range(pieces):
        part = pl.ds(i * step, step)
        sent[2 * i].wait_recv()
        copy = push(
            xo_ref.at[across, part],
            xo_ref.at[across, part],
            c_send.at[2, i],
            c_recv.at[2, i],
            {"col": sib},
        )
        copy.start()
        late.append(copy)
    for i in range(pieces):
        sent[2 * i].wait_send()
        sent[2 * i + 1].wait()
        late[i].wait()
        rows = slice(i * step, (i + 1) * step)
        for half in range(2):
            feats = slice(half * width, (half + 1) * width)
            start = half * (tokens // 2) + i * step
            out = slice(start, start + step)
            wide = jnp.concatenate([xo_ref[b, rows, feats] for b in range(COLS)], axis=1)
            wide_ref[out] = wide
            do = nn(wide, w).astype(BF16)
            do_ref[out] = do
            both = (do.astype(F32) * att_ref[out]).T
            for h in range(width // HD):
                delta_ref[h : h + 1, out] = jnp.sum(
                    both[h * HD : (h + 1) * HD], axis=0, keepdims=True
                )
    gw_ref[...] = tn(wide_ref[...], low_ref[...]).astype(BF16)


def mid_gradient(x, w, attended, low, collective):
    pieces = 4
    tokens, width = x.shape
    packed = (tokens // 2, 2 * width)
    return pl.pallas_call(
        functools.partial(mid_kernel, pieces),
        out_shape=(
            jax.ShapeDtypeStruct((tokens, width), BF16),
            jax.ShapeDtypeStruct((8, tokens), F32),
            jax.ShapeDtypeStruct((D, width), BF16),
        ),
        in_specs=[VSPEC] * 4,
        out_specs=(VSPEC,) * 3,
        scratch_shapes=[
            pltpu.VMEM(packed, BF16),
            pltpu.VMEM((COLS,) + packed, BF16),
            pltpu.VMEM((tokens, D), BF16),
            DMA((3, pieces)),
            DMA((3, pieces)),
        ],
        compiler_params=params(collective),
    )(x, w, attended, low)


def small_kernel(x_ref, xo_ref, c_send, c_recv):
    me = lax.axis_index("col")
    peers = [{"col": (me + k) % COLS} for k in range(1, COLS)]
    greet(peers)
    copies = []
    for k, peer in enumerate(peers):
        copy = push(x_ref, xo_ref.at[me], c_send.at[k], c_recv.at[k], peer)
        copy.start()
        copies.append(copy)
    xo_ref[me] = x_ref[...]
    for copy in copies:
        copy.wait()


def small_gather(x, collective):
    return pl.pallas_call(
        small_kernel,
        out_shape=jax.ShapeDtypeStruct((COLS,) + x.shape, x.dtype),
        in_specs=[VSPEC],
        out_specs=VSPEC,
        scratch_shapes=[DMA((COLS - 1,)), DMA((COLS - 1,))],
        compiler_params=params(collective),
    )(x)


def line_greet(levels, row, level, partner):
    barrier = pltpu.get_barrier_semaphore()
    me = lax.axis_index("col")
    for k in range(1, COLS):
        peer = {"col": (me + k) % COLS}
        pl.semaphore_signal(barrier, inc=1, device_id=peer, device_id_type=MESH)
    pl.semaphore_signal(barrier, inc=1, device_id={"row": partner}, device_id_type=MESH)

    @pl.when(level > 0)
    def _():
        pl.semaphore_signal(barrier, inc=1, device_id={"row": row - 2}, device_id_type=MESH)

    @pl.when(level < levels - 1)
    def _():
        pl.semaphore_signal(barrier, inc=1, device_id={"row": row + 2}, device_id_type=MESH)

    count = COLS + (level > 0).astype(jnp.int32) + (level < levels - 1).astype(jnp.int32)
    pl.semaphore_wait(barrier, count)


def seen(key_start, query_start, shape, prefix):
    key = key_start + lax.broadcasted_iota(jnp.int32, shape, 0)
    query = query_start + lax.broadcasted_iota(jnp.int32, shape, 1)
    return (key < prefix) | (key <= query)


def forward_kernel(
    group,
    low,
    pieces,
    qb,
    info_ref,
    q_ref,
    kv_ref,
    g_ref,
    out_ref,
    o_ref,
    ob_ref,
    lse_ref,
    ga_ref,
    m_ref,
    acc_ref,
    u_send,
    u_recv,
    d_send,
    d_recv,
    x_send,
    x_recv,
    g_send,
    g_recv,
):
    levels = group // 2
    row, place, level, side, partner = line_places(group)
    prefix = info_ref[0]
    tokens, width = q_ref.shape
    heads = width // HD
    step = tokens // pieces
    line_greet(levels, row, level, partner)

    def make(at, i, way, src=None):
        part = pl.ds(i * step, step)
        dst = out_ref.at[2 * at + side, part]
        sems = ((u_send, u_recv), (d_send, d_recv), (x_send, x_recv))[way]
        peer = (row + 2, row - 2, partner)[way]
        return push(
            dst if src is None else src.at[part],
            dst,
            sems[0].at[at, i],
            sems[1].at[at, i],
            {"row": peer},
        )

    def other(at, i):
        part = pl.ds(i * step, step)
        dst = out_ref.at[2 * at + 1 - side, part]
        return push(dst, dst, x_send.at[at, i], x_recv.at[at, i], {"row": partner})

    def when(cond, run):
        @pl.when(cond)
        def _():
            for i in range(pieces):
                run(i)

    to_up = level < levels - 1
    own_down = (level > 0) & (level < low)
    own_side = (level < low) | (side == 0)
    for i in range(pieces):

        @pl.when(to_up)
        def _(i=i):
            make(level, i, 0, kv_ref).start()

        @pl.when(own_side)
        def _(i=i):
            make(level, i, 2, kv_ref).start()

        @pl.when(own_down)
        def _(i=i):
            make(level, i, 1, kv_ref).start()

    me = lax.axis_index("col")
    wide = []
    for k in range(1, COLS):
        peer = {"col": (me + k) % COLS}
        copy = push(g_ref, ga_ref.at[me], g_send.at[k - 1], g_recv.at[k - 1], peer)
        copy.start()
        wide.append(copy)
    ga_ref[me] = g_ref[...]
    out_ref[place] = kv_ref[...]
    m_ref[...] = jnp.full(m_ref.shape, neg_big, F32)
    acc_ref[...] = jnp.zeros(acc_ref.shape, F32)
    units = [(h, i) for h in range(heads) for i in range(tokens // qb)]

    def block(blk, masked):
        def raw_of(h, i):
            feats = slice(h * HD, (h + 1) * HD)
            raw = nt(out_ref[blk, :, feats], q_ref[i * qb : (i + 1) * qb, feats])
            if masked:
                allowed = seen(blk * tokens, place * tokens + i * qb, raw.shape, prefix)
                raw = jnp.where(allowed, raw, neg_big)
            return raw

        def soften(h, i, raw):
            cols = slice(i * qb, (i + 1) * qb)
            old = m_ref[h : h + 1, cols]
            new = jnp.maximum(old, jnp.max(raw, axis=0, keepdims=True))
            m_ref[h : h + 1, cols] = new
            weights = jnp.exp2((raw - new) * LOG2E).astype(BF16)
            return weights, jnp.exp2((old - new) * LOG2E)

        def gather(h, i, weights, scale):
            cols = slice(i * qb, (i + 1) * qb)
            v = out_ref[blk, :, width + h * HD : width + (h + 1) * HD]
            v_ext = jnp.concatenate([v.T, jnp.ones((16, tokens), BF16)], axis=0)
            acc_ref[h, :, cols] = acc_ref[h, :, cols] * scale + nn(v_ext, weights)

        coming, waiting = raw_of(*units[0]), None
        for n, unit in enumerate(units):
            raw = coming
            if n + 1 < len(units):
                coming = raw_of(*units[n + 1])
            soft = soften(*unit, raw)
            if waiting is not None:
                gather(*waiting)
            waiting = unit + soft
        gather(*waiting)

    def event(e, carry):
        t, cross = e // 2, e % 2
        at = jnp.where(t <= level, level - t, t)
        live = (t <= level) | (t < low)
        line_in = live & (cross == 0)

        @pl.when(line_in & (at < level))
        def _():
            for i in range(pieces):
                make(at, i, 0).wait_recv()

                @pl.when(to_up)
                def _(i=i):
                    make(at, i, 0).start()

                make(at, i, 2).start()

        @pl.when(line_in & (at > level))
        def _():
            for i in range(pieces):
                make(at, i, 1).wait_recv()

                @pl.when(level > 0)
                def _(i=i):
                    make(at, i, 1).start()

                make(at, i, 2).start()

        comes = live & (cross == 1) & ((at < low) | (at < level) | (side == 1))
        when(comes, lambda i: other(at, i).wait_recv())
        blk = 2 * at + jnp.where(cross == 0, side, 1 - side)
        needed = line_in | comes

        @pl.when(needed & (blk < place))
        def _():
            block(blk, False)

        @pl.when(needed & (blk >= place))
        def _():
            block(blk, True)

        return carry

    lax.fori_loop(0, 2 * levels, event, 0)

    for h in range(heads):
        total = acc_ref[h, HD : HD + 1, :]
        out = (acc_ref[h, :HD, :] / total).T
        o_ref[:, h * HD : (h + 1) * HD] = out
        ob_ref[:, h * HD : (h + 1) * HD] = out.astype(BF16)
        lse_ref[h : h + 1, :] = m_ref[h : h + 1, :] * LOG2E + jnp.log2(total)

    when(to_up, lambda i: make(level, i, 0, kv_ref).wait_send())
    when(own_side, lambda i: make(level, i, 2, kv_ref).wait_send())
    when(own_down, lambda i: make(level, i, 1, kv_ref).wait_send())
    for k in range(1, levels):
        at = level - k
        when((at >= 0) & to_up, lambda i, at=at: make(at, i, 0).wait_send())
        when(at >= 0, lambda i, at=at: make(at, i, 2).wait_send())
    for k in range(1, low):
        at = level + k
        when((at < low) & (level > 0), lambda i, at=at: make(at, i, 1).wait_send())
        when(at < low, lambda i, at=at: make(at, i, 2).wait_send())
    for copy in wide:
        copy.wait()


def attention_forward(info, q, kv, g, group, low, collective):
    pieces = 4
    levels = group // 2
    tokens, width = q.shape
    heads = width // HD
    return pl.pallas_call(
        functools.partial(forward_kernel, group, low, pieces, tokens // 2),
        out_shape=(
            jax.ShapeDtypeStruct((group,) + kv.shape, kv.dtype),
            jax.ShapeDtypeStruct((tokens, width), F32),
            jax.ShapeDtypeStruct((tokens, width), BF16),
            jax.ShapeDtypeStruct((8, tokens), F32),
            jax.ShapeDtypeStruct((COLS,) + g.shape, g.dtype),
        ),
        in_specs=[SSPEC, VSPEC, VSPEC, VSPEC],
        out_specs=(VSPEC,) * 5,
        scratch_shapes=[
            pltpu.VMEM((8, tokens), F32),
            pltpu.VMEM((heads, HD + 16, tokens), F32),
        ]
        + [DMA((levels, pieces))] * 6
        + [DMA((COLS - 1,))] * 2,
        compiler_params=params(collective),
    )(info, q, kv, g)


def backward_kernel(
    group,
    low,
    pieces,
    kb,
    info_ref,
    q_ref,
    kv_ref,
    do_ref,
    lse_ref,
    delta_ref,
    e_ref,
    bias_ref,
    dq_ref,
    out_ref,
    eo_ref,
    part_ref,
    rx_ref,
    above_ref,
    below_ref,
    snd_ref,
    acc_ref,
    dqt_ref,
    er_ref,
    u_send,
    u_recv,
    d_send,
    d_recv,
    x_send,
    x_recv,
    e_send,
    e_recv,
):
    levels = group // 2
    row, place, level, side, partner = line_places(group)
    prefix = info_ref[0]
    tokens, width = q_ref.shape
    heads = width // HD
    step = tokens // pieces
    line_greet(levels, row, level, partner)
    me = lax.axis_index("col")
    terms = []
    for k in range(1, COLS):
        peer = (me + k) % COLS
        copy = push(
            e_ref.at[peer], er_ref.at[k - 1], e_send.at[k - 1], e_recv.at[k - 1], {"col": peer}
        )
        copy.start()
        terms.append(copy)
    dqt_ref[...] = jnp.zeros(dqt_ref.shape, F32)

    def block(blk, masked):
        def body(j, carry):
            start = pl.multiple_of(j * kb, kb)
            keys = pl.ds(start, kb)
            for h in range(heads):
                feats = slice(h * HD, (h + 1) * HD)
                vals = slice(width + h * HD, width + (h + 1) * HD)
                k, v = kv_ref[blk, keys, feats], kv_ref[blk, keys, vals]
                q, do = q_ref[:, feats], do_ref[:, feats]
                probs = jnp.exp2(nt(k, q) * LOG2E - lse_ref[h : h + 1, :])
                if masked:
                    allowed = seen(blk * tokens + start, place * tokens, probs.shape, prefix)
                    probs = jnp.where(allowed, probs, 0.0)
                grad = (probs * (nt(v, do) - delta_ref[h : h + 1, :])).astype(BF16)
                part_ref[blk, keys, feats] = nn(grad, q).astype(BF16)
                part_ref[blk, keys, vals] = nn(probs.astype(BF16), do).astype(BF16)
                dqt_ref[feats, :] += nn(k.T, grad)
            return carry

        lax.fori_loop(0, tokens // kb, body, 0)

    def cross(at, i):
        part = pl.ds(i * step, step)
        return push(
            part_ref.at[2 * at + 1 - side, part],
            rx_ref.at[at, part],
            x_send.at[at, i],
            x_recv.at[at, i],
            {"row": partner},
        )

    def line(at, i, up):
        part = pl.ds(i * step, step)
        sems = (u_send, u_recv) if up else (d_send, d_recv)
        return push(
            snd_ref.at[at, part],
            (below_ref if up else above_ref).at[at, part],
            sems[0].at[at, i],
            sems[1].at[at, i],
            {"row": row + 2 if up else row - 2},
        )

    def gone(at):
        return (at < low) | (at < level) | ((at == level) & (side == 1))

    def comes(at):
        return (at < low) | (at < level) | ((at == level) & (side == 0))

    def total(at, i, from_above, from_below):
        part = pl.ds(i * step, step)
        acc_ref[...] = part_ref[2 * at + side, part].astype(F32)

        @pl.when(comes(at))
        def _():
            cross(at, i).wait_recv()
            acc_ref[...] += rx_ref[at, part].astype(F32)

        if from_above is not None:

            @pl.when(from_above)
            def _():
                line(at, i, False).wait_recv()
                acc_ref[...] += above_ref[at, part].astype(F32)

        if from_below is not None:

            @pl.when(from_below)
            def _():
                line(at, i, True).wait_recv()
                acc_ref[...] += below_ref[at, part].astype(F32)

    not_top = level < levels - 1
    above = jnp.maximum(low - 1 - level, 0)

    def level_of(t):
        return jnp.where(t < above, low - 1 - t, t - above)

    def event(e, carry):
        t, own = e // 2, e % 2
        at = level_of(t)
        live = (t < above) | (at <= level)

        down = t - (levels - level)

        @pl.when((own == 1) & (down >= 0) & (down < level))
        def _():
            for i in range(pieces):
                total(down, i, not_top, None)
                snd_ref[down, pl.ds(i * step, step)] = acc_ref[...].astype(BF16)
                line(down, i, False).start()

        @pl.when((own == 1) & (t >= 1) & (t - 1 < above))
        def _():
            up = level_of(t - 1)
            for i in range(pieces):
                total(up, i, None, level > 0)
                snd_ref[up, pl.ds(i * step, step)] = acc_ref[...].astype(BF16)
                line(up, i, True).start()

        goes = live & (own == 0) & gone(at)
        blk = 2 * at + jnp.where(own == 1, side, 1 - side)
        needed = goes | (live & (own == 1))

        @pl.when(needed & (blk < place))
        def _():
            block(blk, False)

        @pl.when(needed & (blk >= place))
        def _():
            block(blk, True)

        @pl.when(goes)
        def _():
            for i in range(pieces):
                cross(at, i).start()

        return carry

    lax.fori_loop(0, 2 * levels, event, 0)
    for copy in terms:
        copy.wait()

    def finish(r, carry):
        total = e_ref[me, r].astype(F32) + bias_ref[...]
        for k in range(COLS - 1):
            total = total + er_ref[k, r].astype(F32)
        eo_ref[r] = total.astype(BF16)
        return carry

    lax.fori_loop(0, e_ref.shape[1], finish, 0)
    dq_ref[...] = (dqt_ref[...] * HD**-0.5).T.astype(BF16)

    for i in range(pieces):
        total(level, i, not_top, (level > 0) & (level < low))
        out_ref[pl.ds(i * step, step)] = acc_ref[...].astype(BF16)

    for at in range(levels):
        for i in range(pieces):

            @pl.when(gone(at))
            def _(at=at, i=i):
                cross(at, i).wait_send()

            @pl.when(at < level)
            def _(at=at, i=i):
                line(at, i, False).wait_send()

            if at < low:

                @pl.when(at > level)
                def _(at=at, i=i):
                    line(at, i, True).wait_send()


def attention_backward(info, q, kv_all, do, lse, delta, e, bias, group, low, collective):
    pieces = 4
    levels = group // 2
    tokens, width = q.shape
    both = 2 * width
    block = pltpu.VMEM((levels, tokens, both), BF16)
    return pl.pallas_call(
        functools.partial(backward_kernel, group, low, pieces, tokens // 2),
        out_shape=(
            jax.ShapeDtypeStruct((tokens, width), BF16),
            jax.ShapeDtypeStruct((tokens, both), BF16),
            jax.ShapeDtypeStruct(e.shape[1:], BF16),
        ),
        in_specs=[SSPEC] + [VSPEC] * 7,
        out_specs=(VSPEC,) * 3,
        scratch_shapes=[
            pltpu.VMEM(kv_all.shape, BF16),
            block,
            block,
            pltpu.VMEM((low, tokens, both), BF16),
            block,
            pltpu.VMEM((tokens // pieces, both), F32),
            pltpu.VMEM((width, tokens), F32),
            pltpu.VMEM((COLS - 1,) + e.shape[1:], BF16),
        ]
        + [DMA((levels, pieces))] * 6
        + [DMA((COLS - 1,))] * 2,
        compiler_params=params(collective),
    )(info, q, kv_all, do, lse, delta, e, bias)


def product_kernel(pieces, rows, *refs):
    if rows:
        a_ref, b_ref, e_ref, out_ref, eo_ref = refs[:5]
        snd_ref, rx_ref, far_ref, tot_ref, send, recv, e_send, e_recv = refs[5:]
    else:
        a_ref, b_ref, out_ref, snd_ref, rx_ref, far_ref, tot_ref, send, recv = refs
    me, sib, across, diag = col_places()
    row = lax.axis_index("row")
    order = far_first(rows)
    greet([{"row": (row + k) % rows} for k in order] + [{"col": sib}, {"col": across}])
    home = []
    for n, k in enumerate(order):
        peer = (row + k) % rows
        copy = push(e_ref.at[peer], eo_ref.at[row], e_send.at[n], e_recv.at[n], {"row": peer})
        copy.start()
        home.append(copy)
    if rows:
        eo_ref[row] = e_ref[row]
    half = a_ref.shape[0] // 2
    step = half // pieces

    def term(i, who):
        parts = [nt(a_ref[pl.ds(n * half + i * step, step)], b_ref[who]) for n in range(2)]
        return jnp.concatenate(parts, axis=1)

    def near(i, j):
        part = pl.ds(i * step, step)
        return push(
            snd_ref.at[j, part], rx_ref.at[j, part], send.at[j, i], recv.at[j, i], {"col": sib}
        )

    def over(i):
        part = pl.ds(i * step, step)
        return push(tot_ref.at[part], far_ref.at[part], send.at[2, i], recv.at[2, i], {"col": across})

    for i in range(pieces):
        snd_ref[0, pl.ds(i * step, step)] = term(i, diag).astype(BF16)
        near(i, 0).start()
    for i in range(pieces):
        part = pl.ds(i * step, step)
        mine = term(i, across)
        near(i, 0).wait_recv()
        tot_ref[part] = (mine + rx_ref[0, part].astype(F32)).astype(BF16)
        over(i).start()
    for i in range(pieces):
        snd_ref[1, pl.ds(i * step, step)] = term(i, sib).astype(BF16)
        near(i, 1).start()
    for i in range(pieces):
        part = pl.ds(i * step, step)
        mine = term(i, me)
        near(i, 1).wait_recv()
        mine = mine + rx_ref[1, part].astype(F32)
        over(i).wait_recv()
        mine = mine + far_ref[part].astype(F32)
        width = mine.shape[1] // 2
        out_ref[part] = mine[:, :width]
        out_ref[pl.ds(half + i * step, step)] = mine[:, width:]
    for i in range(pieces):
        near(i, 0).wait_send()
        near(i, 1).wait_send()
        over(i).wait_send()
    for copy in home:
        copy.wait()


def product_scatter(a, b, collective, back=None):
    pieces = 4
    tokens, width = a.shape[0], b.shape[1]
    block = pltpu.VMEM((tokens // 2, 2 * width), BF16)
    pair = pltpu.VMEM((2, tokens // 2, 2 * width), BF16)
    out = jax.ShapeDtypeStruct((tokens, width), F32)
    scratch = [pair, pair, block, block, DMA((3, pieces)), DMA((3, pieces))]
    rows = 0
    if back is not None:
        rows = back.shape[0]
        out = (out, jax.ShapeDtypeStruct(back.shape, back.dtype))
        scratch = scratch + [DMA((rows - 1,))] * 2
    return pl.pallas_call(
        functools.partial(product_kernel, pieces, rows),
        out_shape=out,
        in_specs=[VSPEC] * (3 if rows else 2),
        out_specs=(VSPEC, VSPEC) if rows else VSPEC,
        scratch_shapes=scratch,
        compiler_params=params(collective),
    )(*((a, b, back) if rows else (a, b)))


def dispatch_kernel(rows, x_ref, t_ref, out_ref, in_ref, r_send, r_recv, c_send, c_recv):
    me, sib, across, _ = col_places()
    row = lax.axis_index("row")
    order = far_first(rows)
    peers = [(row + k) % rows for k in order]
    greet([{"row": p} for p in peers] + [{"col": sib}, {"col": across}])
    copies = []
    cap = in_ref.shape[1]
    for k, peer in enumerate(peers):
        in_ref[peer] = placed(t_ref, x_ref[...], peer, cap)
        copy = push(
            in_ref.at[peer], out_ref.at[me, row], r_send.at[k], r_recv.at[k], {"row": peer}
        )
        copy.start()
        copies.append(copy)
    in_ref[row] = placed(t_ref, x_ref[...], row, cap)

    def col(src, dst, k, way):
        return push(
            src, dst, c_send.at[way, k], c_recv.at[way, k], {"col": across if way == 0 else sib}
        )

    done, first = [], []
    for way in range(2):
        copy = col(in_ref.at[row], out_ref.at[me, row], 0, way)
        copy.start()
        (first if way == 0 else done).append(copy)
    out_ref[me, row] = in_ref[row]
    sources = [row] + [(row + rows - k) % rows for k in order]

    def forward(k):
        first[k].wait_recv()
        src = sources[k]
        copy = col(out_ref.at[across, src], out_ref.at[across, src], k, 2)
        copy.start()
        done.append(copy)

    for k in range(1, rows):
        copies[k - 1].wait_recv()
        block = out_ref.at[me, sources[k]]
        for way in range(2):
            copy = col(block, block, k, way)
            copy.start()
            (first if way == 0 else done).append(copy)
        forward(k - 1)
    forward(rows - 1)
    for copy in copies:
        copy.wait_send()
    for copy in first:
        copy.wait_send()
    for copy in done:
        copy.wait()


def dispatch(x, target, rows, cap, collective):
    block = (rows, cap, 2 * x.shape[1])
    return pl.pallas_call(
        functools.partial(dispatch_kernel, rows),
        out_shape=jax.ShapeDtypeStruct((COLS,) + block, x.dtype),
        in_specs=[VSPEC] * 2,
        out_specs=VSPEC,
        scratch_shapes=[
            pltpu.VMEM(block, x.dtype),
            DMA((rows - 1,)),
            DMA((rows - 1,)),
            DMA((3, rows)),
            DMA((3, rows)),
        ],
        compiler_params=params(collective),
    )(x, target)


def giveback_kernel(
    rows,
    in_ref,
    t_ref,
    sum_ref,
    out_ref,
    rx_ref,
    far_ref,
    tot_ref,
    fin_ref,
    send,
    recv,
    r_send,
    r_recv,
):
    me, sib, across, diag = col_places()
    row = lax.axis_index("row")
    order = [(row + k) % rows for k in far_first(rows)] + [row]
    greet([{"row": p} for p in order[:-1]] + [{"col": sib}, {"col": across}])

    def near(k, j):
        who = diag if j == 0 else sib
        return push(
            in_ref.at[who, order[k]], rx_ref.at[j, k], send.at[j, k], recv.at[j, k], {"col": sib}
        )

    def over(k):
        return push(tot_ref.at[k], far_ref.at[k], send.at[2, k], recv.at[2, k], {"col": across})

    def home(k):
        return push(
            fin_ref.at[k], out_ref.at[row], r_send.at[k], r_recv.at[k], {"row": order[k]}
        )

    for k in range(rows):
        near(k, 0).start()
        near(k, 1).start()

    def finish(k):
        near(k, 1).wait_recv()
        over(k).wait_recv()
        total = in_ref[me, order[k]].astype(F32) + rx_ref[1, k].astype(F32)
        total = total + far_ref[k].astype(F32)
        if k == rows - 1:
            out_ref[row] = total.astype(BF16)
        else:
            fin_ref[k] = total.astype(BF16)
            home(k).start()

    for k in range(rows):
        near(k, 0).wait_recv()
        tot_ref[k] = (in_ref[across, order[k]].astype(F32) + rx_ref[0, k].astype(F32)).astype(BF16)
        over(k).start()
        if k >= 1:
            finish(k - 1)
    finish(rows - 1)
    cap = out_ref.shape[1]
    sum_ref[...] = combined(t_ref, out_ref[row], row, cap)
    for k, gap in enumerate(far_first(rows)):
        source = (row + rows - gap) % rows
        home(k).wait_recv()
        sum_ref[...] += combined(t_ref, out_ref[source], source, cap)
    for k in range(rows):
        near(k, 0).wait_send()
        near(k, 1).wait_send()
        over(k).wait_send()
        if k < rows - 1:
            home(k).wait_send()


def giveback(parts, target, rows, collective):
    block = parts.shape[2:]
    one = pltpu.VMEM((rows,) + block, BF16)
    return pl.pallas_call(
        functools.partial(giveback_kernel, rows),
        out_shape=jax.ShapeDtypeStruct((target.shape[1], block[1] // 2), F32),
        in_specs=[VSPEC] * 2,
        out_specs=VSPEC,
        scratch_shapes=[
            one,
            pltpu.VMEM((2, rows) + block, BF16),
            one,
            one,
            one,
            DMA((3, rows)),
            DMA((3, rows)),
            DMA((rows - 1,)),
            DMA((rows - 1,)),
        ],
        compiler_params=params(collective),
    )(parts, target)


def end_kernel(
    rows, w_ref, s_ref, e_ref, t_ref, mid_ref, wo_ref, so_ref, lo_ref, wr_ref, sr_ref, send, recv
):
    row = lax.axis_index("row")
    peers = [(row + k) % rows for k in range(1, rows)]
    greet([{"row": p} for p in peers])
    copies = []
    for k, peer in enumerate(peers):
        for j, (src, dst) in enumerate(((w_ref, wr_ref), (s_ref, sr_ref))):
            copy = push(src.at[peer], dst.at[k], send.at[j, k], recv.at[j, k], {"row": peer})
            copy.start()
            copies.append(copy)
    wo_ref[...] = w_ref[row].astype(F32)
    so_ref[...] = s_ref[row]
    total = mid_ref[...]
    for r in range(rows):
        total = total + combined(t_ref, e_ref[r], r, e_ref.shape[1])
    lo_ref[...] = total.astype(BF16)
    for k in range(rows - 1):
        copies[2 * k].wait_recv()
        copies[2 * k + 1].wait_recv()
        wo_ref[...] += wr_ref[k].astype(F32)
        so_ref[...] += sr_ref[k]
    for copy in copies:
        copy.wait_send()


def end_scatter(w, s, outs, target, mid, rows, collective):
    return pl.pallas_call(
        functools.partial(end_kernel, rows),
        out_shape=(
            jax.ShapeDtypeStruct(w.shape[1:], F32),
            jax.ShapeDtypeStruct(s.shape[1:], F32),
            jax.ShapeDtypeStruct(mid.shape, BF16),
        ),
        in_specs=[VSPEC] * 5,
        out_specs=(VSPEC,) * 3,
        scratch_shapes=[
            pltpu.VMEM((rows - 1,) + w.shape[1:], w.dtype),
            pltpu.VMEM((rows - 1,) + s.shape[1:], s.dtype),
            DMA((2, rows - 1)),
            DMA((2, rows - 1)),
        ],
        compiler_params=params(collective),
    )(w, s, outs, target, mid)


def expert_kernel(
    x_ref,
    g_ref,
    up_ref,
    bias_ref,
    down_ref,
    part_ref,
    gx_ref,
    gup_ref,
    gbu_ref,
    gdown_ref,
    gbd_ref,
):
    cols, rows, cap, both = x_ref.shape
    width = both // 2
    slots = rows * cap
    first = pl.program_id(0) == 0

    def mine(ref):
        blocks = [ref[b].reshape(slots, both) for b in range(cols)]
        blocks = [jnp.where(first, v[:, :width], v[:, width:]) for v in blocks]
        return jnp.concatenate(blocks, axis=1)

    x, g = mine(x_ref), mine(g_ref)
    gbd_ref[...] = jnp.sum(g.astype(F32), axis=0).reshape(gbd_ref.shape)
    hidden_units = up_ref.shape[2]
    chunk = 256
    part = jnp.zeros((slots, cols * width), F32)
    gx = jnp.zeros((slots, cols * width), F32)
    for f in range(hidden_units // chunk):
        cut = slice(f * chunk, (f + 1) * chunk)
        up, down = up_ref[0, :, cut], down_ref[0, cut, :]
        pre = nn(x, up) + bias_ref[0, :, cut].astype(F32)
        cdf = 0.5 * (1.0 + lax.erf(pre * (0.5**0.5)))
        slope = cdf + pre * (jnp.exp(-0.5 * pre * pre) * 0.3989422804014327)
        hidden = (pre * cdf).astype(BF16)
        grad = nt(g, down) * slope
        grad = grad.astype(BF16)
        part = part + nn(hidden, down)
        gx = gx + nt(grad, up)
        gdown_ref[0, cut, :] = tn(hidden, g)
        gup_ref[0, :, cut] = tn(x, grad)
        gbu_ref[0, :, cut] = jnp.sum(grad.astype(F32), axis=0, keepdims=True)
    for e in range(EXP_DEV):

        @pl.when(pl.program_id(0) == e)
        def _(e=e):
            lanes = slice(e * width, (e + 1) * width)
            for b in range(cols):
                cut = slice(b * width, (b + 1) * width)
                part_ref[b, :, :, lanes] = part[:, cut].astype(BF16).reshape(rows, cap, width)
                gx_ref[b, :, :, lanes] = gx[:, cut].astype(BF16).reshape(rows, cap, width)


def experts(x, g, w_up, bias_up, w_down):
    slots = pl.BlockSpec(x.shape, lambda e: (0, 0, 0, 0))
    count, features, hidden = w_up.shape
    return pl.pallas_call(
        expert_kernel,
        grid=(count,),
        out_shape=(
            jax.ShapeDtypeStruct(x.shape, BF16),
            jax.ShapeDtypeStruct(x.shape, BF16),
            jax.ShapeDtypeStruct(w_up.shape, F32),
            jax.ShapeDtypeStruct((count, 1, hidden), F32),
            jax.ShapeDtypeStruct(w_down.shape, F32),
            jax.ShapeDtypeStruct((count, 1, features), F32),
        ),
        in_specs=[
            slots,
            slots,
            pl.BlockSpec((1, features, hidden), lambda e: (e, 0, 0)),
            pl.BlockSpec((1, 1, hidden), lambda e: (e, 0, 0)),
            pl.BlockSpec((1, hidden, features), lambda e: (e, 0, 0)),
        ],
        out_specs=(
            slots,
            slots,
            pl.BlockSpec((1, features, hidden), lambda e: (e, 0, 0)),
            pl.BlockSpec((1, 1, hidden), lambda e: (e, 0, 0)),
            pl.BlockSpec((1, hidden, features), lambda e: (e, 0, 0)),
            pl.BlockSpec((1, 1, features), lambda e: (e, 0, 0)),
        ),
        compiler_params=params(),
    )(x, g, w_up, bias_up.reshape(count, 1, hidden), w_down)


def per_device(
    layer_in,
    cotangent,
    token_ids,
    hash_table,
    prefix_len,
    w_query,
    w_key,
    w_value,
    w_output,
    bias_query,
    bias_value,
    gain_attn,
    shift_attn,
    gain_moe,
    shift_moe,
    bias_output,
    w_up,
    bias_up,
    w_down,
    bias_down,
):
    rows = lax.axis_size("row")
    row = lax.axis_index("row")
    col = lax.axis_index("col")
    tokens, width = layer_in.shape
    heads = width // HD
    seq_len = min(LENGTH, tokens * rows)
    group = seq_len // tokens
    low = -(-PREFIX_MAX // (2 * tokens))
    share = w_query.shape[0]
    bias_share = bias_query.shape[0]

    def line(v):
        return jnp.pad(v.astype(F32), (0, 128 - v.shape[0]))

    small = jnp.stack(
        [
            line(gain_attn),
            line(shift_attn),
            line(gain_moe),
            line(shift_moe),
            line(bias_output),
            line(bias_query.T.reshape(-1)),
            line(bias_value.T.reshape(-1)),
            jnp.zeros((128,), F32),
        ]
    )
    expert_total = EXP_DEV * rows
    capacity = max(2, 2 * tokens // expert_total)
    expert_of = hash_table[token_ids]
    hits = expert_of[:, None] == jnp.arange(expert_total, dtype=jnp.int32)[None, :]
    earlier = (
        jnp.arange(tokens, dtype=jnp.int32)[None, :] < jnp.arange(tokens, dtype=jnp.int32)[:, None]
    )
    before = jnp.dot(earlier.astype(BF16), hits.astype(BF16), preferred_element_type=F32)
    slot_of = jnp.sum(jnp.where(hits, before, 0.0), axis=1).astype(jnp.int32)
    target = expert_of * capacity + slot_of
    target = target[None, :]

    weights = jnp.concatenate([w_query, w_key, w_value, w_output], axis=1)
    x_all, g_own, w_all, s_all = start_gather(
        layer_in, cotangent, target, weights, small, rows, capacity
    )
    w_flat = w_all.reshape(D, 4 * width)
    w_qkv = w_flat[:, : 3 * width]
    w_out = w_flat[:, 3 * width :].reshape(COLS, width, width)
    gain_one, shift_one, gain_two, shift_two, out_bias = (
        s_all[:, i, :share].reshape(D) for i in range(5)
    )

    def own(v):
        return lax.dynamic_slice_in_dim(v, col * width, width, 0)

    query_bias, value_bias = (
        s_all[:, i, : heads * bias_share]
        .reshape(rows, heads, bias_share)
        .transpose(1, 0, 2)
        .reshape(width)
        for i in (5, 6)
    )

    qkv_bias = jnp.concatenate([query_bias, jnp.zeros_like(query_bias), value_bias])
    queries, keys_values, h_one, normed_one, rstd_one = project(
        x_all, w_all, gain_one[None], shift_one[None], qkv_bias[None]
    )
    seq_hit = row // group == jnp.arange(prefix_len.shape[0], dtype=jnp.int32)
    prefix = jnp.sum(jnp.where(seq_hit, prefix_len, 0))
    info = prefix.astype(jnp.int32).reshape(1)
    kv_all, attended, attended_low, lse, g_all = attention_forward(
        info, queries, keys_values, g_own, group, low, 1
    )
    branch = product_scatter(attended_low, w_out, 2)
    x_own = layer_in.astype(F32)
    mid = x_own + branch + own(out_bias)

    part_mean = jnp.mean(mid, axis=-1)
    part_spread = jnp.sum((mid - part_mean[:, None]) ** 2, axis=-1)
    stats = jnp.stack([part_mean, part_spread]).reshape(-1, 128)
    stats = small_gather(stats, 3).reshape(COLS, 2, tokens)
    mean_two = jnp.mean(stats[:, 0], axis=0)
    spread = jnp.sum(stats[:, 1] + width * (stats[:, 0] - mean_two) ** 2, axis=0) / D
    rstd_two = lax.rsqrt(spread + epsilon)[:, None]
    normed_two = (mid - mean_two[:, None]) * rstd_two
    gain_two_own = own(gain_two)
    h_two = (normed_two * gain_two_own + own(shift_two)).astype(BF16)

    received = dispatch(h_two, target, rows, capacity, 4)
    parts, grad_parts, grad_w_up, grad_bias_up, grad_w_down, grad_bias_down = experts(
        received, g_all, w_up, bias_up, w_down
    )
    grad_h_two = giveback(grad_parts, target, rows, 5)

    scaled = grad_h_two * gain_two_own
    sums = jnp.stack([jnp.sum(scaled, axis=-1), jnp.sum(scaled * normed_two, axis=-1)])
    sums = small_gather(sums.reshape(-1, 128), 6).reshape(COLS, 2, tokens)
    sums = jnp.sum(sums, axis=0) / D
    grad_mid = cotangent.astype(F32) + rstd_two * (
        scaled - sums[0][:, None] - normed_two * sums[1][:, None]
    )
    grad_attended, delta, grad_w_out = mid_gradient(grad_mid, w_all, attended, attended_low, 7)
    down_own = lax.dynamic_slice_in_dim(bias_down, col * width, width, 1).astype(F32)
    down_own = down_own.reshape(1, EXP_DEV * width)
    grad_q, grad_kv, outs = attention_backward(
        info,
        queries,
        kv_all,
        grad_attended,
        lse,
        delta,
        parts,
        down_own,
        group,
        low,
        8,
    )
    grad_qkv = jnp.concatenate([grad_q, grad_kv], axis=1)
    grad_w_qkv = lax.dot_general(
        h_one, grad_qkv, (((0,), (0,)), ((), ())), preferred_element_type=F32
    )
    grad_bias = jnp.sum(grad_qkv, axis=0, dtype=F32)
    grad_h_one, outs = product_scatter(grad_qkv, w_qkv.reshape(COLS, width, 3 * width), 9, outs)
    scaled = grad_h_one * own(gain_one)
    sums = jnp.stack([jnp.sum(scaled, axis=-1), jnp.sum(scaled * normed_one, axis=-1)])
    vectors = jnp.stack(
        [
            jnp.sum(grad_h_one * normed_one, axis=0),
            jnp.sum(grad_h_one, axis=0),
            jnp.sum(grad_h_two * normed_two, axis=0),
            jnp.sum(grad_h_two, axis=0),
            jnp.sum(grad_mid, axis=0),
        ]
    )
    vectors = jnp.pad(vectors, ((0, 3), (0, 256 - width))).reshape(-1, 128)
    shared = small_gather(jnp.concatenate([sums.reshape(-1, 128), vectors]), 10)
    used = 2 * tokens // 128
    sums = jnp.sum(shared[:, :used].reshape(COLS, 2, tokens), axis=0) / D
    grad_in = grad_mid + rstd_one * (scaled - sums[0][:, None] - normed_one * sums[1][:, None])
    vectors = shared[:, used:].reshape(COLS, 8, 256)[:, :5, :width]
    vectors = vectors.transpose(1, 0, 2).reshape(5, rows, share).transpose(1, 0, 2)

    def by_row(v):
        v = v.reshape(heads, rows, bias_share).transpose(1, 0, 2).reshape(rows, 1, -1)
        return jnp.pad(v, ((0, 0), (0, 0), (0, 128 - v.shape[2])))

    small_terms = jnp.concatenate(
        [
            jnp.pad(vectors, ((0, 0), (0, 0), (0, 128 - share))),
            by_row(grad_bias[:width]),
            by_row(grad_bias[2 * width :]),
            jnp.zeros((rows, 1, 128), F32),
        ],
        axis=1,
    )
    weight_terms = jnp.concatenate([grad_w_qkv.astype(BF16), grad_w_out], axis=1)
    weight_terms = weight_terms.reshape(rows, share, 4 * width)
    weight_sums, small_sums, layer_out = end_scatter(
        weight_terms, small_terms, outs, target, mid, rows, 11
    )

    def bias_back(v):
        return v[: heads * bias_share].reshape(heads, bias_share).T

    return (
        layer_out,
        grad_in,
        weight_sums[:, :width],
        weight_sums[:, width : 2 * width],
        weight_sums[:, 2 * width : 3 * width],
        weight_sums[:, 3 * width :],
        bias_back(small_sums[5]),
        bias_back(small_sums[6]),
        small_sums[0, :share],
        small_sums[1, :share],
        small_sums[2, :share],
        small_sums[3, :share],
        small_sums[4, :share],
        grad_w_up,
        grad_bias_up[:, 0],
        grad_w_down,
        grad_bias_down[:, 0],
    )


def solution(mesh):
    placed = (
        P("row", "col"),
        P("row", "col"),
        P("row"),
        P(),
        P(),
        P("row", "col"),
        P("row", "col"),
        P("row", "col"),
        P("row", "col"),
        P("row", "col"),
        P("row", "col"),
        P("row"),
        P("row"),
        P("row"),
        P("row"),
        P("row"),
        P("row", None, "col"),
        P("row", "col"),
        P("row", "col", None),
        P("row", None),
    )
    return jax.shard_map(
        per_device,
        mesh=mesh,
        in_specs=placed,
        out_specs=(
            P("row", "col"),
            P("row", "col"),
            P("row", "col"),
            P("row", "col"),
            P("row", "col"),
            P("row", "col"),
            P("row", "col"),
            P("row", "col"),
            P("row"),
            P("row"),
            P("row"),
            P("row"),
            P("row"),
            P("row", None, "col"),
            P("row", "col"),
            P("row", "col", None),
            P("row", None),
        ),
        check_vma=False,
    )
```

```python
import functools

import jax
import jax.numpy as jnp
from jax import lax
from jax.experimental import pallas as pl
from jax.experimental.pallas import tpu as pltpu
from jax.sharding import PartitionSpec as P

D = 768
HD = 64
EXP_DEV = 2
LENGTH = 8192
PREFIX_MAX = 4096
COLS = 4

F32 = jnp.float32
BF16 = jnp.bfloat16
MESH = pl.DeviceIdType.MESH
LOG2E = 1.4426950408889634

epsilon = 1e-05
neg_big = -1e30

VSPEC = pl.BlockSpec(memory_space=pltpu.VMEM)
SSPEC = pl.BlockSpec(memory_space=pltpu.SMEM)
VMEM_BYTES = 64 * 1000 * 1000
DMA = pltpu.SemaphoreType.DMA


def params(collective=None):
    if collective is None:
        return pltpu.CompilerParams(vmem_limit_bytes=VMEM_BYTES)
    return pltpu.CompilerParams(
        vmem_limit_bytes=VMEM_BYTES, collective_id=collective, has_side_effects=True
    )


def push(src, dst, send_sem, recv_sem, peer):
    return pltpu.make_async_remote_copy(
        src_ref=src,
        dst_ref=dst,
        send_sem=send_sem,
        recv_sem=recv_sem,
        device_id=peer,
        device_id_type=MESH,
    )


def greet(peers):
    barrier = pltpu.get_barrier_semaphore()
    for peer in peers:
        pl.semaphore_signal(barrier, inc=1, device_id=peer, device_id_type=MESH)
    pl.semaphore_wait(barrier, len(peers))


def col_places():
    me = lax.axis_index("col")
    sib = me + 1 - 2 * (me % 2)
    across = (me + 2) % COLS
    diag = (sib + 2) % COLS
    return me, sib, across, diag


def line_places(group):
    row = lax.axis_index("row")
    place = row % group
    level, side = place // 2, place % 2
    return row, place, level, side, row + 1 - 2 * side


def far_first(rows):
    return sorted(range(1, rows), key=lambda k: -min(k, rows - k))


def nt(left, right):
    return lax.dot_general(left, right, (((1,), (1,)), ((), ())), preferred_element_type=F32)


def nn(left, right):
    return lax.dot_general(left, right, (((1,), (0,)), ((), ())), preferred_element_type=F32)


def tn(left, right):
    return lax.dot_general(left, right, (((0,), (0,)), ((), ())), preferred_element_type=F32)


def side_by_side(v):
    half = v.shape[0] // 2
    return jnp.concatenate([v[:half], v[half:]], axis=1)


def slots_of(target_ref, row, count):
    base = row * count
    slot = base + lax.broadcasted_iota(jnp.int32, (count, target_ref.shape[1]), 0)
    return jnp.where(slot == target_ref[...], 1.0, 0.0).astype(BF16)


def placed(target_ref, v, row, cap):
    return side_by_side(nn(slots_of(target_ref, row, 2 * cap), v).astype(BF16))


def combined(target_ref, block, row, cap):
    width = block.shape[1] // 2
    stacked = jnp.concatenate([block[:, :width], block[:, width:]], axis=0)
    return tn(slots_of(target_ref, row, 2 * cap), stacked)


def start_kernel(
    rows,
    pieces,
    x_ref,
    g_ref,
    t_ref,
    w_ref,
    s_ref,
    xo_ref,
    go_ref,
    wo_ref,
    so_ref,
    xp_ref,
    gp_ref,
    c_send,
    c_recv,
    r_send,
    r_recv,
    l_send,
    l_recv,
):
    me, sib, across, _ = col_places()
    row, _, level, side, partner = line_places(rows)
    levels = rows // 2
    order = far_first(rows)
    peers = [{"row": (row + k) % rows} for k in order]
    greet(peers + [{"col": sib}, {"col": across}])
    xp_ref[...] = side_by_side(x_ref[...])
    step = xp_ref.shape[0] // pieces
    cap = gp_ref.shape[1]
    to_up, to_down = level < levels - 1, level > 0

    def weight(at, way, src=None):
        dst = wo_ref.at[2 * at + side]
        peer = (row + 2, row - 2, partner)[way]
        return push(
            dst if src is None else src,
            dst,
            l_send.at[way, at],
            l_recv.at[way, at],
            {"row": peer},
        )

    def weight_other(at):
        dst = wo_ref.at[2 * at + 1 - side]
        return push(dst, dst, l_send.at[2, at], l_recv.at[2, at], {"row": partner})

    @pl.when(to_up)
    def _():
        weight(level, 0, w_ref).start()

    @pl.when(to_down)
    def _():
        weight(level, 1, w_ref).start()

    weight(level, 2, w_ref).start()
    sent = []
    for i in range(pieces):
        part = pl.ds(i * step, step)
        for way, peer in ((0, across), (1, sib)):
            copy = push(
                xp_ref.at[part],
                xo_ref.at[me, part],
                c_send.at[way, i],
                c_recv.at[way, i],
                {"col": peer},
            )
            copy.start()
            sent.append(copy)
    row_copies = []
    for k, peer in enumerate(peers):
        copy = push(s_ref, so_ref.at[row], r_send.at[0, k], r_recv.at[0, k], peer)
        copy.start()
        row_copies.append(copy)

    def send_rows(k):
        target = (row + order[k]) % rows
        gp_ref[k] = placed(t_ref, g_ref[...], target, cap)
        copy = push(gp_ref.at[k], go_ref.at[row], r_send.at[1, k], r_recv.at[1, k], peers[k])
        copy.start()
        row_copies.append(copy)

    send_rows(0)
    xo_ref[me] = xp_ref[...]
    wo_ref[row] = w_ref[...]
    so_ref[row] = s_ref[...]
    todo = list(range(1, rows - 1))

    def pass_on(k):
        at = level - k

        @pl.when(at >= 0)
        def _():
            weight(at, 0).wait_recv()

            @pl.when(to_up)
            def _():
                weight(at, 0).start()

            weight(at, 2).start()

        up = level + k

        @pl.when(up < levels)
        def _():
            weight(up, 1).wait_recv()

            @pl.when(to_down)
            def _():
                weight(up, 1).start()

            weight(up, 2).start()

    late = []
    for k in range(1, max(levels, pieces + 1)):
        if k < levels:
            pass_on(k)
        if k <= pieces:
            part = pl.ds((k - 1) * step, step)
            sent[2 * k - 2].wait_recv()
            copy = push(
                xo_ref.at[across, part],
                xo_ref.at[across, part],
                c_send.at[2, k - 1],
                c_recv.at[2, k - 1],
                {"col": sib},
            )
            copy.start()
            late.append(copy)
        for _ in range(2):
            if todo:
                send_rows(todo.pop(0))
    while todo:
        send_rows(todo.pop(0))
    go_ref[row] = placed(t_ref, g_ref[...], row, cap)
    for i in range(pieces):
        sent[2 * i].wait_send()
        sent[2 * i + 1].wait()
        late[i].wait()
    for at in range(levels):
        weight_other(at).wait_recv()
        weight(at, 2).wait_send()

        @pl.when((at <= level) & to_up)
        def _(at=at):
            weight(at, 0).wait_send()

        @pl.when((at >= level) & to_down)
        def _(at=at):
            weight(at, 1).wait_send()

    for copy in row_copies:
        copy.wait()


def start_gather(x, g, target, w, s, rows, cap):
    pieces = 4
    tokens, width = x.shape
    packed = (tokens // 2, 2 * width)
    return pl.pallas_call(
        functools.partial(start_kernel, rows, pieces),
        out_shape=(
            jax.ShapeDtypeStruct((COLS,) + packed, x.dtype),
            jax.ShapeDtypeStruct((rows, cap, 2 * width), g.dtype),
            jax.ShapeDtypeStruct((rows,) + w.shape, w.dtype),
            jax.ShapeDtypeStruct((rows,) + s.shape, s.dtype),
        ),
        in_specs=[VSPEC] * 5,
        out_specs=(VSPEC,) * 4,
        scratch_shapes=[
            pltpu.VMEM(packed, x.dtype),
            pltpu.VMEM((rows - 1, cap, 2 * width), g.dtype),
            DMA((3, pieces)),
            DMA((3, pieces)),
            DMA((2, rows - 1)),
            DMA((2, rows - 1)),
            DMA((3, rows // 2)),
            DMA((3, rows // 2)),
        ],
        compiler_params=params(0),
    )(x, g, target, w, s)


def project_kernel(
    x_ref, w_ref, gain_ref, shift_ref, bias_ref, q_ref, kv_ref, h_ref, n_ref, r_ref
):
    me = lax.axis_index("col")
    half, width = x_ref.shape[1], x_ref.shape[2] // 2
    w = w_ref[...].reshape(D, 4 * width)[:, : 3 * width]
    step = min(half, 256)
    for i in range(2 * half // step):
        side, start = i * step // half, i * step % half
        rows, feats = slice(start, start + step), slice(side * width, (side + 1) * width)
        x = jnp.concatenate([x_ref[b, rows, feats] for b in range(COLS)], axis=1).astype(F32)
        mean = jnp.mean(x, axis=-1, keepdims=True)
        centred = x - mean
        rstd = lax.rsqrt(jnp.mean(centred * centred, axis=-1, keepdims=True) + epsilon)
        h = (centred * rstd * gain_ref[...] + shift_ref[...]).astype(BF16)
        out = slice(i * step, (i + 1) * step)
        h_ref[out] = h
        n_ref[out] = (x_ref[me, rows, feats].astype(F32) - mean) * rstd
        r_ref[out] = rstd
        qkv = (nn(h, w) + bias_ref[...]).astype(BF16)
        q_ref[out] = qkv[:, :width] * jnp.asarray(HD**-0.5, BF16)
        kv_ref[out] = qkv[:, width:]


def project(x, w, gain, shift, bias):
    tokens, width = 2 * x.shape[1], x.shape[2] // 2
    return pl.pallas_call(
        project_kernel,
        out_shape=(
            jax.ShapeDtypeStruct((tokens, width), BF16),
            jax.ShapeDtypeStruct((tokens, 2 * width), BF16),
            jax.ShapeDtypeStruct((tokens, D), BF16),
            jax.ShapeDtypeStruct((tokens, width), F32),
            jax.ShapeDtypeStruct((tokens, 1), F32),
        ),
        in_specs=[VSPEC] * 5,
        out_specs=(VSPEC,) * 5,
        compiler_params=params(),
    )(x, w, gain, shift, bias)


def mid_kernel(
    pieces,
    x_ref,
    w_ref,
    att_ref,
    low_ref,
    do_ref,
    delta_ref,
    gw_ref,
    xp_ref,
    xo_ref,
    wide_ref,
    c_send,
    c_recv,
):
    me, sib, across, _ = col_places()
    greet([{"col": sib}, {"col": across}])
    xp_ref[...] = side_by_side(x_ref[...].astype(BF16))
    step = xp_ref.shape[0] // pieces
    sent, late = [], []
    for i in range(pieces):
        part = pl.ds(i * step, step)
        for way, peer in ((0, across), (1, sib)):
            copy = push(
                xp_ref.at[part],
                xo_ref.at[me, part],
                c_send.at[way, i],
                c_recv.at[way, i],
                {"col": peer},
            )
            copy.start()
            sent.append(copy)
    xo_ref[me] = xp_ref[...]
    tokens, width = x_ref.shape
    w = w_ref[...].reshape(D, 4 * width)[:, 3 * width :]
    for i in range(pieces):
        part = pl.ds(i * step, step)
        sent[2 * i].wait_recv()
        copy = push(
            xo_ref.at[across, part],
            xo_ref.at[across, part],
            c_send.at[2, i],
            c_recv.at[2, i],
            {"col": sib},
        )
        copy.start()
        late.append(copy)
    for i in range(pieces):
        sent[2 * i].wait_send()
        sent[2 * i + 1].wait()
        late[i].wait()
        rows = slice(i * step, (i + 1) * step)
        for half in range(2):
            feats = slice(half * width, (half + 1) * width)
            start = half * (tokens // 2) + i * step
            out = slice(start, start + step)
            wide = jnp.concatenate([xo_ref[b, rows, feats] for b in range(COLS)], axis=1)
            wide_ref[out] = wide
            do = nn(wide, w).astype(BF16)
            do_ref[out] = do
            both = (do.astype(F32) * att_ref[out]).T
            for h in range(width // HD):
                delta_ref[h : h + 1, out] = jnp.sum(
                    both[h * HD : (h + 1) * HD], axis=0, keepdims=True
                )
    gw_ref[...] = tn(wide_ref[...], low_ref[...]).astype(BF16)


def mid_gradient(x, w, attended, low, collective):
    pieces = 4
    tokens, width = x.shape
    packed = (tokens // 2, 2 * width)
    return pl.pallas_call(
        functools.partial(mid_kernel, pieces),
        out_shape=(
            jax.ShapeDtypeStruct((tokens, width), BF16),
            jax.ShapeDtypeStruct((8, tokens), F32),
            jax.ShapeDtypeStruct((D, width), BF16),
        ),
        in_specs=[VSPEC] * 4,
        out_specs=(VSPEC,) * 3,
        scratch_shapes=[
            pltpu.VMEM(packed, BF16),
            pltpu.VMEM((COLS,) + packed, BF16),
            pltpu.VMEM((tokens, D), BF16),
            DMA((3, pieces)),
            DMA((3, pieces)),
        ],
        compiler_params=params(collective),
    )(x, w, attended, low)


def col_peers():
    me = lax.axis_index("col")
    return [{"col": (me + k) % COLS} for k in range(1, COLS)]


def to_rows(columns):
    lane = lax.broadcasted_iota(jnp.int32, (columns[0].shape[0], 128), 1)
    v = jnp.zeros(lane.shape, F32)
    for i, column in enumerate(columns):
        v = jnp.where(lane == i, column, v)
    return v.T[:8]


def to_columns(lines):
    place = lax.broadcasted_iota(jnp.int32, (8, lines[0].shape[1]), 0)
    v = jnp.zeros(place.shape, F32)
    for i, one in enumerate(lines):
        v = jnp.where(place == i, one, v)
    v = v.T
    return [v[:, i : i + 1] for i in range(len(lines))]


def share(snd_ref, all_ref, send, recv):
    me = lax.axis_index("col")
    copies = []
    for k, peer in enumerate(col_peers()):
        copy = push(snd_ref, all_ref.at[me], send.at[k], recv.at[k], peer)
        copy.start()
        copies.append(copy)
    all_ref[me] = snd_ref[...]
    for copy in copies:
        copy.wait()


def norm_back(grad, normed, gain, rstd, snd_ref, all_ref, send, recv):
    tokens = grad.shape[0]
    scaled = grad * gain
    sums = [
        jnp.sum(scaled, axis=-1, keepdims=True),
        jnp.sum(scaled * normed, axis=-1, keepdims=True),
    ]
    snd_ref[:, :tokens] = to_rows(sums)
    share(snd_ref, all_ref, send, recv)
    total = all_ref[0, :, :tokens]
    for b in range(1, COLS):
        total = total + all_ref[b, :, :tokens]
    total = total / D
    first, second = to_columns([total[0:1], total[1:2]])
    return rstd * (scaled - first - normed * second)


def line_greet(levels, row, level, partner):
    barrier = pltpu.get_barrier_semaphore()
    me = lax.axis_index("col")
    for k in range(1, COLS):
        peer = {"col": (me + k) % COLS}
        pl.semaphore_signal(barrier, inc=1, device_id=peer, device_id_type=MESH)
    pl.semaphore_signal(barrier, inc=1, device_id={"row": partner}, device_id_type=MESH)

    @pl.when(level > 0)
    def _():
        pl.semaphore_signal(barrier, inc=1, device_id={"row": row - 2}, device_id_type=MESH)

    @pl.when(level < levels - 1)
    def _():
        pl.semaphore_signal(barrier, inc=1, device_id={"row": row + 2}, device_id_type=MESH)

    count = COLS + (level > 0).astype(jnp.int32) + (level < levels - 1).astype(jnp.int32)
    pl.semaphore_wait(barrier, count)


def seen(key_start, query_start, shape, prefix):
    key = key_start + lax.broadcasted_iota(jnp.int32, shape, 0)
    query = query_start + lax.broadcasted_iota(jnp.int32, shape, 1)
    return (key < prefix) | (key <= query)


def forward_kernel(
    group,
    low,
    pieces,
    qb,
    info_ref,
    q_ref,
    kv_ref,
    g_ref,
    out_ref,
    o_ref,
    ob_ref,
    lse_ref,
    ga_ref,
    m_ref,
    acc_ref,
    u_send,
    u_recv,
    d_send,
    d_recv,
    x_send,
    x_recv,
    g_send,
    g_recv,
):
    levels = group // 2
    row, place, level, side, partner = line_places(group)
    prefix = info_ref[0]
    tokens, width = q_ref.shape
    heads = width // HD
    step = tokens // pieces
    line_greet(levels, row, level, partner)

    def make(at, i, way, src=None):
        part = pl.ds(i * step, step)
        dst = out_ref.at[2 * at + side, part]
        sems = ((u_send, u_recv), (d_send, d_recv), (x_send, x_recv))[way]
        peer = (row + 2, row - 2, partner)[way]
        return push(
            dst if src is None else src.at[part],
            dst,
            sems[0].at[at, i],
            sems[1].at[at, i],
            {"row": peer},
        )

    def other(at, i):
        part = pl.ds(i * step, step)
        dst = out_ref.at[2 * at + 1 - side, part]
        return push(dst, dst, x_send.at[at, i], x_recv.at[at, i], {"row": partner})

    def when(cond, run):
        @pl.when(cond)
        def _():
            for i in range(pieces):
                run(i)

    to_up = level < levels - 1
    own_down = (level > 0) & (level < low)
    own_side = (level < low) | (side == 0)
    for i in range(pieces):

        @pl.when(to_up)
        def _(i=i):
            make(level, i, 0, kv_ref).start()

        @pl.when(own_side)
        def _(i=i):
            make(level, i, 2, kv_ref).start()

        @pl.when(own_down)
        def _(i=i):
            make(level, i, 1, kv_ref).start()

    me = lax.axis_index("col")
    wide = []
    for k in range(1, COLS):
        peer = {"col": (me + k) % COLS}
        copy = push(g_ref, ga_ref.at[me], g_send.at[k - 1], g_recv.at[k - 1], peer)
        copy.start()
        wide.append(copy)
    ga_ref[me] = g_ref[...]
    out_ref[place] = kv_ref[...]
    m_ref[...] = jnp.full(m_ref.shape, neg_big, F32)
    acc_ref[...] = jnp.zeros(acc_ref.shape, F32)
    units = [(h, i) for h in range(heads) for i in range(tokens // qb)]

    def block(blk, masked):
        def raw_of(h, i):
            feats = slice(h * HD, (h + 1) * HD)
            raw = nt(out_ref[blk, :, feats], q_ref[i * qb : (i + 1) * qb, feats])
            if masked:
                allowed = seen(blk * tokens, place * tokens + i * qb, raw.shape, prefix)
                raw = jnp.where(allowed, raw, neg_big)
            return raw

        def soften(h, i, raw):
            cols = slice(i * qb, (i + 1) * qb)
            old = m_ref[h : h + 1, cols]
            new = jnp.maximum(old, jnp.max(raw, axis=0, keepdims=True))
            m_ref[h : h + 1, cols] = new
            weights = jnp.exp2((raw - new) * LOG2E).astype(BF16)
            return weights, jnp.exp2((old - new) * LOG2E)

        def gather(h, i, weights, scale):
            cols = slice(i * qb, (i + 1) * qb)
            v = out_ref[blk, :, width + h * HD : width + (h + 1) * HD]
            v_ext = jnp.concatenate([v.T, jnp.ones((16, tokens), BF16)], axis=0)
            acc_ref[h, :, cols] = acc_ref[h, :, cols] * scale + nn(v_ext, weights)

        coming, waiting = raw_of(*units[0]), None
        for n, unit in enumerate(units):
            raw = coming
            if n + 1 < len(units):
                coming = raw_of(*units[n + 1])
            soft = soften(*unit, raw)
            if waiting is not None:
                gather(*waiting)
            waiting = unit + soft
        gather(*waiting)

    def event(e, carry):
        t, cross = e // 2, e % 2
        at = jnp.where(t <= level, level - t, t)
        live = (t <= level) | (t < low)
        line_in = live & (cross == 0)

        @pl.when(line_in & (at < level))
        def _():
            for i in range(pieces):
                make(at, i, 0).wait_recv()

                @pl.when(to_up)
                def _(i=i):
                    make(at, i, 0).start()

                make(at, i, 2).start()

        @pl.when(line_in & (at > level))
        def _():
            for i in range(pieces):
                make(at, i, 1).wait_recv()

                @pl.when(level > 0)
                def _(i=i):
                    make(at, i, 1).start()

                make(at, i, 2).start()

        comes = live & (cross == 1) & ((at < low) | (at < level) | (side == 1))
        when(comes, lambda i: other(at, i).wait_recv())
        blk = 2 * at + jnp.where(cross == 0, side, 1 - side)
        needed = line_in | comes

        @pl.when(needed & (blk < place))
        def _():
            block(blk, False)

        @pl.when(needed & (blk >= place))
        def _():
            block(blk, True)

        return carry

    lax.fori_loop(0, 2 * levels, event, 0)

    for h in range(heads):
        total = acc_ref[h, HD : HD + 1, :]
        out = (acc_ref[h, :HD, :] / total).T
        o_ref[:, h * HD : (h + 1) * HD] = out
        ob_ref[:, h * HD : (h + 1) * HD] = out.astype(BF16)
        lse_ref[h : h + 1, :] = m_ref[h : h + 1, :] * LOG2E + jnp.log2(total)

    when(to_up, lambda i: make(level, i, 0, kv_ref).wait_send())
    when(own_side, lambda i: make(level, i, 2, kv_ref).wait_send())
    when(own_down, lambda i: make(level, i, 1, kv_ref).wait_send())
    for k in range(1, levels):
        at = level - k
        when((at >= 0) & to_up, lambda i, at=at: make(at, i, 0).wait_send())
        when(at >= 0, lambda i, at=at: make(at, i, 2).wait_send())
    for k in range(1, low):
        at = level + k
        when((at < low) & (level > 0), lambda i, at=at: make(at, i, 1).wait_send())
        when(at < low, lambda i, at=at: make(at, i, 2).wait_send())
    for copy in wide:
        copy.wait()


def attention_forward(info, q, kv, g, group, low, collective):
    pieces = 4
    levels = group // 2
    tokens, width = q.shape
    heads = width // HD
    return pl.pallas_call(
        functools.partial(forward_kernel, group, low, pieces, tokens // 2),
        out_shape=(
            jax.ShapeDtypeStruct((group,) + kv.shape, kv.dtype),
            jax.ShapeDtypeStruct((tokens, width), F32),
            jax.ShapeDtypeStruct((tokens, width), BF16),
            jax.ShapeDtypeStruct((8, tokens), F32),
            jax.ShapeDtypeStruct((COLS,) + g.shape, g.dtype),
        ),
        in_specs=[SSPEC, VSPEC, VSPEC, VSPEC],
        out_specs=(VSPEC,) * 5,
        scratch_shapes=[
            pltpu.VMEM((8, tokens), F32),
            pltpu.VMEM((heads, HD + 16, tokens), F32),
        ]
        + [DMA((levels, pieces))] * 6
        + [DMA((COLS - 1,))] * 2,
        compiler_params=params(collective),
    )(info, q, kv, g)


def backward_kernel(
    group,
    low,
    pieces,
    kb,
    info_ref,
    q_ref,
    kv_ref,
    do_ref,
    lse_ref,
    delta_ref,
    e_ref,
    bias_ref,
    out_ref,
    eo_ref,
    part_ref,
    rx_ref,
    above_ref,
    below_ref,
    snd_ref,
    acc_ref,
    dqt_ref,
    er_ref,
    u_send,
    u_recv,
    d_send,
    d_recv,
    x_send,
    x_recv,
    e_send,
    e_recv,
):
    levels = group // 2
    row, place, level, side, partner = line_places(group)
    prefix = info_ref[0]
    tokens, width = q_ref.shape
    heads = width // HD
    step = tokens // pieces
    line_greet(levels, row, level, partner)
    me = lax.axis_index("col")
    terms = []
    for k in range(1, COLS):
        peer = (me + k) % COLS
        copy = push(
            e_ref.at[peer], er_ref.at[k - 1], e_send.at[k - 1], e_recv.at[k - 1], {"col": peer}
        )
        copy.start()
        terms.append(copy)
    dqt_ref[...] = jnp.zeros(dqt_ref.shape, F32)

    def block(blk, masked):
        def body(j, carry):
            start = pl.multiple_of(j * kb, kb)
            keys = pl.ds(start, kb)
            for h in range(heads):
                feats = slice(h * HD, (h + 1) * HD)
                vals = slice(width + h * HD, width + (h + 1) * HD)
                k, v = kv_ref[blk, keys, feats], kv_ref[blk, keys, vals]
                q, do = q_ref[:, feats], do_ref[:, feats]
                probs = jnp.exp2(nt(k, q) * LOG2E - lse_ref[h : h + 1, :])
                if masked:
                    allowed = seen(blk * tokens + start, place * tokens, probs.shape, prefix)
                    probs = jnp.where(allowed, probs, 0.0)
                grad = (probs * (nt(v, do) - delta_ref[h : h + 1, :])).astype(BF16)
                part_ref[blk, keys, feats] = nn(grad, q).astype(BF16)
                part_ref[blk, keys, vals] = nn(probs.astype(BF16), do).astype(BF16)
                dqt_ref[feats, :] += nn(k.T, grad)
            return carry

        lax.fori_loop(0, tokens // kb, body, 0)

    def cross(at, i):
        part = pl.ds(i * step, step)
        return push(
            part_ref.at[2 * at + 1 - side, part],
            rx_ref.at[at, part],
            x_send.at[at, i],
            x_recv.at[at, i],
            {"row": partner},
        )

    def line(at, i, up):
        part = pl.ds(i * step, step)
        sems = (u_send, u_recv) if up else (d_send, d_recv)
        return push(
            snd_ref.at[at, part],
            (below_ref if up else above_ref).at[at, part],
            sems[0].at[at, i],
            sems[1].at[at, i],
            {"row": row + 2 if up else row - 2},
        )

    def gone(at):
        return (at < low) | (at < level) | ((at == level) & (side == 1))

    def comes(at):
        return (at < low) | (at < level) | ((at == level) & (side == 0))

    def total(at, i, from_above, from_below):
        part = pl.ds(i * step, step)
        acc_ref[...] = part_ref[2 * at + side, part].astype(F32)

        @pl.when(comes(at))
        def _():
            cross(at, i).wait_recv()
            acc_ref[...] += rx_ref[at, part].astype(F32)

        if from_above is not None:

            @pl.when(from_above)
            def _():
                line(at, i, False).wait_recv()
                acc_ref[...] += above_ref[at, part].astype(F32)

        if from_below is not None:

            @pl.when(from_below)
            def _():
                line(at, i, True).wait_recv()
                acc_ref[...] += below_ref[at, part].astype(F32)

    not_top = level < levels - 1
    above = jnp.maximum(low - 1 - level, 0)

    def level_of(t):
        return jnp.where(t < above, low - 1 - t, t - above)

    def event(e, carry):
        t, own = e // 2, e % 2
        at = level_of(t)
        live = (t < above) | (at <= level)

        down = t - (levels - level)

        @pl.when((own == 1) & (down >= 0) & (down < level))
        def _():
            for i in range(pieces):
                total(down, i, not_top, None)
                snd_ref[down, pl.ds(i * step, step)] = acc_ref[...].astype(BF16)
                line(down, i, False).start()

        @pl.when((own == 1) & (t >= 1) & (t - 1 < above))
        def _():
            up = level_of(t - 1)
            for i in range(pieces):
                total(up, i, None, level > 0)
                snd_ref[up, pl.ds(i * step, step)] = acc_ref[...].astype(BF16)
                line(up, i, True).start()

        goes = live & (own == 0) & gone(at)
        blk = 2 * at + jnp.where(own == 1, side, 1 - side)
        needed = goes | (live & (own == 1))

        @pl.when(needed & (blk < place))
        def _():
            block(blk, False)

        @pl.when(needed & (blk >= place))
        def _():
            block(blk, True)

        @pl.when(goes)
        def _():
            for i in range(pieces):
                cross(at, i).start()

        return carry

    lax.fori_loop(0, 2 * levels, event, 0)
    for copy in terms:
        copy.wait()

    def finish(r, carry):
        total = e_ref[me, r].astype(F32) + bias_ref[...]
        for k in range(COLS - 1):
            total = total + er_ref[k, r].astype(F32)
        eo_ref[r] = total.astype(BF16)
        return carry

    lax.fori_loop(0, e_ref.shape[1], finish, 0)
    out_ref[:, :width] = (dqt_ref[...] * HD**-0.5).T.astype(BF16)

    for i in range(pieces):
        total(level, i, not_top, (level > 0) & (level < low))
        out_ref[pl.ds(i * step, step), width:] = acc_ref[...].astype(BF16)

    for at in range(levels):
        for i in range(pieces):

            @pl.when(gone(at))
            def _(at=at, i=i):
                cross(at, i).wait_send()

            @pl.when(at < level)
            def _(at=at, i=i):
                line(at, i, False).wait_send()

            if at < low:

                @pl.when(at > level)
                def _(at=at, i=i):
                    line(at, i, True).wait_send()


def attention_backward(info, q, kv_all, do, lse, delta, e, bias, group, low, collective):
    pieces = 4
    levels = group // 2
    tokens, width = q.shape
    both = 2 * width
    block = pltpu.VMEM((levels, tokens, both), BF16)
    return pl.pallas_call(
        functools.partial(backward_kernel, group, low, pieces, tokens // 2),
        out_shape=(
            jax.ShapeDtypeStruct((tokens, width + both), BF16),
            jax.ShapeDtypeStruct(e.shape[1:], BF16),
        ),
        in_specs=[SSPEC] + [VSPEC] * 7,
        out_specs=(VSPEC,) * 2,
        scratch_shapes=[
            pltpu.VMEM(kv_all.shape, BF16),
            block,
            block,
            pltpu.VMEM((low, tokens, both), BF16),
            block,
            pltpu.VMEM((tokens // pieces, both), F32),
            pltpu.VMEM((width, tokens), F32),
            pltpu.VMEM((COLS - 1,) + e.shape[1:], BF16),
        ]
        + [DMA((levels, pieces))] * 6
        + [DMA((COLS - 1,))] * 2,
        compiler_params=params(collective),
    )(info, q, kv_all, do, lse, delta, e, bias)


def product(pieces, a_ref, w_ref, feats, out_ref, snd_ref, rx_ref, far_ref, tot_ref, sems, fill):
    send, recv = sems
    me, sib, across, diag = col_places()
    half = a_ref.shape[0] // 2
    step = half // pieces
    per = w_ref.shape[0] // COLS
    width = out_ref.shape[1]

    def weight(who):
        return w_ref[pl.ds(who * per, per)].reshape(width, 4 * width)[:, feats]

    def term(i, w):
        parts = [nt(a_ref[pl.ds(n * half + i * step, step)], w) for n in range(2)]
        return jnp.concatenate(parts, axis=1)

    def near(i, j):
        part = pl.ds(i * step, step)
        return push(
            snd_ref.at[j, part], rx_ref.at[j, part], send.at[j, i], recv.at[j, i], {"col": sib}
        )

    def over(i):
        part = pl.ds(i * step, step)
        return push(tot_ref.at[part], far_ref.at[part], send.at[2, i], recv.at[2, i], {"col": across})

    w = weight(diag)
    for i in range(pieces):
        snd_ref[0, pl.ds(i * step, step)] = term(i, w).astype(BF16)
        near(i, 0).start()
    w = weight(across)
    for i in range(pieces):
        part = pl.ds(i * step, step)
        mine = term(i, w)
        near(i, 0).wait_recv()
        tot_ref[part] = (mine + rx_ref[0, part].astype(F32)).astype(BF16)
        over(i).start()
    w = weight(sib)
    for i in range(pieces):
        snd_ref[1, pl.ds(i * step, step)] = term(i, w).astype(BF16)
        near(i, 1).start()
    fill()
    w = weight(me)
    for i in range(pieces):
        part = pl.ds(i * step, step)
        mine = term(i, w)
        near(i, 1).wait_recv()
        mine = mine + rx_ref[1, part].astype(F32)
        over(i).wait_recv()
        mine = mine + far_ref[part].astype(F32)
        out_ref[part] = mine[:, :width]
        out_ref[pl.ds(half + i * step, step)] = mine[:, width:]
    for i in range(pieces):
        near(i, 0).wait_send()
        near(i, 1).wait_send()
        over(i).wait_send()


def product_scratch(pieces, tokens, width):
    block = pltpu.VMEM((tokens // 2, 2 * width), BF16)
    pair = pltpu.VMEM((2, tokens // 2, 2 * width), BF16)
    return [pair, pair, block, block, DMA((3, pieces)), DMA((3, pieces))]


def branch_kernel(
    pieces,
    a_ref,
    w_ref,
    x_ref,
    bias_ref,
    gain_ref,
    shift_ref,
    mid_ref,
    normed_ref,
    rstd_ref,
    h_ref,
    snd_ref,
    rx_ref,
    far_ref,
    tot_ref,
    send,
    recv,
    st_ref,
    all_ref,
    st_send,
    st_recv,
):
    greet(col_peers())
    tokens, width = x_ref.shape
    product(
        pieces,
        a_ref,
        w_ref,
        slice(3 * width, 4 * width),
        mid_ref,
        snd_ref,
        rx_ref,
        far_ref,
        tot_ref,
        (send, recv),
        lambda: None,
    )
    mid = x_ref[...].astype(F32) + mid_ref[...] + bias_ref[...]
    mid_ref[...] = mid
    part_mean = jnp.mean(mid, axis=-1, keepdims=True)
    part_spread = jnp.sum((mid - part_mean) ** 2, axis=-1, keepdims=True)
    st_ref[...] = to_rows([part_mean, part_spread])
    share(st_ref, all_ref, st_send, st_recv)
    mean = sum(all_ref[b, 0:1] for b in range(COLS)) / COLS
    spread = sum(
        all_ref[b, 1:2] + width * (all_ref[b, 0:1] - mean) ** 2 for b in range(COLS)
    )
    mean, rstd = to_columns([mean, lax.rsqrt(spread / D + epsilon)])
    normed = (mid - mean) * rstd
    normed_ref[...] = normed
    rstd_ref[...] = rstd
    h_ref[...] = (normed * gain_ref[...] + shift_ref[...]).astype(BF16)


def branch(a, w, x, bias, gain, shift, collective):
    pieces = 4
    tokens, width = a.shape
    rows = jax.ShapeDtypeStruct((tokens, width), F32)
    return pl.pallas_call(
        functools.partial(branch_kernel, pieces),
        out_shape=(
            rows,
            rows,
            jax.ShapeDtypeStruct((tokens, 1), F32),
            jax.ShapeDtypeStruct((tokens, width), BF16),
        ),
        in_specs=[VSPEC] * 6,
        out_specs=(VSPEC,) * 4,
        scratch_shapes=product_scratch(pieces, tokens, width)
        + [
            pltpu.VMEM((8, tokens), F32),
            pltpu.VMEM((COLS, 8, tokens), F32),
            DMA((COLS - 1,)),
            DMA((COLS - 1,)),
        ],
        compiler_params=params(collective),
    )(a, w, x, bias, gain, shift)


def input_kernel(
    pieces,
    a_ref,
    w_ref,
    e_ref,
    h_ref,
    gwo_ref,
    mid_ref,
    normed_ref,
    rstd_ref,
    gain_ref,
    vec_ref,
    gin_ref,
    eo_ref,
    wt_ref,
    all_ref,
    grad_ref,
    snd_ref,
    rx_ref,
    far_ref,
    tot_ref,
    send,
    recv,
    st_ref,
    st_send,
    st_recv,
    e_send,
    e_recv,
):
    rows = e_ref.shape[0]
    row = lax.axis_index("row")
    order = far_first(rows)
    greet([{"row": (row + k) % rows} for k in order] + col_peers())
    home = []
    for n, k in enumerate(order):
        peer = (row + k) % rows
        copy = push(e_ref.at[peer], eo_ref.at[row], e_send.at[n], e_recv.at[n], {"row": peer})
        copy.start()
        home.append(copy)
    eo_ref[row] = e_ref[row]
    tokens, width = grad_ref.shape

    def fill():
        both = [tn(h_ref[...], a_ref[...]).astype(BF16), gwo_ref[...]]
        wt_ref[...] = jnp.concatenate(both, axis=1)

    product(
        pieces,
        a_ref,
        w_ref,
        slice(0, 3 * width),
        grad_ref,
        snd_ref,
        rx_ref,
        far_ref,
        tot_ref,
        (send, recv),
        fill,
    )
    grad, normed = grad_ref[...], normed_ref[...]
    st_ref[:, tokens:] = jnp.zeros((8, st_ref.shape[1] - tokens), F32)
    st_ref[0:1, tokens : tokens + width] = jnp.sum(grad * normed, axis=0, keepdims=True)
    st_ref[1:2, tokens : tokens + width] = jnp.sum(grad, axis=0, keepdims=True)
    st_ref[2:5, tokens : tokens + width] = vec_ref[0:3]
    gin_ref[...] = mid_ref[...] + norm_back(
        grad, normed, gain_ref[...], rstd_ref[...], st_ref, all_ref, st_send, st_recv
    )
    for copy in home:
        copy.wait()


def input_gradient(a, w, e, h, gwo, mid, normed, rstd, gain, vec, collective):
    pieces = 4
    tokens, width = mid.shape
    wide = tokens + 256
    return pl.pallas_call(
        functools.partial(input_kernel, pieces),
        out_shape=(
            jax.ShapeDtypeStruct((tokens, width), F32),
            jax.ShapeDtypeStruct(e.shape, BF16),
            jax.ShapeDtypeStruct((D, 4 * width), BF16),
            jax.ShapeDtypeStruct((COLS, 8, wide), F32),
        ),
        in_specs=[VSPEC] * 10,
        out_specs=(VSPEC,) * 4,
        scratch_shapes=[pltpu.VMEM((tokens, width), F32)]
        + product_scratch(pieces, tokens, width)
        + [
            pltpu.VMEM((8, wide), F32),
            DMA((COLS - 1,)),
            DMA((COLS - 1,)),
            DMA((e.shape[0] - 1,)),
            DMA((e.shape[0] - 1,)),
        ],
        compiler_params=params(collective),
    )(a, w, e, h, gwo, mid, normed, rstd, gain, vec)


def dispatch_kernel(rows, x_ref, t_ref, out_ref, in_ref, r_send, r_recv, c_send, c_recv):
    me, sib, across, _ = col_places()
    row = lax.axis_index("row")
    order = far_first(rows)
    peers = [(row + k) % rows for k in order]
    greet([{"row": p} for p in peers] + [{"col": sib}, {"col": across}])
    copies = []
    cap = in_ref.shape[1]
    for k, peer in enumerate(peers):
        in_ref[peer] = placed(t_ref, x_ref[...], peer, cap)
        copy = push(
            in_ref.at[peer], out_ref.at[me, row], r_send.at[k], r_recv.at[k], {"row": peer}
        )
        copy.start()
        copies.append(copy)
    in_ref[row] = placed(t_ref, x_ref[...], row, cap)

    def col(src, dst, k, way):
        return push(
            src, dst, c_send.at[way, k], c_recv.at[way, k], {"col": across if way == 0 else sib}
        )

    done, first = [], []
    for way in range(2):
        copy = col(in_ref.at[row], out_ref.at[me, row], 0, way)
        copy.start()
        (first if way == 0 else done).append(copy)
    out_ref[me, row] = in_ref[row]
    sources = [row] + [(row + rows - k) % rows for k in order]

    def forward(k):
        first[k].wait_recv()
        src = sources[k]
        copy = col(out_ref.at[across, src], out_ref.at[across, src], k, 2)
        copy.start()
        done.append(copy)

    for k in range(1, rows):
        copies[k - 1].wait_recv()
        block = out_ref.at[me, sources[k]]
        for way in range(2):
            copy = col(block, block, k, way)
            copy.start()
            (first if way == 0 else done).append(copy)
        forward(k - 1)
    forward(rows - 1)
    for copy in copies:
        copy.wait_send()
    for copy in first:
        copy.wait_send()
    for copy in done:
        copy.wait()


def dispatch(x, target, rows, cap, collective):
    block = (rows, cap, 2 * x.shape[1])
    return pl.pallas_call(
        functools.partial(dispatch_kernel, rows),
        out_shape=jax.ShapeDtypeStruct((COLS,) + block, x.dtype),
        in_specs=[VSPEC] * 2,
        out_specs=VSPEC,
        scratch_shapes=[
            pltpu.VMEM(block, x.dtype),
            DMA((rows - 1,)),
            DMA((rows - 1,)),
            DMA((3, rows)),
            DMA((3, rows)),
        ],
        compiler_params=params(collective),
    )(x, target)


def giveback_kernel(
    rows,
    in_ref,
    t_ref,
    cot_ref,
    normed_ref,
    rstd_ref,
    gain_ref,
    mid_ref,
    vec_ref,
    sum_ref,
    out_ref,
    rx_ref,
    far_ref,
    tot_ref,
    fin_ref,
    st_ref,
    all_ref,
    send,
    recv,
    r_send,
    r_recv,
    st_send,
    st_recv,
):
    me, sib, across, diag = col_places()
    row = lax.axis_index("row")
    order = [(row + k) % rows for k in far_first(rows)] + [row]
    greet([{"row": p} for p in order[:-1]] + col_peers())

    def near(k, j):
        who = diag if j == 0 else sib
        return push(
            in_ref.at[who, order[k]], rx_ref.at[j, k], send.at[j, k], recv.at[j, k], {"col": sib}
        )

    def over(k):
        return push(tot_ref.at[k], far_ref.at[k], send.at[2, k], recv.at[2, k], {"col": across})

    def home(k):
        return push(
            fin_ref.at[k], out_ref.at[row], r_send.at[k], r_recv.at[k], {"row": order[k]}
        )

    for k in range(rows):
        near(k, 0).start()
        near(k, 1).start()

    def finish(k):
        near(k, 1).wait_recv()
        over(k).wait_recv()
        total = in_ref[me, order[k]].astype(F32) + rx_ref[1, k].astype(F32)
        total = total + far_ref[k].astype(F32)
        if k == rows - 1:
            out_ref[row] = total.astype(BF16)
        else:
            fin_ref[k] = total.astype(BF16)
            home(k).start()

    for k in range(rows):
        near(k, 0).wait_recv()
        tot_ref[k] = (in_ref[across, order[k]].astype(F32) + rx_ref[0, k].astype(F32)).astype(BF16)
        over(k).start()
        if k >= 1:
            finish(k - 1)
    finish(rows - 1)
    cap = out_ref.shape[1]
    sum_ref[...] = combined(t_ref, out_ref[row], row, cap)
    for k, gap in enumerate(far_first(rows)):
        source = (row + rows - gap) % rows
        home(k).wait_recv()
        sum_ref[...] += combined(t_ref, out_ref[source], source, cap)
    grad, normed = sum_ref[...], normed_ref[...]
    mid = cot_ref[...].astype(F32) + norm_back(
        grad, normed, gain_ref[...], rstd_ref[...], st_ref, all_ref, st_send, st_recv
    )
    mid_ref[...] = mid
    vec_ref[...] = jnp.zeros(vec_ref.shape, F32)
    vec_ref[0:1] = jnp.sum(grad * normed, axis=0, keepdims=True)
    vec_ref[1:2] = jnp.sum(grad, axis=0, keepdims=True)
    vec_ref[2:3] = jnp.sum(mid, axis=0, keepdims=True)
    for k in range(rows):
        near(k, 0).wait_send()
        near(k, 1).wait_send()
        over(k).wait_send()
        if k < rows - 1:
            home(k).wait_send()


def giveback(parts, target, cot, normed, rstd, gain, rows, collective):
    block = parts.shape[2:]
    one = pltpu.VMEM((rows,) + block, BF16)
    return pl.pallas_call(
        functools.partial(giveback_kernel, rows),
        out_shape=(
            jax.ShapeDtypeStruct(cot.shape, F32),
            jax.ShapeDtypeStruct((8, cot.shape[1]), F32),
        ),
        in_specs=[VSPEC] * 6,
        out_specs=(VSPEC,) * 2,
        scratch_shapes=[
            pltpu.VMEM(cot.shape, F32),
            one,
            pltpu.VMEM((2, rows) + block, BF16),
            one,
            one,
            one,
            pltpu.VMEM((8, cot.shape[0]), F32),
            pltpu.VMEM((COLS, 8, cot.shape[0]), F32),
            DMA((3, rows)),
            DMA((3, rows)),
            DMA((rows - 1,)),
            DMA((rows - 1,)),
            DMA((COLS - 1,)),
            DMA((COLS - 1,)),
        ],
        compiler_params=params(collective),
    )(parts, target, cot, normed, rstd, gain)


def end_kernel(
    rows,
    w_ref,
    s_ref,
    e_ref,
    t_ref,
    mid_ref,
    wo_ref,
    so_ref,
    lo_ref,
    px_ref,
    pt_ref,
    wr_ref,
    sr_ref,
    p_send,
    p_recv,
    l_send,
    l_recv,
    send,
    recv,
):
    row, _, level, side, partner = line_places(rows)
    levels = rows // 2
    peers = [(row + k) % rows for k in far_first(rows)]
    greet([{"row": p} for p in peers])
    gaps = far_first(levels)
    targets = [(level + k) % levels for k in gaps] + [level]

    def cross(n):
        src = w_ref.at[2 * targets[n] + 1 - side]
        return push(src, px_ref.at[n], p_send.at[n], p_recv.at[n], {"row": partner})

    def along(n):
        peer = {"row": 2 * targets[n] + side}
        return push(pt_ref.at[n], wr_ref.at[n], l_send.at[n], l_recv.at[n], peer)

    def total(n):
        return w_ref[2 * targets[n] + side].astype(F32) + px_ref[n].astype(F32)

    for n in range(levels):
        cross(n).start()
    copies = []
    for k, peer in enumerate(peers):
        copy = push(s_ref.at[peer], sr_ref.at[k], send.at[k], recv.at[k], {"row": peer})
        copy.start()
        copies.append(copy)
    for n in range(levels - 1):
        cross(n).wait_recv()
        pt_ref[n] = total(n).astype(BF16)
        along(n).start()
    result = mid_ref[...]
    for r in range(rows):
        result = result + combined(t_ref, e_ref[r], r, e_ref.shape[1])
    lo_ref[...] = result.astype(BF16)
    small = s_ref[row]
    for k, copy in enumerate(copies):
        copy.wait_recv()
        small = small + sr_ref[k]
    so_ref[...] = small
    cross(levels - 1).wait_recv()
    mine = total(levels - 1)
    for n in range(levels - 1):
        along(n).wait_recv()
        mine = mine + wr_ref[n].astype(F32)
    wo_ref[...] = mine
    for n in range(levels):
        cross(n).wait_send()
        if n < levels - 1:
            along(n).wait_send()
    for copy in copies:
        copy.wait_send()


def end_scatter(w, s, outs, target, mid, rows, collective):
    levels = rows // 2
    one = w.shape[1:]
    return pl.pallas_call(
        functools.partial(end_kernel, rows),
        out_shape=(
            jax.ShapeDtypeStruct(one, F32),
            jax.ShapeDtypeStruct(s.shape[1:], F32),
            jax.ShapeDtypeStruct(mid.shape, BF16),
        ),
        in_specs=[VSPEC] * 5,
        out_specs=(VSPEC,) * 3,
        scratch_shapes=[
            pltpu.VMEM((levels,) + one, w.dtype),
            pltpu.VMEM((levels - 1,) + one, w.dtype),
            pltpu.VMEM((levels - 1,) + one, w.dtype),
            pltpu.VMEM((rows - 1,) + s.shape[1:], s.dtype),
            DMA((levels,)),
            DMA((levels,)),
            DMA((levels - 1,)),
            DMA((levels - 1,)),
            DMA((rows - 1,)),
            DMA((rows - 1,)),
        ],
        compiler_params=params(collective),
    )(w, s, outs, target, mid)


def expert_kernel(
    x_ref,
    g_ref,
    up_ref,
    bias_ref,
    down_ref,
    part_ref,
    gx_ref,
    gup_ref,
    gbu_ref,
    gdown_ref,
    gbd_ref,
):
    cols, rows, cap, both = x_ref.shape
    width = both // 2
    slots = rows * cap
    first = pl.program_id(0) == 0

    def mine(ref):
        blocks = [ref[b].reshape(slots, both) for b in range(cols)]
        blocks = [jnp.where(first, v[:, :width], v[:, width:]) for v in blocks]
        return jnp.concatenate(blocks, axis=1)

    x, g = mine(x_ref), mine(g_ref)
    gbd_ref[...] = jnp.sum(g.astype(F32), axis=0).reshape(gbd_ref.shape)
    hidden_units = up_ref.shape[2]
    chunk = 256
    part = jnp.zeros((slots, cols * width), F32)
    gx = jnp.zeros((slots, cols * width), F32)
    for f in range(hidden_units // chunk):
        cut = slice(f * chunk, (f + 1) * chunk)
        up, down = up_ref[0, :, cut], down_ref[0, cut, :]
        pre = nn(x, up) + bias_ref[0, :, cut].astype(F32)
        cdf = 0.5 * (1.0 + lax.erf(pre * (0.5**0.5)))
        slope = cdf + pre * (jnp.exp(-0.5 * pre * pre) * 0.3989422804014327)
        hidden = (pre * cdf).astype(BF16)
        grad = nt(g, down) * slope
        grad = grad.astype(BF16)
        part = part + nn(hidden, down)
        gx = gx + nt(grad, up)
        gdown_ref[0, cut, :] = tn(hidden, g)
        gup_ref[0, :, cut] = tn(x, grad)
        gbu_ref[0, :, cut] = jnp.sum(grad.astype(F32), axis=0, keepdims=True)
    for e in range(EXP_DEV):

        @pl.when(pl.program_id(0) == e)
        def _(e=e):
            lanes = slice(e * width, (e + 1) * width)
            for b in range(cols):
                cut = slice(b * width, (b + 1) * width)
                part_ref[b, :, :, lanes] = part[:, cut].astype(BF16).reshape(rows, cap, width)
                gx_ref[b, :, :, lanes] = gx[:, cut].astype(BF16).reshape(rows, cap, width)


def experts(x, g, w_up, bias_up, w_down):
    slots = pl.BlockSpec(x.shape, lambda e: (0, 0, 0, 0))
    count, features, hidden = w_up.shape
    return pl.pallas_call(
        expert_kernel,
        grid=(count,),
        out_shape=(
            jax.ShapeDtypeStruct(x.shape, BF16),
            jax.ShapeDtypeStruct(x.shape, BF16),
            jax.ShapeDtypeStruct(w_up.shape, F32),
            jax.ShapeDtypeStruct((count, 1, hidden), F32),
            jax.ShapeDtypeStruct(w_down.shape, F32),
            jax.ShapeDtypeStruct((count, 1, features), F32),
        ),
        in_specs=[
            slots,
            slots,
            pl.BlockSpec((1, features, hidden), lambda e: (e, 0, 0)),
            pl.BlockSpec((1, 1, hidden), lambda e: (e, 0, 0)),
            pl.BlockSpec((1, hidden, features), lambda e: (e, 0, 0)),
        ],
        out_specs=(
            slots,
            slots,
            pl.BlockSpec((1, features, hidden), lambda e: (e, 0, 0)),
            pl.BlockSpec((1, 1, hidden), lambda e: (e, 0, 0)),
            pl.BlockSpec((1, hidden, features), lambda e: (e, 0, 0)),
            pl.BlockSpec((1, 1, features), lambda e: (e, 0, 0)),
        ),
        compiler_params=params(),
    )(x, g, w_up, bias_up.reshape(count, 1, hidden), w_down)


def per_device(
    layer_in,
    cotangent,
    token_ids,
    hash_table,
    prefix_len,
    w_query,
    w_key,
    w_value,
    w_output,
    bias_query,
    bias_value,
    gain_attn,
    shift_attn,
    gain_moe,
    shift_moe,
    bias_output,
    w_up,
    bias_up,
    w_down,
    bias_down,
):
    rows = lax.axis_size("row")
    row = lax.axis_index("row")
    col = lax.axis_index("col")
    tokens, width = layer_in.shape
    heads = width // HD
    seq_len = min(LENGTH, tokens * rows)
    group = seq_len // tokens
    low = -(-PREFIX_MAX // (2 * tokens))
    share = w_query.shape[0]
    bias_share = bias_query.shape[0]

    def line(v):
        return jnp.pad(v.astype(F32), (0, 128 - v.shape[0]))

    small = jnp.stack(
        [
            line(gain_attn),
            line(shift_attn),
            line(gain_moe),
            line(shift_moe),
            line(bias_output),
            line(bias_query.T.reshape(-1)),
            line(bias_value.T.reshape(-1)),
            jnp.zeros((128,), F32),
        ]
    )
    expert_total = EXP_DEV * rows
    capacity = max(2, 2 * tokens // expert_total)
    expert_of = hash_table[token_ids]
    hits = expert_of[:, None] == jnp.arange(expert_total, dtype=jnp.int32)[None, :]
    earlier = (
        jnp.arange(tokens, dtype=jnp.int32)[None, :] < jnp.arange(tokens, dtype=jnp.int32)[:, None]
    )
    before = jnp.dot(earlier.astype(BF16), hits.astype(BF16), preferred_element_type=F32)
    slot_of = jnp.sum(jnp.where(hits, before, 0.0), axis=1).astype(jnp.int32)
    target = expert_of * capacity + slot_of
    target = target[None, :]

    weights = jnp.concatenate([w_query, w_key, w_value, w_output], axis=1)
    x_all, g_own, w_all, s_all = start_gather(
        layer_in, cotangent, target, weights, small, rows, capacity
    )
    gain_one, shift_one, gain_two, shift_two, out_bias = (
        s_all[:, i, :share].reshape(D) for i in range(5)
    )

    def own(v):
        return lax.dynamic_slice_in_dim(v, col * width, width, 0)

    query_bias, value_bias = (
        s_all[:, i, : heads * bias_share]
        .reshape(rows, heads, bias_share)
        .transpose(1, 0, 2)
        .reshape(width)
        for i in (5, 6)
    )

    qkv_bias = jnp.concatenate([query_bias, jnp.zeros_like(query_bias), value_bias])
    queries, keys_values, h_one, normed_one, rstd_one = project(
        x_all, w_all, gain_one[None], shift_one[None], qkv_bias[None]
    )
    seq_hit = row // group == jnp.arange(prefix_len.shape[0], dtype=jnp.int32)
    prefix = jnp.sum(jnp.where(seq_hit, prefix_len, 0))
    info = prefix.astype(jnp.int32).reshape(1)
    kv_all, attended, attended_low, lse, g_all = attention_forward(
        info, queries, keys_values, g_own, group, low, 1
    )
    gain_two_own = own(gain_two)[None]
    mid, normed_two, rstd_two, h_two = branch(
        attended_low,
        w_all,
        layer_in,
        own(out_bias)[None],
        gain_two_own,
        own(shift_two)[None],
        2,
    )

    received = dispatch(h_two, target, rows, capacity, 4)
    parts, grad_parts, grad_w_up, grad_bias_up, grad_w_down, grad_bias_down = experts(
        received, g_all, w_up, bias_up, w_down
    )
    grad_mid, vectors = giveback(
        grad_parts, target, cotangent, normed_two, rstd_two, gain_two_own, rows, 5
    )
    grad_attended, delta, grad_w_out = mid_gradient(grad_mid, w_all, attended, attended_low, 7)
    down_own = lax.dynamic_slice_in_dim(bias_down, col * width, width, 1).astype(F32)
    down_own = down_own.reshape(1, EXP_DEV * width)
    grad_qkv, outs = attention_backward(
        info,
        queries,
        kv_all,
        grad_attended,
        lse,
        delta,
        parts,
        down_own,
        group,
        low,
        8,
    )
    grad_bias = jnp.sum(grad_qkv, axis=0, dtype=F32)
    grad_in, outs, weight_terms, shared = input_gradient(
        grad_qkv,
        w_all,
        outs,
        h_one,
        grad_w_out,
        grad_mid,
        normed_one,
        rstd_one,
        own(gain_one)[None],
        vectors,
        9,
    )
    vectors = shared[:, :5, tokens : tokens + width]
    vectors = vectors.transpose(1, 0, 2).reshape(5, rows, share).transpose(1, 0, 2)

    def by_row(v):
        v = v.reshape(heads, rows, bias_share).transpose(1, 0, 2).reshape(rows, 1, -1)
        return jnp.pad(v, ((0, 0), (0, 0), (0, 128 - v.shape[2])))

    small_terms = jnp.concatenate(
        [
            jnp.pad(vectors, ((0, 0), (0, 0), (0, 128 - share))),
            by_row(grad_bias[:width]),
            by_row(grad_bias[2 * width :]),
            jnp.zeros((rows, 1, 128), F32),
        ],
        axis=1,
    )
    weight_terms = weight_terms.reshape(rows, share, 4 * width)
    weight_sums, small_sums, layer_out = end_scatter(
        weight_terms, small_terms, outs, target, mid, rows, 11
    )

    def bias_back(v):
        return v[: heads * bias_share].reshape(heads, bias_share).T

    return (
        layer_out,
        grad_in,
        weight_sums[:, :width],
        weight_sums[:, width : 2 * width],
        weight_sums[:, 2 * width : 3 * width],
        weight_sums[:, 3 * width :],
        bias_back(small_sums[5]),
        bias_back(small_sums[6]),
        small_sums[0, :share],
        small_sums[1, :share],
        small_sums[2, :share],
        small_sums[3, :share],
        small_sums[4, :share],
        grad_w_up,
        grad_bias_up[:, 0],
        grad_w_down,
        grad_bias_down[:, 0],
    )


def solution(mesh):
    placed = (
        P("row", "col"),
        P("row", "col"),
        P("row"),
        P(),
        P(),
        P("row", "col"),
        P("row", "col"),
        P("row", "col"),
        P("row", "col"),
        P("row", "col"),
        P("row", "col"),
        P("row"),
        P("row"),
        P("row"),
        P("row"),
        P("row"),
        P("row", None, "col"),
        P("row", "col"),
        P("row", "col", None),
        P("row", None),
    )
    return jax.shard_map(
        per_device,
        mesh=mesh,
        in_specs=placed,
        out_specs=(
            P("row", "col"),
            P("row", "col"),
            P("row", "col"),
            P("row", "col"),
            P("row", "col"),
            P("row", "col"),
            P("row", "col"),
            P("row", "col"),
            P("row"),
            P("row"),
            P("row"),
            P("row"),
            P("row"),
            P("row", None, "col"),
            P("row", "col"),
            P("row", "col", None),
            P("row", None),
        ),
        check_vma=False,
    )
```

```python
import functools

import jax
import jax.numpy as jnp
from jax import lax
from jax.experimental import pallas as pl
from jax.experimental.pallas import tpu as pltpu
from jax.sharding import PartitionSpec as P

D = 768
HD = 64
EXP_DEV = 2
LENGTH = 8192
PREFIX_MAX = 4096
COLS = 4

F32 = jnp.float32
BF16 = jnp.bfloat16
MESH = pl.DeviceIdType.MESH
LOG2E = 1.4426950408889634

epsilon = 1e-05
neg_big = -1e30

VSPEC = pl.BlockSpec(memory_space=pltpu.VMEM)
SSPEC = pl.BlockSpec(memory_space=pltpu.SMEM)
VMEM_BYTES = 64 * 1000 * 1000
DMA = pltpu.SemaphoreType.DMA


def params(collective=None):
    if collective is None:
        return pltpu.CompilerParams(vmem_limit_bytes=VMEM_BYTES)
    return pltpu.CompilerParams(
        vmem_limit_bytes=VMEM_BYTES, collective_id=collective, has_side_effects=True
    )


def push(src, dst, send_sem, recv_sem, peer):
    return pltpu.make_async_remote_copy(
        src_ref=src,
        dst_ref=dst,
        send_sem=send_sem,
        recv_sem=recv_sem,
        device_id=peer,
        device_id_type=MESH,
    )


def greet(peers):
    barrier = pltpu.get_barrier_semaphore()
    for peer in peers:
        pl.semaphore_signal(barrier, inc=1, device_id=peer, device_id_type=MESH)
    pl.semaphore_wait(barrier, len(peers))


def col_places():
    me = lax.axis_index("col")
    sib = me + 1 - 2 * (me % 2)
    across = (me + 2) % COLS
    diag = (sib + 2) % COLS
    return me, sib, across, diag


def line_places(group):
    row = lax.axis_index("row")
    place = row % group
    level, side = place // 2, place % 2
    return row, place, level, side, row + 1 - 2 * side


def far_first(rows):
    return sorted(range(1, rows), key=lambda k: -min(k, rows - k))


def nt(left, right):
    return lax.dot_general(left, right, (((1,), (1,)), ((), ())), preferred_element_type=F32)


def nn(left, right):
    return lax.dot_general(left, right, (((1,), (0,)), ((), ())), preferred_element_type=F32)


def tn(left, right):
    return lax.dot_general(left, right, (((0,), (0,)), ((), ())), preferred_element_type=F32)


def side_by_side(v):
    half = v.shape[0] // 2
    return jnp.concatenate([v[:half], v[half:]], axis=1)


def number(shape, axis):
    return lax.broadcasted_iota(jnp.int32, shape, axis)


def route(ids, table, experts, cap):
    tokens = ids.shape[1]
    pick = jnp.where(number((table.shape[0], tokens), 0) == ids >> 7, 1.0, 0.0).astype(BF16)
    found = tn(table, pick)
    expert = jnp.where(number((128, tokens), 0) == ids & 127, found, 0.0)
    expert = jnp.sum(expert, axis=0, keepdims=True)
    hit = number((experts, tokens), 0).astype(F32) == expert
    pair = (tokens, tokens)
    earlier = jnp.where(number(pair, 0) < number(pair, 1), 1.0, 0.0).astype(BF16)
    before = nn(jnp.where(hit, 1.0, 0.0).astype(BF16), earlier)
    slot = jnp.sum(jnp.where(hit, before, 0.0), axis=0, keepdims=True)
    return (expert * cap + slot).astype(jnp.int32)


def all_features(s_ref, i):
    rows = s_ref.shape[0]
    return jnp.concatenate([s_ref[r, i : i + 1, : D // rows] for r in range(rows)], axis=1)


def own_features(s_ref, i):
    rows = s_ref.shape[0]
    per = rows // COLS
    block = s_ref[pl.ds(lax.axis_index("col") * per, per)]
    return jnp.concatenate([block[r, i : i + 1, : D // rows] for r in range(per)], axis=1)


def head_features(s_ref, i, heads):
    rows = s_ref.shape[0]
    size = HD // rows
    cuts = [slice(h * size, (h + 1) * size) for h in range(heads)]
    return jnp.concatenate([s_ref[r, i : i + 1, c] for c in cuts for r in range(rows)], axis=1)


def slots_of(target_ref, row, count):
    base = row * count
    slot = base + lax.broadcasted_iota(jnp.int32, (count, target_ref.shape[1]), 0)
    return jnp.where(slot == target_ref[...], 1.0, 0.0).astype(BF16)


def placed(target_ref, v, row, cap):
    return side_by_side(nn(slots_of(target_ref, row, 2 * cap), v).astype(BF16))


def combined(target_ref, block, row, cap):
    width = block.shape[1] // 2
    stacked = jnp.concatenate([block[:, :width], block[:, width:]], axis=0)
    return tn(slots_of(target_ref, row, 2 * cap), stacked)


def start_kernel(
    rows,
    pieces,
    x_ref,
    g_ref,
    ids_ref,
    table_ref,
    w_ref,
    s_ref,
    xo_ref,
    go_ref,
    wo_ref,
    so_ref,
    t_ref,
    xp_ref,
    gp_ref,
    c_send,
    c_recv,
    r_send,
    r_recv,
    l_send,
    l_recv,
):
    me, sib, across, _ = col_places()
    row, _, level, side, partner = line_places(rows)
    levels = rows // 2
    order = far_first(rows)
    peers = [{"row": (row + k) % rows} for k in order]
    greet(peers + [{"col": sib}, {"col": across}])
    xp_ref[...] = side_by_side(x_ref[...])
    step = xp_ref.shape[0] // pieces
    cap = gp_ref.shape[1]
    to_up, to_down = level < levels - 1, level > 0

    def weight(at, way, src=None):
        dst = wo_ref.at[2 * at + side]
        peer = (row + 2, row - 2, partner)[way]
        return push(
            dst if src is None else src,
            dst,
            l_send.at[way, at],
            l_recv.at[way, at],
            {"row": peer},
        )

    def weight_other(at):
        dst = wo_ref.at[2 * at + 1 - side]
        return push(dst, dst, l_send.at[2, at], l_recv.at[2, at], {"row": partner})

    @pl.when(to_up)
    def _():
        weight(level, 0, w_ref).start()

    @pl.when(to_down)
    def _():
        weight(level, 1, w_ref).start()

    weight(level, 2, w_ref).start()
    sent = []
    for i in range(pieces):
        part = pl.ds(i * step, step)
        for way, peer in ((0, across), (1, sib)):
            copy = push(
                xp_ref.at[part],
                xo_ref.at[me, part],
                c_send.at[way, i],
                c_recv.at[way, i],
                {"col": peer},
            )
            copy.start()
            sent.append(copy)
    row_copies = []
    for k, peer in enumerate(peers):
        copy = push(s_ref, so_ref.at[row], r_send.at[0, k], r_recv.at[0, k], peer)
        copy.start()
        row_copies.append(copy)

    def send_rows(k):
        target = (row + order[k]) % rows
        gp_ref[k] = placed(t_ref, g_ref[...], target, cap)
        copy = push(gp_ref.at[k], go_ref.at[row], r_send.at[1, k], r_recv.at[1, k], peers[k])
        copy.start()
        row_copies.append(copy)

    t_ref[...] = route(ids_ref[...], table_ref[...], EXP_DEV * rows, cap)
    send_rows(0)
    xo_ref[me] = xp_ref[...]
    wo_ref[row] = w_ref[...]
    so_ref[row] = s_ref[...]
    todo = list(range(1, rows - 1))

    def pass_on(k):
        at = level - k

        @pl.when(at >= 0)
        def _():
            weight(at, 0).wait_recv()

            @pl.when(to_up)
            def _():
                weight(at, 0).start()

            weight(at, 2).start()

        up = level + k

        @pl.when(up < levels)
        def _():
            weight(up, 1).wait_recv()

            @pl.when(to_down)
            def _():
                weight(up, 1).start()

            weight(up, 2).start()

    late = []
    for k in range(1, max(levels, pieces + 1)):
        if k < levels:
            pass_on(k)
        if k <= pieces:
            part = pl.ds((k - 1) * step, step)
            sent[2 * k - 2].wait_recv()
            copy = push(
                xo_ref.at[across, part],
                xo_ref.at[across, part],
                c_send.at[2, k - 1],
                c_recv.at[2, k - 1],
                {"col": sib},
            )
            copy.start()
            late.append(copy)
        for _ in range(2):
            if todo:
                send_rows(todo.pop(0))
    while todo:
        send_rows(todo.pop(0))
    go_ref[row] = placed(t_ref, g_ref[...], row, cap)
    for i in range(pieces):
        sent[2 * i].wait_send()
        sent[2 * i + 1].wait()
        late[i].wait()
    for at in range(levels):
        weight_other(at).wait_recv()
        weight(at, 2).wait_send()

        @pl.when((at <= level) & to_up)
        def _(at=at):
            weight(at, 0).wait_send()

        @pl.when((at >= level) & to_down)
        def _(at=at):
            weight(at, 1).wait_send()

    for copy in row_copies:
        copy.wait()


def start_gather(x, g, ids, table, w, s, rows, cap):
    pieces = 4
    tokens, width = x.shape
    packed = (tokens // 2, 2 * width)
    return pl.pallas_call(
        functools.partial(start_kernel, rows, pieces),
        out_shape=(
            jax.ShapeDtypeStruct((COLS,) + packed, x.dtype),
            jax.ShapeDtypeStruct((rows, cap, 2 * width), g.dtype),
            jax.ShapeDtypeStruct((rows,) + w.shape, w.dtype),
            jax.ShapeDtypeStruct((rows,) + s.shape, s.dtype),
            jax.ShapeDtypeStruct((1, tokens), jnp.int32),
        ),
        in_specs=[VSPEC] * 6,
        out_specs=(VSPEC,) * 5,
        scratch_shapes=[
            pltpu.VMEM(packed, x.dtype),
            pltpu.VMEM((rows - 1, cap, 2 * width), g.dtype),
            DMA((3, pieces)),
            DMA((3, pieces)),
            DMA((2, rows - 1)),
            DMA((2, rows - 1)),
            DMA((3, rows // 2)),
            DMA((3, rows // 2)),
        ],
        compiler_params=params(0),
    )(x, g, ids, table, w, s)


def project_kernel(
    x_ref, w_ref, s_ref, q_ref, kv_ref, h_ref, n_ref, r_ref
):
    me = lax.axis_index("col")
    half, width = x_ref.shape[1], x_ref.shape[2] // 2
    gain, shift = all_features(s_ref, 0), all_features(s_ref, 1)
    query = head_features(s_ref, 5, width // HD)
    value = head_features(s_ref, 6, width // HD)
    bias = jnp.concatenate([query, jnp.zeros_like(query), value], axis=1)
    w = w_ref[...].reshape(D, 4 * width)[:, : 3 * width]
    step = min(half, 256)
    for i in range(2 * half // step):
        side, start = i * step // half, i * step % half
        rows, feats = slice(start, start + step), slice(side * width, (side + 1) * width)
        x = jnp.concatenate([x_ref[b, rows, feats] for b in range(COLS)], axis=1).astype(F32)
        mean = jnp.mean(x, axis=-1, keepdims=True)
        centred = x - mean
        rstd = lax.rsqrt(jnp.mean(centred * centred, axis=-1, keepdims=True) + epsilon)
        h = (centred * rstd * gain + shift).astype(BF16)
        out = slice(i * step, (i + 1) * step)
        h_ref[out] = h
        n_ref[out] = (x_ref[me, rows, feats].astype(F32) - mean) * rstd
        r_ref[out] = rstd
        qkv = (nn(h, w) + bias).astype(BF16)
        q_ref[out] = qkv[:, :width] * jnp.asarray(HD**-0.5, BF16)
        kv_ref[out] = qkv[:, width:]


def project(x, w, s):
    tokens, width = 2 * x.shape[1], x.shape[2] // 2
    return pl.pallas_call(
        project_kernel,
        out_shape=(
            jax.ShapeDtypeStruct((tokens, width), BF16),
            jax.ShapeDtypeStruct((tokens, 2 * width), BF16),
            jax.ShapeDtypeStruct((tokens, D), BF16),
            jax.ShapeDtypeStruct((tokens, width), F32),
            jax.ShapeDtypeStruct((tokens, 1), F32),
        ),
        in_specs=[VSPEC] * 3,
        out_specs=(VSPEC,) * 5,
        compiler_params=params(),
    )(x, w, s)


def mid_kernel(
    pieces,
    x_ref,
    w_ref,
    att_ref,
    low_ref,
    do_ref,
    delta_ref,
    gw_ref,
    xp_ref,
    xo_ref,
    wide_ref,
    c_send,
    c_recv,
):
    me, sib, across, _ = col_places()
    greet([{"col": sib}, {"col": across}])
    xp_ref[...] = side_by_side(x_ref[...].astype(BF16))
    step = xp_ref.shape[0] // pieces
    sent, late = [], []
    for i in range(pieces):
        part = pl.ds(i * step, step)
        for way, peer in ((0, across), (1, sib)):
            copy = push(
                xp_ref.at[part],
                xo_ref.at[me, part],
                c_send.at[way, i],
                c_recv.at[way, i],
                {"col": peer},
            )
            copy.start()
            sent.append(copy)
    xo_ref[me] = xp_ref[...]
    tokens, width = x_ref.shape
    w = w_ref[...].reshape(D, 4 * width)[:, 3 * width :]
    for i in range(pieces):
        part = pl.ds(i * step, step)
        sent[2 * i].wait_recv()
        copy = push(
            xo_ref.at[across, part],
            xo_ref.at[across, part],
            c_send.at[2, i],
            c_recv.at[2, i],
            {"col": sib},
        )
        copy.start()
        late.append(copy)
    for i in range(pieces):
        sent[2 * i].wait_send()
        sent[2 * i + 1].wait()
        late[i].wait()
        rows = slice(i * step, (i + 1) * step)
        for half in range(2):
            feats = slice(half * width, (half + 1) * width)
            start = half * (tokens // 2) + i * step
            out = slice(start, start + step)
            wide = jnp.concatenate([xo_ref[b, rows, feats] for b in range(COLS)], axis=1)
            wide_ref[out] = wide
            do = nn(wide, w).astype(BF16)
            do_ref[out] = do
            both = (do.astype(F32) * att_ref[out]).T
            for h in range(width // HD):
                delta_ref[h : h + 1, out] = jnp.sum(
                    both[h * HD : (h + 1) * HD], axis=0, keepdims=True
                )
    gw_ref[...] = tn(wide_ref[...], low_ref[...]).astype(BF16)


def mid_gradient(x, w, attended, low, collective):
    pieces = 4
    tokens, width = x.shape
    packed = (tokens // 2, 2 * width)
    return pl.pallas_call(
        functools.partial(mid_kernel, pieces),
        out_shape=(
            jax.ShapeDtypeStruct((tokens, width), BF16),
            jax.ShapeDtypeStruct((8, tokens), F32),
            jax.ShapeDtypeStruct((D, width), BF16),
        ),
        in_specs=[VSPEC] * 4,
        out_specs=(VSPEC,) * 3,
        scratch_shapes=[
            pltpu.VMEM(packed, BF16),
            pltpu.VMEM((COLS,) + packed, BF16),
            pltpu.VMEM((tokens, D), BF16),
            DMA((3, pieces)),
            DMA((3, pieces)),
        ],
        compiler_params=params(collective),
    )(x, w, attended, low)


def col_peers():
    me = lax.axis_index("col")
    return [{"col": (me + k) % COLS} for k in range(1, COLS)]


def to_rows(columns):
    lane = lax.broadcasted_iota(jnp.int32, (columns[0].shape[0], 128), 1)
    v = jnp.zeros(lane.shape, F32)
    for i, column in enumerate(columns):
        v = jnp.where(lane == i, column, v)
    return v.T[:8]


def to_columns(lines):
    place = lax.broadcasted_iota(jnp.int32, (8, lines[0].shape[1]), 0)
    v = jnp.zeros(place.shape, F32)
    for i, one in enumerate(lines):
        v = jnp.where(place == i, one, v)
    v = v.T
    return [v[:, i : i + 1] for i in range(len(lines))]


def share(snd_ref, all_ref, send, recv):
    me = lax.axis_index("col")
    copies = []
    for k, peer in enumerate(col_peers()):
        copy = push(snd_ref, all_ref.at[me], send.at[k], recv.at[k], peer)
        copy.start()
        copies.append(copy)
    all_ref[me] = snd_ref[...]
    for copy in copies:
        copy.wait()


def norm_back(grad, normed, gain, rstd, snd_ref, all_ref, send, recv):
    tokens = grad.shape[0]
    scaled = grad * gain
    sums = [
        jnp.sum(scaled, axis=-1, keepdims=True),
        jnp.sum(scaled * normed, axis=-1, keepdims=True),
    ]
    snd_ref[:, :tokens] = to_rows(sums)
    share(snd_ref, all_ref, send, recv)
    total = all_ref[0, :, :tokens]
    for b in range(1, COLS):
        total = total + all_ref[b, :, :tokens]
    total = total / D
    first, second = to_columns([total[0:1], total[1:2]])
    return rstd * (scaled - first - normed * second)


def line_greet(levels, row, level, partner):
    barrier = pltpu.get_barrier_semaphore()
    me = lax.axis_index("col")
    for k in range(1, COLS):
        peer = {"col": (me + k) % COLS}
        pl.semaphore_signal(barrier, inc=1, device_id=peer, device_id_type=MESH)
    pl.semaphore_signal(barrier, inc=1, device_id={"row": partner}, device_id_type=MESH)

    @pl.when(level > 0)
    def _():
        pl.semaphore_signal(barrier, inc=1, device_id={"row": row - 2}, device_id_type=MESH)

    @pl.when(level < levels - 1)
    def _():
        pl.semaphore_signal(barrier, inc=1, device_id={"row": row + 2}, device_id_type=MESH)

    count = COLS + (level > 0).astype(jnp.int32) + (level < levels - 1).astype(jnp.int32)
    pl.semaphore_wait(barrier, count)


def seen(key_start, query_start, shape, prefix):
    key = key_start + lax.broadcasted_iota(jnp.int32, shape, 0)
    query = query_start + lax.broadcasted_iota(jnp.int32, shape, 1)
    return (key < prefix) | (key <= query)


def forward_kernel(
    group,
    low,
    pieces,
    qb,
    info_ref,
    q_ref,
    kv_ref,
    g_ref,
    out_ref,
    o_ref,
    ob_ref,
    lse_ref,
    ga_ref,
    m_ref,
    acc_ref,
    u_send,
    u_recv,
    d_send,
    d_recv,
    x_send,
    x_recv,
    g_send,
    g_recv,
):
    levels = group // 2
    row, place, level, side, partner = line_places(group)
    prefix = info_ref[0]
    tokens, width = q_ref.shape
    heads = width // HD
    step = tokens // pieces
    line_greet(levels, row, level, partner)

    def make(at, i, way, src=None):
        part = pl.ds(i * step, step)
        dst = out_ref.at[2 * at + side, part]
        sems = ((u_send, u_recv), (d_send, d_recv), (x_send, x_recv))[way]
        peer = (row + 2, row - 2, partner)[way]
        return push(
            dst if src is None else src.at[part],
            dst,
            sems[0].at[at, i],
            sems[1].at[at, i],
            {"row": peer},
        )

    def other(at, i):
        part = pl.ds(i * step, step)
        dst = out_ref.at[2 * at + 1 - side, part]
        return push(dst, dst, x_send.at[at, i], x_recv.at[at, i], {"row": partner})

    def when(cond, run):
        @pl.when(cond)
        def _():
            for i in range(pieces):
                run(i)

    to_up = level < levels - 1
    own_down = (level > 0) & (level < low)
    own_side = (level < low) | (side == 0)
    for i in range(pieces):

        @pl.when(to_up)
        def _(i=i):
            make(level, i, 0, kv_ref).start()

        @pl.when(own_side)
        def _(i=i):
            make(level, i, 2, kv_ref).start()

        @pl.when(own_down)
        def _(i=i):
            make(level, i, 1, kv_ref).start()

    me = lax.axis_index("col")
    wide = []
    for k in range(1, COLS):
        peer = {"col": (me + k) % COLS}
        copy = push(g_ref, ga_ref.at[me], g_send.at[k - 1], g_recv.at[k - 1], peer)
        copy.start()
        wide.append(copy)
    ga_ref[me] = g_ref[...]
    out_ref[place] = kv_ref[...]
    m_ref[...] = jnp.full(m_ref.shape, neg_big, F32)
    acc_ref[...] = jnp.zeros(acc_ref.shape, F32)
    units = [(h, i) for h in range(heads) for i in range(tokens // qb)]

    def block(blk, masked):
        def raw_of(h, i):
            feats = slice(h * HD, (h + 1) * HD)
            raw = nt(out_ref[blk, :, feats], q_ref[i * qb : (i + 1) * qb, feats])
            if masked:
                allowed = seen(blk * tokens, place * tokens + i * qb, raw.shape, prefix)
                raw = jnp.where(allowed, raw, neg_big)
            return raw

        def soften(h, i, raw):
            cols = slice(i * qb, (i + 1) * qb)
            old = m_ref[h : h + 1, cols]
            new = jnp.maximum(old, jnp.max(raw, axis=0, keepdims=True))
            m_ref[h : h + 1, cols] = new
            weights = jnp.exp2((raw - new) * LOG2E).astype(BF16)
            return weights, jnp.exp2((old - new) * LOG2E)

        def gather(h, i, weights, scale):
            cols = slice(i * qb, (i + 1) * qb)
            v = out_ref[blk, :, width + h * HD : width + (h + 1) * HD]
            v_ext = jnp.concatenate([v.T, jnp.ones((16, tokens), BF16)], axis=0)
            acc_ref[h, :, cols] = acc_ref[h, :, cols] * scale + nn(v_ext, weights)

        coming, waiting = raw_of(*units[0]), None
        for n, unit in enumerate(units):
            raw = coming
            if n + 1 < len(units):
                coming = raw_of(*units[n + 1])
            soft = soften(*unit, raw)
            if waiting is not None:
                gather(*waiting)
            waiting = unit + soft
        gather(*waiting)

    def event(e, carry):
        t, cross = e // 2, e % 2
        at = jnp.where(t <= level, level - t, t)
        live = (t <= level) | (t < low)
        line_in = live & (cross == 0)
        coming = t + 1
        via = jnp.where(coming <= level, level - coming, coming)
        relays = (cross == 1) & ((coming <= level) | (coming < low))

        @pl.when(relays & (via < level))
        def _():
            for i in range(pieces):
                make(via, i, 0).wait_recv()

                @pl.when(to_up)
                def _(i=i):
                    make(via, i, 0).start()

                make(via, i, 2).start()

        @pl.when(relays & (via > level))
        def _():
            for i in range(pieces):
                make(via, i, 1).wait_recv()

                @pl.when(level > 0)
                def _(i=i):
                    make(via, i, 1).start()

                make(via, i, 2).start()

        comes = live & (cross == 1) & ((at < low) | (at < level) | (side == 1))
        when(comes, lambda i: other(at, i).wait_recv())
        blk = 2 * at + jnp.where(cross == 0, side, 1 - side)
        needed = line_in | comes

        @pl.when(needed & (blk < place))
        def _():
            block(blk, False)

        @pl.when(needed & (blk >= place))
        def _():
            block(blk, True)

        return carry

    lax.fori_loop(0, 2 * levels, event, 0)

    for h in range(heads):
        total = acc_ref[h, HD : HD + 1, :]
        out = (acc_ref[h, :HD, :] / total).T
        o_ref[:, h * HD : (h + 1) * HD] = out
        ob_ref[:, h * HD : (h + 1) * HD] = out.astype(BF16)
        lse_ref[h : h + 1, :] = m_ref[h : h + 1, :] * LOG2E + jnp.log2(total)

    when(to_up, lambda i: make(level, i, 0, kv_ref).wait_send())
    when(own_side, lambda i: make(level, i, 2, kv_ref).wait_send())
    when(own_down, lambda i: make(level, i, 1, kv_ref).wait_send())
    for k in range(1, levels):
        at = level - k
        when((at >= 0) & to_up, lambda i, at=at: make(at, i, 0).wait_send())
        when(at >= 0, lambda i, at=at: make(at, i, 2).wait_send())
    for k in range(1, low):
        at = level + k
        when((at < low) & (level > 0), lambda i, at=at: make(at, i, 1).wait_send())
        when(at < low, lambda i, at=at: make(at, i, 2).wait_send())
    for copy in wide:
        copy.wait()


def attention_forward(info, q, kv, g, group, low, collective):
    pieces = 4
    levels = group // 2
    tokens, width = q.shape
    heads = width // HD
    return pl.pallas_call(
        functools.partial(forward_kernel, group, low, pieces, tokens // 2),
        out_shape=(
            jax.ShapeDtypeStruct((group,) + kv.shape, kv.dtype),
            jax.ShapeDtypeStruct((tokens, width), F32),
            jax.ShapeDtypeStruct((tokens, width), BF16),
            jax.ShapeDtypeStruct((8, tokens), F32),
            jax.ShapeDtypeStruct((COLS,) + g.shape, g.dtype),
        ),
        in_specs=[SSPEC, VSPEC, VSPEC, VSPEC],
        out_specs=(VSPEC,) * 5,
        scratch_shapes=[
            pltpu.VMEM((8, tokens), F32),
            pltpu.VMEM((heads, HD + 16, tokens), F32),
        ]
        + [DMA((levels, pieces))] * 6
        + [DMA((COLS - 1,))] * 2,
        compiler_params=params(collective),
    )(info, q, kv, g)


def backward_kernel(
    group,
    low,
    pieces,
    kb,
    info_ref,
    q_ref,
    kv_ref,
    do_ref,
    lse_ref,
    delta_ref,
    e_ref,
    bias_ref,
    out_ref,
    eo_ref,
    part_ref,
    rx_ref,
    above_ref,
    below_ref,
    snd_ref,
    acc_ref,
    dqt_ref,
    er_ref,
    u_send,
    u_recv,
    d_send,
    d_recv,
    x_send,
    x_recv,
    e_send,
    e_recv,
):
    levels = group // 2
    row, place, level, side, partner = line_places(group)
    prefix = info_ref[0]
    tokens, width = q_ref.shape
    heads = width // HD
    step = tokens // pieces
    line_greet(levels, row, level, partner)
    me = lax.axis_index("col")
    terms = []
    for k in range(1, COLS):
        peer = (me + k) % COLS
        copy = push(
            e_ref.at[peer], er_ref.at[k - 1], e_send.at[k - 1], e_recv.at[k - 1], {"col": peer}
        )
        copy.start()
        terms.append(copy)
    dqt_ref[...] = jnp.zeros(dqt_ref.shape, F32)

    def block(blk, masked):
        def body(j, carry):
            start = pl.multiple_of(j * kb, kb)
            keys = pl.ds(start, kb)
            for h in range(heads):
                feats = slice(h * HD, (h + 1) * HD)
                vals = slice(width + h * HD, width + (h + 1) * HD)
                k, v = kv_ref[blk, keys, feats], kv_ref[blk, keys, vals]
                q, do = q_ref[:, feats], do_ref[:, feats]
                probs = jnp.exp2(nt(k, q) * LOG2E - lse_ref[h : h + 1, :])
                if masked:
                    allowed = seen(blk * tokens + start, place * tokens, probs.shape, prefix)
                    probs = jnp.where(allowed, probs, 0.0)
                grad = (probs * (nt(v, do) - delta_ref[h : h + 1, :])).astype(BF16)
                part_ref[blk, keys, feats] = nn(grad, q).astype(BF16)
                part_ref[blk, keys, vals] = nn(probs.astype(BF16), do).astype(BF16)
                dqt_ref[feats, :] += nn(k.T, grad)
            return carry

        lax.fori_loop(0, tokens // kb, body, 0)

    def cross(at, i):
        part = pl.ds(i * step, step)
        return push(
            part_ref.at[2 * at + 1 - side, part],
            rx_ref.at[at, part],
            x_send.at[at, i],
            x_recv.at[at, i],
            {"row": partner},
        )

    def line(at, i, up):
        part = pl.ds(i * step, step)
        sems = (u_send, u_recv) if up else (d_send, d_recv)
        return push(
            snd_ref.at[at, part],
            (below_ref if up else above_ref).at[at, part],
            sems[0].at[at, i],
            sems[1].at[at, i],
            {"row": row + 2 if up else row - 2},
        )

    def gone(at):
        return (at < low) | (at < level) | ((at == level) & (side == 1))

    def comes(at):
        return (at < low) | (at < level) | ((at == level) & (side == 0))

    def total(at, i, from_above, from_below):
        part = pl.ds(i * step, step)
        acc_ref[...] = part_ref[2 * at + side, part].astype(F32)

        @pl.when(comes(at))
        def _():
            cross(at, i).wait_recv()
            acc_ref[...] += rx_ref[at, part].astype(F32)

        if from_above is not None:

            @pl.when(from_above)
            def _():
                line(at, i, False).wait_recv()
                acc_ref[...] += above_ref[at, part].astype(F32)

        if from_below is not None:

            @pl.when(from_below)
            def _():
                line(at, i, True).wait_recv()
                acc_ref[...] += below_ref[at, part].astype(F32)

    not_top = level < levels - 1
    above = jnp.maximum(low - 1 - level, 0)

    def level_of(t):
        return jnp.where(t < above, low - 1 - t, t - above)

    def event(e, carry):
        t, own = e // 2, e % 2
        at = level_of(t)
        live = (t < above) | (at <= level)

        down = t - (levels - level)

        @pl.when((own == 1) & (down >= 0) & (down < level))
        def _():
            for i in range(pieces):
                total(down, i, not_top, None)
                snd_ref[down, pl.ds(i * step, step)] = acc_ref[...].astype(BF16)
                line(down, i, False).start()

        @pl.when((own == 1) & (t >= 1) & (t - 1 < above))
        def _():
            up = level_of(t - 1)
            for i in range(pieces):
                total(up, i, None, level > 0)
                snd_ref[up, pl.ds(i * step, step)] = acc_ref[...].astype(BF16)
                line(up, i, True).start()

        goes = live & (own == 0) & gone(at)
        blk = 2 * at + jnp.where(own == 1, side, 1 - side)
        needed = goes | (live & (own == 1))

        @pl.when(needed & (blk < place))
        def _():
            block(blk, False)

        @pl.when(needed & (blk >= place))
        def _():
            block(blk, True)

        @pl.when(goes)
        def _():
            for i in range(pieces):
                cross(at, i).start()

        return carry

    lax.fori_loop(0, 2 * levels, event, 0)
    for copy in terms:
        copy.wait()

    def finish(r, carry):
        total = e_ref[me, r].astype(F32) + bias_ref[...]
        for k in range(COLS - 1):
            total = total + er_ref[k, r].astype(F32)
        eo_ref[r] = total.astype(BF16)
        return carry

    lax.fori_loop(0, e_ref.shape[1], finish, 0)
    out_ref[:, :width] = (dqt_ref[...] * HD**-0.5).T.astype(BF16)

    for i in range(pieces):
        total(level, i, not_top, (level > 0) & (level < low))
        out_ref[pl.ds(i * step, step), width:] = acc_ref[...].astype(BF16)

    for at in range(levels):
        for i in range(pieces):

            @pl.when(gone(at))
            def _(at=at, i=i):
                cross(at, i).wait_send()

            @pl.when(at < level)
            def _(at=at, i=i):
                line(at, i, False).wait_send()

            if at < low:

                @pl.when(at > level)
                def _(at=at, i=i):
                    line(at, i, True).wait_send()


def attention_backward(info, q, kv_all, do, lse, delta, e, bias, group, low, collective):
    pieces = 4
    levels = group // 2
    tokens, width = q.shape
    both = 2 * width
    block = pltpu.VMEM((levels, tokens, both), BF16)
    return pl.pallas_call(
        functools.partial(backward_kernel, group, low, pieces, tokens // 2),
        out_shape=(
            jax.ShapeDtypeStruct((tokens, width + both), BF16),
            jax.ShapeDtypeStruct(e.shape[1:], BF16),
        ),
        in_specs=[SSPEC] + [VSPEC] * 7,
        out_specs=(VSPEC,) * 2,
        scratch_shapes=[
            pltpu.VMEM(kv_all.shape, BF16),
            block,
            block,
            pltpu.VMEM((low, tokens, both), BF16),
            block,
            pltpu.VMEM((tokens // pieces, both), F32),
            pltpu.VMEM((width, tokens), F32),
            pltpu.VMEM((COLS - 1,) + e.shape[1:], BF16),
        ]
        + [DMA((levels, pieces))] * 6
        + [DMA((COLS - 1,))] * 2,
        compiler_params=params(collective),
    )(info, q, kv_all, do, lse, delta, e, bias)


def product(pieces, a_ref, w_ref, feats, out_ref, snd_ref, rx_ref, far_ref, tot_ref, sems, fill):
    send, recv = sems
    me, sib, across, diag = col_places()
    half = a_ref.shape[0] // 2
    step = half // pieces
    per = w_ref.shape[0] // COLS
    width = out_ref.shape[1]

    def weight(who):
        return w_ref[pl.ds(who * per, per)].reshape(width, 4 * width)[:, feats]

    def term(i, w):
        parts = [nt(a_ref[pl.ds(n * half + i * step, step)], w) for n in range(2)]
        return jnp.concatenate(parts, axis=1)

    def near(i, j):
        part = pl.ds(i * step, step)
        return push(
            snd_ref.at[j, part], rx_ref.at[j, part], send.at[j, i], recv.at[j, i], {"col": sib}
        )

    def over(i):
        part = pl.ds(i * step, step)
        return push(tot_ref.at[part], far_ref.at[part], send.at[2, i], recv.at[2, i], {"col": across})

    w = weight(diag)
    for i in range(pieces):
        snd_ref[0, pl.ds(i * step, step)] = term(i, w).astype(BF16)
        near(i, 0).start()
    w = weight(across)
    for i in range(pieces):
        part = pl.ds(i * step, step)
        mine = term(i, w)
        near(i, 0).wait_recv()
        tot_ref[part] = (mine + rx_ref[0, part].astype(F32)).astype(BF16)
        over(i).start()
    w = weight(sib)
    for i in range(pieces):
        snd_ref[1, pl.ds(i * step, step)] = term(i, w).astype(BF16)
        near(i, 1).start()
    fill()
    w = weight(me)
    for i in range(pieces):
        part = pl.ds(i * step, step)
        mine = term(i, w)
        near(i, 1).wait_recv()
        mine = mine + rx_ref[1, part].astype(F32)
        over(i).wait_recv()
        mine = mine + far_ref[part].astype(F32)
        out_ref[part] = mine[:, :width]
        out_ref[pl.ds(half + i * step, step)] = mine[:, width:]
    for i in range(pieces):
        near(i, 0).wait_send()
        near(i, 1).wait_send()
        over(i).wait_send()


def product_scratch(pieces, tokens, width):
    block = pltpu.VMEM((tokens // 2, 2 * width), BF16)
    pair = pltpu.VMEM((2, tokens // 2, 2 * width), BF16)
    return [pair, pair, block, block, DMA((3, pieces)), DMA((3, pieces))]


def branch_kernel(
    pieces,
    a_ref,
    w_ref,
    x_ref,
    s_ref,
    mid_ref,
    normed_ref,
    rstd_ref,
    h_ref,
    snd_ref,
    rx_ref,
    far_ref,
    tot_ref,
    send,
    recv,
    st_ref,
    all_ref,
    st_send,
    st_recv,
):
    greet(col_peers())
    tokens, width = x_ref.shape
    product(
        pieces,
        a_ref,
        w_ref,
        slice(3 * width, 4 * width),
        mid_ref,
        snd_ref,
        rx_ref,
        far_ref,
        tot_ref,
        (send, recv),
        lambda: None,
    )
    mid = x_ref[...].astype(F32) + mid_ref[...] + own_features(s_ref, 4)
    mid_ref[...] = mid
    part_mean = jnp.mean(mid, axis=-1, keepdims=True)
    part_spread = jnp.sum((mid - part_mean) ** 2, axis=-1, keepdims=True)
    st_ref[...] = to_rows([part_mean, part_spread])
    share(st_ref, all_ref, st_send, st_recv)
    mean = sum(all_ref[b, 0:1] for b in range(COLS)) / COLS
    spread = sum(
        all_ref[b, 1:2] + width * (all_ref[b, 0:1] - mean) ** 2 for b in range(COLS)
    )
    mean, rstd = to_columns([mean, lax.rsqrt(spread / D + epsilon)])
    normed = (mid - mean) * rstd
    normed_ref[...] = normed
    rstd_ref[...] = rstd
    h_ref[...] = (normed * own_features(s_ref, 2) + own_features(s_ref, 3)).astype(BF16)


def branch(a, w, x, s, collective):
    pieces = 4
    tokens, width = a.shape
    rows = jax.ShapeDtypeStruct((tokens, width), F32)
    return pl.pallas_call(
        functools.partial(branch_kernel, pieces),
        out_shape=(
            rows,
            rows,
            jax.ShapeDtypeStruct((tokens, 1), F32),
            jax.ShapeDtypeStruct((tokens, width), BF16),
        ),
        in_specs=[VSPEC] * 4,
        out_specs=(VSPEC,) * 4,
        scratch_shapes=product_scratch(pieces, tokens, width)
        + [
            pltpu.VMEM((8, tokens), F32),
            pltpu.VMEM((COLS, 8, tokens), F32),
            DMA((COLS - 1,)),
            DMA((COLS - 1,)),
        ],
        compiler_params=params(collective),
    )(a, w, x, s)


def input_kernel(
    pieces,
    a_ref,
    w_ref,
    e_ref,
    h_ref,
    gwo_ref,
    mid_ref,
    normed_ref,
    rstd_ref,
    s_ref,
    vec_ref,
    gin_ref,
    eo_ref,
    wt_ref,
    all_ref,
    grad_ref,
    snd_ref,
    rx_ref,
    far_ref,
    tot_ref,
    send,
    recv,
    st_ref,
    st_send,
    st_recv,
    e_send,
    e_recv,
):
    rows = e_ref.shape[0]
    row = lax.axis_index("row")
    order = far_first(rows)
    greet([{"row": (row + k) % rows} for k in order] + col_peers())
    home = []
    for n, k in enumerate(order):
        peer = (row + k) % rows
        copy = push(e_ref.at[peer], eo_ref.at[row], e_send.at[n], e_recv.at[n], {"row": peer})
        copy.start()
        home.append(copy)
    eo_ref[row] = e_ref[row]
    tokens, width = grad_ref.shape

    def fill():
        both = [tn(h_ref[...], a_ref[...]).astype(BF16), gwo_ref[...]]
        wt_ref[...] = jnp.concatenate(both, axis=1)

    product(
        pieces,
        a_ref,
        w_ref,
        slice(0, 3 * width),
        grad_ref,
        snd_ref,
        rx_ref,
        far_ref,
        tot_ref,
        (send, recv),
        fill,
    )
    grad, normed = grad_ref[...], normed_ref[...]
    st_ref[:, tokens:] = jnp.zeros((8, st_ref.shape[1] - tokens), F32)
    st_ref[0:1, tokens : tokens + width] = jnp.sum(grad * normed, axis=0, keepdims=True)
    st_ref[1:2, tokens : tokens + width] = jnp.sum(grad, axis=0, keepdims=True)
    st_ref[2:5, tokens : tokens + width] = vec_ref[0:3]
    gin_ref[...] = mid_ref[...] + norm_back(
        grad, normed, own_features(s_ref, 0), rstd_ref[...], st_ref, all_ref, st_send, st_recv
    )
    for copy in home:
        copy.wait()


def input_gradient(a, w, e, h, gwo, mid, normed, rstd, gain, vec, collective):
    pieces = 4
    tokens, width = mid.shape
    wide = tokens + 256
    return pl.pallas_call(
        functools.partial(input_kernel, pieces),
        out_shape=(
            jax.ShapeDtypeStruct((tokens, width), F32),
            jax.ShapeDtypeStruct(e.shape, BF16),
            jax.ShapeDtypeStruct((D, 4 * width), BF16),
            jax.ShapeDtypeStruct((COLS, 8, wide), F32),
        ),
        in_specs=[VSPEC] * 10,
        out_specs=(VSPEC,) * 4,
        scratch_shapes=[pltpu.VMEM((tokens, width), F32)]
        + product_scratch(pieces, tokens, width)
        + [
            pltpu.VMEM((8, wide), F32),
            DMA((COLS - 1,)),
            DMA((COLS - 1,)),
            DMA((e.shape[0] - 1,)),
            DMA((e.shape[0] - 1,)),
        ],
        compiler_params=params(collective),
    )(a, w, e, h, gwo, mid, normed, rstd, gain, vec)


def dispatch_kernel(rows, x_ref, t_ref, out_ref, in_ref, r_send, r_recv, c_send, c_recv):
    me, sib, across, _ = col_places()
    row = lax.axis_index("row")
    order = far_first(rows)
    peers = [(row + k) % rows for k in order]
    greet([{"row": p} for p in peers] + [{"col": sib}, {"col": across}])
    copies = []
    cap = in_ref.shape[1]
    for k, peer in enumerate(peers):
        in_ref[peer] = placed(t_ref, x_ref[...], peer, cap)
        copy = push(
            in_ref.at[peer], out_ref.at[me, row], r_send.at[k], r_recv.at[k], {"row": peer}
        )
        copy.start()
        copies.append(copy)
    in_ref[row] = placed(t_ref, x_ref[...], row, cap)

    def col(src, dst, k, way):
        return push(
            src, dst, c_send.at[way, k], c_recv.at[way, k], {"col": across if way == 0 else sib}
        )

    done, first = [], []
    for way in range(2):
        copy = col(in_ref.at[row], out_ref.at[me, row], 0, way)
        copy.start()
        (first if way == 0 else done).append(copy)
    out_ref[me, row] = in_ref[row]
    sources = [row] + [(row + rows - k) % rows for k in order]

    def forward(k):
        first[k].wait_recv()
        src = sources[k]
        copy = col(out_ref.at[across, src], out_ref.at[across, src], k, 2)
        copy.start()
        done.append(copy)

    for k in range(1, rows):
        copies[k - 1].wait_recv()
        block = out_ref.at[me, sources[k]]
        for way in range(2):
            copy = col(block, block, k, way)
            copy.start()
            (first if way == 0 else done).append(copy)
        forward(k - 1)
    forward(rows - 1)
    for copy in copies:
        copy.wait_send()
    for copy in first:
        copy.wait_send()
    for copy in done:
        copy.wait()


def dispatch(x, target, rows, cap, collective):
    block = (rows, cap, 2 * x.shape[1])
    return pl.pallas_call(
        functools.partial(dispatch_kernel, rows),
        out_shape=jax.ShapeDtypeStruct((COLS,) + block, x.dtype),
        in_specs=[VSPEC] * 2,
        out_specs=VSPEC,
        scratch_shapes=[
            pltpu.VMEM(block, x.dtype),
            DMA((rows - 1,)),
            DMA((rows - 1,)),
            DMA((3, rows)),
            DMA((3, rows)),
        ],
        compiler_params=params(collective),
    )(x, target)


def giveback_kernel(
    rows,
    in_ref,
    t_ref,
    cot_ref,
    normed_ref,
    rstd_ref,
    s_ref,
    mid_ref,
    vec_ref,
    sum_ref,
    out_ref,
    rx_ref,
    far_ref,
    tot_ref,
    fin_ref,
    st_ref,
    all_ref,
    send,
    recv,
    r_send,
    r_recv,
    st_send,
    st_recv,
):
    me, sib, across, diag = col_places()
    row = lax.axis_index("row")
    order = [(row + k) % rows for k in far_first(rows)] + [row]
    greet([{"row": p} for p in order[:-1]] + col_peers())

    def near(k, j):
        who = diag if j == 0 else sib
        return push(
            in_ref.at[who, order[k]], rx_ref.at[j, k], send.at[j, k], recv.at[j, k], {"col": sib}
        )

    def over(k):
        return push(tot_ref.at[k], far_ref.at[k], send.at[2, k], recv.at[2, k], {"col": across})

    def home(k):
        return push(
            fin_ref.at[k], out_ref.at[row], r_send.at[k], r_recv.at[k], {"row": order[k]}
        )

    for k in range(rows):
        near(k, 0).start()
        near(k, 1).start()

    def finish(k):
        near(k, 1).wait_recv()
        over(k).wait_recv()
        total = in_ref[me, order[k]].astype(F32) + rx_ref[1, k].astype(F32)
        total = total + far_ref[k].astype(F32)
        if k == rows - 1:
            out_ref[row] = total.astype(BF16)
        else:
            fin_ref[k] = total.astype(BF16)
            home(k).start()

    for k in range(rows):
        near(k, 0).wait_recv()
        tot_ref[k] = (in_ref[across, order[k]].astype(F32) + rx_ref[0, k].astype(F32)).astype(BF16)
        over(k).start()
        if k >= 1:
            finish(k - 1)
    finish(rows - 1)
    cap = out_ref.shape[1]
    sum_ref[...] = combined(t_ref, out_ref[row], row, cap)
    for k, gap in enumerate(far_first(rows)):
        source = (row + rows - gap) % rows
        home(k).wait_recv()
        sum_ref[...] += combined(t_ref, out_ref[source], source, cap)
    grad, normed = sum_ref[...], normed_ref[...]
    mid = cot_ref[...].astype(F32) + norm_back(
        grad, normed, own_features(s_ref, 2), rstd_ref[...], st_ref, all_ref, st_send, st_recv
    )
    mid_ref[...] = mid
    vec_ref[...] = jnp.zeros(vec_ref.shape, F32)
    vec_ref[0:1] = jnp.sum(grad * normed, axis=0, keepdims=True)
    vec_ref[1:2] = jnp.sum(grad, axis=0, keepdims=True)
    vec_ref[2:3] = jnp.sum(mid, axis=0, keepdims=True)
    for k in range(rows):
        near(k, 0).wait_send()
        near(k, 1).wait_send()
        over(k).wait_send()
        if k < rows - 1:
            home(k).wait_send()


def giveback(parts, target, cot, normed, rstd, gain, rows, collective):
    block = parts.shape[2:]
    one = pltpu.VMEM((rows,) + block, BF16)
    return pl.pallas_call(
        functools.partial(giveback_kernel, rows),
        out_shape=(
            jax.ShapeDtypeStruct(cot.shape, F32),
            jax.ShapeDtypeStruct((8, cot.shape[1]), F32),
        ),
        in_specs=[VSPEC] * 6,
        out_specs=(VSPEC,) * 2,
        scratch_shapes=[
            pltpu.VMEM(cot.shape, F32),
            one,
            pltpu.VMEM((2, rows) + block, BF16),
            one,
            one,
            one,
            pltpu.VMEM((8, cot.shape[0]), F32),
            pltpu.VMEM((COLS, 8, cot.shape[0]), F32),
            DMA((3, rows)),
            DMA((3, rows)),
            DMA((rows - 1,)),
            DMA((rows - 1,)),
            DMA((COLS - 1,)),
            DMA((COLS - 1,)),
        ],
        compiler_params=params(collective),
    )(parts, target, cot, normed, rstd, gain)


def end_kernel(
    rows,
    w_ref,
    s_ref,
    e_ref,
    t_ref,
    mid_ref,
    wo_ref,
    so_ref,
    lo_ref,
    px_ref,
    pt_ref,
    wr_ref,
    sr_ref,
    p_send,
    p_recv,
    l_send,
    l_recv,
    send,
    recv,
):
    row, _, level, side, partner = line_places(rows)
    levels = rows // 2
    peers = [(row + k) % rows for k in far_first(rows)]
    greet([{"row": p} for p in peers])
    gaps = far_first(levels)
    targets = [(level + k) % levels for k in gaps] + [level]

    def cross(n):
        src = w_ref.at[2 * targets[n] + 1 - side]
        return push(src, px_ref.at[n], p_send.at[n], p_recv.at[n], {"row": partner})

    def along(n):
        peer = {"row": 2 * targets[n] + side}
        return push(pt_ref.at[n], wr_ref.at[n], l_send.at[n], l_recv.at[n], peer)

    def total(n):
        return w_ref[2 * targets[n] + side].astype(F32) + px_ref[n].astype(F32)

    for n in range(levels):
        cross(n).start()
    copies = []
    for k, peer in enumerate(peers):
        copy = push(s_ref.at[peer], sr_ref.at[k], send.at[k], recv.at[k], {"row": peer})
        copy.start()
        copies.append(copy)
    for n in range(levels - 1):
        cross(n).wait_recv()
        pt_ref[n] = total(n).astype(BF16)
        along(n).start()
    result = mid_ref[...]
    for r in range(rows):
        result = result + combined(t_ref, e_ref[r], r, e_ref.shape[1])
    lo_ref[...] = result.astype(BF16)
    small = s_ref[row]
    for k, copy in enumerate(copies):
        copy.wait_recv()
        small = small + sr_ref[k]
    so_ref[...] = small
    cross(levels - 1).wait_recv()
    mine = total(levels - 1)
    for n in range(levels - 1):
        along(n).wait_recv()
        mine = mine + wr_ref[n].astype(F32)
    wo_ref[...] = mine
    for n in range(levels):
        cross(n).wait_send()
        if n < levels - 1:
            along(n).wait_send()
    for copy in copies:
        copy.wait_send()


def end_scatter(w, s, outs, target, mid, rows, collective):
    levels = rows // 2
    one = w.shape[1:]
    return pl.pallas_call(
        functools.partial(end_kernel, rows),
        out_shape=(
            jax.ShapeDtypeStruct(one, F32),
            jax.ShapeDtypeStruct(s.shape[1:], F32),
            jax.ShapeDtypeStruct(mid.shape, BF16),
        ),
        in_specs=[VSPEC] * 5,
        out_specs=(VSPEC,) * 3,
        scratch_shapes=[
            pltpu.VMEM((levels,) + one, w.dtype),
            pltpu.VMEM((levels - 1,) + one, w.dtype),
            pltpu.VMEM((levels - 1,) + one, w.dtype),
            pltpu.VMEM((rows - 1,) + s.shape[1:], s.dtype),
            DMA((levels,)),
            DMA((levels,)),
            DMA((levels - 1,)),
            DMA((levels - 1,)),
            DMA((rows - 1,)),
            DMA((rows - 1,)),
        ],
        compiler_params=params(collective),
    )(w, s, outs, target, mid)


def expert_kernel(
    x_ref,
    g_ref,
    up_ref,
    bias_ref,
    down_ref,
    part_ref,
    gx_ref,
    gup_ref,
    gbu_ref,
    gdown_ref,
    gbd_ref,
):
    cols, rows, cap, both = x_ref.shape
    width = both // 2
    slots = rows * cap
    first = pl.program_id(0) == 0

    def mine(ref):
        blocks = [ref[b].reshape(slots, both) for b in range(cols)]
        blocks = [jnp.where(first, v[:, :width], v[:, width:]) for v in blocks]
        return jnp.concatenate(blocks, axis=1)

    x, g = mine(x_ref), mine(g_ref)
    gbd_ref[...] = jnp.sum(g.astype(F32), axis=0).reshape(gbd_ref.shape)
    hidden_units = up_ref.shape[2]
    chunk = 256
    part = jnp.zeros((slots, cols * width), F32)
    gx = jnp.zeros((slots, cols * width), F32)
    for f in range(hidden_units // chunk):
        cut = slice(f * chunk, (f + 1) * chunk)
        up, down = up_ref[0, :, cut], down_ref[0, cut, :]
        pre = nn(x, up) + bias_ref[0, :, cut].astype(F32)
        cdf = 0.5 * (1.0 + lax.erf(pre * (0.5**0.5)))
        slope = cdf + pre * (jnp.exp(-0.5 * pre * pre) * 0.3989422804014327)
        hidden = (pre * cdf).astype(BF16)
        grad = nt(g, down) * slope
        grad = grad.astype(BF16)
        part = part + nn(hidden, down)
        gx = gx + nt(grad, up)
        gdown_ref[0, cut, :] = tn(hidden, g)
        gup_ref[0, :, cut] = tn(x, grad)
        gbu_ref[0, :, cut] = jnp.sum(grad.astype(F32), axis=0, keepdims=True)
    for e in range(EXP_DEV):

        @pl.when(pl.program_id(0) == e)
        def _(e=e):
            lanes = slice(e * width, (e + 1) * width)
            for b in range(cols):
                cut = slice(b * width, (b + 1) * width)
                part_ref[b, :, :, lanes] = part[:, cut].astype(BF16).reshape(rows, cap, width)
                gx_ref[b, :, :, lanes] = gx[:, cut].astype(BF16).reshape(rows, cap, width)


def experts(x, g, w_up, bias_up, w_down):
    slots = pl.BlockSpec(x.shape, lambda e: (0, 0, 0, 0))
    count, features, hidden = w_up.shape
    return pl.pallas_call(
        expert_kernel,
        grid=(count,),
        out_shape=(
            jax.ShapeDtypeStruct(x.shape, BF16),
            jax.ShapeDtypeStruct(x.shape, BF16),
            jax.ShapeDtypeStruct(w_up.shape, F32),
            jax.ShapeDtypeStruct((count, 1, hidden), F32),
            jax.ShapeDtypeStruct(w_down.shape, F32),
            jax.ShapeDtypeStruct((count, 1, features), F32),
        ),
        in_specs=[
            slots,
            slots,
            pl.BlockSpec((1, features, hidden), lambda e: (e, 0, 0)),
            pl.BlockSpec((1, 1, hidden), lambda e: (e, 0, 0)),
            pl.BlockSpec((1, hidden, features), lambda e: (e, 0, 0)),
        ],
        out_specs=(
            slots,
            slots,
            pl.BlockSpec((1, features, hidden), lambda e: (e, 0, 0)),
            pl.BlockSpec((1, 1, hidden), lambda e: (e, 0, 0)),
            pl.BlockSpec((1, hidden, features), lambda e: (e, 0, 0)),
            pl.BlockSpec((1, 1, features), lambda e: (e, 0, 0)),
        ),
        compiler_params=params(),
    )(x, g, w_up, bias_up.reshape(count, 1, hidden), w_down)


def per_device(
    layer_in,
    cotangent,
    token_ids,
    hash_table,
    prefix_len,
    w_query,
    w_key,
    w_value,
    w_output,
    bias_query,
    bias_value,
    gain_attn,
    shift_attn,
    gain_moe,
    shift_moe,
    bias_output,
    w_up,
    bias_up,
    w_down,
    bias_down,
):
    rows = lax.axis_size("row")
    row = lax.axis_index("row")
    col = lax.axis_index("col")
    tokens, width = layer_in.shape
    heads = width // HD
    seq_len = min(LENGTH, tokens * rows)
    group = seq_len // tokens
    low = -(-PREFIX_MAX // (2 * tokens))
    share = w_query.shape[0]
    bias_share = bias_query.shape[0]

    def line(v):
        return jnp.pad(v.astype(F32), (0, 128 - v.shape[0]))

    small = jnp.stack(
        [
            line(gain_attn),
            line(shift_attn),
            line(gain_moe),
            line(shift_moe),
            line(bias_output),
            line(bias_query.T.reshape(-1)),
            line(bias_value.T.reshape(-1)),
            jnp.zeros((128,), F32),
        ]
    )
    expert_total = EXP_DEV * rows
    capacity = max(2, 2 * tokens // expert_total)
    table = jnp.pad(hash_table, (0, -hash_table.shape[0] % (128 * 128)))
    table = table.reshape(-1, 128).astype(BF16)

    weights = jnp.concatenate([w_query, w_key, w_value, w_output], axis=1)
    x_all, g_own, w_all, s_all, target = start_gather(
        layer_in, cotangent, token_ids[None], table, weights, small, rows, capacity
    )

    queries, keys_values, h_one, normed_one, rstd_one = project(x_all, w_all, s_all)
    seq_hit = row // group == jnp.arange(prefix_len.shape[0], dtype=jnp.int32)
    prefix = jnp.sum(jnp.where(seq_hit, prefix_len, 0))
    info = prefix.astype(jnp.int32).reshape(1)
    kv_all, attended, attended_low, lse, g_all = attention_forward(
        info, queries, keys_values, g_own, group, low, 1
    )
    mid, normed_two, rstd_two, h_two = branch(attended_low, w_all, layer_in, s_all, 2)

    received = dispatch(h_two, target, rows, capacity, 4)
    parts, grad_parts, grad_w_up, grad_bias_up, grad_w_down, grad_bias_down = experts(
        received, g_all, w_up, bias_up, w_down
    )
    grad_mid, vectors = giveback(
        grad_parts, target, cotangent, normed_two, rstd_two, s_all, rows, 5
    )
    grad_attended, delta, grad_w_out = mid_gradient(grad_mid, w_all, attended, attended_low, 7)
    down_own = lax.dynamic_slice_in_dim(bias_down, col * width, width, 1).astype(F32)
    down_own = down_own.reshape(1, EXP_DEV * width)
    grad_qkv, outs = attention_backward(
        info,
        queries,
        kv_all,
        grad_attended,
        lse,
        delta,
        parts,
        down_own,
        group,
        low,
        8,
    )
    grad_bias = jnp.sum(grad_qkv, axis=0, dtype=F32)
    grad_in, outs, weight_terms, shared = input_gradient(
        grad_qkv,
        w_all,
        outs,
        h_one,
        grad_w_out,
        grad_mid,
        normed_one,
        rstd_one,
        s_all,
        vectors,
        9,
    )
    vectors = shared[:, :5, tokens : tokens + width]
    vectors = vectors.transpose(1, 0, 2).reshape(5, rows, share).transpose(1, 0, 2)

    def by_row(v):
        v = v.reshape(heads, rows, bias_share).transpose(1, 0, 2).reshape(rows, 1, -1)
        return jnp.pad(v, ((0, 0), (0, 0), (0, 128 - v.shape[2])))

    small_terms = jnp.concatenate(
        [
            jnp.pad(vectors, ((0, 0), (0, 0), (0, 128 - share))),
            by_row(grad_bias[:width]),
            by_row(grad_bias[2 * width :]),
            jnp.zeros((rows, 1, 128), F32),
        ],
        axis=1,
    )
    weight_terms = weight_terms.reshape(rows, share, 4 * width)
    weight_sums, small_sums, layer_out = end_scatter(
        weight_terms, small_terms, outs, target, mid, rows, 11
    )

    def bias_back(v):
        return v[: heads * bias_share].reshape(heads, bias_share).T

    return (
        layer_out,
        grad_in,
        weight_sums[:, :width],
        weight_sums[:, width : 2 * width],
        weight_sums[:, 2 * width : 3 * width],
        weight_sums[:, 3 * width :],
        bias_back(small_sums[5]),
        bias_back(small_sums[6]),
        small_sums[0, :share],
        small_sums[1, :share],
        small_sums[2, :share],
        small_sums[3, :share],
        small_sums[4, :share],
        grad_w_up,
        grad_bias_up[:, 0],
        grad_w_down,
        grad_bias_down[:, 0],
    )


def solution(mesh):
    placed = (
        P("row", "col"),
        P("row", "col"),
        P("row"),
        P(),
        P(),
        P("row", "col"),
        P("row", "col"),
        P("row", "col"),
        P("row", "col"),
        P("row", "col"),
        P("row", "col"),
        P("row"),
        P("row"),
        P("row"),
        P("row"),
        P("row"),
        P("row", None, "col"),
        P("row", "col"),
        P("row", "col", None),
        P("row", None),
    )
    return jax.shard_map(
        per_device,
        mesh=mesh,
        in_specs=placed,
        out_specs=(
            P("row", "col"),
            P("row", "col"),
            P("row", "col"),
            P("row", "col"),
            P("row", "col"),
            P("row", "col"),
            P("row", "col"),
            P("row", "col"),
            P("row"),
            P("row"),
            P("row"),
            P("row"),
            P("row"),
            P("row", None, "col"),
            P("row", "col"),
            P("row", "col", None),
            P("row", None),
        ),
        check_vma=False,
    )
```

```python
import functools

import jax
import jax.numpy as jnp
from jax import lax
from jax.experimental import pallas as pl
from jax.experimental.pallas import tpu as pltpu
from jax.sharding import PartitionSpec as P

D = 768
HD = 64
EXP_DEV = 2
LENGTH = 8192
PREFIX_MAX = 4096
COLS = 4

F32 = jnp.float32
BF16 = jnp.bfloat16
MESH = pl.DeviceIdType.MESH
LOG2E = 1.4426950408889634

epsilon = 1e-05
neg_big = -1e30

VSPEC = pl.BlockSpec(memory_space=pltpu.VMEM)
SSPEC = pl.BlockSpec(memory_space=pltpu.SMEM)
VMEM_BYTES = 64 * 1000 * 1000
DMA = pltpu.SemaphoreType.DMA


def params(collective=None):
    if collective is None:
        return pltpu.CompilerParams(vmem_limit_bytes=VMEM_BYTES)
    return pltpu.CompilerParams(
        vmem_limit_bytes=VMEM_BYTES, collective_id=collective, has_side_effects=True
    )


def push(src, dst, send_sem, recv_sem, peer):
    return pltpu.make_async_remote_copy(
        src_ref=src,
        dst_ref=dst,
        send_sem=send_sem,
        recv_sem=recv_sem,
        device_id=peer,
        device_id_type=MESH,
    )


def greet(peers):
    barrier = pltpu.get_barrier_semaphore()
    for peer in peers:
        pl.semaphore_signal(barrier, inc=1, device_id=peer, device_id_type=MESH)
    pl.semaphore_wait(barrier, len(peers))


def col_places():
    me = lax.axis_index("col")
    sib = me + 1 - 2 * (me % 2)
    across = (me + 2) % COLS
    diag = (sib + 2) % COLS
    return me, sib, across, diag


def line_places(group):
    row = lax.axis_index("row")
    place = row % group
    level, side = place // 2, place % 2
    return row, place, level, side, row + 1 - 2 * side


def far_first(rows):
    return sorted(range(1, rows), key=lambda k: -min(k, rows - k))


def nt(left, right):
    return lax.dot_general(left, right, (((1,), (1,)), ((), ())), preferred_element_type=F32)


def nn(left, right):
    return lax.dot_general(left, right, (((1,), (0,)), ((), ())), preferred_element_type=F32)


def tn(left, right):
    return lax.dot_general(left, right, (((0,), (0,)), ((), ())), preferred_element_type=F32)


def side_by_side(v):
    half = v.shape[0] // 2
    return jnp.concatenate([v[:half], v[half:]], axis=1)


def number(shape, axis):
    return lax.broadcasted_iota(jnp.int32, shape, axis)


def route(ids, table, experts, cap):
    tokens = ids.shape[1]
    pick = jnp.where(number((table.shape[0], tokens), 0) == ids >> 7, 1.0, 0.0).astype(BF16)
    found = tn(table, pick)
    expert = jnp.where(number((128, tokens), 0) == ids & 127, found, 0.0)
    expert = jnp.sum(expert, axis=0, keepdims=True)
    hit = number((experts, tokens), 0).astype(F32) == expert
    pair = (tokens, tokens)
    earlier = jnp.where(number(pair, 0) < number(pair, 1), 1.0, 0.0).astype(BF16)
    before = nn(jnp.where(hit, 1.0, 0.0).astype(BF16), earlier)
    slot = jnp.sum(jnp.where(hit, before, 0.0), axis=0, keepdims=True)
    return (expert * cap + slot).astype(jnp.int32)


def all_features(s_ref, i):
    rows = s_ref.shape[0]
    return jnp.concatenate([s_ref[r, i : i + 1, : D // rows] for r in range(rows)], axis=1)


def own_features(s_ref, i):
    rows = s_ref.shape[0]
    per = rows // COLS
    block = s_ref[pl.ds(lax.axis_index("col") * per, per)]
    return jnp.concatenate([block[r, i : i + 1, : D // rows] for r in range(per)], axis=1)


def head_features(s_ref, i, heads):
    rows = s_ref.shape[0]
    size = HD // rows
    cuts = [slice(h * size, (h + 1) * size) for h in range(heads)]
    return jnp.concatenate([s_ref[r, i : i + 1, c] for c in cuts for r in range(rows)], axis=1)


def slots_of(target_ref, row, count):
    base = row * count
    slot = base + lax.broadcasted_iota(jnp.int32, (count, target_ref.shape[1]), 0)
    return jnp.where(slot == target_ref[...], 1.0, 0.0).astype(BF16)


def placed(target_ref, v, row, cap):
    return side_by_side(nn(slots_of(target_ref, row, 2 * cap), v).astype(BF16))


def combined(target_ref, block, row, cap):
    width = block.shape[1] // 2
    stacked = jnp.concatenate([block[:, :width], block[:, width:]], axis=0)
    return tn(slots_of(target_ref, row, 2 * cap), stacked)


def start_kernel(
    rows,
    pieces,
    x_ref,
    g_ref,
    ids_ref,
    table_ref,
    w_ref,
    s_ref,
    xo_ref,
    go_ref,
    wo_ref,
    so_ref,
    t_ref,
    xp_ref,
    gp_ref,
    c_send,
    c_recv,
    r_send,
    r_recv,
    l_send,
    l_recv,
):
    me, sib, across, _ = col_places()
    row, _, level, side, partner = line_places(rows)
    levels = rows // 2
    order = far_first(rows)
    peers = [{"row": (row + k) % rows} for k in order]
    greet(peers + [{"col": sib}, {"col": across}])
    xp_ref[...] = side_by_side(x_ref[...])
    step = xp_ref.shape[0] // pieces
    cap = gp_ref.shape[1]
    to_up, to_down = level < levels - 1, level > 0

    def weight(at, way, src=None):
        dst = wo_ref.at[2 * at + side]
        peer = (row + 2, row - 2, partner)[way]
        return push(
            dst if src is None else src,
            dst,
            l_send.at[way, at],
            l_recv.at[way, at],
            {"row": peer},
        )

    def weight_other(at):
        dst = wo_ref.at[2 * at + 1 - side]
        return push(dst, dst, l_send.at[2, at], l_recv.at[2, at], {"row": partner})

    @pl.when(to_up)
    def _():
        weight(level, 0, w_ref).start()

    @pl.when(to_down)
    def _():
        weight(level, 1, w_ref).start()

    weight(level, 2, w_ref).start()
    sent = []
    for i in range(pieces):
        part = pl.ds(i * step, step)
        for way, peer in ((0, across), (1, sib)):
            copy = push(
                xp_ref.at[part],
                xo_ref.at[me, part],
                c_send.at[way, i],
                c_recv.at[way, i],
                {"col": peer},
            )
            copy.start()
            sent.append(copy)
    row_copies = []
    for k, peer in enumerate(peers):
        copy = push(s_ref, so_ref.at[row], r_send.at[0, k], r_recv.at[0, k], peer)
        copy.start()
        row_copies.append(copy)

    def send_rows(k):
        target = (row + order[k]) % rows
        gp_ref[k] = placed(t_ref, g_ref[...], target, cap)
        copy = push(gp_ref.at[k], go_ref.at[row], r_send.at[1, k], r_recv.at[1, k], peers[k])
        copy.start()
        row_copies.append(copy)

    t_ref[...] = route(ids_ref[...], table_ref[...], EXP_DEV * rows, cap)
    send_rows(0)
    xo_ref[me] = xp_ref[...]
    wo_ref[row] = w_ref[...]
    so_ref[row] = s_ref[...]
    todo = list(range(1, rows - 1))

    def pass_on(k):
        at = level - k

        @pl.when(at >= 0)
        def _():
            weight(at, 0).wait_recv()

            @pl.when(to_up)
            def _():
                weight(at, 0).start()

            weight(at, 2).start()

        up = level + k

        @pl.when(up < levels)
        def _():
            weight(up, 1).wait_recv()

            @pl.when(to_down)
            def _():
                weight(up, 1).start()

            weight(up, 2).start()

    late = []
    for k in range(1, max(levels, pieces + 1)):
        if k < levels:
            pass_on(k)
        if k <= pieces:
            part = pl.ds((k - 1) * step, step)
            sent[2 * k - 2].wait_recv()
            copy = push(
                xo_ref.at[across, part],
                xo_ref.at[across, part],
                c_send.at[2, k - 1],
                c_recv.at[2, k - 1],
                {"col": sib},
            )
            copy.start()
            late.append(copy)
        for _ in range(2):
            if todo:
                send_rows(todo.pop(0))
    while todo:
        send_rows(todo.pop(0))
    go_ref[row] = placed(t_ref, g_ref[...], row, cap)
    for i in range(pieces):
        sent[2 * i].wait_send()
        sent[2 * i + 1].wait()
        late[i].wait()
    for at in range(levels):
        weight_other(at).wait_recv()
        weight(at, 2).wait_send()

        @pl.when((at <= level) & to_up)
        def _(at=at):
            weight(at, 0).wait_send()

        @pl.when((at >= level) & to_down)
        def _(at=at):
            weight(at, 1).wait_send()

    for copy in row_copies:
        copy.wait()


def start_gather(x, g, ids, table, w, s, rows, cap):
    pieces = 4
    tokens, width = x.shape
    packed = (tokens // 2, 2 * width)
    return pl.pallas_call(
        functools.partial(start_kernel, rows, pieces),
        out_shape=(
            jax.ShapeDtypeStruct((COLS,) + packed, x.dtype),
            jax.ShapeDtypeStruct((rows, cap, 2 * width), g.dtype),
            jax.ShapeDtypeStruct((rows,) + w.shape, w.dtype),
            jax.ShapeDtypeStruct((rows,) + s.shape, s.dtype),
            jax.ShapeDtypeStruct((1, tokens), jnp.int32),
        ),
        in_specs=[VSPEC] * 6,
        out_specs=(VSPEC,) * 5,
        scratch_shapes=[
            pltpu.VMEM(packed, x.dtype),
            pltpu.VMEM((rows - 1, cap, 2 * width), g.dtype),
            DMA((3, pieces)),
            DMA((3, pieces)),
            DMA((2, rows - 1)),
            DMA((2, rows - 1)),
            DMA((3, rows // 2)),
            DMA((3, rows // 2)),
        ],
        compiler_params=params(0),
    )(x, g, ids, table, w, s)


def project_kernel(
    x_ref, w_ref, s_ref, q_ref, kv_ref, h_ref, n_ref, r_ref
):
    me = lax.axis_index("col")
    half, width = x_ref.shape[1], x_ref.shape[2] // 2
    gain, shift = all_features(s_ref, 0), all_features(s_ref, 1)
    query = head_features(s_ref, 5, width // HD)
    value = head_features(s_ref, 6, width // HD)
    bias = jnp.concatenate([query, jnp.zeros_like(query), value], axis=1)
    w = w_ref[...].reshape(D, 4 * width)[:, : 3 * width]
    step = min(half, 256)
    for i in range(2 * half // step):
        side, start = i * step // half, i * step % half
        rows, feats = slice(start, start + step), slice(side * width, (side + 1) * width)
        x = jnp.concatenate([x_ref[b, rows, feats] for b in range(COLS)], axis=1).astype(F32)
        mean = jnp.mean(x, axis=-1, keepdims=True)
        centred = x - mean
        rstd = lax.rsqrt(jnp.mean(centred * centred, axis=-1, keepdims=True) + epsilon)
        h = (centred * rstd * gain + shift).astype(BF16)
        out = slice(i * step, (i + 1) * step)
        h_ref[out] = h
        n_ref[out] = (x_ref[me, rows, feats].astype(F32) - mean) * rstd
        r_ref[out] = rstd
        qkv = (nn(h, w) + bias).astype(BF16)
        q_ref[out] = qkv[:, :width] * jnp.asarray(HD**-0.5, BF16)
        kv_ref[out] = qkv[:, width:]


def project(x, w, s):
    tokens, width = 2 * x.shape[1], x.shape[2] // 2
    return pl.pallas_call(
        project_kernel,
        out_shape=(
            jax.ShapeDtypeStruct((tokens, width), BF16),
            jax.ShapeDtypeStruct((tokens, 2 * width), BF16),
            jax.ShapeDtypeStruct((tokens, D), BF16),
            jax.ShapeDtypeStruct((tokens, width), F32),
            jax.ShapeDtypeStruct((tokens, 1), F32),
        ),
        in_specs=[VSPEC] * 3,
        out_specs=(VSPEC,) * 5,
        compiler_params=params(),
    )(x, w, s)


def mid_kernel(
    pieces,
    x_ref,
    w_ref,
    att_ref,
    low_ref,
    do_ref,
    delta_ref,
    gw_ref,
    xp_ref,
    xo_ref,
    wide_ref,
    c_send,
    c_recv,
):
    me, sib, across, _ = col_places()
    greet([{"col": sib}, {"col": across}])
    xp_ref[...] = side_by_side(x_ref[...].astype(BF16))
    step = xp_ref.shape[0] // pieces
    sent, late = [], []
    for i in range(pieces):
        part = pl.ds(i * step, step)
        for way, peer in ((0, across), (1, sib)):
            copy = push(
                xp_ref.at[part],
                xo_ref.at[me, part],
                c_send.at[way, i],
                c_recv.at[way, i],
                {"col": peer},
            )
            copy.start()
            sent.append(copy)
    xo_ref[me] = xp_ref[...]
    tokens, width = x_ref.shape
    w = w_ref[...].reshape(D, 4 * width)[:, 3 * width :]
    for i in range(pieces):
        part = pl.ds(i * step, step)
        sent[2 * i].wait_recv()
        copy = push(
            xo_ref.at[across, part],
            xo_ref.at[across, part],
            c_send.at[2, i],
            c_recv.at[2, i],
            {"col": sib},
        )
        copy.start()
        late.append(copy)
    for i in range(pieces):
        sent[2 * i].wait_send()
        sent[2 * i + 1].wait()
        late[i].wait()
        rows = slice(i * step, (i + 1) * step)
        for half in range(2):
            feats = slice(half * width, (half + 1) * width)
            start = half * (tokens // 2) + i * step
            out = slice(start, start + step)
            wide = jnp.concatenate([xo_ref[b, rows, feats] for b in range(COLS)], axis=1)
            wide_ref[out] = wide
            do = nn(wide, w).astype(BF16)
            do_ref[out] = do
            both = (do.astype(F32) * att_ref[out]).T
            for h in range(width // HD):
                delta_ref[h : h + 1, out] = jnp.sum(
                    both[h * HD : (h + 1) * HD], axis=0, keepdims=True
                )
    gw_ref[...] = tn(wide_ref[...], low_ref[...]).astype(BF16)


def mid_gradient(x, w, attended, low, collective):
    pieces = 4
    tokens, width = x.shape
    packed = (tokens // 2, 2 * width)
    return pl.pallas_call(
        functools.partial(mid_kernel, pieces),
        out_shape=(
            jax.ShapeDtypeStruct((tokens, width), BF16),
            jax.ShapeDtypeStruct((8, tokens), F32),
            jax.ShapeDtypeStruct((D, width), BF16),
        ),
        in_specs=[VSPEC] * 4,
        out_specs=(VSPEC,) * 3,
        scratch_shapes=[
            pltpu.VMEM(packed, BF16),
            pltpu.VMEM((COLS,) + packed, BF16),
            pltpu.VMEM((tokens, D), BF16),
            DMA((3, pieces)),
            DMA((3, pieces)),
        ],
        compiler_params=params(collective),
    )(x, w, attended, low)


def col_peers():
    me = lax.axis_index("col")
    return [{"col": (me + k) % COLS} for k in range(1, COLS)]


def to_rows(columns):
    lane = lax.broadcasted_iota(jnp.int32, (columns[0].shape[0], 128), 1)
    v = jnp.zeros(lane.shape, F32)
    for i, column in enumerate(columns):
        v = jnp.where(lane == i, column, v)
    return v.T[:8]


def to_columns(lines):
    place = lax.broadcasted_iota(jnp.int32, (8, lines[0].shape[1]), 0)
    v = jnp.zeros(place.shape, F32)
    for i, one in enumerate(lines):
        v = jnp.where(place == i, one, v)
    v = v.T
    return [v[:, i : i + 1] for i in range(len(lines))]


def share(snd_ref, all_ref, send, recv):
    me = lax.axis_index("col")
    copies = []
    for k, peer in enumerate(col_peers()):
        copy = push(snd_ref, all_ref.at[me], send.at[k], recv.at[k], peer)
        copy.start()
        copies.append(copy)
    all_ref[me] = snd_ref[...]
    for copy in copies:
        copy.wait()


def norm_back(grad, normed, gain, rstd, snd_ref, all_ref, send, recv):
    tokens = grad.shape[0]
    scaled = grad * gain
    sums = [
        jnp.sum(scaled, axis=-1, keepdims=True),
        jnp.sum(scaled * normed, axis=-1, keepdims=True),
    ]
    snd_ref[:, :tokens] = to_rows(sums)
    share(snd_ref, all_ref, send, recv)
    total = all_ref[0, :, :tokens]
    for b in range(1, COLS):
        total = total + all_ref[b, :, :tokens]
    total = total / D
    first, second = to_columns([total[0:1], total[1:2]])
    return rstd * (scaled - first - normed * second)


def line_greet(levels, row, level, partner):
    barrier = pltpu.get_barrier_semaphore()
    me = lax.axis_index("col")
    for k in range(1, COLS):
        peer = {"col": (me + k) % COLS}
        pl.semaphore_signal(barrier, inc=1, device_id=peer, device_id_type=MESH)
    pl.semaphore_signal(barrier, inc=1, device_id={"row": partner}, device_id_type=MESH)

    @pl.when(level > 0)
    def _():
        pl.semaphore_signal(barrier, inc=1, device_id={"row": row - 2}, device_id_type=MESH)

    @pl.when(level < levels - 1)
    def _():
        pl.semaphore_signal(barrier, inc=1, device_id={"row": row + 2}, device_id_type=MESH)

    count = COLS + (level > 0).astype(jnp.int32) + (level < levels - 1).astype(jnp.int32)
    pl.semaphore_wait(barrier, count)


def seen(key_start, query_start, shape, prefix):
    key = key_start + lax.broadcasted_iota(jnp.int32, shape, 0)
    query = query_start + lax.broadcasted_iota(jnp.int32, shape, 1)
    return (key < prefix) | (key <= query)


def forward_kernel(
    group,
    low,
    pieces,
    qb,
    info_ref,
    q_ref,
    kv_ref,
    g_ref,
    out_ref,
    o_ref,
    ob_ref,
    lse_ref,
    ga_ref,
    m_ref,
    acc_ref,
    u_send,
    u_recv,
    d_send,
    d_recv,
    x_send,
    x_recv,
    g_send,
    g_recv,
):
    levels = group // 2
    row, place, level, side, partner = line_places(group)
    prefix = info_ref[0]
    tokens, width = q_ref.shape
    heads = width // HD
    step = tokens // pieces
    line_greet(levels, row, level, partner)

    def make(at, i, way, src=None):
        part = pl.ds(i * step, step)
        dst = out_ref.at[2 * at + side, part]
        sems = ((u_send, u_recv), (d_send, d_recv), (x_send, x_recv))[way]
        peer = (row + 2, row - 2, partner)[way]
        return push(
            dst if src is None else src.at[part],
            dst,
            sems[0].at[at, i],
            sems[1].at[at, i],
            {"row": peer},
        )

    def other(at, i):
        part = pl.ds(i * step, step)
        dst = out_ref.at[2 * at + 1 - side, part]
        return push(dst, dst, x_send.at[at, i], x_recv.at[at, i], {"row": partner})

    def when(cond, run):
        @pl.when(cond)
        def _():
            for i in range(pieces):
                run(i)

    to_up = level < levels - 1
    own_down = (level > 0) & (level < low)
    own_side = (level < low) | (side == 0)
    for i in range(pieces):

        @pl.when(to_up)
        def _(i=i):
            make(level, i, 0, kv_ref).start()

        @pl.when(own_side)
        def _(i=i):
            make(level, i, 2, kv_ref).start()

        @pl.when(own_down)
        def _(i=i):
            make(level, i, 1, kv_ref).start()

    me = lax.axis_index("col")
    wide = []
    for k in range(1, COLS):
        peer = {"col": (me + k) % COLS}
        copy = push(g_ref, ga_ref.at[me], g_send.at[k - 1], g_recv.at[k - 1], peer)
        copy.start()
        wide.append(copy)
    ga_ref[me] = g_ref[...]
    out_ref[place] = kv_ref[...]
    m_ref[...] = jnp.full(m_ref.shape, neg_big, F32)
    acc_ref[...] = jnp.zeros(acc_ref.shape, F32)
    units = [(h, i) for h in range(heads) for i in range(tokens // qb)]

    def block(blk, masked):
        def raw_of(h, i):
            feats = slice(h * HD, (h + 1) * HD)
            raw = nt(out_ref[blk, :, feats], q_ref[i * qb : (i + 1) * qb, feats])
            if masked:
                allowed = seen(blk * tokens, place * tokens + i * qb, raw.shape, prefix)
                raw = jnp.where(allowed, raw, neg_big)
            return raw

        def soften(h, i, raw):
            cols = slice(i * qb, (i + 1) * qb)
            old = m_ref[h : h + 1, cols]
            new = jnp.maximum(old, jnp.max(raw, axis=0, keepdims=True))
            m_ref[h : h + 1, cols] = new
            weights = jnp.exp2((raw - new) * LOG2E).astype(BF16)
            return weights, jnp.exp2((old - new) * LOG2E)

        def gather(h, i, weights, scale):
            cols = slice(i * qb, (i + 1) * qb)
            v = out_ref[blk, :, width + h * HD : width + (h + 1) * HD]
            v_ext = jnp.concatenate([v.T, jnp.ones((16, tokens), BF16)], axis=0)
            acc_ref[h, :, cols] = acc_ref[h, :, cols] * scale + nn(v_ext, weights)

        coming, waiting = raw_of(*units[0]), None
        for n, unit in enumerate(units):
            raw = coming
            if n + 1 < len(units):
                coming = raw_of(*units[n + 1])
            soft = soften(*unit, raw)
            if waiting is not None:
                gather(*waiting)
            waiting = unit + soft
        gather(*waiting)

    def event(e, carry):
        t, cross = e // 2, e % 2
        at = jnp.where(t <= level, level - t, t)
        live = (t <= level) | (t < low)
        line_in = live & (cross == 0)
        coming = t + 1
        via = jnp.where(coming <= level, level - coming, coming)
        relays = (cross == 1) & ((coming <= level) | (coming < low))

        @pl.when(relays & (via < level))
        def _():
            for i in range(pieces):
                make(via, i, 0).wait_recv()

                @pl.when(to_up)
                def _(i=i):
                    make(via, i, 0).start()

                make(via, i, 2).start()

        @pl.when(relays & (via > level))
        def _():
            for i in range(pieces):
                make(via, i, 1).wait_recv()

                @pl.when(level > 0)
                def _(i=i):
                    make(via, i, 1).start()

                make(via, i, 2).start()

        comes = live & (cross == 1) & ((at < low) | (at < level) | (side == 1))
        when(comes, lambda i: other(at, i).wait_recv())
        blk = 2 * at + jnp.where(cross == 0, side, 1 - side)
        needed = line_in | comes

        @pl.when(needed & (blk < place))
        def _():
            block(blk, False)

        @pl.when(needed & (blk >= place))
        def _():
            block(blk, True)

        return carry

    lax.fori_loop(0, 2 * levels, event, 0)

    for h in range(heads):
        total = acc_ref[h, HD : HD + 1, :]
        out = (acc_ref[h, :HD, :] / total).T
        o_ref[:, h * HD : (h + 1) * HD] = out
        ob_ref[:, h * HD : (h + 1) * HD] = out.astype(BF16)
        lse_ref[h : h + 1, :] = m_ref[h : h + 1, :] * LOG2E + jnp.log2(total)

    when(to_up, lambda i: make(level, i, 0, kv_ref).wait_send())
    when(own_side, lambda i: make(level, i, 2, kv_ref).wait_send())
    when(own_down, lambda i: make(level, i, 1, kv_ref).wait_send())
    for k in range(1, levels):
        at = level - k
        when((at >= 0) & to_up, lambda i, at=at: make(at, i, 0).wait_send())
        when(at >= 0, lambda i, at=at: make(at, i, 2).wait_send())
    for k in range(1, low):
        at = level + k
        when((at < low) & (level > 0), lambda i, at=at: make(at, i, 1).wait_send())
        when(at < low, lambda i, at=at: make(at, i, 2).wait_send())
    for copy in wide:
        copy.wait()


def attention_forward(info, q, kv, g, group, low, collective):
    pieces = 4
    levels = group // 2
    tokens, width = q.shape
    heads = width // HD
    return pl.pallas_call(
        functools.partial(forward_kernel, group, low, pieces, tokens // 2),
        out_shape=(
            jax.ShapeDtypeStruct((group,) + kv.shape, kv.dtype),
            jax.ShapeDtypeStruct((tokens, width), F32),
            jax.ShapeDtypeStruct((tokens, width), BF16),
            jax.ShapeDtypeStruct((8, tokens), F32),
            jax.ShapeDtypeStruct((COLS,) + g.shape, g.dtype),
        ),
        in_specs=[SSPEC, VSPEC, VSPEC, VSPEC],
        out_specs=(VSPEC,) * 5,
        scratch_shapes=[
            pltpu.VMEM((8, tokens), F32),
            pltpu.VMEM((heads, HD + 16, tokens), F32),
        ]
        + [DMA((levels, pieces))] * 6
        + [DMA((COLS - 1,))] * 2,
        compiler_params=params(collective),
    )(info, q, kv, g)


def backward_kernel(
    group,
    low,
    pieces,
    kb,
    info_ref,
    q_ref,
    kv_ref,
    do_ref,
    lse_ref,
    delta_ref,
    e_ref,
    bias_ref,
    out_ref,
    eo_ref,
    part_ref,
    rx_ref,
    above_ref,
    below_ref,
    snd_ref,
    acc_ref,
    dqt_ref,
    er_ref,
    u_send,
    u_recv,
    d_send,
    d_recv,
    x_send,
    x_recv,
    e_send,
    e_recv,
):
    levels = group // 2
    row, place, level, side, partner = line_places(group)
    prefix = info_ref[0]
    tokens, width = q_ref.shape
    heads = width // HD
    step = tokens // pieces
    line_greet(levels, row, level, partner)
    me = lax.axis_index("col")
    terms = []
    for k in range(1, COLS):
        peer = (me + k) % COLS
        copy = push(
            e_ref.at[peer], er_ref.at[k - 1], e_send.at[k - 1], e_recv.at[k - 1], {"col": peer}
        )
        copy.start()
        terms.append(copy)
    dqt_ref[...] = jnp.zeros(dqt_ref.shape, F32)

    def block(blk, masked, leaves, at):
        def body(j, carry):
            start = pl.multiple_of(j * kb, kb)
            keys = pl.ds(start, kb)
            for h in range(heads):
                feats = slice(h * HD, (h + 1) * HD)
                vals = slice(width + h * HD, width + (h + 1) * HD)
                k, v = kv_ref[blk, keys, feats], kv_ref[blk, keys, vals]
                q, do = q_ref[:, feats], do_ref[:, feats]
                probs = jnp.exp2(nt(k, q) * LOG2E - lse_ref[h : h + 1, :])
                if masked:
                    allowed = seen(blk * tokens + start, place * tokens, probs.shape, prefix)
                    probs = jnp.where(allowed, probs, 0.0)
                grad = (probs * (nt(v, do) - delta_ref[h : h + 1, :])).astype(BF16)
                part_ref[blk, keys, feats] = nn(grad, q).astype(BF16)
                part_ref[blk, keys, vals] = nn(probs.astype(BF16), do).astype(BF16)
                dqt_ref[feats, :] += nn(k.T, grad)

            @pl.when(leaves)
            def _():
                for n in range(kb // step):
                    cross(at, j * (kb // step) + n).start()

            return carry

        lax.fori_loop(0, tokens // kb, body, 0)

    def cross(at, i):
        part = pl.ds(i * step, step)
        return push(
            part_ref.at[2 * at + 1 - side, part],
            rx_ref.at[at, part],
            x_send.at[at, i],
            x_recv.at[at, i],
            {"row": partner},
        )

    def line(at, i, up):
        part = pl.ds(i * step, step)
        sems = (u_send, u_recv) if up else (d_send, d_recv)
        return push(
            snd_ref.at[at, part],
            (below_ref if up else above_ref).at[at, part],
            sems[0].at[at, i],
            sems[1].at[at, i],
            {"row": row + 2 if up else row - 2},
        )

    def gone(at):
        return (at < low) | (at < level) | ((at == level) & (side == 1))

    def comes(at):
        return (at < low) | (at < level) | ((at == level) & (side == 0))

    def total(at, i, from_above, from_below):
        part = pl.ds(i * step, step)
        acc_ref[...] = part_ref[2 * at + side, part].astype(F32)

        @pl.when(comes(at))
        def _():
            cross(at, i).wait_recv()
            acc_ref[...] += rx_ref[at, part].astype(F32)

        if from_above is not None:

            @pl.when(from_above)
            def _():
                line(at, i, False).wait_recv()
                acc_ref[...] += above_ref[at, part].astype(F32)

        if from_below is not None:

            @pl.when(from_below)
            def _():
                line(at, i, True).wait_recv()
                acc_ref[...] += below_ref[at, part].astype(F32)

    not_top = level < levels - 1
    above = jnp.maximum(low - 1 - level, 0)

    def level_of(t):
        return jnp.where(t < above, low - 1 - t, t - above)

    def event(e, carry):
        t, own = e // 2, e % 2
        at = level_of(t)
        live = (t < above) | (at <= level)

        down = t - (levels - level)

        @pl.when((own == 1) & (down >= 0) & (down < level))
        def _():
            for i in range(pieces):
                total(down, i, not_top, None)
                snd_ref[down, pl.ds(i * step, step)] = acc_ref[...].astype(BF16)
                line(down, i, False).start()

        @pl.when((own == 1) & (t >= 1) & (t - 1 < above))
        def _():
            up = level_of(t - 1)
            for i in range(pieces):
                total(up, i, None, level > 0)
                snd_ref[up, pl.ds(i * step, step)] = acc_ref[...].astype(BF16)
                line(up, i, True).start()

        goes = live & (own == 0) & gone(at)
        blk = 2 * at + jnp.where(own == 1, side, 1 - side)
        needed = goes | (live & (own == 1))

        @pl.when(needed & (blk < place))
        def _():
            block(blk, False, goes, at)

        @pl.when(needed & (blk >= place))
        def _():
            block(blk, True, goes, at)

        return carry

    lax.fori_loop(0, 2 * levels, event, 0)
    for copy in terms:
        copy.wait()

    def finish(r, carry):
        total = e_ref[me, r].astype(F32) + bias_ref[...]
        for k in range(COLS - 1):
            total = total + er_ref[k, r].astype(F32)
        eo_ref[r] = total.astype(BF16)
        return carry

    lax.fori_loop(0, e_ref.shape[1], finish, 0)
    out_ref[:, :width] = (dqt_ref[...] * HD**-0.5).T.astype(BF16)

    for i in range(pieces):
        total(level, i, not_top, (level > 0) & (level < low))
        out_ref[pl.ds(i * step, step), width:] = acc_ref[...].astype(BF16)

    for at in range(levels):
        for i in range(pieces):

            @pl.when(gone(at))
            def _(at=at, i=i):
                cross(at, i).wait_send()

            @pl.when(at < level)
            def _(at=at, i=i):
                line(at, i, False).wait_send()

            if at < low:

                @pl.when(at > level)
                def _(at=at, i=i):
                    line(at, i, True).wait_send()


def attention_backward(info, q, kv_all, do, lse, delta, e, bias, group, low, collective):
    pieces = 4
    levels = group // 2
    tokens, width = q.shape
    both = 2 * width
    block = pltpu.VMEM((levels, tokens, both), BF16)
    return pl.pallas_call(
        functools.partial(backward_kernel, group, low, pieces, tokens // 2),
        out_shape=(
            jax.ShapeDtypeStruct((tokens, width + both), BF16),
            jax.ShapeDtypeStruct(e.shape[1:], BF16),
        ),
        in_specs=[SSPEC] + [VSPEC] * 7,
        out_specs=(VSPEC,) * 2,
        scratch_shapes=[
            pltpu.VMEM(kv_all.shape, BF16),
            block,
            block,
            pltpu.VMEM((low, tokens, both), BF16),
            block,
            pltpu.VMEM((tokens // pieces, both), F32),
            pltpu.VMEM((width, tokens), F32),
            pltpu.VMEM((COLS - 1,) + e.shape[1:], BF16),
        ]
        + [DMA((levels, pieces))] * 6
        + [DMA((COLS - 1,))] * 2,
        compiler_params=params(collective),
    )(info, q, kv_all, do, lse, delta, e, bias)


def product(pieces, a_ref, w_ref, feats, out_ref, snd_ref, rx_ref, far_ref, tot_ref, sems, fill):
    send, recv = sems
    me, sib, across, diag = col_places()
    half = a_ref.shape[0] // 2
    step = half // pieces
    per = w_ref.shape[0] // COLS
    width = out_ref.shape[1]

    def weight(who):
        return w_ref[pl.ds(who * per, per)].reshape(width, 4 * width)[:, feats]

    def term(i, w):
        parts = [nt(a_ref[pl.ds(n * half + i * step, step)], w) for n in range(2)]
        return jnp.concatenate(parts, axis=1)

    def near(i, j):
        part = pl.ds(i * step, step)
        return push(
            snd_ref.at[j, part], rx_ref.at[j, part], send.at[j, i], recv.at[j, i], {"col": sib}
        )

    def over(i):
        part = pl.ds(i * step, step)
        return push(tot_ref.at[part], far_ref.at[part], send.at[2, i], recv.at[2, i], {"col": across})

    w = weight(diag)
    for i in range(pieces):
        snd_ref[0, pl.ds(i * step, step)] = term(i, w).astype(BF16)
        near(i, 0).start()
    w = weight(across)
    for i in range(pieces):
        part = pl.ds(i * step, step)
        mine = term(i, w)
        near(i, 0).wait_recv()
        tot_ref[part] = (mine + rx_ref[0, part].astype(F32)).astype(BF16)
        over(i).start()
    w = weight(sib)
    for i in range(pieces):
        snd_ref[1, pl.ds(i * step, step)] = term(i, w).astype(BF16)
        near(i, 1).start()
    fill()
    w = weight(me)
    for i in range(pieces):
        part = pl.ds(i * step, step)
        mine = term(i, w)
        near(i, 1).wait_recv()
        mine = mine + rx_ref[1, part].astype(F32)
        over(i).wait_recv()
        mine = mine + far_ref[part].astype(F32)
        out_ref[part] = mine[:, :width]
        out_ref[pl.ds(half + i * step, step)] = mine[:, width:]
    for i in range(pieces):
        near(i, 0).wait_send()
        near(i, 1).wait_send()
        over(i).wait_send()


def product_scratch(pieces, tokens, width):
    block = pltpu.VMEM((tokens // 2, 2 * width), BF16)
    pair = pltpu.VMEM((2, tokens // 2, 2 * width), BF16)
    return [pair, pair, block, block, DMA((3, pieces)), DMA((3, pieces))]


def branch_kernel(
    pieces,
    a_ref,
    w_ref,
    x_ref,
    s_ref,
    mid_ref,
    normed_ref,
    rstd_ref,
    h_ref,
    snd_ref,
    rx_ref,
    far_ref,
    tot_ref,
    send,
    recv,
    st_ref,
    all_ref,
    st_send,
    st_recv,
):
    greet(col_peers())
    tokens, width = x_ref.shape
    product(
        pieces,
        a_ref,
        w_ref,
        slice(3 * width, 4 * width),
        mid_ref,
        snd_ref,
        rx_ref,
        far_ref,
        tot_ref,
        (send, recv),
        lambda: None,
    )
    mid = x_ref[...].astype(F32) + mid_ref[...] + own_features(s_ref, 4)
    mid_ref[...] = mid
    part_mean = jnp.mean(mid, axis=-1, keepdims=True)
    part_spread = jnp.sum((mid - part_mean) ** 2, axis=-1, keepdims=True)
    st_ref[...] = to_rows([part_mean, part_spread])
    share(st_ref, all_ref, st_send, st_recv)
    mean = sum(all_ref[b, 0:1] for b in range(COLS)) / COLS
    spread = sum(
        all_ref[b, 1:2] + width * (all_ref[b, 0:1] - mean) ** 2 for b in range(COLS)
    )
    mean, rstd = to_columns([mean, lax.rsqrt(spread / D + epsilon)])
    normed = (mid - mean) * rstd
    normed_ref[...] = normed
    rstd_ref[...] = rstd
    h_ref[...] = (normed * own_features(s_ref, 2) + own_features(s_ref, 3)).astype(BF16)


def branch(a, w, x, s, collective):
    pieces = 4
    tokens, width = a.shape
    rows = jax.ShapeDtypeStruct((tokens, width), F32)
    return pl.pallas_call(
        functools.partial(branch_kernel, pieces),
        out_shape=(
            rows,
            rows,
            jax.ShapeDtypeStruct((tokens, 1), F32),
            jax.ShapeDtypeStruct((tokens, width), BF16),
        ),
        in_specs=[VSPEC] * 4,
        out_specs=(VSPEC,) * 4,
        scratch_shapes=product_scratch(pieces, tokens, width)
        + [
            pltpu.VMEM((8, tokens), F32),
            pltpu.VMEM((COLS, 8, tokens), F32),
            DMA((COLS - 1,)),
            DMA((COLS - 1,)),
        ],
        compiler_params=params(collective),
    )(a, w, x, s)


def input_kernel(
    pieces,
    a_ref,
    w_ref,
    e_ref,
    h_ref,
    gwo_ref,
    mid_ref,
    normed_ref,
    rstd_ref,
    s_ref,
    vec_ref,
    gin_ref,
    eo_ref,
    wt_ref,
    all_ref,
    grad_ref,
    snd_ref,
    rx_ref,
    far_ref,
    tot_ref,
    send,
    recv,
    st_ref,
    st_send,
    st_recv,
    e_send,
    e_recv,
):
    rows = e_ref.shape[0]
    row = lax.axis_index("row")
    order = far_first(rows)
    greet([{"row": (row + k) % rows} for k in order] + col_peers())
    home = []
    for n, k in enumerate(order):
        peer = (row + k) % rows
        copy = push(e_ref.at[peer], eo_ref.at[row], e_send.at[n], e_recv.at[n], {"row": peer})
        copy.start()
        home.append(copy)
    eo_ref[row] = e_ref[row]
    tokens, width = grad_ref.shape

    def fill():
        both = [tn(h_ref[...], a_ref[...]).astype(BF16), gwo_ref[...]]
        wt_ref[...] = jnp.concatenate(both, axis=1)

    product(
        pieces,
        a_ref,
        w_ref,
        slice(0, 3 * width),
        grad_ref,
        snd_ref,
        rx_ref,
        far_ref,
        tot_ref,
        (send, recv),
        fill,
    )
    grad, normed = grad_ref[...], normed_ref[...]
    st_ref[:, tokens:] = jnp.zeros((8, st_ref.shape[1] - tokens), F32)
    st_ref[0:1, tokens : tokens + width] = jnp.sum(grad * normed, axis=0, keepdims=True)
    st_ref[1:2, tokens : tokens + width] = jnp.sum(grad, axis=0, keepdims=True)
    st_ref[2:5, tokens : tokens + width] = vec_ref[0:3]
    gin_ref[...] = mid_ref[...] + norm_back(
        grad, normed, own_features(s_ref, 0), rstd_ref[...], st_ref, all_ref, st_send, st_recv
    )
    for copy in home:
        copy.wait()


def input_gradient(a, w, e, h, gwo, mid, normed, rstd, gain, vec, collective):
    pieces = 4
    tokens, width = mid.shape
    wide = tokens + 256
    return pl.pallas_call(
        functools.partial(input_kernel, pieces),
        out_shape=(
            jax.ShapeDtypeStruct((tokens, width), F32),
            jax.ShapeDtypeStruct(e.shape, BF16),
            jax.ShapeDtypeStruct((D, 4 * width), BF16),
            jax.ShapeDtypeStruct((COLS, 8, wide), F32),
        ),
        in_specs=[VSPEC] * 10,
        out_specs=(VSPEC,) * 4,
        scratch_shapes=[pltpu.VMEM((tokens, width), F32)]
        + product_scratch(pieces, tokens, width)
        + [
            pltpu.VMEM((8, wide), F32),
            DMA((COLS - 1,)),
            DMA((COLS - 1,)),
            DMA((e.shape[0] - 1,)),
            DMA((e.shape[0] - 1,)),
        ],
        compiler_params=params(collective),
    )(a, w, e, h, gwo, mid, normed, rstd, gain, vec)


def dispatch_kernel(rows, x_ref, t_ref, out_ref, in_ref, r_send, r_recv, c_send, c_recv):
    me, sib, across, _ = col_places()
    row = lax.axis_index("row")
    order = far_first(rows)
    peers = [(row + k) % rows for k in order]
    greet([{"row": p} for p in peers] + [{"col": sib}, {"col": across}])
    copies = []
    cap = in_ref.shape[1]

    def col(src, dst, k, way):
        return push(
            src, dst, c_send.at[way, k], c_recv.at[way, k], {"col": across if way == 0 else sib}
        )

    done, first = [], []
    for k, peer in enumerate(peers):
        in_ref[peer] = placed(t_ref, x_ref[...], peer, cap)
        copy = push(
            in_ref.at[peer], out_ref.at[me, row], r_send.at[k], r_recv.at[k], {"row": peer}
        )
        copy.start()
        copies.append(copy)
        if k == 1:
            in_ref[row] = placed(t_ref, x_ref[...], row, cap)
            for way in range(2):
                copy = col(in_ref.at[row], out_ref.at[me, row], 0, way)
                copy.start()
                (first if way == 0 else done).append(copy)
    out_ref[me, row] = in_ref[row]
    sources = [row] + [(row + rows - k) % rows for k in order]

    def forward(k):
        first[k].wait_recv()
        src = sources[k]
        copy = col(out_ref.at[across, src], out_ref.at[across, src], k, 2)
        copy.start()
        done.append(copy)

    for k in range(1, rows):
        copies[k - 1].wait_recv()
        block = out_ref.at[me, sources[k]]
        for way in range(2):
            copy = col(block, block, k, way)
            copy.start()
            (first if way == 0 else done).append(copy)
        forward(k - 1)
    forward(rows - 1)
    for copy in copies:
        copy.wait_send()
    for copy in first:
        copy.wait_send()
    for copy in done:
        copy.wait()


def dispatch(x, target, rows, cap, collective):
    block = (rows, cap, 2 * x.shape[1])
    return pl.pallas_call(
        functools.partial(dispatch_kernel, rows),
        out_shape=jax.ShapeDtypeStruct((COLS,) + block, x.dtype),
        in_specs=[VSPEC] * 2,
        out_specs=VSPEC,
        scratch_shapes=[
            pltpu.VMEM(block, x.dtype),
            DMA((rows - 1,)),
            DMA((rows - 1,)),
            DMA((3, rows)),
            DMA((3, rows)),
        ],
        compiler_params=params(collective),
    )(x, target)


def giveback_kernel(
    rows,
    in_ref,
    t_ref,
    cot_ref,
    normed_ref,
    rstd_ref,
    s_ref,
    mid_ref,
    vec_ref,
    sum_ref,
    out_ref,
    rx_ref,
    far_ref,
    tot_ref,
    fin_ref,
    st_ref,
    all_ref,
    send,
    recv,
    r_send,
    r_recv,
    st_send,
    st_recv,
):
    me, sib, across, diag = col_places()
    row = lax.axis_index("row")
    order = [(row + k) % rows for k in far_first(rows)] + [row]
    greet([{"row": p} for p in order[:-1]] + col_peers())

    def near(k, j):
        who = diag if j == 0 else sib
        return push(
            in_ref.at[who, order[k]], rx_ref.at[j, k], send.at[j, k], recv.at[j, k], {"col": sib}
        )

    def over(k):
        return push(tot_ref.at[k], far_ref.at[k], send.at[2, k], recv.at[2, k], {"col": across})

    def home(k):
        return push(
            fin_ref.at[k], out_ref.at[row], r_send.at[k], r_recv.at[k], {"row": order[k]}
        )

    for k in range(rows):
        near(k, 0).start()
        near(k, 1).start()

    def finish(k):
        near(k, 1).wait_recv()
        over(k).wait_recv()
        total = in_ref[me, order[k]].astype(F32) + rx_ref[1, k].astype(F32)
        total = total + far_ref[k].astype(F32)
        if k == rows - 1:
            out_ref[row] = total.astype(BF16)
        else:
            fin_ref[k] = total.astype(BF16)
            home(k).start()

    for k in range(rows):
        near(k, 0).wait_recv()
        tot_ref[k] = (in_ref[across, order[k]].astype(F32) + rx_ref[0, k].astype(F32)).astype(BF16)
        over(k).start()
        if k >= 1:
            finish(k - 1)
    finish(rows - 1)
    cap = out_ref.shape[1]
    sum_ref[...] = combined(t_ref, out_ref[row], row, cap)
    for k, gap in enumerate(far_first(rows)):
        source = (row + rows - gap) % rows
        home(k).wait_recv()
        sum_ref[...] += combined(t_ref, out_ref[source], source, cap)
    grad, normed = sum_ref[...], normed_ref[...]
    mid = cot_ref[...].astype(F32) + norm_back(
        grad, normed, own_features(s_ref, 2), rstd_ref[...], st_ref, all_ref, st_send, st_recv
    )
    mid_ref[...] = mid
    vec_ref[...] = jnp.zeros(vec_ref.shape, F32)
    vec_ref[0:1] = jnp.sum(grad * normed, axis=0, keepdims=True)
    vec_ref[1:2] = jnp.sum(grad, axis=0, keepdims=True)
    vec_ref[2:3] = jnp.sum(mid, axis=0, keepdims=True)
    for k in range(rows):
        near(k, 0).wait_send()
        near(k, 1).wait_send()
        over(k).wait_send()
        if k < rows - 1:
            home(k).wait_send()


def giveback(parts, target, cot, normed, rstd, gain, rows, collective):
    block = parts.shape[2:]
    one = pltpu.VMEM((rows,) + block, BF16)
    return pl.pallas_call(
        functools.partial(giveback_kernel, rows),
        out_shape=(
            jax.ShapeDtypeStruct(cot.shape, F32),
            jax.ShapeDtypeStruct((8, cot.shape[1]), F32),
        ),
        in_specs=[VSPEC] * 6,
        out_specs=(VSPEC,) * 2,
        scratch_shapes=[
            pltpu.VMEM(cot.shape, F32),
            one,
            pltpu.VMEM((2, rows) + block, BF16),
            one,
            one,
            one,
            pltpu.VMEM((8, cot.shape[0]), F32),
            pltpu.VMEM((COLS, 8, cot.shape[0]), F32),
            DMA((3, rows)),
            DMA((3, rows)),
            DMA((rows - 1,)),
            DMA((rows - 1,)),
            DMA((COLS - 1,)),
            DMA((COLS - 1,)),
        ],
        compiler_params=params(collective),
    )(parts, target, cot, normed, rstd, gain)


def end_kernel(
    rows,
    w_ref,
    s_ref,
    e_ref,
    t_ref,
    mid_ref,
    wo_ref,
    so_ref,
    lo_ref,
    px_ref,
    pt_ref,
    wr_ref,
    sr_ref,
    p_send,
    p_recv,
    l_send,
    l_recv,
    send,
    recv,
):
    row, _, level, side, partner = line_places(rows)
    levels = rows // 2
    peers = [(row + k) % rows for k in far_first(rows)]
    greet([{"row": p} for p in peers])
    gaps = far_first(levels)
    targets = [(level + k) % levels for k in gaps] + [level]

    def cross(n):
        src = w_ref.at[2 * targets[n] + 1 - side]
        return push(src, px_ref.at[n], p_send.at[n], p_recv.at[n], {"row": partner})

    def along(n):
        peer = {"row": 2 * targets[n] + side}
        return push(pt_ref.at[n], wr_ref.at[n], l_send.at[n], l_recv.at[n], peer)

    def total(n):
        return w_ref[2 * targets[n] + side].astype(F32) + px_ref[n].astype(F32)

    for n in range(levels):
        cross(n).start()
    copies = []
    for k, peer in enumerate(peers):
        copy = push(s_ref.at[peer], sr_ref.at[k], send.at[k], recv.at[k], {"row": peer})
        copy.start()
        copies.append(copy)
    for n in range(levels - 1):
        cross(n).wait_recv()
        pt_ref[n] = total(n).astype(BF16)
        along(n).start()
    result = mid_ref[...]
    for r in range(rows):
        result = result + combined(t_ref, e_ref[r], r, e_ref.shape[1])
    lo_ref[...] = result.astype(BF16)
    small = s_ref[row]
    for k, copy in enumerate(copies):
        copy.wait_recv()
        small = small + sr_ref[k]
    so_ref[...] = small
    cross(levels - 1).wait_recv()
    mine = total(levels - 1)
    for n in range(levels - 1):
        along(n).wait_recv()
        mine = mine + wr_ref[n].astype(F32)
    wo_ref[...] = mine
    for n in range(levels):
        cross(n).wait_send()
        if n < levels - 1:
            along(n).wait_send()
    for copy in copies:
        copy.wait_send()


def end_scatter(w, s, outs, target, mid, rows, collective):
    levels = rows // 2
    one = w.shape[1:]
    return pl.pallas_call(
        functools.partial(end_kernel, rows),
        out_shape=(
            jax.ShapeDtypeStruct(one, F32),
            jax.ShapeDtypeStruct(s.shape[1:], F32),
            jax.ShapeDtypeStruct(mid.shape, BF16),
        ),
        in_specs=[VSPEC] * 5,
        out_specs=(VSPEC,) * 3,
        scratch_shapes=[
            pltpu.VMEM((levels,) + one, w.dtype),
            pltpu.VMEM((levels - 1,) + one, w.dtype),
            pltpu.VMEM((levels - 1,) + one, w.dtype),
            pltpu.VMEM((rows - 1,) + s.shape[1:], s.dtype),
            DMA((levels,)),
            DMA((levels,)),
            DMA((levels - 1,)),
            DMA((levels - 1,)),
            DMA((rows - 1,)),
            DMA((rows - 1,)),
        ],
        compiler_params=params(collective),
    )(w, s, outs, target, mid)


def expert_kernel(
    x_ref,
    g_ref,
    up_hbm,
    bias_ref,
    down_hbm,
    part_ref,
    gx_ref,
    gup_hbm,
    gbu_ref,
    gdown_hbm,
    gbd_ref,
    up_ref,
    down_ref,
    gup_ref,
    gdown_ref,
    xs_ref,
    gs_ref,
    sum_ref,
    gsum_ref,
    in_sems,
    out_sems,
):
    cols, rows, cap, both = x_ref.shape
    width = both // 2
    slots = rows * cap
    count, _, hidden_units = up_ref.shape
    chunk = 256
    loads = []
    for e in range(count):
        for j, (src, dst) in enumerate(((up_hbm, up_ref), (down_hbm, down_ref))):
            copy = pltpu.make_async_copy(src.at[e], dst.at[e], in_sems.at[j, e])
            copy.start()
            loads.append(copy)

    def gup_out(e, f):
        cut = pl.ds(pl.multiple_of(f * chunk, chunk), chunk)
        return pltpu.make_async_copy(
            gup_ref.at[e, :, cut], gup_hbm.at[e, :, cut], out_sems.at[0, e, f]
        )

    def gdown_out(e, f):
        cut = pl.ds(pl.multiple_of(f * chunk, chunk), chunk)
        return pltpu.make_async_copy(
            gdown_ref.at[e, cut], gdown_hbm.at[e, cut], out_sems.at[1, e, f]
        )

    for e in range(count):
        lanes = slice(e * width, (e + 1) * width)
        for ref, dst in ((x_ref, xs_ref), (g_ref, gs_ref)):
            blocks = [ref[b].reshape(slots, both)[:, lanes] for b in range(cols)]
            dst[...] = jnp.concatenate(blocks, axis=1)
        gbd_ref[e] = jnp.sum(gs_ref[...].astype(F32), axis=0, keepdims=True)
        sum_ref[...] = jnp.zeros(sum_ref.shape, F32)
        gsum_ref[...] = jnp.zeros(gsum_ref.shape, F32)
        loads[2 * e].wait()
        loads[2 * e + 1].wait()

        def body(f, carry, e=e):
            cut = pl.ds(pl.multiple_of(f * chunk, chunk), chunk)
            x, g = xs_ref[...], gs_ref[...]
            up, down = up_ref[e, :, cut], down_ref[e, cut, :]
            pre = nn(x, up) + bias_ref[e, :, cut].astype(F32)
            cdf = 0.5 * (1.0 + lax.erf(pre * (0.5**0.5)))
            slope = cdf + pre * (jnp.exp(-0.5 * pre * pre) * 0.3989422804014327)
            hidden = (pre * cdf).astype(BF16)
            grad = nt(g, down) * slope
            grad = grad.astype(BF16)
            sum_ref[...] += nn(hidden, down)
            gsum_ref[...] += nt(grad, up)
            gdown_ref[e, cut, :] = tn(hidden, g)
            gdown_out(e, f).start()
            gup_ref[e, :, cut] = tn(x, grad)
            gup_out(e, f).start()
            gbu_ref[e, :, cut] = jnp.sum(grad.astype(F32), axis=0, keepdims=True)
            return carry

        lax.fori_loop(0, hidden_units // chunk, body, 0)
        for b in range(cols):
            cut = slice(b * width, (b + 1) * width)
            part_ref[b, :, :, lanes] = sum_ref[:, cut].astype(BF16).reshape(rows, cap, width)
            gx_ref[b, :, :, lanes] = gsum_ref[:, cut].astype(BF16).reshape(rows, cap, width)
    for e in range(count):
        for f in range(hidden_units // chunk):
            gdown_out(e, f).wait()
            gup_out(e, f).wait()


def experts(x, g, w_up, bias_up, w_down):
    cols, rows, cap, _ = x.shape
    count, features, hidden = w_up.shape
    slots = rows * cap
    anywhere = pl.BlockSpec(memory_space=pl.ANY)
    return pl.pallas_call(
        expert_kernel,
        out_shape=(
            jax.ShapeDtypeStruct(x.shape, BF16),
            jax.ShapeDtypeStruct(x.shape, BF16),
            jax.ShapeDtypeStruct(w_up.shape, F32),
            jax.ShapeDtypeStruct((count, 1, hidden), F32),
            jax.ShapeDtypeStruct(w_down.shape, F32),
            jax.ShapeDtypeStruct((count, 1, features), F32),
        ),
        in_specs=[VSPEC, VSPEC, anywhere, VSPEC, anywhere],
        out_specs=(VSPEC, VSPEC, anywhere, VSPEC, anywhere, VSPEC),
        scratch_shapes=[
            pltpu.VMEM(w_up.shape, BF16),
            pltpu.VMEM(w_down.shape, BF16),
            pltpu.VMEM(w_up.shape, F32),
            pltpu.VMEM(w_down.shape, F32),
            pltpu.VMEM((slots, features), BF16),
            pltpu.VMEM((slots, features), BF16),
            pltpu.VMEM((slots, features), F32),
            pltpu.VMEM((slots, features), F32),
            DMA((2, count)),
            DMA((2, count, hidden // 256)),
        ],
        compiler_params=params(),
    )(x, g, w_up, bias_up.reshape(count, 1, hidden), w_down)


def per_device(
    layer_in,
    cotangent,
    token_ids,
    hash_table,
    prefix_len,
    w_query,
    w_key,
    w_value,
    w_output,
    bias_query,
    bias_value,
    gain_attn,
    shift_attn,
    gain_moe,
    shift_moe,
    bias_output,
    w_up,
    bias_up,
    w_down,
    bias_down,
):
    rows = lax.axis_size("row")
    row = lax.axis_index("row")
    col = lax.axis_index("col")
    tokens, width = layer_in.shape
    heads = width // HD
    seq_len = min(LENGTH, tokens * rows)
    group = seq_len // tokens
    low = -(-PREFIX_MAX // (2 * tokens))
    share = w_query.shape[0]
    bias_share = bias_query.shape[0]

    def line(v):
        return jnp.pad(v.astype(F32), (0, 128 - v.shape[0]))

    small = jnp.stack(
        [
            line(gain_attn),
            line(shift_attn),
            line(gain_moe),
            line(shift_moe),
            line(bias_output),
            line(bias_query.T.reshape(-1)),
            line(bias_value.T.reshape(-1)),
            jnp.zeros((128,), F32),
        ]
    )
    expert_total = EXP_DEV * rows
    capacity = max(2, 2 * tokens // expert_total)
    table = jnp.pad(hash_table, (0, -hash_table.shape[0] % (128 * 128)))
    table = table.reshape(-1, 128).astype(BF16)

    weights = jnp.concatenate([w_query, w_key, w_value, w_output], axis=1)
    x_all, g_own, w_all, s_all, target = start_gather(
        layer_in, cotangent, token_ids[None], table, weights, small, rows, capacity
    )

    queries, keys_values, h_one, normed_one, rstd_one = project(x_all, w_all, s_all)
    seq_hit = row // group == jnp.arange(prefix_len.shape[0], dtype=jnp.int32)
    prefix = jnp.sum(jnp.where(seq_hit, prefix_len, 0))
    info = prefix.astype(jnp.int32).reshape(1)
    kv_all, attended, attended_low, lse, g_all = attention_forward(
        info, queries, keys_values, g_own, group, low, 1
    )
    mid, normed_two, rstd_two, h_two = branch(attended_low, w_all, layer_in, s_all, 2)

    received = dispatch(h_two, target, rows, capacity, 4)
    parts, grad_parts, grad_w_up, grad_bias_up, grad_w_down, grad_bias_down = experts(
        received, g_all, w_up, bias_up, w_down
    )
    grad_mid, vectors = giveback(
        grad_parts, target, cotangent, normed_two, rstd_two, s_all, rows, 5
    )
    grad_attended, delta, grad_w_out = mid_gradient(grad_mid, w_all, attended, attended_low, 7)
    down_own = lax.dynamic_slice_in_dim(bias_down, col * width, width, 1).astype(F32)
    down_own = down_own.reshape(1, EXP_DEV * width)
    grad_qkv, outs = attention_backward(
        info,
        queries,
        kv_all,
        grad_attended,
        lse,
        delta,
        parts,
        down_own,
        group,
        low,
        8,
    )
    grad_bias = jnp.sum(grad_qkv, axis=0, dtype=F32)
    grad_in, outs, weight_terms, shared = input_gradient(
        grad_qkv,
        w_all,
        outs,
        h_one,
        grad_w_out,
        grad_mid,
        normed_one,
        rstd_one,
        s_all,
        vectors,
        9,
    )
    vectors = shared[:, :5, tokens : tokens + width]
    vectors = vectors.transpose(1, 0, 2).reshape(5, rows, share).transpose(1, 0, 2)

    def by_row(v):
        v = v.reshape(heads, rows, bias_share).transpose(1, 0, 2).reshape(rows, 1, -1)
        return jnp.pad(v, ((0, 0), (0, 0), (0, 128 - v.shape[2])))

    small_terms = jnp.concatenate(
        [
            jnp.pad(vectors, ((0, 0), (0, 0), (0, 128 - share))),
            by_row(grad_bias[:width]),
            by_row(grad_bias[2 * width :]),
            jnp.zeros((rows, 1, 128), F32),
        ],
        axis=1,
    )
    weight_terms = weight_terms.reshape(rows, share, 4 * width)
    weight_sums, small_sums, layer_out = end_scatter(
        weight_terms, small_terms, outs, target, mid, rows, 11
    )

    def bias_back(v):
        return v[: heads * bias_share].reshape(heads, bias_share).T

    return (
        layer_out,
        grad_in,
        weight_sums[:, :width],
        weight_sums[:, width : 2 * width],
        weight_sums[:, 2 * width : 3 * width],
        weight_sums[:, 3 * width :],
        bias_back(small_sums[5]),
        bias_back(small_sums[6]),
        small_sums[0, :share],
        small_sums[1, :share],
        small_sums[2, :share],
        small_sums[3, :share],
        small_sums[4, :share],
        grad_w_up,
        grad_bias_up[:, 0],
        grad_w_down,
        grad_bias_down[:, 0],
    )


def solution(mesh):
    placed = (
        P("row", "col"),
        P("row", "col"),
        P("row"),
        P(),
        P(),
        P("row", "col"),
        P("row", "col"),
        P("row", "col"),
        P("row", "col"),
        P("row", "col"),
        P("row", "col"),
        P("row"),
        P("row"),
        P("row"),
        P("row"),
        P("row"),
        P("row", None, "col"),
        P("row", "col"),
        P("row", "col", None),
        P("row", None),
    )
    return jax.shard_map(
        per_device,
        mesh=mesh,
        in_specs=placed,
        out_specs=(
            P("row", "col"),
            P("row", "col"),
            P("row", "col"),
            P("row", "col"),
            P("row", "col"),
            P("row", "col"),
            P("row", "col"),
            P("row", "col"),
            P("row"),
            P("row"),
            P("row"),
            P("row"),
            P("row"),
            P("row", None, "col"),
            P("row", "col"),
            P("row", "col", None),
            P("row", None),
        ),
        check_vma=False,
    )
```

```python
import functools

import jax
import jax.numpy as jnp
from jax import lax
from jax.experimental import pallas as pl
from jax.experimental.pallas import tpu as pltpu
from jax.sharding import PartitionSpec as P

D = 768
HD = 64
EXP_DEV = 2
LENGTH = 8192
PREFIX_MAX = 4096
COLS = 4

F32 = jnp.float32
BF16 = jnp.bfloat16
MESH = pl.DeviceIdType.MESH
LOG2E = 1.4426950408889634

epsilon = 1e-05
neg_big = -1e30

VSPEC = pl.BlockSpec(memory_space=pltpu.VMEM)
SSPEC = pl.BlockSpec(memory_space=pltpu.SMEM)
VMEM_BYTES = 64 * 1000 * 1000
DMA = pltpu.SemaphoreType.DMA


def params(collective=None):
    if collective is None:
        return pltpu.CompilerParams(vmem_limit_bytes=VMEM_BYTES)
    return pltpu.CompilerParams(
        vmem_limit_bytes=VMEM_BYTES, collective_id=collective, has_side_effects=True
    )


def push(src, dst, send_sem, recv_sem, peer):
    return pltpu.make_async_remote_copy(
        src_ref=src,
        dst_ref=dst,
        send_sem=send_sem,
        recv_sem=recv_sem,
        device_id=peer,
        device_id_type=MESH,
    )


def greet(peers):
    barrier = pltpu.get_barrier_semaphore()
    for peer in peers:
        pl.semaphore_signal(barrier, inc=1, device_id=peer, device_id_type=MESH)
    pl.semaphore_wait(barrier, len(peers))


def col_places():
    me = lax.axis_index("col")
    sib = me + 1 - 2 * (me % 2)
    across = (me + 2) % COLS
    diag = (sib + 2) % COLS
    return me, sib, across, diag


def line_places(group):
    row = lax.axis_index("row")
    place = row % group
    level, side = place // 2, place % 2
    return row, place, level, side, row + 1 - 2 * side


def paired(row, mask):
    other, bit = row, 1
    while bit <= mask:
        if mask & bit:
            other = other + bit * (1 - 2 * ((row // bit) % 2))
        bit *= 2
    return other


def far_first(rows):
    return sorted(range(1, rows), key=lambda k: -min(k, rows - k))


def nt(left, right):
    return lax.dot_general(left, right, (((1,), (1,)), ((), ())), preferred_element_type=F32)


def nn(left, right):
    return lax.dot_general(left, right, (((1,), (0,)), ((), ())), preferred_element_type=F32)


def tn(left, right):
    return lax.dot_general(left, right, (((0,), (0,)), ((), ())), preferred_element_type=F32)


def side_by_side(v):
    half = v.shape[0] // 2
    return jnp.concatenate([v[:half], v[half:]], axis=1)


def number(shape, axis):
    return lax.broadcasted_iota(jnp.int32, shape, axis)


def route(ids, table, experts, cap):
    tokens = ids.shape[1]
    pick = jnp.where(number((table.shape[0], tokens), 0) == ids >> 7, 1.0, 0.0).astype(BF16)
    found = tn(table, pick)
    expert = jnp.where(number((128, tokens), 0) == ids & 127, found, 0.0)
    expert = jnp.sum(expert, axis=0, keepdims=True)
    hit = number((experts, tokens), 0).astype(F32) == expert
    pair = (tokens, tokens)
    earlier = jnp.where(number(pair, 0) < number(pair, 1), 1.0, 0.0).astype(BF16)
    before = nn(jnp.where(hit, 1.0, 0.0).astype(BF16), earlier)
    slot = jnp.sum(jnp.where(hit, before, 0.0), axis=0, keepdims=True)
    return (expert * cap + slot).astype(jnp.int32)


def all_features(s_ref, i):
    rows = s_ref.shape[0]
    return jnp.concatenate([s_ref[r, i : i + 1, : D // rows] for r in range(rows)], axis=1)


def own_features(s_ref, i):
    rows = s_ref.shape[0]
    per = rows // COLS
    block = s_ref[pl.ds(lax.axis_index("col") * per, per)]
    return jnp.concatenate([block[r, i : i + 1, : D // rows] for r in range(per)], axis=1)


def head_features(s_ref, i, heads):
    rows = s_ref.shape[0]
    size = HD // rows
    cuts = [slice(h * size, (h + 1) * size) for h in range(heads)]
    return jnp.concatenate([s_ref[r, i : i + 1, c] for c in cuts for r in range(rows)], axis=1)


def slots_of(target_ref, row, count):
    base = row * count
    slot = base + lax.broadcasted_iota(jnp.int32, (count, target_ref.shape[1]), 0)
    return jnp.where(slot == target_ref[...], 1.0, 0.0).astype(BF16)


def placed(target_ref, v, row, cap):
    return side_by_side(nn(slots_of(target_ref, row, 2 * cap), v).astype(BF16))


def combined(target_ref, block, row, cap):
    width = block.shape[1] // 2
    stacked = jnp.concatenate([block[:, :width], block[:, width:]], axis=0)
    return tn(slots_of(target_ref, row, 2 * cap), stacked)


def start_kernel(
    rows,
    pieces,
    x_hbm,
    g_hbm,
    ids_ref,
    table_ref,
    w_ref,
    s_ref,
    xo_ref,
    go_ref,
    wo_ref,
    so_ref,
    t_ref,
    x_ref,
    g_ref,
    f_sems,
    xp_ref,
    gp_ref,
    c_send,
    c_recv,
    r_send,
    r_recv,
    l_send,
    l_recv,
):
    me, sib, across, _ = col_places()
    row, _, level, side, partner = line_places(rows)
    levels = rows // 2
    order = far_first(rows)
    peers = [{"row": (row + k) % rows} for k in order]
    fetch = [
        pltpu.make_async_copy(x_hbm, x_ref, f_sems.at[0]),
        pltpu.make_async_copy(g_hbm, g_ref, f_sems.at[1]),
    ]
    fetch[0].start()
    fetch[1].start()
    greet(peers + [{"col": sib}, {"col": across}])
    fetch[0].wait()
    fetch[1].wait()
    xp_ref[...] = side_by_side(x_ref[...])
    step = xp_ref.shape[0] // pieces
    cap = gp_ref.shape[1]
    to_up, to_down = level < levels - 1, level > 0

    def weight(at, way, src=None):
        dst = wo_ref.at[2 * at + side]
        peer = (row + 2, row - 2, partner)[way]
        return push(
            dst if src is None else src,
            dst,
            l_send.at[way, at],
            l_recv.at[way, at],
            {"row": peer},
        )

    def weight_other(at):
        dst = wo_ref.at[2 * at + 1 - side]
        return push(dst, dst, l_send.at[2, at], l_recv.at[2, at], {"row": partner})

    @pl.when(to_up)
    def _():
        weight(level, 0, w_ref).start()

    @pl.when(to_down)
    def _():
        weight(level, 1, w_ref).start()

    weight(level, 2, w_ref).start()
    sent = []
    for i in range(pieces):
        part = pl.ds(i * step, step)
        for way, peer in ((0, across), (1, sib)):
            copy = push(
                xp_ref.at[part],
                xo_ref.at[me, part],
                c_send.at[way, i],
                c_recv.at[way, i],
                {"col": peer},
            )
            copy.start()
            sent.append(copy)
    row_copies = []
    for k, peer in enumerate(peers):
        copy = push(s_ref, so_ref.at[row], r_send.at[0, k], r_recv.at[0, k], peer)
        copy.start()
        row_copies.append(copy)

    def send_rows(k):
        target = (row + order[k]) % rows
        gp_ref[k] = placed(t_ref, g_ref[...], target, cap)
        copy = push(gp_ref.at[k], go_ref.at[row], r_send.at[1, k], r_recv.at[1, k], peers[k])
        copy.start()
        row_copies.append(copy)

    t_ref[...] = route(ids_ref[...], table_ref[...], EXP_DEV * rows, cap)
    send_rows(0)
    xo_ref[me] = xp_ref[...]
    wo_ref[row] = w_ref[...]
    so_ref[row] = s_ref[...]
    todo = list(range(1, rows - 1))

    def pass_on(k):
        at = level - k

        @pl.when(at >= 0)
        def _():
            weight(at, 0).wait_recv()

            @pl.when(to_up)
            def _():
                weight(at, 0).start()

            weight(at, 2).start()

        up = level + k

        @pl.when(up < levels)
        def _():
            weight(up, 1).wait_recv()

            @pl.when(to_down)
            def _():
                weight(up, 1).start()

            weight(up, 2).start()

    late = []
    for k in range(1, max(levels, pieces + 1)):
        if k < levels:
            pass_on(k)
        if k <= pieces:
            part = pl.ds((k - 1) * step, step)
            sent[2 * k - 2].wait_recv()
            copy = push(
                xo_ref.at[across, part],
                xo_ref.at[across, part],
                c_send.at[2, k - 1],
                c_recv.at[2, k - 1],
                {"col": sib},
            )
            copy.start()
            late.append(copy)
        for _ in range(2):
            if todo:
                send_rows(todo.pop(0))
    while todo:
        send_rows(todo.pop(0))
    go_ref[row] = placed(t_ref, g_ref[...], row, cap)
    for i in range(pieces):
        sent[2 * i].wait_send()
        sent[2 * i + 1].wait()
        late[i].wait()
    for at in range(levels):
        weight_other(at).wait_recv()
        weight(at, 2).wait_send()

        @pl.when((at <= level) & to_up)
        def _(at=at):
            weight(at, 0).wait_send()

        @pl.when((at >= level) & to_down)
        def _(at=at):
            weight(at, 1).wait_send()

    for copy in row_copies:
        copy.wait()


def start_gather(x, g, ids, table, w, s, rows, cap):
    pieces = 4
    tokens, width = x.shape
    packed = (tokens // 2, 2 * width)
    return pl.pallas_call(
        functools.partial(start_kernel, rows, pieces),
        out_shape=(
            jax.ShapeDtypeStruct((COLS,) + packed, x.dtype),
            jax.ShapeDtypeStruct((rows, cap, 2 * width), g.dtype),
            jax.ShapeDtypeStruct((rows,) + w.shape, w.dtype),
            jax.ShapeDtypeStruct((rows,) + s.shape, s.dtype),
            jax.ShapeDtypeStruct((1, tokens), jnp.int32),
        ),
        in_specs=[pl.BlockSpec(memory_space=pl.ANY)] * 2 + [VSPEC] * 4,
        out_specs=(VSPEC,) * 5,
        scratch_shapes=[
            pltpu.VMEM(x.shape, x.dtype),
            pltpu.VMEM(g.shape, g.dtype),
            DMA((2,)),
            pltpu.VMEM(packed, x.dtype),
            pltpu.VMEM((rows - 1, cap, 2 * width), g.dtype),
            DMA((3, pieces)),
            DMA((3, pieces)),
            DMA((2, rows - 1)),
            DMA((2, rows - 1)),
            DMA((3, rows // 2)),
            DMA((3, rows // 2)),
        ],
        compiler_params=params(0),
    )(x, g, ids, table, w, s)


def project_kernel(
    x_ref, w_ref, s_ref, q_ref, kv_ref, h_ref, n_ref, r_ref
):
    me = lax.axis_index("col")
    half, width = x_ref.shape[1], x_ref.shape[2] // 2
    gain, shift = all_features(s_ref, 0), all_features(s_ref, 1)
    query = head_features(s_ref, 5, width // HD)
    value = head_features(s_ref, 6, width // HD)
    bias = jnp.concatenate([query, jnp.zeros_like(query), value], axis=1)
    w = w_ref[...].reshape(D, 4 * width)[:, : 3 * width]
    step = min(half, 256)
    for i in range(2 * half // step):
        side, start = i * step // half, i * step % half
        rows, feats = slice(start, start + step), slice(side * width, (side + 1) * width)
        x = jnp.concatenate([x_ref[b, rows, feats] for b in range(COLS)], axis=1).astype(F32)
        mean = jnp.mean(x, axis=-1, keepdims=True)
        centred = x - mean
        rstd = lax.rsqrt(jnp.mean(centred * centred, axis=-1, keepdims=True) + epsilon)
        h = (centred * rstd * gain + shift).astype(BF16)
        out = slice(i * step, (i + 1) * step)
        h_ref[out] = h
        n_ref[out] = (x_ref[me, rows, feats].astype(F32) - mean) * rstd
        r_ref[out] = rstd
        qkv = (nn(h, w) + bias).astype(BF16)
        q_ref[out] = qkv[:, :width] * jnp.asarray(HD**-0.5, BF16)
        kv_ref[out] = qkv[:, width:]


def project(x, w, s):
    tokens, width = 2 * x.shape[1], x.shape[2] // 2
    return pl.pallas_call(
        project_kernel,
        out_shape=(
            jax.ShapeDtypeStruct((tokens, width), BF16),
            jax.ShapeDtypeStruct((tokens, 2 * width), BF16),
            jax.ShapeDtypeStruct((tokens, D), BF16),
            jax.ShapeDtypeStruct((tokens, width), F32),
            jax.ShapeDtypeStruct((tokens, 1), F32),
        ),
        in_specs=[VSPEC] * 3,
        out_specs=(VSPEC,) * 5,
        compiler_params=params(),
    )(x, w, s)


def mid_kernel(
    pieces,
    x_ref,
    w_ref,
    att_ref,
    low_ref,
    do_ref,
    delta_ref,
    gw_ref,
    xp_ref,
    xo_ref,
    wide_ref,
    c_send,
    c_recv,
):
    me, sib, across, _ = col_places()
    greet([{"col": sib}, {"col": across}])
    xp_ref[...] = side_by_side(x_ref[...].astype(BF16))
    step = xp_ref.shape[0] // pieces
    sent, late = [], []
    for i in range(pieces):
        part = pl.ds(i * step, step)
        for way, peer in ((0, across), (1, sib)):
            copy = push(
                xp_ref.at[part],
                xo_ref.at[me, part],
                c_send.at[way, i],
                c_recv.at[way, i],
                {"col": peer},
            )
            copy.start()
            sent.append(copy)
    xo_ref[me] = xp_ref[...]
    tokens, width = x_ref.shape
    w = w_ref[...].reshape(D, 4 * width)[:, 3 * width :]
    for i in range(pieces):
        part = pl.ds(i * step, step)
        sent[2 * i].wait_recv()
        copy = push(
            xo_ref.at[across, part],
            xo_ref.at[across, part],
            c_send.at[2, i],
            c_recv.at[2, i],
            {"col": sib},
        )
        copy.start()
        late.append(copy)
    for i in range(pieces):
        sent[2 * i].wait_send()
        sent[2 * i + 1].wait()
        late[i].wait()
        rows = slice(i * step, (i + 1) * step)
        for half in range(2):
            feats = slice(half * width, (half + 1) * width)
            start = half * (tokens // 2) + i * step
            out = slice(start, start + step)
            wide = jnp.concatenate([xo_ref[b, rows, feats] for b in range(COLS)], axis=1)
            wide_ref[out] = wide
            do = nn(wide, w).astype(BF16)
            do_ref[out] = do
            both = (do.astype(F32) * att_ref[out]).T
            for h in range(width // HD):
                delta_ref[h : h + 1, out] = jnp.sum(
                    both[h * HD : (h + 1) * HD], axis=0, keepdims=True
                )
    gw_ref[...] = tn(wide_ref[...], low_ref[...]).astype(BF16)


def mid_gradient(x, w, attended, low, collective):
    pieces = 4
    tokens, width = x.shape
    packed = (tokens // 2, 2 * width)
    return pl.pallas_call(
        functools.partial(mid_kernel, pieces),
        out_shape=(
            jax.ShapeDtypeStruct((tokens, width), BF16),
            jax.ShapeDtypeStruct((8, tokens), F32),
            jax.ShapeDtypeStruct((D, width), BF16),
        ),
        in_specs=[VSPEC] * 4,
        out_specs=(VSPEC,) * 3,
        scratch_shapes=[
            pltpu.VMEM(packed, BF16),
            pltpu.VMEM((COLS,) + packed, BF16),
            pltpu.VMEM((tokens, D), BF16),
            DMA((3, pieces)),
            DMA((3, pieces)),
        ],
        compiler_params=params(collective),
    )(x, w, attended, low)


def col_peers():
    me = lax.axis_index("col")
    return [{"col": (me + k) % COLS} for k in range(1, COLS)]


def to_rows(columns):
    lane = lax.broadcasted_iota(jnp.int32, (columns[0].shape[0], 128), 1)
    v = jnp.zeros(lane.shape, F32)
    for i, column in enumerate(columns):
        v = jnp.where(lane == i, column, v)
    return v.T[:8]


def to_columns(lines):
    place = lax.broadcasted_iota(jnp.int32, (8, lines[0].shape[1]), 0)
    v = jnp.zeros(place.shape, F32)
    for i, one in enumerate(lines):
        v = jnp.where(place == i, one, v)
    v = v.T
    return [v[:, i : i + 1] for i in range(len(lines))]


def share(snd_ref, all_ref, send, recv):
    me = lax.axis_index("col")
    copies = []
    for k, peer in enumerate(col_peers()):
        copy = push(snd_ref, all_ref.at[me], send.at[k], recv.at[k], peer)
        copy.start()
        copies.append(copy)
    all_ref[me] = snd_ref[...]
    for copy in copies:
        copy.wait()


def norm_back(grad, normed, gain, rstd, snd_ref, all_ref, send, recv):
    tokens = grad.shape[0]
    scaled = grad * gain
    sums = [
        jnp.sum(scaled, axis=-1, keepdims=True),
        jnp.sum(scaled * normed, axis=-1, keepdims=True),
    ]
    snd_ref[:, :tokens] = to_rows(sums)
    share(snd_ref, all_ref, send, recv)
    total = all_ref[0, :, :tokens]
    for b in range(1, COLS):
        total = total + all_ref[b, :, :tokens]
    total = total / D
    first, second = to_columns([total[0:1], total[1:2]])
    return rstd * (scaled - first - normed * second)


def line_greet(levels, row, level, partner):
    barrier = pltpu.get_barrier_semaphore()
    me = lax.axis_index("col")
    for k in range(1, COLS):
        peer = {"col": (me + k) % COLS}
        pl.semaphore_signal(barrier, inc=1, device_id=peer, device_id_type=MESH)
    pl.semaphore_signal(barrier, inc=1, device_id={"row": partner}, device_id_type=MESH)

    @pl.when(level > 0)
    def _():
        pl.semaphore_signal(barrier, inc=1, device_id={"row": row - 2}, device_id_type=MESH)

    @pl.when(level < levels - 1)
    def _():
        pl.semaphore_signal(barrier, inc=1, device_id={"row": row + 2}, device_id_type=MESH)

    count = COLS + (level > 0).astype(jnp.int32) + (level < levels - 1).astype(jnp.int32)
    pl.semaphore_wait(barrier, count)


def seen(key_start, query_start, shape, prefix):
    key = key_start + lax.broadcasted_iota(jnp.int32, shape, 0)
    query = query_start + lax.broadcasted_iota(jnp.int32, shape, 1)
    return (key < prefix) | (key <= query)


def forward_kernel(
    group,
    low,
    pieces,
    qb,
    info_ref,
    q_ref,
    kv_ref,
    g_ref,
    out_ref,
    o_ref,
    ob_ref,
    lse_ref,
    ga_ref,
    m_ref,
    acc_ref,
    u_send,
    u_recv,
    d_send,
    d_recv,
    x_send,
    x_recv,
    g_send,
    g_recv,
):
    levels = group // 2
    row, place, level, side, partner = line_places(group)
    prefix = info_ref[0]
    tokens, width = q_ref.shape
    heads = width // HD
    step = tokens // pieces
    line_greet(levels, row, level, partner)

    def make(at, i, way, src=None):
        part = pl.ds(i * step, step)
        dst = out_ref.at[2 * at + side, part]
        sems = ((u_send, u_recv), (d_send, d_recv), (x_send, x_recv))[way]
        peer = (row + 2, row - 2, partner)[way]
        return push(
            dst if src is None else src.at[part],
            dst,
            sems[0].at[at, i],
            sems[1].at[at, i],
            {"row": peer},
        )

    def other(at, i):
        part = pl.ds(i * step, step)
        dst = out_ref.at[2 * at + 1 - side, part]
        return push(dst, dst, x_send.at[at, i], x_recv.at[at, i], {"row": partner})

    def when(cond, run):
        @pl.when(cond)
        def _():
            for i in range(pieces):
                run(i)

    to_up = level < levels - 1
    own_down = (level > 0) & (level < low)
    own_side = (level < low) | (side == 0)
    for i in range(pieces):

        @pl.when(to_up)
        def _(i=i):
            make(level, i, 0, kv_ref).start()

        @pl.when(own_side)
        def _(i=i):
            make(level, i, 2, kv_ref).start()

        @pl.when(own_down)
        def _(i=i):
            make(level, i, 1, kv_ref).start()

    me = lax.axis_index("col")
    wide = []
    for k in range(1, COLS):
        peer = {"col": (me + k) % COLS}
        copy = push(g_ref, ga_ref.at[me], g_send.at[k - 1], g_recv.at[k - 1], peer)
        copy.start()
        wide.append(copy)
    ga_ref[me] = g_ref[...]
    out_ref[place] = kv_ref[...]
    m_ref[...] = jnp.full(m_ref.shape, neg_big, F32)
    acc_ref[...] = jnp.zeros(acc_ref.shape, F32)
    units = [(h, i) for h in range(heads) for i in range(tokens // qb)]

    def block(blk, masked):
        def raw_of(h, i):
            feats = slice(h * HD, (h + 1) * HD)
            raw = nt(out_ref[blk, :, feats], q_ref[i * qb : (i + 1) * qb, feats])
            if masked:
                allowed = seen(blk * tokens, place * tokens + i * qb, raw.shape, prefix)
                raw = jnp.where(allowed, raw, neg_big)
            return raw

        def soften(h, i, raw):
            cols = slice(i * qb, (i + 1) * qb)
            old = m_ref[h : h + 1, cols]
            new = jnp.maximum(old, jnp.max(raw, axis=0, keepdims=True))
            m_ref[h : h + 1, cols] = new
            weights = jnp.exp2((raw - new) * LOG2E).astype(BF16)
            return weights, jnp.exp2((old - new) * LOG2E)

        def gather(h, i, weights, scale):
            cols = slice(i * qb, (i + 1) * qb)
            v = out_ref[blk, :, width + h * HD : width + (h + 1) * HD]
            v_ext = jnp.concatenate([v.T, jnp.ones((16, tokens), BF16)], axis=0)
            acc_ref[h, :, cols] = acc_ref[h, :, cols] * scale + nn(v_ext, weights)

        coming, waiting = raw_of(*units[0]), None
        for n, unit in enumerate(units):
            raw = coming
            if n + 1 < len(units):
                coming = raw_of(*units[n + 1])
            soft = soften(*unit, raw)
            if waiting is not None:
                gather(*waiting)
            waiting = unit + soft
        gather(*waiting)

    def event(e, carry):
        t, cross = e // 2, e % 2
        at = jnp.where(t <= level, level - t, t)
        live = (t <= level) | (t < low)
        line_in = live & (cross == 0)
        coming = t + 1
        via = jnp.where(coming <= level, level - coming, coming)
        relays = (cross == 1) & ((coming <= level) | (coming < low))

        @pl.when(relays & (via < level))
        def _():
            for i in range(pieces):
                make(via, i, 0).wait_recv()

                @pl.when(to_up)
                def _(i=i):
                    make(via, i, 0).start()

                make(via, i, 2).start()

        @pl.when(relays & (via > level))
        def _():
            for i in range(pieces):
                make(via, i, 1).wait_recv()

                @pl.when(level > 0)
                def _(i=i):
                    make(via, i, 1).start()

                make(via, i, 2).start()

        comes = live & (cross == 1) & ((at < low) | (at < level) | (side == 1))
        when(comes, lambda i: other(at, i).wait_recv())
        blk = 2 * at + jnp.where(cross == 0, side, 1 - side)
        needed = line_in | comes

        @pl.when(needed & (blk < place))
        def _():
            block(blk, False)

        @pl.when(needed & (blk >= place))
        def _():
            block(blk, True)

        return carry

    lax.fori_loop(0, 2 * levels, event, 0)

    for h in range(heads):
        total = acc_ref[h, HD : HD + 1, :]
        out = (acc_ref[h, :HD, :] / total).T
        o_ref[:, h * HD : (h + 1) * HD] = out
        ob_ref[:, h * HD : (h + 1) * HD] = out.astype(BF16)
        lse_ref[h : h + 1, :] = m_ref[h : h + 1, :] * LOG2E + jnp.log2(total)

    when(to_up, lambda i: make(level, i, 0, kv_ref).wait_send())
    when(own_side, lambda i: make(level, i, 2, kv_ref).wait_send())
    when(own_down, lambda i: make(level, i, 1, kv_ref).wait_send())
    for k in range(1, levels):
        at = level - k
        when((at >= 0) & to_up, lambda i, at=at: make(at, i, 0).wait_send())
        when(at >= 0, lambda i, at=at: make(at, i, 2).wait_send())
    for k in range(1, low):
        at = level + k
        when((at < low) & (level > 0), lambda i, at=at: make(at, i, 1).wait_send())
        when(at < low, lambda i, at=at: make(at, i, 2).wait_send())
    for copy in wide:
        copy.wait()


def attention_forward(info, q, kv, g, group, low, collective):
    pieces = 4
    levels = group // 2
    tokens, width = q.shape
    heads = width // HD
    return pl.pallas_call(
        functools.partial(forward_kernel, group, low, pieces, tokens // 2),
        out_shape=(
            jax.ShapeDtypeStruct((group,) + kv.shape, kv.dtype),
            jax.ShapeDtypeStruct((tokens, width), F32),
            jax.ShapeDtypeStruct((tokens, width), BF16),
            jax.ShapeDtypeStruct((8, tokens), F32),
            jax.ShapeDtypeStruct((COLS,) + g.shape, g.dtype),
        ),
        in_specs=[SSPEC, VSPEC, VSPEC, VSPEC],
        out_specs=(VSPEC,) * 5,
        scratch_shapes=[
            pltpu.VMEM((8, tokens), F32),
            pltpu.VMEM((heads, HD + 16, tokens), F32),
        ]
        + [DMA((levels, pieces))] * 6
        + [DMA((COLS - 1,))] * 2,
        compiler_params=params(collective),
    )(info, q, kv, g)


def backward_kernel(
    group,
    low,
    pieces,
    kb,
    info_ref,
    q_ref,
    kv_ref,
    do_ref,
    lse_ref,
    delta_ref,
    e_ref,
    bias_ref,
    out_ref,
    eo_ref,
    part_ref,
    rx_ref,
    above_ref,
    below_ref,
    snd_ref,
    acc_ref,
    dqt_ref,
    er_ref,
    u_send,
    u_recv,
    d_send,
    d_recv,
    x_send,
    x_recv,
    e_send,
    e_recv,
):
    levels = group // 2
    row, place, level, side, partner = line_places(group)
    prefix = info_ref[0]
    tokens, width = q_ref.shape
    heads = width // HD
    step = tokens // pieces
    line_greet(levels, row, level, partner)
    me = lax.axis_index("col")
    terms = []
    for k in range(1, COLS):
        peer = (me + k) % COLS
        copy = push(
            e_ref.at[peer], er_ref.at[k - 1], e_send.at[k - 1], e_recv.at[k - 1], {"col": peer}
        )
        copy.start()
        terms.append(copy)
    dqt_ref[...] = jnp.zeros(dqt_ref.shape, F32)

    def block(blk, masked, leaves, at):
        def body(j, carry):
            start = pl.multiple_of(j * kb, kb)
            keys = pl.ds(start, kb)
            for h in range(heads):
                feats = slice(h * HD, (h + 1) * HD)
                vals = slice(width + h * HD, width + (h + 1) * HD)
                k, v = kv_ref[blk, keys, feats], kv_ref[blk, keys, vals]
                q, do = q_ref[:, feats], do_ref[:, feats]
                probs = jnp.exp2(nt(k, q) * LOG2E - lse_ref[h : h + 1, :])
                if masked:
                    allowed = seen(blk * tokens + start, place * tokens, probs.shape, prefix)
                    probs = jnp.where(allowed, probs, 0.0)
                grad = (probs * (nt(v, do) - delta_ref[h : h + 1, :])).astype(BF16)
                part_ref[blk, keys, feats] = nn(grad, q).astype(BF16)
                part_ref[blk, keys, vals] = nn(probs.astype(BF16), do).astype(BF16)
                dqt_ref[feats, :] += nn(k.T, grad)

            @pl.when(leaves)
            def _():
                for n in range(kb // step):
                    cross(at, j * (kb // step) + n).start()

            return carry

        lax.fori_loop(0, tokens // kb, body, 0)

    def cross(at, i):
        part = pl.ds(i * step, step)
        return push(
            part_ref.at[2 * at + 1 - side, part],
            rx_ref.at[at, part],
            x_send.at[at, i],
            x_recv.at[at, i],
            {"row": partner},
        )

    def line(at, i, up):
        part = pl.ds(i * step, step)
        sems = (u_send, u_recv) if up else (d_send, d_recv)
        return push(
            snd_ref.at[at, part],
            (below_ref if up else above_ref).at[at, part],
            sems[0].at[at, i],
            sems[1].at[at, i],
            {"row": row + 2 if up else row - 2},
        )

    def gone(at):
        return (at < low) | (at < level) | ((at == level) & (side == 1))

    def comes(at):
        return (at < low) | (at < level) | ((at == level) & (side == 0))

    def total(at, i, from_above, from_below):
        part = pl.ds(i * step, step)
        acc_ref[...] = part_ref[2 * at + side, part].astype(F32)

        @pl.when(comes(at))
        def _():
            cross(at, i).wait_recv()
            acc_ref[...] += rx_ref[at, part].astype(F32)

        if from_above is not None:

            @pl.when(from_above)
            def _():
                line(at, i, False).wait_recv()
                acc_ref[...] += above_ref[at, part].astype(F32)

        if from_below is not None:

            @pl.when(from_below)
            def _():
                line(at, i, True).wait_recv()
                acc_ref[...] += below_ref[at, part].astype(F32)

    not_top = level < levels - 1
    above = jnp.maximum(low - 1 - level, 0)

    def level_of(t):
        return jnp.where(t < above, low - 1 - t, t - above)

    def event(e, carry):
        t, own = e // 2, e % 2
        at = level_of(t)
        live = (t < above) | (at <= level)

        down = t - (levels - level)

        @pl.when((own == 1) & (down >= 0) & (down < level))
        def _():
            for i in range(pieces):
                total(down, i, not_top, None)
                snd_ref[down, pl.ds(i * step, step)] = acc_ref[...].astype(BF16)
                line(down, i, False).start()

        @pl.when((own == 1) & (t >= 1) & (t - 1 < above))
        def _():
            up = level_of(t - 1)
            for i in range(pieces):
                total(up, i, None, level > 0)
                snd_ref[up, pl.ds(i * step, step)] = acc_ref[...].astype(BF16)
                line(up, i, True).start()

        goes = live & (own == 0) & gone(at)
        blk = 2 * at + jnp.where(own == 1, side, 1 - side)
        needed = goes | (live & (own == 1))

        @pl.when(needed & (blk < place))
        def _():
            block(blk, False, goes, at)

        @pl.when(needed & (blk >= place))
        def _():
            block(blk, True, goes, at)

        return carry

    lax.fori_loop(0, 2 * levels, event, 0)
    for copy in terms:
        copy.wait()

    def finish(r, carry):
        total = e_ref[me, r].astype(F32) + bias_ref[...]
        for k in range(COLS - 1):
            total = total + er_ref[k, r].astype(F32)
        eo_ref[r] = total.astype(BF16)
        return carry

    lax.fori_loop(0, e_ref.shape[1], finish, 0)
    out_ref[:, :width] = (dqt_ref[...] * HD**-0.5).T.astype(BF16)

    for i in range(pieces):
        total(level, i, not_top, (level > 0) & (level < low))
        out_ref[pl.ds(i * step, step), width:] = acc_ref[...].astype(BF16)

    for at in range(levels):
        for i in range(pieces):

            @pl.when(gone(at))
            def _(at=at, i=i):
                cross(at, i).wait_send()

            @pl.when(at < level)
            def _(at=at, i=i):
                line(at, i, False).wait_send()

            if at < low:

                @pl.when(at > level)
                def _(at=at, i=i):
                    line(at, i, True).wait_send()


def attention_backward(info, q, kv_all, do, lse, delta, e, bias, group, low, collective):
    pieces = 4
    levels = group // 2
    tokens, width = q.shape
    both = 2 * width
    block = pltpu.VMEM((levels, tokens, both), BF16)
    return pl.pallas_call(
        functools.partial(backward_kernel, group, low, pieces, tokens // 2),
        out_shape=(
            jax.ShapeDtypeStruct((tokens, width + both), BF16),
            jax.ShapeDtypeStruct(e.shape[1:], BF16),
        ),
        in_specs=[SSPEC] + [VSPEC] * 7,
        out_specs=(VSPEC,) * 2,
        scratch_shapes=[
            pltpu.VMEM(kv_all.shape, BF16),
            block,
            block,
            pltpu.VMEM((low, tokens, both), BF16),
            block,
            pltpu.VMEM((tokens // pieces, both), F32),
            pltpu.VMEM((width, tokens), F32),
            pltpu.VMEM((COLS - 1,) + e.shape[1:], BF16),
        ]
        + [DMA((levels, pieces))] * 6
        + [DMA((COLS - 1,))] * 2,
        compiler_params=params(collective),
    )(info, q, kv_all, do, lse, delta, e, bias)


def product(pieces, a_ref, w_ref, feats, out_ref, snd_ref, rx_ref, far_ref, tot_ref, sems, fill):
    send, recv = sems
    me, sib, across, diag = col_places()
    half = a_ref.shape[0] // 2
    step = half // pieces
    per = w_ref.shape[0] // COLS
    width = out_ref.shape[1]

    def weight(who):
        return w_ref[pl.ds(who * per, per)].reshape(width, 4 * width)[:, feats]

    def term(i, w):
        parts = [nt(a_ref[pl.ds(n * half + i * step, step)], w) for n in range(2)]
        return jnp.concatenate(parts, axis=1)

    def near(i, j):
        part = pl.ds(i * step, step)
        return push(
            snd_ref.at[j, part], rx_ref.at[j, part], send.at[j, i], recv.at[j, i], {"col": sib}
        )

    def over(i):
        part = pl.ds(i * step, step)
        return push(tot_ref.at[part], far_ref.at[part], send.at[2, i], recv.at[2, i], {"col": across})

    w = weight(diag)
    for i in range(pieces):
        snd_ref[0, pl.ds(i * step, step)] = term(i, w).astype(BF16)
        near(i, 0).start()
    w = weight(across)
    for i in range(pieces):
        part = pl.ds(i * step, step)
        mine = term(i, w)
        near(i, 0).wait_recv()
        tot_ref[part] = (mine + rx_ref[0, part].astype(F32)).astype(BF16)
        over(i).start()
    w = weight(sib)
    for i in range(pieces):
        snd_ref[1, pl.ds(i * step, step)] = term(i, w).astype(BF16)
        near(i, 1).start()
    fill()
    w = weight(me)
    for i in range(pieces):
        part = pl.ds(i * step, step)
        mine = term(i, w)
        near(i, 1).wait_recv()
        mine = mine + rx_ref[1, part].astype(F32)
        over(i).wait_recv()
        mine = mine + far_ref[part].astype(F32)
        out_ref[part] = mine[:, :width]
        out_ref[pl.ds(half + i * step, step)] = mine[:, width:]
    for i in range(pieces):
        near(i, 0).wait_send()
        near(i, 1).wait_send()
        over(i).wait_send()


def product_scratch(pieces, tokens, width):
    block = pltpu.VMEM((tokens // 2, 2 * width), BF16)
    pair = pltpu.VMEM((2, tokens // 2, 2 * width), BF16)
    return [pair, pair, block, block, DMA((3, pieces)), DMA((3, pieces))]


def branch_kernel(
    pieces,
    a_ref,
    w_ref,
    x_ref,
    s_ref,
    mid_ref,
    normed_ref,
    rstd_ref,
    h_ref,
    snd_ref,
    rx_ref,
    far_ref,
    tot_ref,
    send,
    recv,
    st_ref,
    all_ref,
    st_send,
    st_recv,
):
    greet(col_peers())
    width = x_ref.shape[2] // 2
    product(
        pieces,
        a_ref,
        w_ref,
        slice(3 * width, 4 * width),
        mid_ref,
        snd_ref,
        rx_ref,
        far_ref,
        tot_ref,
        (send, recv),
        lambda: None,
    )
    own = x_ref[lax.axis_index("col")]
    own = jnp.concatenate([own[:, :width], own[:, width:]], axis=0)
    mid = own.astype(F32) + mid_ref[...] + own_features(s_ref, 4)
    mid_ref[...] = mid
    part_mean = jnp.mean(mid, axis=-1, keepdims=True)
    part_spread = jnp.sum((mid - part_mean) ** 2, axis=-1, keepdims=True)
    st_ref[...] = to_rows([part_mean, part_spread])
    share(st_ref, all_ref, st_send, st_recv)
    mean = sum(all_ref[b, 0:1] for b in range(COLS)) / COLS
    spread = sum(
        all_ref[b, 1:2] + width * (all_ref[b, 0:1] - mean) ** 2 for b in range(COLS)
    )
    mean, rstd = to_columns([mean, lax.rsqrt(spread / D + epsilon)])
    normed = (mid - mean) * rstd
    normed_ref[...] = normed
    rstd_ref[...] = rstd
    h_ref[...] = (normed * own_features(s_ref, 2) + own_features(s_ref, 3)).astype(BF16)


def branch(a, w, x, s, collective):
    pieces = 4
    tokens, width = a.shape
    rows = jax.ShapeDtypeStruct((tokens, width), F32)
    return pl.pallas_call(
        functools.partial(branch_kernel, pieces),
        out_shape=(
            rows,
            rows,
            jax.ShapeDtypeStruct((tokens, 1), F32),
            jax.ShapeDtypeStruct((tokens, width), BF16),
        ),
        in_specs=[VSPEC] * 4,
        out_specs=(VSPEC,) * 4,
        scratch_shapes=product_scratch(pieces, tokens, width)
        + [
            pltpu.VMEM((8, tokens), F32),
            pltpu.VMEM((COLS, 8, tokens), F32),
            DMA((COLS - 1,)),
            DMA((COLS - 1,)),
        ],
        compiler_params=params(collective),
    )(a, w, x, s)


def input_kernel(
    pieces,
    a_ref,
    w_ref,
    e_ref,
    h_ref,
    gwo_ref,
    mid_ref,
    normed_ref,
    rstd_ref,
    s_ref,
    vec_ref,
    gin_ref,
    eo_ref,
    wt_ref,
    all_ref,
    grad_ref,
    snd_ref,
    rx_ref,
    far_ref,
    tot_ref,
    send,
    recv,
    st_ref,
    st_send,
    st_recv,
    e_send,
    e_recv,
):
    rows = e_ref.shape[0]
    row = lax.axis_index("row")
    order = far_first(rows)
    greet([{"row": (row + k) % rows} for k in order] + col_peers())
    home = []
    for n, k in enumerate(order):
        peer = (row + k) % rows
        copy = push(e_ref.at[peer], eo_ref.at[row], e_send.at[n], e_recv.at[n], {"row": peer})
        copy.start()
        home.append(copy)
    eo_ref[row] = e_ref[row]
    tokens, width = grad_ref.shape

    def fill():
        both = [tn(h_ref[...], a_ref[...]).astype(BF16), gwo_ref[...]]
        wt_ref[...] = jnp.concatenate(both, axis=1)

    product(
        pieces,
        a_ref,
        w_ref,
        slice(0, 3 * width),
        grad_ref,
        snd_ref,
        rx_ref,
        far_ref,
        tot_ref,
        (send, recv),
        fill,
    )
    grad, normed = grad_ref[...], normed_ref[...]
    st_ref[:, tokens:] = jnp.zeros((8, st_ref.shape[1] - tokens), F32)
    st_ref[0:1, tokens : tokens + width] = jnp.sum(grad * normed, axis=0, keepdims=True)
    st_ref[1:2, tokens : tokens + width] = jnp.sum(grad, axis=0, keepdims=True)
    st_ref[2:5, tokens : tokens + width] = vec_ref[0:3]
    gin_ref[...] = mid_ref[...] + norm_back(
        grad, normed, own_features(s_ref, 0), rstd_ref[...], st_ref, all_ref, st_send, st_recv
    )
    for copy in home:
        copy.wait()


def input_gradient(a, w, e, h, gwo, mid, normed, rstd, gain, vec, collective):
    pieces = 4
    tokens, width = mid.shape
    wide = tokens + 256
    return pl.pallas_call(
        functools.partial(input_kernel, pieces),
        out_shape=(
            jax.ShapeDtypeStruct((tokens, width), F32),
            jax.ShapeDtypeStruct(e.shape, BF16),
            jax.ShapeDtypeStruct((D, 4 * width), BF16),
            jax.ShapeDtypeStruct((COLS, 8, wide), F32),
        ),
        in_specs=[VSPEC] * 10,
        out_specs=(VSPEC,) * 4,
        scratch_shapes=[pltpu.VMEM((tokens, width), F32)]
        + product_scratch(pieces, tokens, width)
        + [
            pltpu.VMEM((8, wide), F32),
            DMA((COLS - 1,)),
            DMA((COLS - 1,)),
            DMA((e.shape[0] - 1,)),
            DMA((e.shape[0] - 1,)),
        ],
        compiler_params=params(collective),
    )(a, w, e, h, gwo, mid, normed, rstd, gain, vec)


def dispatch_kernel(rows, x_ref, t_ref, out_ref, in_ref, r_send, r_recv, c_send, c_recv):
    me, sib, across, _ = col_places()
    row = lax.axis_index("row")
    peers = [paired(row, k) for k in range(1, rows)]
    greet([{"row": p} for p in peers] + [{"col": sib}, {"col": across}])
    copies = []
    cap = in_ref.shape[1]

    def col(src, dst, k, way):
        return push(
            src, dst, c_send.at[way, k], c_recv.at[way, k], {"col": across if way == 0 else sib}
        )

    done, first = [], []
    for n, k in enumerate(range(rows - 1, 0, -1)):
        peer = peers[k - 1]
        in_ref[peer] = placed(t_ref, x_ref[...], peer, cap)
        copy = push(
            in_ref.at[peer], out_ref.at[me, row], r_send.at[k - 1], r_recv.at[k - 1], {"row": peer}
        )
        copy.start()
        copies.append(copy)
        if n == 1:
            in_ref[row] = placed(t_ref, x_ref[...], row, cap)
            for way in range(2):
                copy = col(in_ref.at[row], out_ref.at[me, row], 0, way)
                copy.start()
                (first if way == 0 else done).append(copy)
    copies.reverse()
    out_ref[me, row] = in_ref[row]
    sources = [row] + peers

    def forward(k):
        first[k].wait_recv()
        src = sources[k]
        copy = col(out_ref.at[across, src], out_ref.at[across, src], k, 2)
        copy.start()
        done.append(copy)

    for k in range(1, rows):
        copies[k - 1].wait_recv()
        block = out_ref.at[me, sources[k]]
        for way in range(2):
            copy = col(block, block, k, way)
            copy.start()
            (first if way == 0 else done).append(copy)
        forward(k - 1)
    forward(rows - 1)
    for copy in copies:
        copy.wait_send()
    for copy in first:
        copy.wait_send()
    for copy in done:
        copy.wait()


def dispatch(x, target, rows, cap, collective):
    block = (rows, cap, 2 * x.shape[1])
    return pl.pallas_call(
        functools.partial(dispatch_kernel, rows),
        out_shape=jax.ShapeDtypeStruct((COLS,) + block, x.dtype),
        in_specs=[VSPEC] * 2,
        out_specs=VSPEC,
        scratch_shapes=[
            pltpu.VMEM(block, x.dtype),
            DMA((rows - 1,)),
            DMA((rows - 1,)),
            DMA((3, rows)),
            DMA((3, rows)),
        ],
        compiler_params=params(collective),
    )(x, target)


def giveback_kernel(
    rows,
    in_ref,
    t_ref,
    cot_ref,
    normed_ref,
    rstd_ref,
    s_ref,
    mid_ref,
    vec_ref,
    sum_ref,
    out_ref,
    rx_ref,
    far_ref,
    tot_ref,
    fin_ref,
    st_ref,
    all_ref,
    send,
    recv,
    r_send,
    r_recv,
    st_send,
    st_recv,
):
    me, sib, across, diag = col_places()
    row = lax.axis_index("row")
    order = [(row + k) % rows for k in far_first(rows)] + [row]
    greet([{"row": p} for p in order[:-1]] + col_peers())

    def near(k, j):
        who = diag if j == 0 else sib
        return push(
            in_ref.at[who, order[k]], rx_ref.at[j, k], send.at[j, k], recv.at[j, k], {"col": sib}
        )

    def over(k):
        return push(tot_ref.at[k], far_ref.at[k], send.at[2, k], recv.at[2, k], {"col": across})

    def home(k):
        return push(
            fin_ref.at[k], out_ref.at[row], r_send.at[k], r_recv.at[k], {"row": order[k]}
        )

    for k in range(rows):
        near(k, 0).start()
        near(k, 1).start()

    def finish(k):
        near(k, 1).wait_recv()
        over(k).wait_recv()
        total = in_ref[me, order[k]].astype(F32) + rx_ref[1, k].astype(F32)
        total = total + far_ref[k].astype(F32)
        if k == rows - 1:
            out_ref[row] = total.astype(BF16)
        else:
            fin_ref[k] = total.astype(BF16)
            home(k).start()

    for k in range(rows):
        near(k, 0).wait_recv()
        tot_ref[k] = (in_ref[across, order[k]].astype(F32) + rx_ref[0, k].astype(F32)).astype(BF16)
        over(k).start()
        if k >= 1:
            finish(k - 1)
    finish(rows - 1)
    cap = out_ref.shape[1]
    sum_ref[...] = combined(t_ref, out_ref[row], row, cap)
    for k, gap in enumerate(far_first(rows)):
        source = (row + rows - gap) % rows
        home(k).wait_recv()
        sum_ref[...] += combined(t_ref, out_ref[source], source, cap)
    grad, normed = sum_ref[...], normed_ref[...]
    mid = cot_ref[...].astype(F32) + norm_back(
        grad, normed, own_features(s_ref, 2), rstd_ref[...], st_ref, all_ref, st_send, st_recv
    )
    mid_ref[...] = mid
    vec_ref[...] = jnp.zeros(vec_ref.shape, F32)
    vec_ref[0:1] = jnp.sum(grad * normed, axis=0, keepdims=True)
    vec_ref[1:2] = jnp.sum(grad, axis=0, keepdims=True)
    vec_ref[2:3] = jnp.sum(mid, axis=0, keepdims=True)
    for k in range(rows):
        near(k, 0).wait_send()
        near(k, 1).wait_send()
        over(k).wait_send()
        if k < rows - 1:
            home(k).wait_send()


def giveback(parts, target, cot, normed, rstd, gain, rows, collective):
    block = parts.shape[2:]
    one = pltpu.VMEM((rows,) + block, BF16)
    return pl.pallas_call(
        functools.partial(giveback_kernel, rows),
        out_shape=(
            jax.ShapeDtypeStruct(cot.shape, F32),
            jax.ShapeDtypeStruct((8, cot.shape[1]), F32),
        ),
        in_specs=[VSPEC] * 6,
        out_specs=(VSPEC,) * 2,
        scratch_shapes=[
            pltpu.VMEM(cot.shape, F32),
            one,
            pltpu.VMEM((2, rows) + block, BF16),
            one,
            one,
            one,
            pltpu.VMEM((8, cot.shape[0]), F32),
            pltpu.VMEM((COLS, 8, cot.shape[0]), F32),
            DMA((3, rows)),
            DMA((3, rows)),
            DMA((rows - 1,)),
            DMA((rows - 1,)),
            DMA((COLS - 1,)),
            DMA((COLS - 1,)),
        ],
        compiler_params=params(collective),
    )(parts, target, cot, normed, rstd, gain)


def end_kernel(
    rows,
    w_ref,
    s_ref,
    e_ref,
    t_ref,
    mid_ref,
    wo_ref,
    so_ref,
    lo_ref,
    px_ref,
    pt_ref,
    wr_ref,
    sr_ref,
    p_send,
    p_recv,
    l_send,
    l_recv,
    send,
    recv,
):
    row, _, level, side, partner = line_places(rows)
    levels = rows // 2
    peers = [(row + k) % rows for k in far_first(rows)]
    greet([{"row": p} for p in peers])
    gaps = far_first(levels)
    targets = [(level + k) % levels for k in gaps] + [level]

    def cross(n):
        src = w_ref.at[2 * targets[n] + 1 - side]
        return push(src, px_ref.at[n], p_send.at[n], p_recv.at[n], {"row": partner})

    def along(n):
        peer = {"row": 2 * targets[n] + side}
        return push(pt_ref.at[n], wr_ref.at[n], l_send.at[n], l_recv.at[n], peer)

    def total(n):
        return w_ref[2 * targets[n] + side].astype(F32) + px_ref[n].astype(F32)

    for n in range(levels):
        cross(n).start()
    copies = []
    for k, peer in enumerate(peers):
        copy = push(s_ref.at[peer], sr_ref.at[k], send.at[k], recv.at[k], {"row": peer})
        copy.start()
        copies.append(copy)
    for n in range(levels - 1):
        cross(n).wait_recv()
        pt_ref[n] = total(n).astype(BF16)
        along(n).start()
    result = mid_ref[...]
    for r in range(rows):
        result = result + combined(t_ref, e_ref[r], r, e_ref.shape[1])
    lo_ref[...] = result.astype(BF16)
    small = s_ref[row]
    for k, copy in enumerate(copies):
        copy.wait_recv()
        small = small + sr_ref[k]
    so_ref[...] = small
    cross(levels - 1).wait_recv()
    mine = total(levels - 1)
    for n in range(levels - 1):
        along(n).wait_recv()
        mine = mine + wr_ref[n].astype(F32)
    wo_ref[...] = mine
    for n in range(levels):
        cross(n).wait_send()
        if n < levels - 1:
            along(n).wait_send()
    for copy in copies:
        copy.wait_send()


def end_scatter(w, s, outs, target, mid, rows, collective):
    levels = rows // 2
    one = w.shape[1:]
    return pl.pallas_call(
        functools.partial(end_kernel, rows),
        out_shape=(
            jax.ShapeDtypeStruct(one, F32),
            jax.ShapeDtypeStruct(s.shape[1:], F32),
            jax.ShapeDtypeStruct(mid.shape, BF16),
        ),
        in_specs=[VSPEC] * 5,
        out_specs=(VSPEC,) * 3,
        scratch_shapes=[
            pltpu.VMEM((levels,) + one, w.dtype),
            pltpu.VMEM((levels - 1,) + one, w.dtype),
            pltpu.VMEM((levels - 1,) + one, w.dtype),
            pltpu.VMEM((rows - 1,) + s.shape[1:], s.dtype),
            DMA((levels,)),
            DMA((levels,)),
            DMA((levels - 1,)),
            DMA((levels - 1,)),
            DMA((rows - 1,)),
            DMA((rows - 1,)),
        ],
        compiler_params=params(collective),
    )(w, s, outs, target, mid)


def expert_kernel(
    x_ref,
    g_ref,
    up_hbm,
    bias_ref,
    down_hbm,
    part_ref,
    gx_ref,
    gup_hbm,
    gbu_ref,
    gdown_hbm,
    gbd_ref,
    up_ref,
    down_ref,
    gup_ref,
    gdown_ref,
    xs_ref,
    gs_ref,
    sum_ref,
    gsum_ref,
    in_sems,
    out_sems,
):
    cols, rows, cap, both = x_ref.shape
    width = both // 2
    slots = rows * cap
    count, _, hidden_units = up_ref.shape
    chunk = 256
    loads = []
    for e in range(count):
        for j, (src, dst) in enumerate(((up_hbm, up_ref), (down_hbm, down_ref))):
            copy = pltpu.make_async_copy(src.at[e], dst.at[e], in_sems.at[j, e])
            copy.start()
            loads.append(copy)

    def gup_out(e, f):
        cut = pl.ds(pl.multiple_of(f * chunk, chunk), chunk)
        return pltpu.make_async_copy(
            gup_ref.at[e, :, cut], gup_hbm.at[e, :, cut], out_sems.at[0, e, f]
        )

    def gdown_out(e, f):
        cut = pl.ds(pl.multiple_of(f * chunk, chunk), chunk)
        return pltpu.make_async_copy(
            gdown_ref.at[e, cut], gdown_hbm.at[e, cut], out_sems.at[1, e, f]
        )

    for e in range(count):
        lanes = slice(e * width, (e + 1) * width)
        for ref, dst in ((x_ref, xs_ref), (g_ref, gs_ref)):
            blocks = [ref[b].reshape(slots, both)[:, lanes] for b in range(cols)]
            dst[...] = jnp.concatenate(blocks, axis=1)
        gbd_ref[e] = jnp.sum(gs_ref[...].astype(F32), axis=0, keepdims=True)
        sum_ref[...] = jnp.zeros(sum_ref.shape, F32)
        gsum_ref[...] = jnp.zeros(gsum_ref.shape, F32)
        loads[2 * e].wait()
        loads[2 * e + 1].wait()

        def body(f, carry, e=e):
            cut = pl.ds(pl.multiple_of(f * chunk, chunk), chunk)
            x, g = xs_ref[...], gs_ref[...]
            up, down = up_ref[e, :, cut], down_ref[e, cut, :]
            pre = nn(x, up) + bias_ref[e, :, cut].astype(F32)
            cdf = 0.5 * (1.0 + lax.erf(pre * (0.5**0.5)))
            slope = cdf + pre * (jnp.exp(-0.5 * pre * pre) * 0.3989422804014327)
            hidden = (pre * cdf).astype(BF16)
            grad = nt(g, down) * slope
            grad = grad.astype(BF16)
            sum_ref[...] += nn(hidden, down)
            gsum_ref[...] += nt(grad, up)
            gdown_ref[e, cut, :] = tn(hidden, g)
            gdown_out(e, f).start()
            gup_ref[e, :, cut] = tn(x, grad)
            gup_out(e, f).start()
            gbu_ref[e, :, cut] = jnp.sum(grad.astype(F32), axis=0, keepdims=True)
            return carry

        lax.fori_loop(0, hidden_units // chunk, body, 0)
        for b in range(cols):
            cut = slice(b * width, (b + 1) * width)
            part_ref[b, :, :, lanes] = sum_ref[:, cut].astype(BF16).reshape(rows, cap, width)
            gx_ref[b, :, :, lanes] = gsum_ref[:, cut].astype(BF16).reshape(rows, cap, width)
    for e in range(count):
        for f in range(hidden_units // chunk):
            gdown_out(e, f).wait()
            gup_out(e, f).wait()


def experts(x, g, w_up, bias_up, w_down):
    cols, rows, cap, _ = x.shape
    count, features, hidden = w_up.shape
    slots = rows * cap
    anywhere = pl.BlockSpec(memory_space=pl.ANY)
    return pl.pallas_call(
        expert_kernel,
        out_shape=(
            jax.ShapeDtypeStruct(x.shape, BF16),
            jax.ShapeDtypeStruct(x.shape, BF16),
            jax.ShapeDtypeStruct(w_up.shape, F32),
            jax.ShapeDtypeStruct((count, 1, hidden), F32),
            jax.ShapeDtypeStruct(w_down.shape, F32),
            jax.ShapeDtypeStruct((count, 1, features), F32),
        ),
        in_specs=[VSPEC, VSPEC, anywhere, VSPEC, anywhere],
        out_specs=(VSPEC, VSPEC, anywhere, VSPEC, anywhere, VSPEC),
        scratch_shapes=[
            pltpu.VMEM(w_up.shape, BF16),
            pltpu.VMEM(w_down.shape, BF16),
            pltpu.VMEM(w_up.shape, F32),
            pltpu.VMEM(w_down.shape, F32),
            pltpu.VMEM((slots, features), BF16),
            pltpu.VMEM((slots, features), BF16),
            pltpu.VMEM((slots, features), F32),
            pltpu.VMEM((slots, features), F32),
            DMA((2, count)),
            DMA((2, count, hidden // 256)),
        ],
        compiler_params=params(),
    )(x, g, w_up, bias_up.reshape(count, 1, hidden), w_down)


def per_device(
    layer_in,
    cotangent,
    token_ids,
    hash_table,
    prefix_len,
    w_query,
    w_key,
    w_value,
    w_output,
    bias_query,
    bias_value,
    gain_attn,
    shift_attn,
    gain_moe,
    shift_moe,
    bias_output,
    w_up,
    bias_up,
    w_down,
    bias_down,
):
    rows = lax.axis_size("row")
    row = lax.axis_index("row")
    col = lax.axis_index("col")
    tokens, width = layer_in.shape
    heads = width // HD
    seq_len = min(LENGTH, tokens * rows)
    group = seq_len // tokens
    low = -(-PREFIX_MAX // (2 * tokens))
    share = w_query.shape[0]
    bias_share = bias_query.shape[0]

    def line(v):
        return jnp.pad(v.astype(F32), (0, 128 - v.shape[0]))

    small = jnp.stack(
        [
            line(gain_attn),
            line(shift_attn),
            line(gain_moe),
            line(shift_moe),
            line(bias_output),
            line(bias_query.T.reshape(-1)),
            line(bias_value.T.reshape(-1)),
            jnp.zeros((128,), F32),
        ]
    )
    expert_total = EXP_DEV * rows
    capacity = max(2, 2 * tokens // expert_total)
    table = jnp.pad(hash_table, (0, -hash_table.shape[0] % (128 * 128)))
    table = table.reshape(-1, 128).astype(BF16)

    weights = jnp.concatenate([w_query, w_key, w_value, w_output], axis=1)
    x_all, g_own, w_all, s_all, target = start_gather(
        layer_in, cotangent, token_ids[None], table, weights, small, rows, capacity
    )

    queries, keys_values, h_one, normed_one, rstd_one = project(x_all, w_all, s_all)
    seq_hit = row // group == jnp.arange(prefix_len.shape[0], dtype=jnp.int32)
    prefix = jnp.sum(jnp.where(seq_hit, prefix_len, 0))
    info = prefix.astype(jnp.int32).reshape(1)
    kv_all, attended, attended_low, lse, g_all = attention_forward(
        info, queries, keys_values, g_own, group, low, 1
    )
    mid, normed_two, rstd_two, h_two = branch(attended_low, w_all, x_all, s_all, 2)

    received = dispatch(h_two, target, rows, capacity, 4)
    parts, grad_parts, grad_w_up, grad_bias_up, grad_w_down, grad_bias_down = experts(
        received, g_all, w_up, bias_up, w_down
    )
    grad_mid, vectors = giveback(
        grad_parts, target, cotangent, normed_two, rstd_two, s_all, rows, 5
    )
    grad_attended, delta, grad_w_out = mid_gradient(grad_mid, w_all, attended, attended_low, 7)
    down_own = lax.dynamic_slice_in_dim(bias_down, col * width, width, 1).astype(F32)
    down_own = down_own.reshape(1, EXP_DEV * width)
    grad_qkv, outs = attention_backward(
        info,
        queries,
        kv_all,
        grad_attended,
        lse,
        delta,
        parts,
        down_own,
        group,
        low,
        8,
    )
    grad_bias = jnp.sum(grad_qkv, axis=0, dtype=F32)
    grad_in, outs, weight_terms, shared = input_gradient(
        grad_qkv,
        w_all,
        outs,
        h_one,
        grad_w_out,
        grad_mid,
        normed_one,
        rstd_one,
        s_all,
        vectors,
        9,
    )
    vectors = shared[:, :5, tokens : tokens + width]
    vectors = vectors.transpose(1, 0, 2).reshape(5, rows, share).transpose(1, 0, 2)

    def by_row(v):
        v = v.reshape(heads, rows, bias_share).transpose(1, 0, 2).reshape(rows, 1, -1)
        return jnp.pad(v, ((0, 0), (0, 0), (0, 128 - v.shape[2])))

    small_terms = jnp.concatenate(
        [
            jnp.pad(vectors, ((0, 0), (0, 0), (0, 128 - share))),
            by_row(grad_bias[:width]),
            by_row(grad_bias[2 * width :]),
            jnp.zeros((rows, 1, 128), F32),
        ],
        axis=1,
    )
    weight_terms = weight_terms.reshape(rows, share, 4 * width)
    weight_sums, small_sums, layer_out = end_scatter(
        weight_terms, small_terms, outs, target, mid, rows, 11
    )

    def bias_back(v):
        return v[: heads * bias_share].reshape(heads, bias_share).T

    return (
        layer_out,
        grad_in,
        weight_sums[:, :width],
        weight_sums[:, width : 2 * width],
        weight_sums[:, 2 * width : 3 * width],
        weight_sums[:, 3 * width :],
        bias_back(small_sums[5]),
        bias_back(small_sums[6]),
        small_sums[0, :share],
        small_sums[1, :share],
        small_sums[2, :share],
        small_sums[3, :share],
        small_sums[4, :share],
        grad_w_up,
        grad_bias_up[:, 0],
        grad_w_down,
        grad_bias_down[:, 0],
    )


def solution(mesh):
    placed = (
        P("row", "col"),
        P("row", "col"),
        P("row"),
        P(),
        P(),
        P("row", "col"),
        P("row", "col"),
        P("row", "col"),
        P("row", "col"),
        P("row", "col"),
        P("row", "col"),
        P("row"),
        P("row"),
        P("row"),
        P("row"),
        P("row"),
        P("row", None, "col"),
        P("row", "col"),
        P("row", "col", None),
        P("row", None),
    )
    return jax.shard_map(
        per_device,
        mesh=mesh,
        in_specs=placed,
        out_specs=(
            P("row", "col"),
            P("row", "col"),
            P("row", "col"),
            P("row", "col"),
            P("row", "col"),
            P("row", "col"),
            P("row", "col"),
            P("row", "col"),
            P("row"),
            P("row"),
            P("row"),
            P("row"),
            P("row"),
            P("row", None, "col"),
            P("row", "col"),
            P("row", "col", None),
            P("row", None),
        ),
        check_vma=False,
    )
```

```python
import functools

import jax
import jax.numpy as jnp
from jax import lax
from jax.experimental import pallas as pl
from jax.experimental.pallas import tpu as pltpu
from jax.sharding import PartitionSpec as P

D = 768
HD = 64
EXP_DEV = 2
LENGTH = 8192
PREFIX_MAX = 4096
COLS = 4

F32 = jnp.float32
BF16 = jnp.bfloat16
MESH = pl.DeviceIdType.MESH
LOG2E = 1.4426950408889634

epsilon = 1e-05
neg_big = -1e30

VSPEC = pl.BlockSpec(memory_space=pltpu.VMEM)
SSPEC = pl.BlockSpec(memory_space=pltpu.SMEM)
VMEM_BYTES = 64 * 1000 * 1000
DMA = pltpu.SemaphoreType.DMA


def params(collective=None):
    if collective is None:
        return pltpu.CompilerParams(vmem_limit_bytes=VMEM_BYTES)
    return pltpu.CompilerParams(
        vmem_limit_bytes=VMEM_BYTES, collective_id=collective, has_side_effects=True
    )


def push(src, dst, send_sem, recv_sem, peer):
    return pltpu.make_async_remote_copy(
        src_ref=src,
        dst_ref=dst,
        send_sem=send_sem,
        recv_sem=recv_sem,
        device_id=peer,
        device_id_type=MESH,
    )


def greet(peers):
    barrier = pltpu.get_barrier_semaphore()
    for peer in peers:
        pl.semaphore_signal(barrier, inc=1, device_id=peer, device_id_type=MESH)
    pl.semaphore_wait(barrier, len(peers))


def col_places():
    me = lax.axis_index("col")
    sib = me + 1 - 2 * (me % 2)
    across = (me + 2) % COLS
    diag = (sib + 2) % COLS
    return me, sib, across, diag


def line_places(group):
    row = lax.axis_index("row")
    place = row % group
    level, side = place // 2, place % 2
    return row, place, level, side, row + 1 - 2 * side


def far_first(rows):
    return sorted(range(1, rows), key=lambda k: -min(k, rows - k))


def nt(left, right):
    return lax.dot_general(left, right, (((1,), (1,)), ((), ())), preferred_element_type=F32)


def nn(left, right):
    return lax.dot_general(left, right, (((1,), (0,)), ((), ())), preferred_element_type=F32)


def tn(left, right):
    return lax.dot_general(left, right, (((0,), (0,)), ((), ())), preferred_element_type=F32)


def side_by_side(v):
    half = v.shape[0] // 2
    return jnp.concatenate([v[:half], v[half:]], axis=1)


def number(shape, axis):
    return lax.broadcasted_iota(jnp.int32, shape, axis)


def route(ids, table, experts, cap):
    tokens = ids.shape[1]
    pick = jnp.where(number((table.shape[0], tokens), 0) == ids >> 7, 1.0, 0.0).astype(BF16)
    found = tn(table, pick)
    expert = jnp.where(number((128, tokens), 0) == ids & 127, found, 0.0)
    expert = jnp.sum(expert, axis=0, keepdims=True)
    hit = number((experts, tokens), 0).astype(F32) == expert
    pair = (tokens, tokens)
    earlier = jnp.where(number(pair, 0) < number(pair, 1), 1.0, 0.0).astype(BF16)
    before = nn(jnp.where(hit, 1.0, 0.0).astype(BF16), earlier)
    slot = jnp.sum(jnp.where(hit, before, 0.0), axis=0, keepdims=True)
    return (expert * cap + slot).astype(jnp.int32)


def all_features(s_ref, i):
    rows = s_ref.shape[0]
    return jnp.concatenate([s_ref[r, i : i + 1, : D // rows] for r in range(rows)], axis=1)


def own_features(s_ref, i):
    rows = s_ref.shape[0]
    per = rows // COLS
    block = s_ref[pl.ds(lax.axis_index("col") * per, per)]
    return jnp.concatenate([block[r, i : i + 1, : D // rows] for r in range(per)], axis=1)


def head_features(s_ref, i, heads):
    rows = s_ref.shape[0]
    size = HD // rows
    cuts = [slice(h * size, (h + 1) * size) for h in range(heads)]
    return jnp.concatenate([s_ref[r, i : i + 1, c] for c in cuts for r in range(rows)], axis=1)


def slots_of(target_ref, row, count):
    base = row * count
    slot = base + lax.broadcasted_iota(jnp.int32, (count, target_ref.shape[1]), 0)
    return jnp.where(slot == target_ref[...], 1.0, 0.0).astype(BF16)


def placed(target_ref, v, row, cap):
    return side_by_side(nn(slots_of(target_ref, row, 2 * cap), v).astype(BF16))


def combined(target_ref, block, row, cap):
    width = block.shape[1] // 2
    stacked = jnp.concatenate([block[:, :width], block[:, width:]], axis=0)
    return tn(slots_of(target_ref, row, 2 * cap), stacked)


def start_kernel(
    rows,
    pieces,
    x_ref,
    g_ref,
    ids_ref,
    table_ref,
    w_ref,
    s_ref,
    xo_ref,
    go_ref,
    wo_ref,
    so_ref,
    t_ref,
    xp_ref,
    gp_ref,
    c_send,
    c_recv,
    r_send,
    r_recv,
    l_send,
    l_recv,
):
    me, sib, across, _ = col_places()
    row, _, level, side, partner = line_places(rows)
    levels = rows // 2
    order = far_first(rows)
    peers = [{"row": (row + k) % rows} for k in order]
    greet(peers + [{"col": sib}, {"col": across}])
    xp_ref[...] = side_by_side(x_ref[...])
    step = xp_ref.shape[0] // pieces
    cap = gp_ref.shape[1]
    to_up, to_down = level < levels - 1, level > 0

    def weight(at, way, src=None):
        dst = wo_ref.at[2 * at + side]
        peer = (row + 2, row - 2, partner)[way]
        return push(
            dst if src is None else src,
            dst,
            l_send.at[way, at],
            l_recv.at[way, at],
            {"row": peer},
        )

    def weight_other(at):
        dst = wo_ref.at[2 * at + 1 - side]
        return push(dst, dst, l_send.at[2, at], l_recv.at[2, at], {"row": partner})

    @pl.when(to_up)
    def _():
        weight(level, 0, w_ref).start()

    @pl.when(to_down)
    def _():
        weight(level, 1, w_ref).start()

    weight(level, 2, w_ref).start()
    sent = []
    for i in range(pieces):
        part = pl.ds(i * step, step)
        for way, peer in ((0, across), (1, sib)):
            copy = push(
                xp_ref.at[part],
                xo_ref.at[me, part],
                c_send.at[way, i],
                c_recv.at[way, i],
                {"col": peer},
            )
            copy.start()
            sent.append(copy)
    row_copies = []
    for k, peer in enumerate(peers):
        copy = push(s_ref, so_ref.at[row], r_send.at[0, k], r_recv.at[0, k], peer)
        copy.start()
        row_copies.append(copy)

    def send_rows(k):
        target = (row + order[k]) % rows
        gp_ref[k] = placed(t_ref, g_ref[...], target, cap)
        copy = push(gp_ref.at[k], go_ref.at[row], r_send.at[1, k], r_recv.at[1, k], peers[k])
        copy.start()
        row_copies.append(copy)

    t_ref[...] = route(ids_ref[...], table_ref[...], EXP_DEV * rows, cap)
    send_rows(0)
    xo_ref[me] = xp_ref[...]
    wo_ref[row] = w_ref[...]
    so_ref[row] = s_ref[...]
    todo = list(range(1, rows - 1))

    def pass_on(k):
        at = level - k

        @pl.when(at >= 0)
        def _():
            weight(at, 0).wait_recv()

            @pl.when(to_up)
            def _():
                weight(at, 0).start()

            weight(at, 2).start()

        up = level + k

        @pl.when(up < levels)
        def _():
            weight(up, 1).wait_recv()

            @pl.when(to_down)
            def _():
                weight(up, 1).start()

            weight(up, 2).start()

    late = []
    for k in range(1, max(levels, pieces + 1)):
        if k < levels:
            pass_on(k)
        if k <= pieces:
            part = pl.ds((k - 1) * step, step)
            sent[2 * k - 2].wait_recv()
            copy = push(
                xo_ref.at[across, part],
                xo_ref.at[across, part],
                c_send.at[2, k - 1],
                c_recv.at[2, k - 1],
                {"col": sib},
            )
            copy.start()
            late.append(copy)
        for _ in range(2):
            if todo:
                send_rows(todo.pop(0))
    while todo:
        send_rows(todo.pop(0))
    go_ref[row] = placed(t_ref, g_ref[...], row, cap)
    for i in range(pieces):
        sent[2 * i].wait_send()
        sent[2 * i + 1].wait()
        late[i].wait()
    for at in range(levels):
        weight_other(at).wait_recv()
        weight(at, 2).wait_send()

        @pl.when((at <= level) & to_up)
        def _(at=at):
            weight(at, 0).wait_send()

        @pl.when((at >= level) & to_down)
        def _(at=at):
            weight(at, 1).wait_send()

    for copy in row_copies:
        copy.wait()


def start_gather(x, g, ids, table, w, s, rows, cap):
    pieces = 4
    tokens, width = x.shape
    packed = (tokens // 2, 2 * width)
    return pl.pallas_call(
        functools.partial(start_kernel, rows, pieces),
        out_shape=(
            jax.ShapeDtypeStruct((COLS,) + packed, x.dtype),
            jax.ShapeDtypeStruct((rows, cap, 2 * width), g.dtype),
            jax.ShapeDtypeStruct((rows,) + w.shape, w.dtype),
            jax.ShapeDtypeStruct((rows,) + s.shape, s.dtype),
            jax.ShapeDtypeStruct((1, tokens), jnp.int32),
        ),
        in_specs=[VSPEC] * 6,
        out_specs=(VSPEC,) * 5,
        scratch_shapes=[
            pltpu.VMEM(packed, x.dtype),
            pltpu.VMEM((rows - 1, cap, 2 * width), g.dtype),
            DMA((3, pieces)),
            DMA((3, pieces)),
            DMA((2, rows - 1)),
            DMA((2, rows - 1)),
            DMA((3, rows // 2)),
            DMA((3, rows // 2)),
        ],
        compiler_params=params(0),
    )(x, g, ids, table, w, s)


def project_kernel(
    x_ref, w_ref, s_ref, q_ref, kv_ref, h_ref, n_ref, r_ref
):
    me = lax.axis_index("col")
    half, width = x_ref.shape[1], x_ref.shape[2] // 2
    gain, shift = all_features(s_ref, 0), all_features(s_ref, 1)
    query = head_features(s_ref, 5, width // HD)
    value = head_features(s_ref, 6, width // HD)
    bias = jnp.concatenate([query, jnp.zeros_like(query), value], axis=1)
    w = w_ref[...].reshape(D, 4 * width)[:, : 3 * width]
    step = min(half, 256)
    for i in range(2 * half // step):
        side, start = i * step // half, i * step % half
        rows, feats = slice(start, start + step), slice(side * width, (side + 1) * width)
        x = jnp.concatenate([x_ref[b, rows, feats] for b in range(COLS)], axis=1).astype(F32)
        mean = jnp.mean(x, axis=-1, keepdims=True)
        centred = x - mean
        rstd = lax.rsqrt(jnp.mean(centred * centred, axis=-1, keepdims=True) + epsilon)
        h = (centred * rstd * gain + shift).astype(BF16)
        out = slice(i * step, (i + 1) * step)
        h_ref[out] = h
        n_ref[out] = (x_ref[me, rows, feats].astype(F32) - mean) * rstd
        r_ref[out] = rstd
        qkv = (nn(h, w) + bias).astype(BF16)
        q_ref[out] = qkv[:, :width] * jnp.asarray(HD**-0.5, BF16)
        kv_ref[out] = qkv[:, width:]


def project(x, w, s):
    tokens, width = 2 * x.shape[1], x.shape[2] // 2
    return pl.pallas_call(
        project_kernel,
        out_shape=(
            jax.ShapeDtypeStruct((tokens, width), BF16),
            jax.ShapeDtypeStruct((tokens, 2 * width), BF16),
            jax.ShapeDtypeStruct((tokens, D), BF16),
            jax.ShapeDtypeStruct((tokens, width), F32),
            jax.ShapeDtypeStruct((tokens, 1), F32),
        ),
        in_specs=[VSPEC] * 3,
        out_specs=(VSPEC,) * 5,
        compiler_params=params(),
    )(x, w, s)


def mid_kernel(
    pieces,
    x_ref,
    w_ref,
    att_ref,
    low_ref,
    do_ref,
    delta_ref,
    gw_ref,
    xp_ref,
    xo_ref,
    wide_ref,
    c_send,
    c_recv,
):
    me, sib, across, _ = col_places()
    greet([{"col": sib}, {"col": across}])
    xp_ref[...] = side_by_side(x_ref[...].astype(BF16))
    step = xp_ref.shape[0] // pieces
    sent, late = [], []
    for i in range(pieces):
        part = pl.ds(i * step, step)
        for way, peer in ((0, across), (1, sib)):
            copy = push(
                xp_ref.at[part],
                xo_ref.at[me, part],
                c_send.at[way, i],
                c_recv.at[way, i],
                {"col": peer},
            )
            copy.start()
            sent.append(copy)
    xo_ref[me] = xp_ref[...]
    tokens, width = x_ref.shape
    w = w_ref[...].reshape(D, 4 * width)[:, 3 * width :]
    for i in range(pieces):
        part = pl.ds(i * step, step)
        sent[2 * i].wait_recv()
        copy = push(
            xo_ref.at[across, part],
            xo_ref.at[across, part],
            c_send.at[2, i],
            c_recv.at[2, i],
            {"col": sib},
        )
        copy.start()
        late.append(copy)
    for i in range(pieces):
        sent[2 * i].wait_send()
        sent[2 * i + 1].wait()
        late[i].wait()
        rows = slice(i * step, (i + 1) * step)
        for half in range(2):
            feats = slice(half * width, (half + 1) * width)
            start = half * (tokens // 2) + i * step
            out = slice(start, start + step)
            wide = jnp.concatenate([xo_ref[b, rows, feats] for b in range(COLS)], axis=1)
            wide_ref[out] = wide
            do = nn(wide, w).astype(BF16)
            do_ref[out] = do
            both = (do.astype(F32) * att_ref[out]).T
            for h in range(width // HD):
                delta_ref[h : h + 1, out] = jnp.sum(
                    both[h * HD : (h + 1) * HD], axis=0, keepdims=True
                )
    gw_ref[...] = tn(wide_ref[...], low_ref[...]).astype(BF16)


def mid_gradient(x, w, attended, low, collective):
    pieces = 4
    tokens, width = x.shape
    packed = (tokens // 2, 2 * width)
    return pl.pallas_call(
        functools.partial(mid_kernel, pieces),
        out_shape=(
            jax.ShapeDtypeStruct((tokens, width), BF16),
            jax.ShapeDtypeStruct((8, tokens), F32),
            jax.ShapeDtypeStruct((D, width), BF16),
        ),
        in_specs=[VSPEC] * 4,
        out_specs=(VSPEC,) * 3,
        scratch_shapes=[
            pltpu.VMEM(packed, BF16),
            pltpu.VMEM((COLS,) + packed, BF16),
            pltpu.VMEM((tokens, D), BF16),
            DMA((3, pieces)),
            DMA((3, pieces)),
        ],
        compiler_params=params(collective),
    )(x, w, attended, low)


def col_peers():
    me = lax.axis_index("col")
    return [{"col": (me + k) % COLS} for k in range(1, COLS)]


def to_rows(columns):
    lane = lax.broadcasted_iota(jnp.int32, (columns[0].shape[0], 128), 1)
    v = jnp.zeros(lane.shape, F32)
    for i, column in enumerate(columns):
        v = jnp.where(lane == i, column, v)
    return v.T[:8]


def to_columns(lines):
    place = lax.broadcasted_iota(jnp.int32, (8, lines[0].shape[1]), 0)
    v = jnp.zeros(place.shape, F32)
    for i, one in enumerate(lines):
        v = jnp.where(place == i, one, v)
    v = v.T
    return [v[:, i : i + 1] for i in range(len(lines))]


def share(snd_ref, all_ref, send, recv):
    me = lax.axis_index("col")
    copies = []
    for k, peer in enumerate(col_peers()):
        copy = push(snd_ref, all_ref.at[me], send.at[k], recv.at[k], peer)
        copy.start()
        copies.append(copy)
    all_ref[me] = snd_ref[...]
    for copy in copies:
        copy.wait()


def norm_back(grad, normed, gain, rstd, snd_ref, all_ref, send, recv):
    tokens = grad.shape[0]
    scaled = grad * gain
    sums = [
        jnp.sum(scaled, axis=-1, keepdims=True),
        jnp.sum(scaled * normed, axis=-1, keepdims=True),
    ]
    snd_ref[:, :tokens] = to_rows(sums)
    share(snd_ref, all_ref, send, recv)
    total = all_ref[0, :, :tokens]
    for b in range(1, COLS):
        total = total + all_ref[b, :, :tokens]
    total = total / D
    first, second = to_columns([total[0:1], total[1:2]])
    return rstd * (scaled - first - normed * second)


def line_greet(levels, row, level, partner):
    barrier = pltpu.get_barrier_semaphore()
    me = lax.axis_index("col")
    for k in range(1, COLS):
        peer = {"col": (me + k) % COLS}
        pl.semaphore_signal(barrier, inc=1, device_id=peer, device_id_type=MESH)
    pl.semaphore_signal(barrier, inc=1, device_id={"row": partner}, device_id_type=MESH)

    @pl.when(level > 0)
    def _():
        pl.semaphore_signal(barrier, inc=1, device_id={"row": row - 2}, device_id_type=MESH)

    @pl.when(level < levels - 1)
    def _():
        pl.semaphore_signal(barrier, inc=1, device_id={"row": row + 2}, device_id_type=MESH)

    count = COLS + (level > 0).astype(jnp.int32) + (level < levels - 1).astype(jnp.int32)
    pl.semaphore_wait(barrier, count)


def seen(key_start, query_start, shape, prefix):
    key = key_start + lax.broadcasted_iota(jnp.int32, shape, 0)
    query = query_start + lax.broadcasted_iota(jnp.int32, shape, 1)
    return (key < prefix) | (key <= query)


def forward_kernel(
    group,
    low,
    pieces,
    qb,
    info_ref,
    q_ref,
    kv_ref,
    g_ref,
    out_ref,
    o_ref,
    ob_ref,
    lse_ref,
    ga_ref,
    m_ref,
    acc_ref,
    u_send,
    u_recv,
    d_send,
    d_recv,
    x_send,
    x_recv,
    g_send,
    g_recv,
    e_send,
    e_recv,
):
    levels = group // 2
    row, place, level, side, partner = line_places(group)
    prefix = info_ref[0]
    tokens, width = q_ref.shape
    heads = width // HD
    step = tokens // pieces
    line_greet(levels, row, level, partner)

    def make(at, i, way, src=None):
        part = pl.ds(i * step, step)
        dst = out_ref.at[2 * at + side, part]
        sems = ((u_send, u_recv), (d_send, d_recv), (x_send, x_recv))[way]
        peer = (row + 2, row - 2, partner)[way]
        return push(
            dst if src is None else src.at[part],
            dst,
            sems[0].at[at, i],
            sems[1].at[at, i],
            {"row": peer},
        )

    def other(at, i):
        part = pl.ds(i * step, step)
        dst = out_ref.at[2 * at + 1 - side, part]
        return push(dst, dst, x_send.at[at, i], x_recv.at[at, i], {"row": partner})

    detour = pieces // 2
    top = level == levels - 1
    by_line = top & (side == 1)
    not_across = top & (side == 0)
    lends = (level == levels - 2) & (side == 1)

    def lent(i):
        dst = out_ref.at[0, pl.ds(i * step, step)]
        return push(dst, dst, e_send.at[i], e_recv.at[i], {"row": row + 2})

    def when(cond, run):
        @pl.when(cond)
        def _():
            for i in range(pieces):
                run(i)

    to_up = level < levels - 1
    own_down = (level > 0) & (level < low)
    own_side = (level < low) | (side == 0)
    for i in range(pieces):

        @pl.when(to_up)
        def _(i=i):
            make(level, i, 0, kv_ref).start()

        @pl.when(own_side)
        def _(i=i):
            make(level, i, 2, kv_ref).start()

        @pl.when(own_down)
        def _(i=i):
            make(level, i, 1, kv_ref).start()

    me = lax.axis_index("col")
    wide = []
    for k in range(1, COLS):
        peer = {"col": (me + k) % COLS}
        copy = push(g_ref, ga_ref.at[me], g_send.at[k - 1], g_recv.at[k - 1], peer)
        copy.start()
        wide.append(copy)
    ga_ref[me] = g_ref[...]
    out_ref[place] = kv_ref[...]
    m_ref[...] = jnp.full(m_ref.shape, neg_big, F32)
    acc_ref[...] = jnp.zeros(acc_ref.shape, F32)
    units = [(h, i) for h in range(heads) for i in range(tokens // qb)]

    def block(blk, masked):
        def raw_of(h, i):
            feats = slice(h * HD, (h + 1) * HD)
            raw = nt(out_ref[blk, :, feats], q_ref[i * qb : (i + 1) * qb, feats])
            if masked:
                allowed = seen(blk * tokens, place * tokens + i * qb, raw.shape, prefix)
                raw = jnp.where(allowed, raw, neg_big)
            return raw

        def soften(h, i, raw):
            cols = slice(i * qb, (i + 1) * qb)
            old = m_ref[h : h + 1, cols]
            new = jnp.maximum(old, jnp.max(raw, axis=0, keepdims=True))
            m_ref[h : h + 1, cols] = new
            weights = jnp.exp2((raw - new) * LOG2E).astype(BF16)
            return weights, jnp.exp2((old - new) * LOG2E)

        def gather(h, i, weights, scale):
            cols = slice(i * qb, (i + 1) * qb)
            v = out_ref[blk, :, width + h * HD : width + (h + 1) * HD]
            v_ext = jnp.concatenate([v.T, jnp.ones((16, tokens), BF16)], axis=0)
            acc_ref[h, :, cols] = acc_ref[h, :, cols] * scale + nn(v_ext, weights)

        coming, waiting = raw_of(*units[0]), None
        for n, unit in enumerate(units):
            raw = coming
            if n + 1 < len(units):
                coming = raw_of(*units[n + 1])
            soft = soften(*unit, raw)
            if waiting is not None:
                gather(*waiting)
            waiting = unit + soft
        gather(*waiting)

    def event(e, carry):
        t, cross = e // 2, e % 2
        at = jnp.where(t <= level, level - t, t)
        live = (t <= level) | (t < low)
        line_in = live & (cross == 0)
        coming = t + 1
        via = jnp.where(coming <= level, level - coming, coming)
        relays = (cross == 1) & ((coming <= level) | (coming < low))

        @pl.when(relays & (via < level))
        def _():
            for i in range(pieces):
                make(via, i, 0).wait_recv()

                @pl.when(to_up)
                def _(i=i):
                    make(via, i, 0).start()

                if i < detour:

                    @pl.when(jnp.logical_not((via == 0) & not_across))
                    def _(i=i):
                        make(via, i, 2).start()

                else:
                    make(via, i, 2).start()

        @pl.when(relays & (via > level))
        def _():
            for i in range(pieces):
                make(via, i, 1).wait_recv()

                @pl.when(level > 0)
                def _(i=i):
                    make(via, i, 1).start()

                make(via, i, 2).start()

        comes = live & (cross == 1) & ((at < low) | (at < level) | (side == 1))

        @pl.when(comes)
        def _():
            for i in range(pieces):
                if i >= detour:
                    other(at, i).wait_recv()
                    continue

                @pl.when((at == 0) & by_line)
                def _(i=i):
                    lent(i).wait_recv()

                @pl.when(jnp.logical_not((at == 0) & by_line))
                def _(i=i):
                    other(at, i).wait_recv()

                @pl.when((at == 0) & lends)
                def _(i=i):
                    lent(i).start()

        blk = 2 * at + jnp.where(cross == 0, side, 1 - side)
        needed = line_in | comes

        @pl.when(needed & (blk < place))
        def _():
            block(blk, False)

        @pl.when(needed & (blk >= place))
        def _():
            block(blk, True)

        return carry

    lax.fori_loop(0, 2 * levels, event, 0)

    for h in range(heads):
        total = acc_ref[h, HD : HD + 1, :]
        out = (acc_ref[h, :HD, :] / total).T
        o_ref[:, h * HD : (h + 1) * HD] = out
        ob_ref[:, h * HD : (h + 1) * HD] = out.astype(BF16)
        lse_ref[h : h + 1, :] = m_ref[h : h + 1, :] * LOG2E + jnp.log2(total)

    when(to_up, lambda i: make(level, i, 0, kv_ref).wait_send())
    when(own_side, lambda i: make(level, i, 2, kv_ref).wait_send())
    when(own_down, lambda i: make(level, i, 1, kv_ref).wait_send())
    for k in range(1, levels):
        at = level - k
        when((at >= 0) & to_up, lambda i, at=at: make(at, i, 0).wait_send())
        for i in range(pieces):
            sent = at >= 0
            if i < detour:
                sent = sent & jnp.logical_not((at == 0) & not_across)

            @pl.when(sent)
            def _(at=at, i=i):
                make(at, i, 2).wait_send()

    for k in range(1, low):
        at = level + k
        when((at < low) & (level > 0), lambda i, at=at: make(at, i, 1).wait_send())
        when(at < low, lambda i, at=at: make(at, i, 2).wait_send())
    for i in range(detour):

        @pl.when(lends)
        def _(i=i):
            lent(i).wait_send()

    for copy in wide:
        copy.wait()


def attention_forward(info, q, kv, g, group, low, collective):
    pieces = 4
    levels = group // 2
    tokens, width = q.shape
    heads = width // HD
    return pl.pallas_call(
        functools.partial(forward_kernel, group, low, pieces, tokens // 2),
        out_shape=(
            jax.ShapeDtypeStruct((group,) + kv.shape, kv.dtype),
            jax.ShapeDtypeStruct((tokens, width), F32),
            jax.ShapeDtypeStruct((tokens, width), BF16),
            jax.ShapeDtypeStruct((8, tokens), F32),
            jax.ShapeDtypeStruct((COLS,) + g.shape, g.dtype),
        ),
        in_specs=[SSPEC, VSPEC, VSPEC, VSPEC],
        out_specs=(VSPEC,) * 5,
        scratch_shapes=[
            pltpu.VMEM((8, tokens), F32),
            pltpu.VMEM((heads, HD + 16, tokens), F32),
        ]
        + [DMA((levels, pieces))] * 6
        + [DMA((COLS - 1,))] * 2
        + [DMA((pieces // 2,))] * 2,
        compiler_params=params(collective),
    )(info, q, kv, g)


def backward_kernel(
    group,
    low,
    pieces,
    kb,
    info_ref,
    q_ref,
    kv_ref,
    do_ref,
    lse_ref,
    delta_ref,
    e_ref,
    bias_ref,
    out_ref,
    eo_ref,
    part_ref,
    rx_ref,
    above_ref,
    below_ref,
    snd_ref,
    acc_ref,
    dqt_ref,
    er_ref,
    u_send,
    u_recv,
    d_send,
    d_recv,
    x_send,
    x_recv,
    e_send,
    e_recv,
):
    levels = group // 2
    row, place, level, side, partner = line_places(group)
    prefix = info_ref[0]
    tokens, width = q_ref.shape
    heads = width // HD
    step = tokens // pieces
    line_greet(levels, row, level, partner)
    me = lax.axis_index("col")
    terms = []
    for k in range(1, COLS):
        peer = (me + k) % COLS
        copy = push(
            e_ref.at[peer], er_ref.at[k - 1], e_send.at[k - 1], e_recv.at[k - 1], {"col": peer}
        )
        copy.start()
        terms.append(copy)
    dqt_ref[...] = jnp.zeros(dqt_ref.shape, F32)

    def block(blk, masked, leaves, at):
        def body(j, carry):
            start = pl.multiple_of(j * kb, kb)
            keys = pl.ds(start, kb)
            for h in range(heads):
                feats = slice(h * HD, (h + 1) * HD)
                vals = slice(width + h * HD, width + (h + 1) * HD)
                k, v = kv_ref[blk, keys, feats], kv_ref[blk, keys, vals]
                q, do = q_ref[:, feats], do_ref[:, feats]
                probs = jnp.exp2(nt(k, q) * LOG2E - lse_ref[h : h + 1, :])
                if masked:
                    allowed = seen(blk * tokens + start, place * tokens, probs.shape, prefix)
                    probs = jnp.where(allowed, probs, 0.0)
                grad = (probs * (nt(v, do) - delta_ref[h : h + 1, :])).astype(BF16)
                part_ref[blk, keys, feats] = nn(grad, q).astype(BF16)
                part_ref[blk, keys, vals] = nn(probs.astype(BF16), do).astype(BF16)
                dqt_ref[feats, :] += nn(k.T, grad)

            @pl.when(leaves)
            def _():
                for n in range(kb // step):
                    cross(at, j * (kb // step) + n).start()

            return carry

        lax.fori_loop(0, tokens // kb, body, 0)

    def cross(at, i):
        part = pl.ds(i * step, step)
        return push(
            part_ref.at[2 * at + 1 - side, part],
            rx_ref.at[at, part],
            x_send.at[at, i],
            x_recv.at[at, i],
            {"row": partner},
        )

    def line(at, i, up):
        part = pl.ds(i * step, step)
        sems = (u_send, u_recv) if up else (d_send, d_recv)
        return push(
            snd_ref.at[at, part],
            (below_ref if up else above_ref).at[at, part],
            sems[0].at[at, i],
            sems[1].at[at, i],
            {"row": row + 2 if up else row - 2},
        )

    def gone(at):
        return (at < low) | (at < level) | ((at == level) & (side == 1))

    def comes(at):
        return (at < low) | (at < level) | ((at == level) & (side == 0))

    def total(at, i, from_above, from_below):
        part = pl.ds(i * step, step)
        acc_ref[...] = part_ref[2 * at + side, part].astype(F32)

        @pl.when(comes(at))
        def _():
            cross(at, i).wait_recv()
            acc_ref[...] += rx_ref[at, part].astype(F32)

        if from_above is not None:

            @pl.when(from_above)
            def _():
                line(at, i, False).wait_recv()
                acc_ref[...] += above_ref[at, part].astype(F32)

        if from_below is not None:

            @pl.when(from_below)
            def _():
                line(at, i, True).wait_recv()
                acc_ref[...] += below_ref[at, part].astype(F32)

    not_top = level < levels - 1
    above = jnp.maximum(low - 1 - level, 0)

    def level_of(t):
        return jnp.where(t < above, low - 1 - t, t - above)

    def event(e, carry):
        t, own = e // 2, e % 2
        at = level_of(t)
        live = (t < above) | (at <= level)

        down = t - (levels - level)

        @pl.when((own == 1) & (down >= 0) & (down < level))
        def _():
            for i in range(pieces):
                total(down, i, not_top, None)
                snd_ref[down, pl.ds(i * step, step)] = acc_ref[...].astype(BF16)
                line(down, i, False).start()

        @pl.when((own == 1) & (t >= 1) & (t - 1 < above))
        def _():
            up = level_of(t - 1)
            for i in range(pieces):
                total(up, i, None, level > 0)
                snd_ref[up, pl.ds(i * step, step)] = acc_ref[...].astype(BF16)
                line(up, i, True).start()

        goes = live & (own == 0) & gone(at)
        blk = 2 * at + jnp.where(own == 1, side, 1 - side)
        needed = goes | (live & (own == 1))

        @pl.when(needed & (blk < place))
        def _():
            block(blk, False, goes, at)

        @pl.when(needed & (blk >= place))
        def _():
            block(blk, True, goes, at)

        return carry

    lax.fori_loop(0, 2 * levels, event, 0)
    for copy in terms:
        copy.wait()

    def finish(r, carry):
        total = e_ref[me, r].astype(F32) + bias_ref[...]
        for k in range(COLS - 1):
            total = total + er_ref[k, r].astype(F32)
        eo_ref[r] = total.astype(BF16)
        return carry

    lax.fori_loop(0, e_ref.shape[1], finish, 0)
    out_ref[:, :width] = (dqt_ref[...] * HD**-0.5).T.astype(BF16)

    for i in range(pieces):
        total(level, i, not_top, (level > 0) & (level < low))
        out_ref[pl.ds(i * step, step), width:] = acc_ref[...].astype(BF16)

    for at in range(levels):
        for i in range(pieces):

            @pl.when(gone(at))
            def _(at=at, i=i):
                cross(at, i).wait_send()

            @pl.when(at < level)
            def _(at=at, i=i):
                line(at, i, False).wait_send()

            if at < low:

                @pl.when(at > level)
                def _(at=at, i=i):
                    line(at, i, True).wait_send()


def attention_backward(info, q, kv_all, do, lse, delta, e, bias, group, low, collective):
    pieces = 4
    levels = group // 2
    tokens, width = q.shape
    both = 2 * width
    block = pltpu.VMEM((levels, tokens, both), BF16)
    return pl.pallas_call(
        functools.partial(backward_kernel, group, low, pieces, tokens // 2),
        out_shape=(
            jax.ShapeDtypeStruct((tokens, width + both), BF16),
            jax.ShapeDtypeStruct(e.shape[1:], BF16),
        ),
        in_specs=[SSPEC] + [VSPEC] * 7,
        out_specs=(VSPEC,) * 2,
        scratch_shapes=[
            pltpu.VMEM(kv_all.shape, BF16),
            block,
            block,
            pltpu.VMEM((low, tokens, both), BF16),
            block,
            pltpu.VMEM((tokens // pieces, both), F32),
            pltpu.VMEM((width, tokens), F32),
            pltpu.VMEM((COLS - 1,) + e.shape[1:], BF16),
        ]
        + [DMA((levels, pieces))] * 6
        + [DMA((COLS - 1,))] * 2,
        compiler_params=params(collective),
    )(info, q, kv_all, do, lse, delta, e, bias)


def product(pieces, a_ref, w_ref, feats, out_ref, snd_ref, rx_ref, far_ref, tot_ref, sems, fill):
    send, recv = sems
    me, sib, across, diag = col_places()
    half = a_ref.shape[0] // 2
    step = half // pieces
    per = w_ref.shape[0] // COLS
    width = out_ref.shape[1]

    def weight(who):
        return w_ref[pl.ds(who * per, per)].reshape(width, 4 * width)[:, feats]

    def term(i, w):
        parts = [nt(a_ref[pl.ds(n * half + i * step, step)], w) for n in range(2)]
        return jnp.concatenate(parts, axis=1)

    def near(i, j):
        part = pl.ds(i * step, step)
        return push(
            snd_ref.at[j, part], rx_ref.at[j, part], send.at[j, i], recv.at[j, i], {"col": sib}
        )

    def over(i):
        part = pl.ds(i * step, step)
        return push(tot_ref.at[part], far_ref.at[part], send.at[2, i], recv.at[2, i], {"col": across})

    w = weight(diag)
    for i in range(pieces):
        snd_ref[0, pl.ds(i * step, step)] = term(i, w).astype(BF16)
        near(i, 0).start()
    w = weight(across)
    for i in range(pieces):
        part = pl.ds(i * step, step)
        mine = term(i, w)
        near(i, 0).wait_recv()
        tot_ref[part] = (mine + rx_ref[0, part].astype(F32)).astype(BF16)
        over(i).start()
    w = weight(sib)
    for i in range(pieces):
        snd_ref[1, pl.ds(i * step, step)] = term(i, w).astype(BF16)
        near(i, 1).start()
    fill()
    w = weight(me)
    for i in range(pieces):
        part = pl.ds(i * step, step)
        mine = term(i, w)
        near(i, 1).wait_recv()
        mine = mine + rx_ref[1, part].astype(F32)
        over(i).wait_recv()
        mine = mine + far_ref[part].astype(F32)
        out_ref[part] = mine[:, :width]
        out_ref[pl.ds(half + i * step, step)] = mine[:, width:]
    for i in range(pieces):
        near(i, 0).wait_send()
        near(i, 1).wait_send()
        over(i).wait_send()


def product_scratch(pieces, tokens, width):
    block = pltpu.VMEM((tokens // 2, 2 * width), BF16)
    pair = pltpu.VMEM((2, tokens // 2, 2 * width), BF16)
    return [pair, pair, block, block, DMA((3, pieces)), DMA((3, pieces))]


def branch_kernel(
    pieces,
    a_ref,
    w_ref,
    x_ref,
    s_ref,
    mid_ref,
    normed_ref,
    rstd_ref,
    h_ref,
    snd_ref,
    rx_ref,
    far_ref,
    tot_ref,
    send,
    recv,
    st_ref,
    all_ref,
    st_send,
    st_recv,
):
    greet(col_peers())
    tokens, width = x_ref.shape
    product(
        pieces,
        a_ref,
        w_ref,
        slice(3 * width, 4 * width),
        mid_ref,
        snd_ref,
        rx_ref,
        far_ref,
        tot_ref,
        (send, recv),
        lambda: None,
    )
    mid = x_ref[...].astype(F32) + mid_ref[...] + own_features(s_ref, 4)
    mid_ref[...] = mid
    part_mean = jnp.mean(mid, axis=-1, keepdims=True)
    part_spread = jnp.sum((mid - part_mean) ** 2, axis=-1, keepdims=True)
    st_ref[...] = to_rows([part_mean, part_spread])
    share(st_ref, all_ref, st_send, st_recv)
    mean = sum(all_ref[b, 0:1] for b in range(COLS)) / COLS
    spread = sum(
        all_ref[b, 1:2] + width * (all_ref[b, 0:1] - mean) ** 2 for b in range(COLS)
    )
    mean, rstd = to_columns([mean, lax.rsqrt(spread / D + epsilon)])
    normed = (mid - mean) * rstd
    normed_ref[...] = normed
    rstd_ref[...] = rstd
    h_ref[...] = (normed * own_features(s_ref, 2) + own_features(s_ref, 3)).astype(BF16)


def branch(a, w, x, s, collective):
    pieces = 4
    tokens, width = a.shape
    rows = jax.ShapeDtypeStruct((tokens, width), F32)
    return pl.pallas_call(
        functools.partial(branch_kernel, pieces),
        out_shape=(
            rows,
            rows,
            jax.ShapeDtypeStruct((tokens, 1), F32),
            jax.ShapeDtypeStruct((tokens, width), BF16),
        ),
        in_specs=[VSPEC] * 4,
        out_specs=(VSPEC,) * 4,
        scratch_shapes=product_scratch(pieces, tokens, width)
        + [
            pltpu.VMEM((8, tokens), F32),
            pltpu.VMEM((COLS, 8, tokens), F32),
            DMA((COLS - 1,)),
            DMA((COLS - 1,)),
        ],
        compiler_params=params(collective),
    )(a, w, x, s)


def input_kernel(
    pieces,
    a_ref,
    w_ref,
    e_ref,
    h_ref,
    gwo_ref,
    mid_ref,
    normed_ref,
    rstd_ref,
    s_ref,
    vec_ref,
    gin_ref,
    eo_ref,
    wt_ref,
    all_ref,
    grad_ref,
    snd_ref,
    rx_ref,
    far_ref,
    tot_ref,
    send,
    recv,
    st_ref,
    st_send,
    st_recv,
    e_send,
    e_recv,
):
    rows = e_ref.shape[0]
    row = lax.axis_index("row")
    order = far_first(rows)
    greet([{"row": (row + k) % rows} for k in order] + col_peers())
    home = []
    for n, k in enumerate(order):
        peer = (row + k) % rows
        copy = push(e_ref.at[peer], eo_ref.at[row], e_send.at[n], e_recv.at[n], {"row": peer})
        copy.start()
        home.append(copy)
    eo_ref[row] = e_ref[row]
    tokens, width = grad_ref.shape

    def fill():
        both = [tn(h_ref[...], a_ref[...]).astype(BF16), gwo_ref[...]]
        wt_ref[...] = jnp.concatenate(both, axis=1)

    product(
        pieces,
        a_ref,
        w_ref,
        slice(0, 3 * width),
        grad_ref,
        snd_ref,
        rx_ref,
        far_ref,
        tot_ref,
        (send, recv),
        fill,
    )
    grad, normed = grad_ref[...], normed_ref[...]
    st_ref[:, tokens:] = jnp.zeros((8, st_ref.shape[1] - tokens), F32)
    st_ref[0:1, tokens : tokens + width] = jnp.sum(grad * normed, axis=0, keepdims=True)
    st_ref[1:2, tokens : tokens + width] = jnp.sum(grad, axis=0, keepdims=True)
    st_ref[2:5, tokens : tokens + width] = vec_ref[0:3]
    gin_ref[...] = mid_ref[...] + norm_back(
        grad, normed, own_features(s_ref, 0), rstd_ref[...], st_ref, all_ref, st_send, st_recv
    )
    for copy in home:
        copy.wait()


def input_gradient(a, w, e, h, gwo, mid, normed, rstd, gain, vec, collective):
    pieces = 4
    tokens, width = mid.shape
    wide = tokens + 256
    return pl.pallas_call(
        functools.partial(input_kernel, pieces),
        out_shape=(
            jax.ShapeDtypeStruct((tokens, width), F32),
            jax.ShapeDtypeStruct(e.shape, BF16),
            jax.ShapeDtypeStruct((D, 4 * width), BF16),
            jax.ShapeDtypeStruct((COLS, 8, wide), F32),
        ),
        in_specs=[VSPEC] * 10,
        out_specs=(VSPEC,) * 4,
        scratch_shapes=[pltpu.VMEM((tokens, width), F32)]
        + product_scratch(pieces, tokens, width)
        + [
            pltpu.VMEM((8, wide), F32),
            DMA((COLS - 1,)),
            DMA((COLS - 1,)),
            DMA((e.shape[0] - 1,)),
            DMA((e.shape[0] - 1,)),
        ],
        compiler_params=params(collective),
    )(a, w, e, h, gwo, mid, normed, rstd, gain, vec)


def dispatch_kernel(rows, x_ref, t_ref, out_ref, in_ref, r_send, r_recv, c_send, c_recv):
    me, sib, across, _ = col_places()
    row = lax.axis_index("row")
    order = far_first(rows)
    peers = [(row + k) % rows for k in order]
    greet([{"row": p} for p in peers] + [{"col": sib}, {"col": across}])
    copies = []
    cap = in_ref.shape[1]

    def col(src, dst, k, way):
        return push(
            src, dst, c_send.at[way, k], c_recv.at[way, k], {"col": across if way == 0 else sib}
        )

    done, first = [], []
    for k, peer in enumerate(peers):
        in_ref[peer] = placed(t_ref, x_ref[...], peer, cap)
        copy = push(
            in_ref.at[peer], out_ref.at[me, row], r_send.at[k], r_recv.at[k], {"row": peer}
        )
        copy.start()
        copies.append(copy)
        if k == 1:
            in_ref[row] = placed(t_ref, x_ref[...], row, cap)
            for way in range(2):
                copy = col(in_ref.at[row], out_ref.at[me, row], 0, way)
                copy.start()
                (first if way == 0 else done).append(copy)
    out_ref[me, row] = in_ref[row]
    sources = [row] + [(row + rows - k) % rows for k in order]

    def forward(k):
        first[k].wait_recv()
        src = sources[k]
        copy = col(out_ref.at[across, src], out_ref.at[across, src], k, 2)
        copy.start()
        done.append(copy)

    for k in range(1, rows):
        copies[k - 1].wait_recv()
        block = out_ref.at[me, sources[k]]
        for way in range(2):
            copy = col(block, block, k, way)
            copy.start()
            (first if way == 0 else done).append(copy)
        forward(k - 1)
    forward(rows - 1)
    for copy in copies:
        copy.wait_send()
    for copy in first:
        copy.wait_send()
    for copy in done:
        copy.wait()


def dispatch(x, target, rows, cap, collective):
    block = (rows, cap, 2 * x.shape[1])
    return pl.pallas_call(
        functools.partial(dispatch_kernel, rows),
        out_shape=jax.ShapeDtypeStruct((COLS,) + block, x.dtype),
        in_specs=[VSPEC] * 2,
        out_specs=VSPEC,
        scratch_shapes=[
            pltpu.VMEM(block, x.dtype),
            DMA((rows - 1,)),
            DMA((rows - 1,)),
            DMA((3, rows)),
            DMA((3, rows)),
        ],
        compiler_params=params(collective),
    )(x, target)


def giveback_kernel(
    rows,
    in_ref,
    t_ref,
    cot_ref,
    normed_ref,
    rstd_ref,
    s_ref,
    mid_ref,
    vec_ref,
    sum_ref,
    out_ref,
    rx_ref,
    far_ref,
    tot_ref,
    fin_ref,
    st_ref,
    all_ref,
    send,
    recv,
    r_send,
    r_recv,
    st_send,
    st_recv,
):
    me, sib, across, diag = col_places()
    row = lax.axis_index("row")
    order = [(row + k) % rows for k in far_first(rows)] + [row]
    greet([{"row": p} for p in order[:-1]] + col_peers())

    def near(k, j):
        who = diag if j == 0 else sib
        return push(
            in_ref.at[who, order[k]], rx_ref.at[j, k], send.at[j, k], recv.at[j, k], {"col": sib}
        )

    def over(k):
        return push(tot_ref.at[k], far_ref.at[k], send.at[2, k], recv.at[2, k], {"col": across})

    def home(k):
        return push(
            fin_ref.at[k], out_ref.at[row], r_send.at[k], r_recv.at[k], {"row": order[k]}
        )

    for k in range(rows):
        near(k, 0).start()
        near(k, 1).start()

    def finish(k):
        near(k, 1).wait_recv()
        over(k).wait_recv()
        total = in_ref[me, order[k]].astype(F32) + rx_ref[1, k].astype(F32)
        total = total + far_ref[k].astype(F32)
        if k == rows - 1:
            out_ref[row] = total.astype(BF16)
        else:
            fin_ref[k] = total.astype(BF16)
            home(k).start()

    for k in range(rows):
        near(k, 0).wait_recv()
        tot_ref[k] = (in_ref[across, order[k]].astype(F32) + rx_ref[0, k].astype(F32)).astype(BF16)
        over(k).start()
        if k >= 1:
            finish(k - 1)
    finish(rows - 1)
    cap = out_ref.shape[1]
    sum_ref[...] = combined(t_ref, out_ref[row], row, cap)
    for k, gap in enumerate(far_first(rows)):
        source = (row + rows - gap) % rows
        home(k).wait_recv()
        sum_ref[...] += combined(t_ref, out_ref[source], source, cap)
    grad, normed = sum_ref[...], normed_ref[...]
    mid = cot_ref[...].astype(F32) + norm_back(
        grad, normed, own_features(s_ref, 2), rstd_ref[...], st_ref, all_ref, st_send, st_recv
    )
    mid_ref[...] = mid
    vec_ref[...] = jnp.zeros(vec_ref.shape, F32)
    vec_ref[0:1] = jnp.sum(grad * normed, axis=0, keepdims=True)
    vec_ref[1:2] = jnp.sum(grad, axis=0, keepdims=True)
    vec_ref[2:3] = jnp.sum(mid, axis=0, keepdims=True)
    for k in range(rows):
        near(k, 0).wait_send()
        near(k, 1).wait_send()
        over(k).wait_send()
        if k < rows - 1:
            home(k).wait_send()


def giveback(parts, target, cot, normed, rstd, gain, rows, collective):
    block = parts.shape[2:]
    one = pltpu.VMEM((rows,) + block, BF16)
    return pl.pallas_call(
        functools.partial(giveback_kernel, rows),
        out_shape=(
            jax.ShapeDtypeStruct(cot.shape, F32),
            jax.ShapeDtypeStruct((8, cot.shape[1]), F32),
        ),
        in_specs=[VSPEC] * 6,
        out_specs=(VSPEC,) * 2,
        scratch_shapes=[
            pltpu.VMEM(cot.shape, F32),
            one,
            pltpu.VMEM((2, rows) + block, BF16),
            one,
            one,
            one,
            pltpu.VMEM((8, cot.shape[0]), F32),
            pltpu.VMEM((COLS, 8, cot.shape[0]), F32),
            DMA((3, rows)),
            DMA((3, rows)),
            DMA((rows - 1,)),
            DMA((rows - 1,)),
            DMA((COLS - 1,)),
            DMA((COLS - 1,)),
        ],
        compiler_params=params(collective),
    )(parts, target, cot, normed, rstd, gain)


def end_kernel(
    rows,
    w_ref,
    s_ref,
    e_ref,
    t_ref,
    mid_ref,
    wo_ref,
    so_ref,
    lo_ref,
    px_ref,
    pt_ref,
    wr_ref,
    sr_ref,
    p_send,
    p_recv,
    l_send,
    l_recv,
    send,
    recv,
):
    row, _, level, side, partner = line_places(rows)
    levels = rows // 2
    peers = [(row + k) % rows for k in far_first(rows)]
    greet([{"row": p} for p in peers])
    gaps = far_first(levels)
    targets = [(level + k) % levels for k in gaps] + [level]

    def cross(n):
        src = w_ref.at[2 * targets[n] + 1 - side]
        return push(src, px_ref.at[n], p_send.at[n], p_recv.at[n], {"row": partner})

    def along(n):
        peer = {"row": 2 * targets[n] + side}
        return push(pt_ref.at[n], wr_ref.at[n], l_send.at[n], l_recv.at[n], peer)

    def total(n):
        return w_ref[2 * targets[n] + side].astype(F32) + px_ref[n].astype(F32)

    for n in range(levels):
        cross(n).start()
    copies = []
    for k, peer in enumerate(peers):
        copy = push(s_ref.at[peer], sr_ref.at[k], send.at[k], recv.at[k], {"row": peer})
        copy.start()
        copies.append(copy)
    for n in range(levels - 1):
        cross(n).wait_recv()
        pt_ref[n] = total(n).astype(BF16)
        along(n).start()
    result = mid_ref[...]
    for r in range(rows):
        result = result + combined(t_ref, e_ref[r], r, e_ref.shape[1])
    lo_ref[...] = result.astype(BF16)
    small = s_ref[row]
    for k, copy in enumerate(copies):
        copy.wait_recv()
        small = small + sr_ref[k]
    so_ref[...] = small
    cross(levels - 1).wait_recv()
    mine = total(levels - 1)
    for n in range(levels - 1):
        along(n).wait_recv()
        mine = mine + wr_ref[n].astype(F32)
    wo_ref[...] = mine
    for n in range(levels):
        cross(n).wait_send()
        if n < levels - 1:
            along(n).wait_send()
    for copy in copies:
        copy.wait_send()


def end_scatter(w, s, outs, target, mid, rows, collective):
    levels = rows // 2
    one = w.shape[1:]
    return pl.pallas_call(
        functools.partial(end_kernel, rows),
        out_shape=(
            jax.ShapeDtypeStruct(one, F32),
            jax.ShapeDtypeStruct(s.shape[1:], F32),
            jax.ShapeDtypeStruct(mid.shape, BF16),
        ),
        in_specs=[VSPEC] * 5,
        out_specs=(VSPEC,) * 3,
        scratch_shapes=[
            pltpu.VMEM((levels,) + one, w.dtype),
            pltpu.VMEM((levels - 1,) + one, w.dtype),
            pltpu.VMEM((levels - 1,) + one, w.dtype),
            pltpu.VMEM((rows - 1,) + s.shape[1:], s.dtype),
            DMA((levels,)),
            DMA((levels,)),
            DMA((levels - 1,)),
            DMA((levels - 1,)),
            DMA((rows - 1,)),
            DMA((rows - 1,)),
        ],
        compiler_params=params(collective),
    )(w, s, outs, target, mid)


def expert_kernel(
    x_ref,
    g_ref,
    up_hbm,
    bias_ref,
    down_hbm,
    part_ref,
    gx_ref,
    gup_hbm,
    gbu_ref,
    gdown_hbm,
    gbd_ref,
    up_ref,
    down_ref,
    gup_ref,
    gdown_ref,
    xs_ref,
    gs_ref,
    sum_ref,
    gsum_ref,
    in_sems,
    out_sems,
):
    cols, rows, cap, both = x_ref.shape
    width = both // 2
    slots = rows * cap
    count, _, hidden_units = up_ref.shape
    chunk = 256
    loads = []
    for e in range(count):
        for j, (src, dst) in enumerate(((up_hbm, up_ref), (down_hbm, down_ref))):
            copy = pltpu.make_async_copy(src.at[e], dst.at[e], in_sems.at[j, e])
            copy.start()
            loads.append(copy)

    def gup_out(e, f):
        cut = pl.ds(pl.multiple_of(f * chunk, chunk), chunk)
        return pltpu.make_async_copy(
            gup_ref.at[e, :, cut], gup_hbm.at[e, :, cut], out_sems.at[0, e, f]
        )

    def gdown_out(e, f):
        cut = pl.ds(pl.multiple_of(f * chunk, chunk), chunk)
        return pltpu.make_async_copy(
            gdown_ref.at[e, cut], gdown_hbm.at[e, cut], out_sems.at[1, e, f]
        )

    for e in range(count):
        lanes = slice(e * width, (e + 1) * width)
        for ref, dst in ((x_ref, xs_ref), (g_ref, gs_ref)):
            blocks = [ref[b].reshape(slots, both)[:, lanes] for b in range(cols)]
            dst[...] = jnp.concatenate(blocks, axis=1)
        gbd_ref[e] = jnp.sum(gs_ref[...].astype(F32), axis=0, keepdims=True)
        sum_ref[...] = jnp.zeros(sum_ref.shape, F32)
        gsum_ref[...] = jnp.zeros(gsum_ref.shape, F32)
        loads[2 * e].wait()
        loads[2 * e + 1].wait()

        def body(f, carry, e=e):
            cut = pl.ds(pl.multiple_of(f * chunk, chunk), chunk)
            x, g = xs_ref[...], gs_ref[...]
            up, down = up_ref[e, :, cut], down_ref[e, cut, :]
            pre = nn(x, up) + bias_ref[e, :, cut].astype(F32)
            cdf = 0.5 * (1.0 + lax.erf(pre * (0.5**0.5)))
            slope = cdf + pre * (jnp.exp(-0.5 * pre * pre) * 0.3989422804014327)
            hidden = (pre * cdf).astype(BF16)
            grad = nt(g, down) * slope
            grad = grad.astype(BF16)
            sum_ref[...] += nn(hidden, down)
            gsum_ref[...] += nt(grad, up)
            gdown_ref[e, cut, :] = tn(hidden, g)
            gdown_out(e, f).start()
            gup_ref[e, :, cut] = tn(x, grad)
            gup_out(e, f).start()
            gbu_ref[e, :, cut] = jnp.sum(grad.astype(F32), axis=0, keepdims=True)
            return carry

        lax.fori_loop(0, hidden_units // chunk, body, 0)
        for b in range(cols):
            cut = slice(b * width, (b + 1) * width)
            part_ref[b, :, :, lanes] = sum_ref[:, cut].astype(BF16).reshape(rows, cap, width)
            gx_ref[b, :, :, lanes] = gsum_ref[:, cut].astype(BF16).reshape(rows, cap, width)
    for e in range(count):
        for f in range(hidden_units // chunk):
            gdown_out(e, f).wait()
            gup_out(e, f).wait()


def experts(x, g, w_up, bias_up, w_down):
    cols, rows, cap, _ = x.shape
    count, features, hidden = w_up.shape
    slots = rows * cap
    anywhere = pl.BlockSpec(memory_space=pl.ANY)
    return pl.pallas_call(
        expert_kernel,
        out_shape=(
            jax.ShapeDtypeStruct(x.shape, BF16),
            jax.ShapeDtypeStruct(x.shape, BF16),
            jax.ShapeDtypeStruct(w_up.shape, F32),
            jax.ShapeDtypeStruct((count, 1, hidden), F32),
            jax.ShapeDtypeStruct(w_down.shape, F32),
            jax.ShapeDtypeStruct((count, 1, features), F32),
        ),
        in_specs=[VSPEC, VSPEC, anywhere, VSPEC, anywhere],
        out_specs=(VSPEC, VSPEC, anywhere, VSPEC, anywhere, VSPEC),
        scratch_shapes=[
            pltpu.VMEM(w_up.shape, BF16),
            pltpu.VMEM(w_down.shape, BF16),
            pltpu.VMEM(w_up.shape, F32),
            pltpu.VMEM(w_down.shape, F32),
            pltpu.VMEM((slots, features), BF16),
            pltpu.VMEM((slots, features), BF16),
            pltpu.VMEM((slots, features), F32),
            pltpu.VMEM((slots, features), F32),
            DMA((2, count)),
            DMA((2, count, hidden // 256)),
        ],
        compiler_params=params(),
    )(x, g, w_up, bias_up.reshape(count, 1, hidden), w_down)


def per_device(
    layer_in,
    cotangent,
    token_ids,
    hash_table,
    prefix_len,
    w_query,
    w_key,
    w_value,
    w_output,
    bias_query,
    bias_value,
    gain_attn,
    shift_attn,
    gain_moe,
    shift_moe,
    bias_output,
    w_up,
    bias_up,
    w_down,
    bias_down,
):
    rows = lax.axis_size("row")
    row = lax.axis_index("row")
    col = lax.axis_index("col")
    tokens, width = layer_in.shape
    heads = width // HD
    seq_len = min(LENGTH, tokens * rows)
    group = seq_len // tokens
    low = -(-PREFIX_MAX // (2 * tokens))
    share = w_query.shape[0]
    bias_share = bias_query.shape[0]

    def line(v):
        return jnp.pad(v.astype(F32), (0, 128 - v.shape[0]))

    small = jnp.stack(
        [
            line(gain_attn),
            line(shift_attn),
            line(gain_moe),
            line(shift_moe),
            line(bias_output),
            line(bias_query.T.reshape(-1)),
            line(bias_value.T.reshape(-1)),
            jnp.zeros((128,), F32),
        ]
    )
    expert_total = EXP_DEV * rows
    capacity = max(2, 2 * tokens // expert_total)
    table = jnp.pad(hash_table, (0, -hash_table.shape[0] % (128 * 128)))
    table = table.reshape(-1, 128).astype(BF16)

    weights = jnp.concatenate([w_query, w_key, w_value, w_output], axis=1)
    x_all, g_own, w_all, s_all, target = start_gather(
        layer_in, cotangent, token_ids[None], table, weights, small, rows, capacity
    )

    queries, keys_values, h_one, normed_one, rstd_one = project(x_all, w_all, s_all)
    seq_hit = row // group == jnp.arange(prefix_len.shape[0], dtype=jnp.int32)
    prefix = jnp.sum(jnp.where(seq_hit, prefix_len, 0))
    info = prefix.astype(jnp.int32).reshape(1)
    kv_all, attended, attended_low, lse, g_all = attention_forward(
        info, queries, keys_values, g_own, group, low, 1
    )
    mid, normed_two, rstd_two, h_two = branch(attended_low, w_all, layer_in, s_all, 2)

    received = dispatch(h_two, target, rows, capacity, 4)
    parts, grad_parts, grad_w_up, grad_bias_up, grad_w_down, grad_bias_down = experts(
        received, g_all, w_up, bias_up, w_down
    )
    grad_mid, vectors = giveback(
        grad_parts, target, cotangent, normed_two, rstd_two, s_all, rows, 5
    )
    grad_attended, delta, grad_w_out = mid_gradient(grad_mid, w_all, attended, attended_low, 7)
    down_own = lax.dynamic_slice_in_dim(bias_down, col * width, width, 1).astype(F32)
    down_own = down_own.reshape(1, EXP_DEV * width)
    grad_qkv, outs = attention_backward(
        info,
        queries,
        kv_all,
        grad_attended,
        lse,
        delta,
        parts,
        down_own,
        group,
        low,
        8,
    )
    grad_bias = jnp.sum(grad_qkv, axis=0, dtype=F32)
    grad_in, outs, weight_terms, shared = input_gradient(
        grad_qkv,
        w_all,
        outs,
        h_one,
        grad_w_out,
        grad_mid,
        normed_one,
        rstd_one,
        s_all,
        vectors,
        9,
    )
    vectors = shared[:, :5, tokens : tokens + width]
    vectors = vectors.transpose(1, 0, 2).reshape(5, rows, share).transpose(1, 0, 2)

    def by_row(v):
        v = v.reshape(heads, rows, bias_share).transpose(1, 0, 2).reshape(rows, 1, -1)
        return jnp.pad(v, ((0, 0), (0, 0), (0, 128 - v.shape[2])))

    small_terms = jnp.concatenate(
        [
            jnp.pad(vectors, ((0, 0), (0, 0), (0, 128 - share))),
            by_row(grad_bias[:width]),
            by_row(grad_bias[2 * width :]),
            jnp.zeros((rows, 1, 128), F32),
        ],
        axis=1,
    )
    weight_terms = weight_terms.reshape(rows, share, 4 * width)
    weight_sums, small_sums, layer_out = end_scatter(
        weight_terms, small_terms, outs, target, mid, rows, 11
    )

    def bias_back(v):
        return v[: heads * bias_share].reshape(heads, bias_share).T

    return (
        layer_out,
        grad_in,
        weight_sums[:, :width],
        weight_sums[:, width : 2 * width],
        weight_sums[:, 2 * width : 3 * width],
        weight_sums[:, 3 * width :],
        bias_back(small_sums[5]),
        bias_back(small_sums[6]),
        small_sums[0, :share],
        small_sums[1, :share],
        small_sums[2, :share],
        small_sums[3, :share],
        small_sums[4, :share],
        grad_w_up,
        grad_bias_up[:, 0],
        grad_w_down,
        grad_bias_down[:, 0],
    )


def solution(mesh):
    placed = (
        P("row", "col"),
        P("row", "col"),
        P("row"),
        P(),
        P(),
        P("row", "col"),
        P("row", "col"),
        P("row", "col"),
        P("row", "col"),
        P("row", "col"),
        P("row", "col"),
        P("row"),
        P("row"),
        P("row"),
        P("row"),
        P("row"),
        P("row", None, "col"),
        P("row", "col"),
        P("row", "col", None),
        P("row", None),
    )
    return jax.shard_map(
        per_device,
        mesh=mesh,
        in_specs=placed,
        out_specs=(
            P("row", "col"),
            P("row", "col"),
            P("row", "col"),
            P("row", "col"),
            P("row", "col"),
            P("row", "col"),
            P("row", "col"),
            P("row", "col"),
            P("row"),
            P("row"),
            P("row"),
            P("row"),
            P("row"),
            P("row", None, "col"),
            P("row", "col"),
            P("row", "col", None),
            P("row", None),
        ),
        check_vma=False,
    )
```

```python
import functools

import jax
import jax.numpy as jnp
from jax import lax
from jax.experimental import pallas as pl
from jax.experimental.pallas import tpu as pltpu
from jax.sharding import PartitionSpec as P

D = 768
HD = 64
EXP_DEV = 2
LENGTH = 8192
PREFIX_MAX = 4096
COLS = 4

F32 = jnp.float32
BF16 = jnp.bfloat16
MESH = pl.DeviceIdType.MESH
LOG2E = 1.4426950408889634

epsilon = 1e-05
neg_big = -1e30

VSPEC = pl.BlockSpec(memory_space=pltpu.VMEM)
SSPEC = pl.BlockSpec(memory_space=pltpu.SMEM)
VMEM_BYTES = 64 * 1000 * 1000
DMA = pltpu.SemaphoreType.DMA


def params(collective=None):
    if collective is None:
        return pltpu.CompilerParams(vmem_limit_bytes=VMEM_BYTES)
    return pltpu.CompilerParams(
        vmem_limit_bytes=VMEM_BYTES, collective_id=collective, has_side_effects=True
    )


def push(src, dst, send_sem, recv_sem, peer):
    return pltpu.make_async_remote_copy(
        src_ref=src,
        dst_ref=dst,
        send_sem=send_sem,
        recv_sem=recv_sem,
        device_id=peer,
        device_id_type=MESH,
    )


def greet(peers):
    barrier = pltpu.get_barrier_semaphore()
    for peer in peers:
        pl.semaphore_signal(barrier, inc=1, device_id=peer, device_id_type=MESH)
    pl.semaphore_wait(barrier, len(peers))


def col_places():
    me = lax.axis_index("col")
    sib = me + 1 - 2 * (me % 2)
    across = (me + 2) % COLS
    diag = (sib + 2) % COLS
    return me, sib, across, diag


def line_places(group):
    row = lax.axis_index("row")
    place = row % group
    level, side = place // 2, place % 2
    return row, place, level, side, row + 1 - 2 * side


def far_first(rows):
    return sorted(range(1, rows), key=lambda k: -min(k, rows - k))


def nt(left, right):
    return lax.dot_general(left, right, (((1,), (1,)), ((), ())), preferred_element_type=F32)


def nn(left, right):
    return lax.dot_general(left, right, (((1,), (0,)), ((), ())), preferred_element_type=F32)


def tn(left, right):
    return lax.dot_general(left, right, (((0,), (0,)), ((), ())), preferred_element_type=F32)


def side_by_side(v):
    half = v.shape[0] // 2
    return jnp.concatenate([v[:half], v[half:]], axis=1)


def number(shape, axis):
    return lax.broadcasted_iota(jnp.int32, shape, axis)


def route(ids, table, experts, cap):
    tokens = ids.shape[1]
    pick = jnp.where(number((table.shape[0], tokens), 0) == ids >> 7, 1.0, 0.0).astype(BF16)
    found = tn(table, pick)
    expert = jnp.where(number((128, tokens), 0) == ids & 127, found, 0.0)
    expert = jnp.sum(expert, axis=0, keepdims=True)
    hit = number((experts, tokens), 0).astype(F32) == expert
    pair = (tokens, tokens)
    earlier = jnp.where(number(pair, 0) < number(pair, 1), 1.0, 0.0).astype(BF16)
    before = nn(jnp.where(hit, 1.0, 0.0).astype(BF16), earlier)
    slot = jnp.sum(jnp.where(hit, before, 0.0), axis=0, keepdims=True)
    return (expert * cap + slot).astype(jnp.int32)


def all_features(s_ref, i):
    rows = s_ref.shape[0]
    return jnp.concatenate([s_ref[r, i : i + 1, : D // rows] for r in range(rows)], axis=1)


def own_features(s_ref, i):
    rows = s_ref.shape[0]
    per = rows // COLS
    block = s_ref[pl.ds(lax.axis_index("col") * per, per)]
    return jnp.concatenate([block[r, i : i + 1, : D // rows] for r in range(per)], axis=1)


def head_features(s_ref, i, heads):
    rows = s_ref.shape[0]
    size = HD // rows
    cuts = [slice(h * size, (h + 1) * size) for h in range(heads)]
    return jnp.concatenate([s_ref[r, i : i + 1, c] for c in cuts for r in range(rows)], axis=1)


def slots_of(target_ref, row, count):
    base = row * count
    slot = base + lax.broadcasted_iota(jnp.int32, (count, target_ref.shape[1]), 0)
    return jnp.where(slot == target_ref[...], 1.0, 0.0).astype(BF16)


def placed(target_ref, v, row, cap):
    return side_by_side(nn(slots_of(target_ref, row, 2 * cap), v).astype(BF16))


def combined(target_ref, block, row, cap):
    width = block.shape[1] // 2
    stacked = jnp.concatenate([block[:, :width], block[:, width:]], axis=0)
    return tn(slots_of(target_ref, row, 2 * cap), stacked)


def start_kernel(
    rows,
    pieces,
    x_ref,
    g_ref,
    ids_ref,
    table_ref,
    w_ref,
    s_ref,
    xo_ref,
    go_ref,
    wo_ref,
    so_ref,
    t_ref,
    xp_ref,
    gp_ref,
    c_send,
    c_recv,
    r_send,
    r_recv,
    l_send,
    l_recv,
):
    me, sib, across, _ = col_places()
    row, _, level, side, partner = line_places(rows)
    levels = rows // 2
    order = far_first(rows)
    peers = [{"row": (row + k) % rows} for k in order]
    greet(peers + [{"col": sib}, {"col": across}])
    xp_ref[...] = side_by_side(x_ref[...])
    step = xp_ref.shape[0] // pieces
    cap = gp_ref.shape[1]
    to_up, to_down = level < levels - 1, level > 0

    def weight(at, way, src=None):
        dst = wo_ref.at[2 * at + side]
        peer = (row + 2, row - 2, partner)[way]
        return push(
            dst if src is None else src,
            dst,
            l_send.at[way, at],
            l_recv.at[way, at],
            {"row": peer},
        )

    def weight_other(at):
        dst = wo_ref.at[2 * at + 1 - side]
        return push(dst, dst, l_send.at[2, at], l_recv.at[2, at], {"row": partner})

    @pl.when(to_up)
    def _():
        weight(level, 0, w_ref).start()

    @pl.when(to_down)
    def _():
        weight(level, 1, w_ref).start()

    weight(level, 2, w_ref).start()
    sent = []
    for i in range(pieces):
        part = pl.ds(i * step, step)
        for way, peer in ((0, across), (1, sib)):
            copy = push(
                xp_ref.at[part],
                xo_ref.at[me, part],
                c_send.at[way, i],
                c_recv.at[way, i],
                {"col": peer},
            )
            copy.start()
            sent.append(copy)
    row_copies = []
    for k, peer in enumerate(peers):
        copy = push(s_ref, so_ref.at[row], r_send.at[0, k], r_recv.at[0, k], peer)
        copy.start()
        row_copies.append(copy)

    def send_rows(k):
        target = (row + order[k]) % rows
        gp_ref[k] = placed(t_ref, g_ref[...], target, cap)
        copy = push(gp_ref.at[k], go_ref.at[row], r_send.at[1, k], r_recv.at[1, k], peers[k])
        copy.start()
        row_copies.append(copy)

    t_ref[...] = route(ids_ref[...], table_ref[...], EXP_DEV * rows, cap)
    send_rows(0)
    xo_ref[me] = xp_ref[...]
    wo_ref[row] = w_ref[...]
    so_ref[row] = s_ref[...]
    todo = list(range(1, rows - 1))

    def pass_on(k):
        at = level - k

        @pl.when(at >= 0)
        def _():
            weight(at, 0).wait_recv()

            @pl.when(to_up)
            def _():
                weight(at, 0).start()

            weight(at, 2).start()

        up = level + k

        @pl.when(up < levels)
        def _():
            weight(up, 1).wait_recv()

            @pl.when(to_down)
            def _():
                weight(up, 1).start()

            weight(up, 2).start()

    late = []
    for k in range(1, max(levels, pieces + 1)):
        if k < levels:
            pass_on(k)
        if k <= pieces:
            part = pl.ds((k - 1) * step, step)
            sent[2 * k - 2].wait_recv()
            copy = push(
                xo_ref.at[across, part],
                xo_ref.at[across, part],
                c_send.at[2, k - 1],
                c_recv.at[2, k - 1],
                {"col": sib},
            )
            copy.start()
            late.append(copy)
        for _ in range(2):
            if todo:
                send_rows(todo.pop(0))
    while todo:
        send_rows(todo.pop(0))
    go_ref[row] = placed(t_ref, g_ref[...], row, cap)
    for i in range(pieces):
        sent[2 * i].wait_send()
        sent[2 * i + 1].wait()
        late[i].wait()
    for at in range(levels):
        weight_other(at).wait_recv()
        weight(at, 2).wait_send()

        @pl.when((at <= level) & to_up)
        def _(at=at):
            weight(at, 0).wait_send()

        @pl.when((at >= level) & to_down)
        def _(at=at):
            weight(at, 1).wait_send()

    for copy in row_copies:
        copy.wait()


def start_gather(x, g, ids, table, w, s, rows, cap):
    pieces = 4
    tokens, width = x.shape
    packed = (tokens // 2, 2 * width)
    return pl.pallas_call(
        functools.partial(start_kernel, rows, pieces),
        out_shape=(
            jax.ShapeDtypeStruct((COLS,) + packed, x.dtype),
            jax.ShapeDtypeStruct((rows, cap, 2 * width), g.dtype),
            jax.ShapeDtypeStruct((rows,) + w.shape, w.dtype),
            jax.ShapeDtypeStruct((rows,) + s.shape, s.dtype),
            jax.ShapeDtypeStruct((1, tokens), jnp.int32),
        ),
        in_specs=[VSPEC] * 6,
        out_specs=(VSPEC,) * 5,
        scratch_shapes=[
            pltpu.VMEM(packed, x.dtype),
            pltpu.VMEM((rows - 1, cap, 2 * width), g.dtype),
            DMA((3, pieces)),
            DMA((3, pieces)),
            DMA((2, rows - 1)),
            DMA((2, rows - 1)),
            DMA((3, rows // 2)),
            DMA((3, rows // 2)),
        ],
        compiler_params=params(0),
    )(x, g, ids, table, w, s)


def project_kernel(
    x_ref, w_ref, s_ref, q_ref, kv_ref, h_ref, n_ref, r_ref
):
    me = lax.axis_index("col")
    half, width = x_ref.shape[1], x_ref.shape[2] // 2
    gain, shift = all_features(s_ref, 0), all_features(s_ref, 1)
    query = head_features(s_ref, 5, width // HD)
    value = head_features(s_ref, 6, width // HD)
    bias = jnp.concatenate([query, jnp.zeros_like(query), value], axis=1)
    w = w_ref[...].reshape(D, 4 * width)[:, : 3 * width]
    step = min(half, 256)
    for i in range(2 * half // step):
        side, start = i * step // half, i * step % half
        rows, feats = slice(start, start + step), slice(side * width, (side + 1) * width)
        x = jnp.concatenate([x_ref[b, rows, feats] for b in range(COLS)], axis=1).astype(F32)
        mean = jnp.mean(x, axis=-1, keepdims=True)
        centred = x - mean
        rstd = lax.rsqrt(jnp.mean(centred * centred, axis=-1, keepdims=True) + epsilon)
        h = (centred * rstd * gain + shift).astype(BF16)
        out = slice(i * step, (i + 1) * step)
        h_ref[out] = h
        n_ref[out] = (x_ref[me, rows, feats].astype(F32) - mean) * rstd
        r_ref[out] = rstd
        qkv = (nn(h, w) + bias).astype(BF16)
        q_ref[out] = qkv[:, :width] * jnp.asarray(HD**-0.5, BF16)
        kv_ref[out] = qkv[:, width:]


def project(x, w, s):
    tokens, width = 2 * x.shape[1], x.shape[2] // 2
    return pl.pallas_call(
        project_kernel,
        out_shape=(
            jax.ShapeDtypeStruct((tokens, width), BF16),
            jax.ShapeDtypeStruct((tokens, 2 * width), BF16),
            jax.ShapeDtypeStruct((tokens, D), BF16),
            jax.ShapeDtypeStruct((tokens, width), F32),
            jax.ShapeDtypeStruct((tokens, 1), F32),
        ),
        in_specs=[VSPEC] * 3,
        out_specs=(VSPEC,) * 5,
        compiler_params=params(),
    )(x, w, s)


def mid_kernel(
    pieces,
    x_ref,
    w_ref,
    att_ref,
    low_ref,
    do_ref,
    delta_ref,
    gw_ref,
    xp_ref,
    xo_ref,
    wide_ref,
    c_send,
    c_recv,
):
    me, sib, across, _ = col_places()
    greet([{"col": sib}, {"col": across}])
    xp_ref[...] = side_by_side(x_ref[...].astype(BF16))
    step = xp_ref.shape[0] // pieces
    sent, late = [], []
    for i in range(pieces):
        part = pl.ds(i * step, step)
        for way, peer in ((0, across), (1, sib)):
            copy = push(
                xp_ref.at[part],
                xo_ref.at[me, part],
                c_send.at[way, i],
                c_recv.at[way, i],
                {"col": peer},
            )
            copy.start()
            sent.append(copy)
    xo_ref[me] = xp_ref[...]
    tokens, width = x_ref.shape
    w = w_ref[...].reshape(D, 4 * width)[:, 3 * width :]
    for i in range(pieces):
        part = pl.ds(i * step, step)
        sent[2 * i].wait_recv()
        copy = push(
            xo_ref.at[across, part],
            xo_ref.at[across, part],
            c_send.at[2, i],
            c_recv.at[2, i],
            {"col": sib},
        )
        copy.start()
        late.append(copy)
    for i in range(pieces):
        sent[2 * i].wait_send()
        sent[2 * i + 1].wait()
        late[i].wait()
        rows = slice(i * step, (i + 1) * step)
        for half in range(2):
            feats = slice(half * width, (half + 1) * width)
            start = half * (tokens // 2) + i * step
            out = slice(start, start + step)
            wide = jnp.concatenate([xo_ref[b, rows, feats] for b in range(COLS)], axis=1)
            wide_ref[out] = wide
            do = nn(wide, w).astype(BF16)
            do_ref[out] = do
            both = (do.astype(F32) * att_ref[out]).T
            for h in range(width // HD):
                delta_ref[h : h + 1, out] = jnp.sum(
                    both[h * HD : (h + 1) * HD], axis=0, keepdims=True
                )
    gw_ref[...] = tn(wide_ref[...], low_ref[...]).astype(BF16)


def mid_gradient(x, w, attended, low, collective):
    pieces = 4
    tokens, width = x.shape
    packed = (tokens // 2, 2 * width)
    return pl.pallas_call(
        functools.partial(mid_kernel, pieces),
        out_shape=(
            jax.ShapeDtypeStruct((tokens, width), BF16),
            jax.ShapeDtypeStruct((8, tokens), F32),
            jax.ShapeDtypeStruct((D, width), BF16),
        ),
        in_specs=[VSPEC] * 4,
        out_specs=(VSPEC,) * 3,
        scratch_shapes=[
            pltpu.VMEM(packed, BF16),
            pltpu.VMEM((COLS,) + packed, BF16),
            pltpu.VMEM((tokens, D), BF16),
            DMA((3, pieces)),
            DMA((3, pieces)),
        ],
        compiler_params=params(collective),
    )(x, w, attended, low)


def col_peers():
    me = lax.axis_index("col")
    return [{"col": (me + k) % COLS} for k in range(1, COLS)]


def to_rows(columns):
    lane = lax.broadcasted_iota(jnp.int32, (columns[0].shape[0], 128), 1)
    v = jnp.zeros(lane.shape, F32)
    for i, column in enumerate(columns):
        v = jnp.where(lane == i, column, v)
    return v.T[:8]


def to_columns(lines):
    place = lax.broadcasted_iota(jnp.int32, (8, lines[0].shape[1]), 0)
    v = jnp.zeros(place.shape, F32)
    for i, one in enumerate(lines):
        v = jnp.where(place == i, one, v)
    v = v.T
    return [v[:, i : i + 1] for i in range(len(lines))]


def share(snd_ref, all_ref, send, recv):
    me = lax.axis_index("col")
    copies = []
    for k, peer in enumerate(col_peers()):
        copy = push(snd_ref, all_ref.at[me], send.at[k], recv.at[k], peer)
        copy.start()
        copies.append(copy)
    all_ref[me] = snd_ref[...]
    for copy in copies:
        copy.wait()


def norm_back(grad, normed, gain, rstd, snd_ref, all_ref, send, recv):
    tokens = grad.shape[0]
    scaled = grad * gain
    sums = [
        jnp.sum(scaled, axis=-1, keepdims=True),
        jnp.sum(scaled * normed, axis=-1, keepdims=True),
    ]
    snd_ref[:, :tokens] = to_rows(sums)
    share(snd_ref, all_ref, send, recv)
    total = all_ref[0, :, :tokens]
    for b in range(1, COLS):
        total = total + all_ref[b, :, :tokens]
    total = total / D
    first, second = to_columns([total[0:1], total[1:2]])
    return rstd * (scaled - first - normed * second)


def line_greet(levels, row, level, partner):
    barrier = pltpu.get_barrier_semaphore()
    me = lax.axis_index("col")
    for k in range(1, COLS):
        peer = {"col": (me + k) % COLS}
        pl.semaphore_signal(barrier, inc=1, device_id=peer, device_id_type=MESH)
    pl.semaphore_signal(barrier, inc=1, device_id={"row": partner}, device_id_type=MESH)

    @pl.when(level > 0)
    def _():
        pl.semaphore_signal(barrier, inc=1, device_id={"row": row - 2}, device_id_type=MESH)

    @pl.when(level < levels - 1)
    def _():
        pl.semaphore_signal(barrier, inc=1, device_id={"row": row + 2}, device_id_type=MESH)

    count = COLS + (level > 0).astype(jnp.int32) + (level < levels - 1).astype(jnp.int32)
    pl.semaphore_wait(barrier, count)


def seen(key_start, query_start, shape, prefix):
    key = key_start + lax.broadcasted_iota(jnp.int32, shape, 0)
    query = query_start + lax.broadcasted_iota(jnp.int32, shape, 1)
    return (key < prefix) | (key <= query)


def forward_kernel(
    group,
    low,
    pieces,
    qb,
    info_ref,
    q_ref,
    kv_ref,
    g_ref,
    out_ref,
    o_ref,
    ob_ref,
    lse_ref,
    ga_ref,
    m_ref,
    acc_ref,
    u_send,
    u_recv,
    d_send,
    d_recv,
    x_send,
    x_recv,
    g_send,
    g_recv,
    e_send,
    e_recv,
):
    levels = group // 2
    row, place, level, side, partner = line_places(group)
    prefix = info_ref[0]
    tokens, width = q_ref.shape
    heads = width // HD
    step = tokens // pieces
    line_greet(levels, row, level, partner)

    def make(at, i, way, src=None):
        part = pl.ds(i * step, step)
        dst = out_ref.at[2 * at + side, part]
        sems = ((u_send, u_recv), (d_send, d_recv), (x_send, x_recv))[way]
        peer = (row + 2, row - 2, partner)[way]
        return push(
            dst if src is None else src.at[part],
            dst,
            sems[0].at[at, i],
            sems[1].at[at, i],
            {"row": peer},
        )

    def other(at, i):
        part = pl.ds(i * step, step)
        dst = out_ref.at[2 * at + 1 - side, part]
        return push(dst, dst, x_send.at[at, i], x_recv.at[at, i], {"row": partner})

    detour = pieces // 2
    top = level == levels - 1
    by_line = top & (side == 1)
    not_across = top & (side == 0)
    lends = (level == levels - 2) & (side == 1)

    def lent(i):
        dst = out_ref.at[0, pl.ds(i * step, step)]
        return push(dst, dst, e_send.at[i], e_recv.at[i], {"row": row + 2})

    def when(cond, run):
        @pl.when(cond)
        def _():
            for i in range(pieces):
                run(i)

    to_up = level < levels - 1
    own_down = (level > 0) & (level < low)
    own_side = (level < low) | (side == 0)
    for i in range(pieces):

        @pl.when(to_up)
        def _(i=i):
            make(level, i, 0, kv_ref).start()

        @pl.when(own_side)
        def _(i=i):
            make(level, i, 2, kv_ref).start()

        @pl.when(own_down)
        def _(i=i):
            make(level, i, 1, kv_ref).start()

    me = lax.axis_index("col")
    wide = []
    for k in range(1, COLS):
        peer = {"col": (me + k) % COLS}
        copy = push(g_ref, ga_ref.at[me], g_send.at[k - 1], g_recv.at[k - 1], peer)
        copy.start()
        wide.append(copy)
    ga_ref[me] = g_ref[...]
    out_ref[place] = kv_ref[...]
    m_ref[...] = jnp.full(m_ref.shape, neg_big, F32)
    acc_ref[...] = jnp.zeros(acc_ref.shape, F32)
    units = [(h, i) for h in range(heads) for i in range(tokens // qb)]

    def block(blk, masked):
        def raw_of(h, i):
            feats = slice(h * HD, (h + 1) * HD)
            raw = nt(out_ref[blk, :, feats], q_ref[i * qb : (i + 1) * qb, feats])
            if masked:
                allowed = seen(blk * tokens, place * tokens + i * qb, raw.shape, prefix)
                raw = jnp.where(allowed, raw, neg_big)
            return raw

        def soften(h, i, raw):
            cols = slice(i * qb, (i + 1) * qb)
            old = m_ref[h : h + 1, cols]
            new = jnp.maximum(old, jnp.max(raw, axis=0, keepdims=True))
            m_ref[h : h + 1, cols] = new
            weights = jnp.exp2((raw - new) * LOG2E).astype(BF16)
            return weights, jnp.exp2((old - new) * LOG2E)

        def gather(h, i, weights, scale):
            cols = slice(i * qb, (i + 1) * qb)
            v = out_ref[blk, :, width + h * HD : width + (h + 1) * HD]
            v_ext = jnp.concatenate([v.T, jnp.ones((16, tokens), BF16)], axis=0)
            acc_ref[h, :, cols] = acc_ref[h, :, cols] * scale + nn(v_ext, weights)

        coming, waiting = raw_of(*units[0]), None
        for n, unit in enumerate(units):
            raw = coming
            if n + 1 < len(units):
                coming = raw_of(*units[n + 1])
            soft = soften(*unit, raw)
            if waiting is not None:
                gather(*waiting)
            waiting = unit + soft
        gather(*waiting)

    def event(e, carry):
        t, cross = e // 2, e % 2
        at = jnp.where(t <= level, level - t, t)
        live = (t <= level) | (t < low)
        line_in = live & (cross == 0)
        coming = t + 1
        via = jnp.where(coming <= level, level - coming, coming)
        relays = (cross == 1) & ((coming <= level) | (coming < low))

        @pl.when(relays & (via < level))
        def _():
            for i in range(pieces):
                make(via, i, 0).wait_recv()

                @pl.when(to_up)
                def _(i=i):
                    make(via, i, 0).start()

                if i < detour:

                    @pl.when(jnp.logical_not((via == 0) & not_across))
                    def _(i=i):
                        make(via, i, 2).start()

                else:
                    make(via, i, 2).start()

        @pl.when(relays & (via > level))
        def _():
            for i in range(pieces):
                make(via, i, 1).wait_recv()

                @pl.when(level > 0)
                def _(i=i):
                    make(via, i, 1).start()

                make(via, i, 2).start()

        comes = live & (cross == 1) & ((at < low) | (at < level) | (side == 1))

        @pl.when(comes)
        def _():
            for i in range(pieces):
                if i >= detour:
                    other(at, i).wait_recv()
                    continue

                @pl.when((at == 0) & by_line)
                def _(i=i):
                    lent(i).wait_recv()

                @pl.when(jnp.logical_not((at == 0) & by_line))
                def _(i=i):
                    other(at, i).wait_recv()

                @pl.when((at == 0) & lends)
                def _(i=i):
                    lent(i).start()

        blk = 2 * at + jnp.where(cross == 0, side, 1 - side)
        needed = line_in | comes

        @pl.when(needed & (blk < place))
        def _():
            block(blk, False)

        @pl.when(needed & (blk >= place))
        def _():
            block(blk, True)

        return carry

    lax.fori_loop(0, 2 * levels, event, 0)

    for h in range(heads):
        total = acc_ref[h, HD : HD + 1, :]
        out = (acc_ref[h, :HD, :] / total).T
        o_ref[:, h * HD : (h + 1) * HD] = out
        ob_ref[:, h * HD : (h + 1) * HD] = out.astype(BF16)
        lse_ref[h : h + 1, :] = m_ref[h : h + 1, :] * LOG2E + jnp.log2(total)

    when(to_up, lambda i: make(level, i, 0, kv_ref).wait_send())
    when(own_side, lambda i: make(level, i, 2, kv_ref).wait_send())
    when(own_down, lambda i: make(level, i, 1, kv_ref).wait_send())
    for k in range(1, levels):
        at = level - k
        when((at >= 0) & to_up, lambda i, at=at: make(at, i, 0).wait_send())
        for i in range(pieces):
            sent = at >= 0
            if i < detour:
                sent = sent & jnp.logical_not((at == 0) & not_across)

            @pl.when(sent)
            def _(at=at, i=i):
                make(at, i, 2).wait_send()

    for k in range(1, low):
        at = level + k
        when((at < low) & (level > 0), lambda i, at=at: make(at, i, 1).wait_send())
        when(at < low, lambda i, at=at: make(at, i, 2).wait_send())
    for i in range(detour):

        @pl.when(lends)
        def _(i=i):
            lent(i).wait_send()

    for copy in wide:
        copy.wait()


def attention_forward(info, q, kv, g, group, low, collective):
    pieces = 4
    levels = group // 2
    tokens, width = q.shape
    heads = width // HD
    return pl.pallas_call(
        functools.partial(forward_kernel, group, low, pieces, tokens // 2),
        out_shape=(
            jax.ShapeDtypeStruct((group,) + kv.shape, kv.dtype),
            jax.ShapeDtypeStruct((tokens, width), F32),
            jax.ShapeDtypeStruct((tokens, width), BF16),
            jax.ShapeDtypeStruct((8, tokens), F32),
            jax.ShapeDtypeStruct((COLS,) + g.shape, g.dtype),
        ),
        in_specs=[SSPEC, VSPEC, VSPEC, VSPEC],
        out_specs=(VSPEC,) * 5,
        scratch_shapes=[
            pltpu.VMEM((8, tokens), F32),
            pltpu.VMEM((heads, HD + 16, tokens), F32),
        ]
        + [DMA((levels, pieces))] * 6
        + [DMA((COLS - 1,))] * 2
        + [DMA((pieces // 2,))] * 2,
        compiler_params=params(collective),
    )(info, q, kv, g)


def backward_kernel(
    group,
    low,
    pieces,
    kb,
    info_ref,
    q_ref,
    kv_ref,
    do_ref,
    lse_ref,
    delta_ref,
    e_ref,
    bias_ref,
    out_ref,
    eo_ref,
    part_ref,
    rx_ref,
    above_ref,
    below_ref,
    snd_ref,
    acc_ref,
    dqt_ref,
    er_ref,
    u_send,
    u_recv,
    d_send,
    d_recv,
    x_send,
    x_recv,
    e_send,
    e_recv,
):
    levels = group // 2
    row, place, level, side, partner = line_places(group)
    prefix = info_ref[0]
    tokens, width = q_ref.shape
    heads = width // HD
    step = tokens // pieces
    line_greet(levels, row, level, partner)
    me = lax.axis_index("col")
    terms = []
    for k in range(1, COLS):
        peer = (me + k) % COLS
        copy = push(
            e_ref.at[peer], er_ref.at[k - 1], e_send.at[k - 1], e_recv.at[k - 1], {"col": peer}
        )
        copy.start()
        terms.append(copy)
    dqt_ref[...] = jnp.zeros(dqt_ref.shape, F32)

    def block(blk, masked, leaves, at):
        def body(j, carry):
            start = pl.multiple_of(j * kb, kb)
            keys = pl.ds(start, kb)
            for h in range(heads):
                feats = slice(h * HD, (h + 1) * HD)
                vals = slice(width + h * HD, width + (h + 1) * HD)
                k, v = kv_ref[blk, keys, feats], kv_ref[blk, keys, vals]
                q, do = q_ref[:, feats], do_ref[:, feats]
                probs = jnp.exp2(nt(k, q) * LOG2E - lse_ref[h : h + 1, :])
                if masked:
                    allowed = seen(blk * tokens + start, place * tokens, probs.shape, prefix)
                    probs = jnp.where(allowed, probs, 0.0)
                grad = (probs * (nt(v, do) - delta_ref[h : h + 1, :])).astype(BF16)
                part_ref[blk, keys, feats] = nn(grad, q).astype(BF16)
                part_ref[blk, keys, vals] = nn(probs.astype(BF16), do).astype(BF16)
                dqt_ref[feats, :] += nn(k.T, grad)

            @pl.when(leaves)
            def _():
                for n in range(kb // step):
                    cross(at, j * (kb // step) + n).start()

            return carry

        lax.fori_loop(0, tokens // kb, body, 0)

    def cross(at, i):
        part = pl.ds(i * step, step)
        return push(
            part_ref.at[2 * at + 1 - side, part],
            rx_ref.at[at, part],
            x_send.at[at, i],
            x_recv.at[at, i],
            {"row": partner},
        )

    def line(at, i, up):
        part = pl.ds(i * step, step)
        sems = (u_send, u_recv) if up else (d_send, d_recv)
        return push(
            snd_ref.at[at, part],
            (below_ref if up else above_ref).at[at, part],
            sems[0].at[at, i],
            sems[1].at[at, i],
            {"row": row + 2 if up else row - 2},
        )

    def gone(at):
        return (at < low) | (at < level) | ((at == level) & (side == 1))

    def comes(at):
        return (at < low) | (at < level) | ((at == level) & (side == 0))

    def total(at, i, from_above, from_below):
        part = pl.ds(i * step, step)
        acc_ref[...] = part_ref[2 * at + side, part].astype(F32)

        @pl.when(comes(at))
        def _():
            cross(at, i).wait_recv()
            acc_ref[...] += rx_ref[at, part].astype(F32)

        if from_above is not None:

            @pl.when(from_above)
            def _():
                line(at, i, False).wait_recv()
                acc_ref[...] += above_ref[at, part].astype(F32)

        if from_below is not None:

            @pl.when(from_below)
            def _():
                line(at, i, True).wait_recv()
                acc_ref[...] += below_ref[at, part].astype(F32)

    not_top = level < levels - 1
    above = jnp.maximum(low - 1 - level, 0)

    def level_of(t):
        return jnp.where(t < above, low - 1 - t, t - above)

    def event(e, carry):
        t, own = e // 2, e % 2
        at = level_of(t)
        live = (t < above) | (at <= level)

        down = t - (levels - level)

        @pl.when((own == 1) & (down >= 0) & (down < level))
        def _():
            for i in range(pieces):
                total(down, i, not_top, None)
                snd_ref[down, pl.ds(i * step, step)] = acc_ref[...].astype(BF16)
                line(down, i, False).start()

        @pl.when((own == 1) & (t >= 1) & (t - 1 < above))
        def _():
            up = level_of(t - 1)
            for i in range(pieces):
                total(up, i, None, level > 0)
                snd_ref[up, pl.ds(i * step, step)] = acc_ref[...].astype(BF16)
                line(up, i, True).start()

        goes = live & (own == 0) & gone(at)
        blk = 2 * at + jnp.where(own == 1, side, 1 - side)
        needed = goes | (live & (own == 1))

        @pl.when(needed & (blk < place))
        def _():
            block(blk, False, goes, at)

        @pl.when(needed & (blk >= place))
        def _():
            block(blk, True, goes, at)

        return carry

    lax.fori_loop(0, 2 * levels, event, 0)
    for copy in terms:
        copy.wait()

    def finish(r, carry):
        total = e_ref[me, r].astype(F32) + bias_ref[...]
        for k in range(COLS - 1):
            total = total + er_ref[k, r].astype(F32)
        eo_ref[r] = total.astype(BF16)
        return carry

    lax.fori_loop(0, e_ref.shape[1], finish, 0)
    out_ref[:, :width] = (dqt_ref[...] * HD**-0.5).T.astype(BF16)

    for i in range(pieces):
        total(level, i, not_top, (level > 0) & (level < low))
        out_ref[pl.ds(i * step, step), width:] = acc_ref[...].astype(BF16)

    for at in range(levels):
        for i in range(pieces):

            @pl.when(gone(at))
            def _(at=at, i=i):
                cross(at, i).wait_send()

            @pl.when(at < level)
            def _(at=at, i=i):
                line(at, i, False).wait_send()

            if at < low:

                @pl.when(at > level)
                def _(at=at, i=i):
                    line(at, i, True).wait_send()


def attention_backward(info, q, kv_all, do, lse, delta, e, bias, group, low, collective):
    pieces = 4
    levels = group // 2
    tokens, width = q.shape
    both = 2 * width
    block = pltpu.VMEM((levels, tokens, both), BF16)
    return pl.pallas_call(
        functools.partial(backward_kernel, group, low, pieces, tokens // 4),
        out_shape=(
            jax.ShapeDtypeStruct((tokens, width + both), BF16),
            jax.ShapeDtypeStruct(e.shape[1:], BF16),
        ),
        in_specs=[SSPEC] + [VSPEC] * 7,
        out_specs=(VSPEC,) * 2,
        scratch_shapes=[
            pltpu.VMEM(kv_all.shape, BF16),
            block,
            block,
            pltpu.VMEM((low, tokens, both), BF16),
            block,
            pltpu.VMEM((tokens // pieces, both), F32),
            pltpu.VMEM((width, tokens), F32),
            pltpu.VMEM((COLS - 1,) + e.shape[1:], BF16),
        ]
        + [DMA((levels, pieces))] * 6
        + [DMA((COLS - 1,))] * 2,
        compiler_params=params(collective),
    )(info, q, kv_all, do, lse, delta, e, bias)


def product(pieces, a_ref, w_ref, feats, out_ref, snd_ref, rx_ref, far_ref, tot_ref, sems, fill):
    send, recv = sems
    me, sib, across, diag = col_places()
    half = a_ref.shape[0] // 2
    step = half // pieces
    per = w_ref.shape[0] // COLS
    width = out_ref.shape[1]

    def weight(who):
        return w_ref[pl.ds(who * per, per)].reshape(width, 4 * width)[:, feats]

    def term(i, w):
        parts = [nt(a_ref[pl.ds(n * half + i * step, step)], w) for n in range(2)]
        return jnp.concatenate(parts, axis=1)

    def near(i, j):
        part = pl.ds(i * step, step)
        return push(
            snd_ref.at[j, part], rx_ref.at[j, part], send.at[j, i], recv.at[j, i], {"col": sib}
        )

    def over(i):
        part = pl.ds(i * step, step)
        return push(tot_ref.at[part], far_ref.at[part], send.at[2, i], recv.at[2, i], {"col": across})

    w = weight(diag)
    for i in range(pieces):
        snd_ref[0, pl.ds(i * step, step)] = term(i, w).astype(BF16)
        near(i, 0).start()
    w = weight(across)
    for i in range(pieces):
        part = pl.ds(i * step, step)
        mine = term(i, w)
        near(i, 0).wait_recv()
        tot_ref[part] = (mine + rx_ref[0, part].astype(F32)).astype(BF16)
        over(i).start()
    w = weight(sib)
    for i in range(pieces):
        snd_ref[1, pl.ds(i * step, step)] = term(i, w).astype(BF16)
        near(i, 1).start()
    fill()
    w = weight(me)
    for i in range(pieces):
        part = pl.ds(i * step, step)
        mine = term(i, w)
        near(i, 1).wait_recv()
        mine = mine + rx_ref[1, part].astype(F32)
        over(i).wait_recv()
        mine = mine + far_ref[part].astype(F32)
        out_ref[part] = mine[:, :width]
        out_ref[pl.ds(half + i * step, step)] = mine[:, width:]
    for i in range(pieces):
        near(i, 0).wait_send()
        near(i, 1).wait_send()
        over(i).wait_send()


def product_scratch(pieces, tokens, width):
    block = pltpu.VMEM((tokens // 2, 2 * width), BF16)
    pair = pltpu.VMEM((2, tokens // 2, 2 * width), BF16)
    return [pair, pair, block, block, DMA((3, pieces)), DMA((3, pieces))]


def branch_kernel(
    pieces,
    a_ref,
    w_ref,
    x_ref,
    s_ref,
    mid_ref,
    normed_ref,
    rstd_ref,
    h_ref,
    snd_ref,
    rx_ref,
    far_ref,
    tot_ref,
    send,
    recv,
    st_ref,
    all_ref,
    st_send,
    st_recv,
):
    greet(col_peers())
    tokens, width = x_ref.shape
    product(
        pieces,
        a_ref,
        w_ref,
        slice(3 * width, 4 * width),
        mid_ref,
        snd_ref,
        rx_ref,
        far_ref,
        tot_ref,
        (send, recv),
        lambda: None,
    )
    mid = x_ref[...].astype(F32) + mid_ref[...] + own_features(s_ref, 4)
    mid_ref[...] = mid
    part_mean = jnp.mean(mid, axis=-1, keepdims=True)
    part_spread = jnp.sum((mid - part_mean) ** 2, axis=-1, keepdims=True)
    st_ref[...] = to_rows([part_mean, part_spread])
    share(st_ref, all_ref, st_send, st_recv)
    mean = sum(all_ref[b, 0:1] for b in range(COLS)) / COLS
    spread = sum(
        all_ref[b, 1:2] + width * (all_ref[b, 0:1] - mean) ** 2 for b in range(COLS)
    )
    mean, rstd = to_columns([mean, lax.rsqrt(spread / D + epsilon)])
    normed = (mid - mean) * rstd
    normed_ref[...] = normed
    rstd_ref[...] = rstd
    h_ref[...] = (normed * own_features(s_ref, 2) + own_features(s_ref, 3)).astype(BF16)


def branch(a, w, x, s, collective):
    pieces = 4
    tokens, width = a.shape
    rows = jax.ShapeDtypeStruct((tokens, width), F32)
    return pl.pallas_call(
        functools.partial(branch_kernel, pieces),
        out_shape=(
            rows,
            rows,
            jax.ShapeDtypeStruct((tokens, 1), F32),
            jax.ShapeDtypeStruct((tokens, width), BF16),
        ),
        in_specs=[VSPEC] * 4,
        out_specs=(VSPEC,) * 4,
        scratch_shapes=product_scratch(pieces, tokens, width)
        + [
            pltpu.VMEM((8, tokens), F32),
            pltpu.VMEM((COLS, 8, tokens), F32),
            DMA((COLS - 1,)),
            DMA((COLS - 1,)),
        ],
        compiler_params=params(collective),
    )(a, w, x, s)


def input_kernel(
    pieces,
    a_ref,
    w_ref,
    e_ref,
    h_ref,
    gwo_ref,
    mid_ref,
    normed_ref,
    rstd_ref,
    s_ref,
    vec_ref,
    gin_ref,
    eo_ref,
    wt_ref,
    all_ref,
    grad_ref,
    snd_ref,
    rx_ref,
    far_ref,
    tot_ref,
    send,
    recv,
    st_ref,
    st_send,
    st_recv,
    e_send,
    e_recv,
):
    rows = e_ref.shape[0]
    row = lax.axis_index("row")
    order = far_first(rows)
    greet([{"row": (row + k) % rows} for k in order] + col_peers())
    home = []
    for n, k in enumerate(order):
        peer = (row + k) % rows
        copy = push(e_ref.at[peer], eo_ref.at[row], e_send.at[n], e_recv.at[n], {"row": peer})
        copy.start()
        home.append(copy)
    eo_ref[row] = e_ref[row]
    tokens, width = grad_ref.shape

    def fill():
        both = [tn(h_ref[...], a_ref[...]).astype(BF16), gwo_ref[...]]
        wt_ref[...] = jnp.concatenate(both, axis=1)

    product(
        pieces,
        a_ref,
        w_ref,
        slice(0, 3 * width),
        grad_ref,
        snd_ref,
        rx_ref,
        far_ref,
        tot_ref,
        (send, recv),
        fill,
    )
    grad, normed = grad_ref[...], normed_ref[...]
    st_ref[:, tokens:] = jnp.zeros((8, st_ref.shape[1] - tokens), F32)
    st_ref[0:1, tokens : tokens + width] = jnp.sum(grad * normed, axis=0, keepdims=True)
    st_ref[1:2, tokens : tokens + width] = jnp.sum(grad, axis=0, keepdims=True)
    st_ref[2:5, tokens : tokens + width] = vec_ref[0:3]
    gin_ref[...] = mid_ref[...] + norm_back(
        grad, normed, own_features(s_ref, 0), rstd_ref[...], st_ref, all_ref, st_send, st_recv
    )
    for copy in home:
        copy.wait()


def input_gradient(a, w, e, h, gwo, mid, normed, rstd, gain, vec, collective):
    pieces = 4
    tokens, width = mid.shape
    wide = tokens + 256
    return pl.pallas_call(
        functools.partial(input_kernel, pieces),
        out_shape=(
            jax.ShapeDtypeStruct((tokens, width), F32),
            jax.ShapeDtypeStruct(e.shape, BF16),
            jax.ShapeDtypeStruct((D, 4 * width), BF16),
            jax.ShapeDtypeStruct((COLS, 8, wide), F32),
        ),
        in_specs=[VSPEC] * 10,
        out_specs=(VSPEC,) * 4,
        scratch_shapes=[pltpu.VMEM((tokens, width), F32)]
        + product_scratch(pieces, tokens, width)
        + [
            pltpu.VMEM((8, wide), F32),
            DMA((COLS - 1,)),
            DMA((COLS - 1,)),
            DMA((e.shape[0] - 1,)),
            DMA((e.shape[0] - 1,)),
        ],
        compiler_params=params(collective),
    )(a, w, e, h, gwo, mid, normed, rstd, gain, vec)


def dispatch_kernel(rows, x_ref, t_ref, out_ref, in_ref, r_send, r_recv, c_send, c_recv):
    me, sib, across, _ = col_places()
    row = lax.axis_index("row")
    order = far_first(rows)
    peers = [(row + k) % rows for k in order]
    greet([{"row": p} for p in peers] + [{"col": sib}, {"col": across}])
    copies = []
    cap = in_ref.shape[1]

    def col(src, dst, k, way):
        return push(
            src, dst, c_send.at[way, k], c_recv.at[way, k], {"col": across if way == 0 else sib}
        )

    done, first = [], []
    for k, peer in enumerate(peers):
        in_ref[peer] = placed(t_ref, x_ref[...], peer, cap)
        copy = push(
            in_ref.at[peer], out_ref.at[me, row], r_send.at[k], r_recv.at[k], {"row": peer}
        )
        copy.start()
        copies.append(copy)
        if k == 1:
            in_ref[row] = placed(t_ref, x_ref[...], row, cap)
            for way in range(2):
                copy = col(in_ref.at[row], out_ref.at[me, row], 0, way)
                copy.start()
                (first if way == 0 else done).append(copy)
    out_ref[me, row] = in_ref[row]
    sources = [row] + [(row + rows - k) % rows for k in order]

    def forward(k):
        first[k].wait_recv()
        src = sources[k]
        copy = col(out_ref.at[across, src], out_ref.at[across, src], k, 2)
        copy.start()
        done.append(copy)

    for k in range(1, rows):
        copies[k - 1].wait_recv()
        block = out_ref.at[me, sources[k]]
        for way in range(2):
            copy = col(block, block, k, way)
            copy.start()
            (first if way == 0 else done).append(copy)
        forward(k - 1)
    forward(rows - 1)
    for copy in copies:
        copy.wait_send()
    for copy in first:
        copy.wait_send()
    for copy in done:
        copy.wait()


def dispatch(x, target, rows, cap, collective):
    block = (rows, cap, 2 * x.shape[1])
    return pl.pallas_call(
        functools.partial(dispatch_kernel, rows),
        out_shape=jax.ShapeDtypeStruct((COLS,) + block, x.dtype),
        in_specs=[VSPEC] * 2,
        out_specs=VSPEC,
        scratch_shapes=[
            pltpu.VMEM(block, x.dtype),
            DMA((rows - 1,)),
            DMA((rows - 1,)),
            DMA((3, rows)),
            DMA((3, rows)),
        ],
        compiler_params=params(collective),
    )(x, target)


def giveback_kernel(
    rows,
    in_ref,
    t_ref,
    cot_ref,
    normed_ref,
    rstd_ref,
    s_ref,
    mid_ref,
    vec_ref,
    sum_ref,
    out_ref,
    rx_ref,
    far_ref,
    tot_ref,
    fin_ref,
    st_ref,
    all_ref,
    send,
    recv,
    r_send,
    r_recv,
    st_send,
    st_recv,
):
    me, sib, across, diag = col_places()
    row = lax.axis_index("row")
    order = [(row + k) % rows for k in far_first(rows)] + [row]
    greet([{"row": p} for p in order[:-1]] + col_peers())

    def near(k, j):
        who = diag if j == 0 else sib
        return push(
            in_ref.at[who, order[k]], rx_ref.at[j, k], send.at[j, k], recv.at[j, k], {"col": sib}
        )

    def over(k):
        return push(tot_ref.at[k], far_ref.at[k], send.at[2, k], recv.at[2, k], {"col": across})

    def home(k):
        return push(
            fin_ref.at[k], out_ref.at[row], r_send.at[k], r_recv.at[k], {"row": order[k]}
        )

    for k in range(rows):
        near(k, 0).start()
        near(k, 1).start()

    def finish(k):
        near(k, 1).wait_recv()
        over(k).wait_recv()
        total = in_ref[me, order[k]].astype(F32) + rx_ref[1, k].astype(F32)
        total = total + far_ref[k].astype(F32)
        if k == rows - 1:
            out_ref[row] = total.astype(BF16)
        else:
            fin_ref[k] = total.astype(BF16)
            home(k).start()

    for k in range(rows):
        near(k, 0).wait_recv()
        tot_ref[k] = (in_ref[across, order[k]].astype(F32) + rx_ref[0, k].astype(F32)).astype(BF16)
        over(k).start()
        if k >= 1:
            finish(k - 1)
    finish(rows - 1)
    cap = out_ref.shape[1]
    sum_ref[...] = combined(t_ref, out_ref[row], row, cap)
    for k, gap in enumerate(far_first(rows)):
        source = (row + rows - gap) % rows
        home(k).wait_recv()
        sum_ref[...] += combined(t_ref, out_ref[source], source, cap)
    grad, normed = sum_ref[...], normed_ref[...]
    mid = cot_ref[...].astype(F32) + norm_back(
        grad, normed, own_features(s_ref, 2), rstd_ref[...], st_ref, all_ref, st_send, st_recv
    )
    mid_ref[...] = mid
    vec_ref[...] = jnp.zeros(vec_ref.shape, F32)
    vec_ref[0:1] = jnp.sum(grad * normed, axis=0, keepdims=True)
    vec_ref[1:2] = jnp.sum(grad, axis=0, keepdims=True)
    vec_ref[2:3] = jnp.sum(mid, axis=0, keepdims=True)
    for k in range(rows):
        near(k, 0).wait_send()
        near(k, 1).wait_send()
        over(k).wait_send()
        if k < rows - 1:
            home(k).wait_send()


def giveback(parts, target, cot, normed, rstd, gain, rows, collective):
    block = parts.shape[2:]
    one = pltpu.VMEM((rows,) + block, BF16)
    return pl.pallas_call(
        functools.partial(giveback_kernel, rows),
        out_shape=(
            jax.ShapeDtypeStruct(cot.shape, F32),
            jax.ShapeDtypeStruct((8, cot.shape[1]), F32),
        ),
        in_specs=[VSPEC] * 6,
        out_specs=(VSPEC,) * 2,
        scratch_shapes=[
            pltpu.VMEM(cot.shape, F32),
            one,
            pltpu.VMEM((2, rows) + block, BF16),
            one,
            one,
            one,
            pltpu.VMEM((8, cot.shape[0]), F32),
            pltpu.VMEM((COLS, 8, cot.shape[0]), F32),
            DMA((3, rows)),
            DMA((3, rows)),
            DMA((rows - 1,)),
            DMA((rows - 1,)),
            DMA((COLS - 1,)),
            DMA((COLS - 1,)),
        ],
        compiler_params=params(collective),
    )(parts, target, cot, normed, rstd, gain)


def end_kernel(
    rows,
    w_ref,
    s_ref,
    e_ref,
    t_ref,
    mid_ref,
    wo_ref,
    so_ref,
    lo_ref,
    px_ref,
    pt_ref,
    wr_ref,
    sr_ref,
    p_send,
    p_recv,
    l_send,
    l_recv,
    send,
    recv,
):
    row, _, level, side, partner = line_places(rows)
    levels = rows // 2
    peers = [(row + k) % rows for k in far_first(rows)]
    greet([{"row": p} for p in peers])
    gaps = far_first(levels)
    targets = [(level + k) % levels for k in gaps] + [level]

    def cross(n):
        src = w_ref.at[2 * targets[n] + 1 - side]
        return push(src, px_ref.at[n], p_send.at[n], p_recv.at[n], {"row": partner})

    def along(n):
        peer = {"row": 2 * targets[n] + side}
        return push(pt_ref.at[n], wr_ref.at[n], l_send.at[n], l_recv.at[n], peer)

    def total(n):
        return w_ref[2 * targets[n] + side].astype(F32) + px_ref[n].astype(F32)

    for n in range(levels):
        cross(n).start()
    copies = []
    for k, peer in enumerate(peers):
        copy = push(s_ref.at[peer], sr_ref.at[k], send.at[k], recv.at[k], {"row": peer})
        copy.start()
        copies.append(copy)
    for n in range(levels - 1):
        cross(n).wait_recv()
        pt_ref[n] = total(n).astype(BF16)
        along(n).start()
    result = mid_ref[...]
    for r in range(rows):
        result = result + combined(t_ref, e_ref[r], r, e_ref.shape[1])
    lo_ref[...] = result.astype(BF16)
    small = s_ref[row]
    for k, copy in enumerate(copies):
        copy.wait_recv()
        small = small + sr_ref[k]
    so_ref[...] = small
    cross(levels - 1).wait_recv()
    mine = total(levels - 1)
    for n in range(levels - 1):
        along(n).wait_recv()
        mine = mine + wr_ref[n].astype(F32)
    wo_ref[...] = mine
    for n in range(levels):
        cross(n).wait_send()
        if n < levels - 1:
            along(n).wait_send()
    for copy in copies:
        copy.wait_send()


def end_scatter(w, s, outs, target, mid, rows, collective):
    levels = rows // 2
    one = w.shape[1:]
    return pl.pallas_call(
        functools.partial(end_kernel, rows),
        out_shape=(
            jax.ShapeDtypeStruct(one, F32),
            jax.ShapeDtypeStruct(s.shape[1:], F32),
            jax.ShapeDtypeStruct(mid.shape, BF16),
        ),
        in_specs=[VSPEC] * 5,
        out_specs=(VSPEC,) * 3,
        scratch_shapes=[
            pltpu.VMEM((levels,) + one, w.dtype),
            pltpu.VMEM((levels - 1,) + one, w.dtype),
            pltpu.VMEM((levels - 1,) + one, w.dtype),
            pltpu.VMEM((rows - 1,) + s.shape[1:], s.dtype),
            DMA((levels,)),
            DMA((levels,)),
            DMA((levels - 1,)),
            DMA((levels - 1,)),
            DMA((rows - 1,)),
            DMA((rows - 1,)),
        ],
        compiler_params=params(collective),
    )(w, s, outs, target, mid)


def expert_kernel(
    x_ref,
    g_ref,
    up_hbm,
    bias_ref,
    down_hbm,
    part_ref,
    gx_ref,
    gup_hbm,
    gbu_ref,
    gdown_hbm,
    gbd_ref,
    up_ref,
    down_ref,
    gup_ref,
    gdown_ref,
    xs_ref,
    gs_ref,
    sum_ref,
    gsum_ref,
    in_sems,
    out_sems,
):
    cols, rows, cap, both = x_ref.shape
    width = both // 2
    slots = rows * cap
    count, _, hidden_units = up_ref.shape
    chunk = 256
    loads = []
    for e in range(count):
        for j, (src, dst) in enumerate(((up_hbm, up_ref), (down_hbm, down_ref))):
            copy = pltpu.make_async_copy(src.at[e], dst.at[e], in_sems.at[j, e])
            copy.start()
            loads.append(copy)

    def gup_out(e, f):
        cut = pl.ds(pl.multiple_of(f * chunk, chunk), chunk)
        return pltpu.make_async_copy(
            gup_ref.at[e, :, cut], gup_hbm.at[e, :, cut], out_sems.at[0, e, f]
        )

    def gdown_out(e, f):
        cut = pl.ds(pl.multiple_of(f * chunk, chunk), chunk)
        return pltpu.make_async_copy(
            gdown_ref.at[e, cut], gdown_hbm.at[e, cut], out_sems.at[1, e, f]
        )

    for e in range(count):
        lanes = slice(e * width, (e + 1) * width)
        for ref, dst in ((x_ref, xs_ref), (g_ref, gs_ref)):
            blocks = [ref[b].reshape(slots, both)[:, lanes] for b in range(cols)]
            dst[...] = jnp.concatenate(blocks, axis=1)
        gbd_ref[e] = jnp.sum(gs_ref[...].astype(F32), axis=0, keepdims=True)
        sum_ref[...] = jnp.zeros(sum_ref.shape, F32)
        gsum_ref[...] = jnp.zeros(gsum_ref.shape, F32)
        loads[2 * e].wait()
        loads[2 * e + 1].wait()

        def body(f, carry, e=e):
            cut = pl.ds(pl.multiple_of(f * chunk, chunk), chunk)
            x, g = xs_ref[...], gs_ref[...]
            up, down = up_ref[e, :, cut], down_ref[e, cut, :]
            pre = nn(x, up) + bias_ref[e, :, cut].astype(F32)
            cdf = 0.5 * (1.0 + lax.erf(pre * (0.5**0.5)))
            slope = cdf + pre * (jnp.exp(-0.5 * pre * pre) * 0.3989422804014327)
            hidden = (pre * cdf).astype(BF16)
            grad = nt(g, down) * slope
            grad = grad.astype(BF16)
            sum_ref[...] += nn(hidden, down)
            gsum_ref[...] += nt(grad, up)
            gdown_ref[e, cut, :] = tn(hidden, g)
            gdown_out(e, f).start()
            gup_ref[e, :, cut] = tn(x, grad)
            gup_out(e, f).start()
            gbu_ref[e, :, cut] = jnp.sum(grad.astype(F32), axis=0, keepdims=True)
            return carry

        lax.fori_loop(0, hidden_units // chunk, body, 0)
        for b in range(cols):
            cut = slice(b * width, (b + 1) * width)
            part_ref[b, :, :, lanes] = sum_ref[:, cut].astype(BF16).reshape(rows, cap, width)
            gx_ref[b, :, :, lanes] = gsum_ref[:, cut].astype(BF16).reshape(rows, cap, width)
    for e in range(count):
        for f in range(hidden_units // chunk):
            gdown_out(e, f).wait()
            gup_out(e, f).wait()


def experts(x, g, w_up, bias_up, w_down):
    cols, rows, cap, _ = x.shape
    count, features, hidden = w_up.shape
    slots = rows * cap
    anywhere = pl.BlockSpec(memory_space=pl.ANY)
    return pl.pallas_call(
        expert_kernel,
        out_shape=(
            jax.ShapeDtypeStruct(x.shape, BF16),
            jax.ShapeDtypeStruct(x.shape, BF16),
            jax.ShapeDtypeStruct(w_up.shape, F32),
            jax.ShapeDtypeStruct((count, 1, hidden), F32),
            jax.ShapeDtypeStruct(w_down.shape, F32),
            jax.ShapeDtypeStruct((count, 1, features), F32),
        ),
        in_specs=[VSPEC, VSPEC, anywhere, VSPEC, anywhere],
        out_specs=(VSPEC, VSPEC, anywhere, VSPEC, anywhere, VSPEC),
        scratch_shapes=[
            pltpu.VMEM(w_up.shape, BF16),
            pltpu.VMEM(w_down.shape, BF16),
            pltpu.VMEM(w_up.shape, F32),
            pltpu.VMEM(w_down.shape, F32),
            pltpu.VMEM((slots, features), BF16),
            pltpu.VMEM((slots, features), BF16),
            pltpu.VMEM((slots, features), F32),
            pltpu.VMEM((slots, features), F32),
            DMA((2, count)),
            DMA((2, count, hidden // 256)),
        ],
        compiler_params=params(),
    )(x, g, w_up, bias_up.reshape(count, 1, hidden), w_down)


def per_device(
    layer_in,
    cotangent,
    token_ids,
    hash_table,
    prefix_len,
    w_query,
    w_key,
    w_value,
    w_output,
    bias_query,
    bias_value,
    gain_attn,
    shift_attn,
    gain_moe,
    shift_moe,
    bias_output,
    w_up,
    bias_up,
    w_down,
    bias_down,
):
    rows = lax.axis_size("row")
    row = lax.axis_index("row")
    col = lax.axis_index("col")
    tokens, width = layer_in.shape
    heads = width // HD
    seq_len = min(LENGTH, tokens * rows)
    group = seq_len // tokens
    low = -(-PREFIX_MAX // (2 * tokens))
    share = w_query.shape[0]
    bias_share = bias_query.shape[0]

    def line(v):
        return jnp.pad(v.astype(F32), (0, 128 - v.shape[0]))

    small = jnp.stack(
        [
            line(gain_attn),
            line(shift_attn),
            line(gain_moe),
            line(shift_moe),
            line(bias_output),
            line(bias_query.T.reshape(-1)),
            line(bias_value.T.reshape(-1)),
            jnp.zeros((128,), F32),
        ]
    )
    expert_total = EXP_DEV * rows
    capacity = max(2, 2 * tokens // expert_total)
    table = jnp.pad(hash_table, (0, -hash_table.shape[0] % (128 * 128)))
    table = table.reshape(-1, 128).astype(BF16)

    weights = jnp.concatenate([w_query, w_key, w_value, w_output], axis=1)
    x_all, g_own, w_all, s_all, target = start_gather(
        layer_in, cotangent, token_ids[None], table, weights, small, rows, capacity
    )

    queries, keys_values, h_one, normed_one, rstd_one = project(x_all, w_all, s_all)
    seq_hit = row // group == jnp.arange(prefix_len.shape[0], dtype=jnp.int32)
    prefix = jnp.sum(jnp.where(seq_hit, prefix_len, 0))
    info = prefix.astype(jnp.int32).reshape(1)
    kv_all, attended, attended_low, lse, g_all = attention_forward(
        info, queries, keys_values, g_own, group, low, 1
    )
    mid, normed_two, rstd_two, h_two = branch(attended_low, w_all, layer_in, s_all, 2)

    received = dispatch(h_two, target, rows, capacity, 4)
    parts, grad_parts, grad_w_up, grad_bias_up, grad_w_down, grad_bias_down = experts(
        received, g_all, w_up, bias_up, w_down
    )
    grad_mid, vectors = giveback(
        grad_parts, target, cotangent, normed_two, rstd_two, s_all, rows, 5
    )
    grad_attended, delta, grad_w_out = mid_gradient(grad_mid, w_all, attended, attended_low, 7)
    down_own = lax.dynamic_slice_in_dim(bias_down, col * width, width, 1).astype(F32)
    down_own = down_own.reshape(1, EXP_DEV * width)
    grad_qkv, outs = attention_backward(
        info,
        queries,
        kv_all,
        grad_attended,
        lse,
        delta,
        parts,
        down_own,
        group,
        low,
        8,
    )
    grad_bias = jnp.sum(grad_qkv, axis=0, dtype=F32)
    grad_in, outs, weight_terms, shared = input_gradient(
        grad_qkv,
        w_all,
        outs,
        h_one,
        grad_w_out,
        grad_mid,
        normed_one,
        rstd_one,
        s_all,
        vectors,
        9,
    )
    vectors = shared[:, :5, tokens : tokens + width]
    vectors = vectors.transpose(1, 0, 2).reshape(5, rows, share).transpose(1, 0, 2)

    def by_row(v):
        v = v.reshape(heads, rows, bias_share).transpose(1, 0, 2).reshape(rows, 1, -1)
        return jnp.pad(v, ((0, 0), (0, 0), (0, 128 - v.shape[2])))

    small_terms = jnp.concatenate(
        [
            jnp.pad(vectors, ((0, 0), (0, 0), (0, 128 - share))),
            by_row(grad_bias[:width]),
            by_row(grad_bias[2 * width :]),
            jnp.zeros((rows, 1, 128), F32),
        ],
        axis=1,
    )
    weight_terms = weight_terms.reshape(rows, share, 4 * width)
    weight_sums, small_sums, layer_out = end_scatter(
        weight_terms, small_terms, outs, target, mid, rows, 11
    )

    def bias_back(v):
        return v[: heads * bias_share].reshape(heads, bias_share).T

    return (
        layer_out,
        grad_in,
        weight_sums[:, :width],
        weight_sums[:, width : 2 * width],
        weight_sums[:, 2 * width : 3 * width],
        weight_sums[:, 3 * width :],
        bias_back(small_sums[5]),
        bias_back(small_sums[6]),
        small_sums[0, :share],
        small_sums[1, :share],
        small_sums[2, :share],
        small_sums[3, :share],
        small_sums[4, :share],
        grad_w_up,
        grad_bias_up[:, 0],
        grad_w_down,
        grad_bias_down[:, 0],
    )


def solution(mesh):
    placed = (
        P("row", "col"),
        P("row", "col"),
        P("row"),
        P(),
        P(),
        P("row", "col"),
        P("row", "col"),
        P("row", "col"),
        P("row", "col"),
        P("row", "col"),
        P("row", "col"),
        P("row"),
        P("row"),
        P("row"),
        P("row"),
        P("row"),
        P("row", None, "col"),
        P("row", "col"),
        P("row", "col", None),
        P("row", None),
    )
    return jax.shard_map(
        per_device,
        mesh=mesh,
        in_specs=placed,
        out_specs=(
            P("row", "col"),
            P("row", "col"),
            P("row", "col"),
            P("row", "col"),
            P("row", "col"),
            P("row", "col"),
            P("row", "col"),
            P("row", "col"),
            P("row"),
            P("row"),
            P("row"),
            P("row"),
            P("row"),
            P("row", None, "col"),
            P("row", "col"),
            P("row", "col", None),
            P("row", None),
        ),
        check_vma=False,
    )
```
